32 devices in a mesh: dp: 8 (over z, y), section: 4 (over x, core).
Axes of the slice: x: 2, y: 2, z: 4, core: 2. Of those that a mesh axis runs over, the one named last changes fastest.
Arguments:
- vis_embed: bfloat16 [12288, 768], P(('dp', 'section')), may hold values from -6 to 6
- latent_cot: bfloat16 [12288, 768], P(('dp', 'section')), may hold values from -6 to 6
- reg_queries: bfloat16 [12288, 768], P(('dp', 'section')), may hold values from -6 to 6
- out_cot: bfloat16 [12288, 768], P(('dp', 'section')), may hold values from -6 to 6
- section_matrix: bfloat16 [4, 768, 3072], P('section')
- down_weight: bfloat16 [6144, 768], P('section'), may hold values from -0.109375 to 0.109375
- enc_vectors: float32 [6, 768], replicated, as said below
- reg_vectors: float32 [10, 768], replicated, as said below
- mlp_vectors: float32 [2, 4, 768], replicated, as said below
- hidden_bias: float32 [2, 3072], replicated, may hold values from -1.5 to 1.5
- pos_table: float32 [256, 768], replicated, may hold values from -6 to 6
- image_lengths: int32 [32, 4], P('dp'), may hold values from 1 to 128, as said below
- vis_index: int32 [12288], P('dp'), may hold values from 0 to 255, as said below
- mask_index: int32 [12288], P('dp'), may hold values from 0 to 255, as said below
Outputs:
- latents: bfloat16 [12288, 768], P(('dp', 'section'))
- regressed: bfloat16 [12288, 768], P(('dp', 'section'))
- vis_grad: bfloat16 [12288, 768], P(('dp', 'section'))
- query_grad: bfloat16 [12288, 768], P(('dp', 'section'))
- grad_section_matrix: float32 [4, 768, 3072], P('section')
- grad_down: float32 [6144, 768], P('section')
- grad_enc_vectors: float32 [6, 768], replicated
- grad_reg_vectors: float32 [10, 768], replicated
- grad_mlp_vectors: float32 [2, 4, 768], replicated
- grad_hidden_bias: float32 [2, 3072], replicated
The draws below stay inside these ranges and needn't reach their ends.
Inputs may be any that keep to these rules, and one draw needn't show every extreme that they name: `image_lengths`: each row sums to 384, and its largest entry is 128. `vis_index`: for an image with n visible patches, its n visible places and the n masked places at the same rows are 0 to 2 n - 1, each once. `mask_index`: see vis_index. `enc_vectors`: gain and layer-scale rows are positive. `reg_vectors`: gain and layer-scale rows are positive. `mlp_vectors`: gain and layer-scale rows are positive.
All inputs are finite; a program needn't handle non-finite values.
Results may differ from the reference program's by a relative error of at most 0.015.
Values may be sent and summed in bfloat16 or wider, within the bound.
A program may use at most 192 MiB of HBM per device.

```python
import math
import jax
import jax.numpy as jnp
from jax import lax

D = 768
H = 12
FF = 3072
LONGEST = 128
POSITIONS = 256
IMGS = 4
CAP = 384
PACKS = 32
TOKENS = 12288


def pack_lengths(key):
    remaining_items = IMGS - 1
    rest_total = CAP - LONGEST
    length_floor = rest_total // remaining_items
    leftover_count = rest_total - length_floor * remaining_items
    reach_limit = max(1, min(length_floor - 1, LONGEST - length_floor - 1))
    random_draws = jax.random.randint(jax.random.fold_in(key, 11), (PACKS, remaining_items), 0, reach_limit)
    jitter_amount = random_draws - jnp.roll(random_draws, 1, axis=1)
    surplus_rows = (jnp.arange(remaining_items) < leftover_count).astype(jnp.int32)
    remainder_lengths = length_floor + surplus_rows[None, :] + jitter_amount
    full_rows = jnp.concatenate([jnp.full((PACKS, 1), LONGEST, jnp.int32), remainder_lengths.astype(jnp.int32)], axis=1)
    shift_by = jax.random.randint(jax.random.fold_in(key, 12), (PACKS,), 0, IMGS)
    rolled_cols = (jnp.arange(IMGS)[None, :] - shift_by[:, None]) % IMGS
    return jnp.take_along_axis(full_rows, rolled_cols, axis=1).astype(jnp.int32)


def patch_places(key):
    lengths = pack_lengths(key)
    image_ends = jnp.cumsum(lengths, axis=1)
    image_starts = image_ends - lengths
    slot_ids = jnp.arange(CAP)
    image_ids = jnp.sum(slot_ids[None, :, None] >= image_ends[:, None, :], axis=-1).astype(jnp.int32)
    local_index = slot_ids[None, :] - jnp.take_along_axis(image_starts, image_ids, axis=1)
    image_count = jnp.take_along_axis(lengths, image_ids, axis=1)
    grid_ids = jnp.arange(POSITIONS)
    raw_scores = jax.random.randint(jax.random.fold_in(key, 13), (PACKS, IMGS, POSITIONS), 0, 1 << 20) * POSITIONS + grid_ids[None, None, :]
    raw_scores = jnp.where(grid_ids[None, None, :] < 2 * lengths[:, :, None], raw_scores, (1 << 30) + grid_ids[None, None, :])
    order_rows = jnp.argsort(raw_scores, axis=-1, stable=True).astype(jnp.int32).reshape(PACKS, IMGS * POSITIONS)
    visible = jnp.take_along_axis(order_rows, image_ids * POSITIONS + local_index, axis=1)
    masked = jnp.take_along_axis(order_rows, image_ids * POSITIONS + image_count + local_index, axis=1)
    return (visible.reshape(-1).astype(jnp.int32), masked.reshape(-1).astype(jnp.int32))


def vector_rows(key, pattern, columns):
    row_total = len(pattern)
    gain_draw = jnp.exp(jax.random.uniform(jax.random.fold_in(key, 31), (row_total, columns), jnp.float32, math.log(0.5), math.log(2.0)))
    offset_draw = 0.3 * jax.random.normal(jax.random.fold_in(key, 32), (row_total, columns), jnp.float32)
    gain_mask = jnp.array(pattern, jnp.float32)[:, None]
    return gain_mask * gain_draw + (1.0 - gain_mask) * offset_draw


def draw_image_lengths(key, part):
    return pack_lengths(key)


def draw_vis_index(key, part):
    return patch_places(key)[0]


def draw_mask_index(key, part):
    return patch_places(key)[1]


def draw_section_matrix(key, part):
    values = jax.random.normal(jax.random.fold_in(key, 21), (4, D, FF), jnp.float32)
    column_ids = jnp.arange(FF)
    section_ids = jnp.arange(4)
    widened = ((section_ids[:, None] % 2 == 0) & (column_ids[None, :] >= 3 * D)).astype(jnp.float32)
    scale_rows = (1.0 + 3.0 * widened) / math.sqrt(D)
    return (values * scale_rows[:, None, :]).astype(jnp.bfloat16)


def draw_enc_vectors(key, part):
    return vector_rows(jax.random.fold_in(key, 41), (1, 0, 0, 0, 0, 1), D)


def draw_reg_vectors(key, part):
    return vector_rows(jax.random.fold_in(key, 42), (1, 0, 1, 0, 1, 0, 0, 0, 0, 1), D)


def draw_mlp_vectors(key, part):
    first_block = vector_rows(jax.random.fold_in(key, 43), (1, 0, 0, 1), D)
    second_block = vector_rows(jax.random.fold_in(key, 44), (1, 0, 0, 1), D)
    return jnp.stack([first_block, second_block])


def block_scale(rng, dims, shards, low, top_value):
    def one(position, parts):
        steps = jax.random.uniform(jax.random.fold_in(jax.random.fold_in(rng, 6), position), (parts,), jnp.float32, low / len(shards), top_value / len(shards))
        return jnp.repeat(jnp.exp(steps), dims[position] // parts).reshape((-1,) + (1,) * (len(dims) - position - 1))

    factor_of = one(*shards[0])
    for cut in shards[1:]:
        factor_of = factor_of * one(*cut)
    return factor_of


def bell_draw(own_key, dims, scale, most, pieces=(), kind=jnp.bfloat16):
    drawn = scale * jax.random.normal(own_key, dims, jnp.float32)
    if pieces:
        drawn = drawn * block_scale(own_key, dims, pieces, -0.22, 0.18)
    return jnp.clip(drawn, -most, most).astype(kind)


def setup_inputs(seed: int = 0) -> dict:
    key_list = jax.random.split(jax.random.key(seed), 15)
    return {
        "vis_embed": bell_draw(key_list[0], (TOKENS, D), 1.0, 6.0, ((0, 32),)),
        "latent_cot": bell_draw(key_list[1], (TOKENS, D), 1.0, 6.0, ((0, 32),)),
        "reg_queries": bell_draw(key_list[2], (TOKENS, D), 1.0, 6.0, ((0, 32),)),
        "out_cot": bell_draw(key_list[3], (TOKENS, D), 1.0, 6.0, ((0, 32),)),
        "section_matrix": draw_section_matrix(jax.random.fold_in(key_list[14], 71), 0),
        "down_weight": bell_draw(key_list[5], (2 * FF, D), FF ** -0.5, 0.109375, ((0, 4),)),
        "enc_vectors": draw_enc_vectors(jax.random.fold_in(key_list[14], 71), 0),
        "reg_vectors": draw_reg_vectors(jax.random.fold_in(key_list[14], 71), 0),
        "mlp_vectors": draw_mlp_vectors(jax.random.fold_in(key_list[14], 71), 0),
        "hidden_bias": bell_draw(key_list[9], (2, FF), 0.3, 1.5, (), jnp.float32),
        "pos_table": bell_draw(key_list[10], (POSITIONS, D), 1.0, 6.0, (), jnp.float32),
        "image_lengths": draw_image_lengths(jax.random.fold_in(key_list[14], 71), 0),
        "vis_index": draw_vis_index(jax.random.fold_in(key_list[14], 71), 0),
        "mask_index": draw_mask_index(jax.random.fold_in(key_list[14], 71), 0),
    }


epsilon = 1e-06
masked_score = -1e+30

@jax.custom_vjp
def low(v):
    return lax.optimization_barrier(v.astype(jnp.bfloat16)).astype(jnp.float32)

@jax.custom_vjp
def low_back(v):
    return v

def low_keep(v):
    return (low(v), None)

def low_pass(kept, grad):
    return (grad,)

def back_keep(v):
    return (v, None)

def back_low(kept, grad):
    return (low(grad),)
low.defvjp(low_keep, low_pass)
low_back.defvjp(back_keep, back_low)

def both_ways(value):
    return low_back(low(value))

def product(left_side, right_side):
    return jnp.dot(left_side, right_side, precision=lax.Precision.HIGHEST)

def layer_norm(values, gain_rows, offsets):
    average = lax.optimization_barrier(jnp.mean(values, axis=-1, keepdims=True))
    centred = values - average
    spread = lax.optimization_barrier(jnp.mean(centred * centred, axis=-1, keepdims=True))
    return centred * lax.rsqrt(spread + epsilon) * gain_rows + offsets

def attend(query_rows, key_rows, value_rows, allowed):
    row_count = query_rows.shape[0]
    key_number = key_rows.shape[0]
    head_width = query_rows.shape[1] // H
    heads_q = query_rows.reshape(row_count, H, head_width)
    heads_k = key_rows.reshape(key_number, H, head_width)
    heads_v = value_rows.reshape(key_number, H, head_width)
    scores = jnp.einsum('qhd,khd->hqk', heads_q, heads_k, precision=lax.Precision.HIGHEST) * head_width ** (-0.5)
    scores = jnp.where(allowed[None], low_back(scores), masked_score)
    prob_rows = low(jax.nn.softmax(scores, axis=-1))
    mixed_heads = jnp.einsum('hqk,khd->qhd', prob_rows, heads_v, precision=lax.Precision.HIGHEST)
    return mixed_heads.reshape(row_count, H * head_width)

def encoder_attention(residual, matrix, vectors, allowed):
    model_width = residual.shape[1]
    normed = low(layer_norm(residual, vectors[0], vectors[1]))
    query_rows = both_ways(product(normed, matrix[:, :model_width]) + vectors[2])
    key_rows = both_ways(product(normed, matrix[:, model_width:2 * model_width]))
    value_rows = both_ways(product(normed, matrix[:, 2 * model_width:3 * model_width]) + vectors[3])
    mixed_heads = both_ways(attend(query_rows, key_rows, value_rows, allowed))
    branch = low_back(product(mixed_heads, matrix[:, 3 * model_width:].T) + vectors[4])
    return residual + vectors[5] * branch

def regressor_attention(latent_rows, queries, pos_vis, pos_mask, matrix, vectors, allowed):
    model_width = queries.shape[1]
    q_source = queries + pos_mask
    k_source = jnp.concatenate([latent_rows + pos_vis, q_source], axis=0)
    v_source = jnp.concatenate([latent_rows, queries], axis=0)
    q_normed = low(layer_norm(q_source, vectors[0], vectors[1]))
    k_normed = low(layer_norm(k_source, vectors[2], vectors[3]))
    v_normed = low(layer_norm(v_source, vectors[4], vectors[5]))
    query_rows = both_ways(product(q_normed, matrix[:, :model_width]) + vectors[6])
    key_rows = both_ways(product(k_normed, matrix[:, model_width:2 * model_width]))
    value_rows = both_ways(product(v_normed, matrix[:, 2 * model_width:3 * model_width]) + vectors[7])
    mixed_heads = both_ways(attend(query_rows, key_rows, value_rows, allowed))
    branch = low_back(product(mixed_heads, matrix[:, 3 * model_width:].T) + vectors[8])
    return queries + vectors[9] * branch

def feed_forward(residual, up_matrix, down_matrix, vectors, hidden_offset):
    normed = low(layer_norm(residual, vectors[0], vectors[1]))
    hidden = low_back(product(normed, up_matrix) + hidden_offset)
    active = low(jax.nn.gelu(hidden, approximate=False))
    branch = low_back(product(active, down_matrix) + vectors[2])
    return residual + vectors[3] * branch

def pack_forward(pack_parts, weights):
    vis_rows, queries, images, pos_vis, pos_mask = pack_parts
    matrices, down_rows, enc_vectors, reg_vectors, mlp_vectors, hidden_bias = weights
    hidden_width = matrices.shape[2]
    same_image = images[:, None] == images[None, :]
    image_keys = images[:, None] == jnp.concatenate([images, images])[None, :]
    enc_out = both_ways(encoder_attention(vis_rows, matrices[0], enc_vectors, same_image))
    latents = low(feed_forward(enc_out, matrices[1], down_rows[:hidden_width], mlp_vectors[0], hidden_bias[0]))
    latent_sent = low_back(latents)
    reg_out = both_ways(regressor_attention(latent_sent, queries, pos_vis, pos_mask, matrices[2], reg_vectors, image_keys))
    regressed = low(feed_forward(reg_out, matrices[3], down_rows[hidden_width:], mlp_vectors[1], hidden_bias[1]))
    return (latents, regressed)

def reference(vis_embed, latent_cot, reg_queries, out_cot, section_matrix, down_weight, enc_vectors, reg_vectors, mlp_vectors, hidden_bias, pos_table, image_lengths, vis_index, mask_index):
    bundle_count = image_lengths.shape[0]
    model_width = vis_embed.shape[1]

    def shaped(array):
        return array.astype(jnp.float32).reshape(bundle_count, CAP, model_width)
    image_ends = jnp.cumsum(image_lengths, axis=1, dtype=jnp.int32)
    images = lax.optimization_barrier(jnp.sum(jnp.arange(CAP, dtype=jnp.int32)[None, :, None] >= image_ends[:, None, :], axis=-1, dtype=jnp.int32)).astype(jnp.int32)
    pos_rows = pos_table.astype(jnp.float32)
    pos_vis = pos_rows[vis_index].reshape(bundle_count, CAP, model_width)
    pos_mask = pos_rows[mask_index].reshape(bundle_count, CAP, model_width)

    def forward(vis_rows, queries, matrices, down_rows, enc_vec, reg_vec, mlp_vec, hidden_vec):
        weights = (matrices, down_rows, enc_vec, reg_vec, mlp_vec, hidden_vec)

        def one_pack(pack_parts):
            return pack_forward(pack_parts, weights)
        return lax.map(jax.checkpoint(one_pack), (vis_rows, queries, images, pos_vis, pos_mask))
    primals = (shaped(vis_embed), shaped(reg_queries), section_matrix.astype(jnp.float32), down_weight.astype(jnp.float32), enc_vectors.astype(jnp.float32), reg_vectors.astype(jnp.float32), mlp_vectors.astype(jnp.float32), hidden_bias.astype(jnp.float32))
    outputs, pullback = jax.vjp(forward, *primals)
    grads = pullback((shaped(latent_cot), shaped(out_cot)))
    latents = outputs[0].reshape(-1, model_width).astype(jnp.bfloat16)
    regressed = outputs[1].reshape(-1, model_width).astype(jnp.bfloat16)
    vis_grad = grads[0].reshape(-1, model_width).astype(jnp.bfloat16)
    query_grad = grads[1].reshape(-1, model_width).astype(jnp.bfloat16)
    return (latents, regressed, vis_grad, query_grad, grads[2], grads[3], grads[4], grads[5], grads[6], grads[7])
```

```python
import functools

import jax
import jax.numpy as jnp
from jax import lax
from jax.experimental import pallas as pl
from jax.experimental.pallas import tpu as pltpu
from jax.sharding import PartitionSpec as P

F32 = jnp.float32
BF16 = jnp.bfloat16
CAP = 384
IMGS = 4
SLOT = 128
PAD = IMGS * SLOT
D = 768
FF = 3072
LANES = 128
PAIRS = D // LANES
HB = 512
EPS = 1e-06
MIB = 1 << 20
ANY = pl.BlockSpec(memory_space=pl.ANY)
SMEM = pl.BlockSpec(memory_space=pltpu.SMEM)


def params(limit=48, **more):
    return pltpu.CompilerParams(vmem_limit_bytes=limit * MIB, **more)


def sds(shape, dtype):
    return jax.ShapeDtypeStruct(shape, dtype)


def dot(a, b):
    return jnp.dot(a, b, preferred_element_type=F32)


def dot_nt(a, b):
    return lax.dot_general(a, b, (((1,), (1,)), ((), ())), preferred_element_type=F32)


def dot_tn(a, b):
    return lax.dot_general(a, b, (((0,), (0,)), ((), ())), preferred_element_type=F32)


def row(ref, i):
    return ref[i : i + 1, :]


def colsum(values):
    return jnp.sum(values, axis=0, keepdims=True)


def normalize(values):
    centred = values - jnp.mean(values, axis=-1, keepdims=True)
    spread = jnp.mean(centred * centred, axis=-1, keepdims=True)
    inverse = lax.rsqrt(spread + EPS)
    return centred * inverse, inverse


def norm_back(gradient, gain, normed, inverse):
    scaled = gradient * gain
    level = jnp.mean(scaled, axis=-1, keepdims=True)
    slope = jnp.mean(scaled * normed, axis=-1, keepdims=True)
    return inverse * (scaled - level - normed * slope)


def gelu_parts(t):
    e = jnp.exp(-0.5 * t * t)
    k = 1.0 / (1.0 + (0.3275911 * 0.7071067811865476) * jnp.abs(t))
    poly = k * (
        0.127414796
        + k * (-0.142248368 + k * (0.7107068705 + k * (-0.7265760135 + k * 0.5307027145)))
    )
    tail = poly * e
    phi = jnp.where(t >= 0.0, 1.0 - tail, tail)
    return t * phi, phi + t * (e * 0.3989422804014327)


def image_bounds(lens, pack):
    sizes = [lens[pack, j] for j in range(IMGS)]
    starts = [jnp.int32(0)]
    for j in range(IMGS - 1):
        starts.append(starts[-1] + sizes[j])
    return starts, sizes


def pick_image(slots, values):
    image = lax.shift_right_logical(slots, 7)
    out = jnp.where(image == 1, values[1], values[0])
    out = jnp.where(image == 2, values[2], out)
    return jnp.where(image == 3, values[3], out)


def regroup_matrix(lens, pack):
    starts, sizes = image_bounds(lens, pack)
    slots = lax.broadcasted_iota(jnp.int32, (PAD, CAP), 0)
    rows = lax.broadcasted_iota(jnp.int32, (PAD, CAP), 1)
    place = lax.bitwise_and(slots, SLOT - 1)
    wanted = pick_image(slots, starts) + place
    hit = (wanted == rows) & (place < pick_image(slots, sizes))
    return jnp.where(hit, 1.0, 0.0).astype(BF16)


def ungroup_matrix(lens, pack):
    starts, sizes = image_bounds(lens, pack)
    rows = lax.broadcasted_iota(jnp.int32, (CAP, PAD), 0)
    slots = lax.broadcasted_iota(jnp.int32, (CAP, PAD), 1)
    place = lax.bitwise_and(slots, SLOT - 1)
    wanted = pick_image(slots, starts) + place
    hit = (wanted == rows) & (place < pick_image(slots, sizes))
    return jnp.where(hit, 1.0, 0.0).astype(BF16)


def lane_halves():
    lane = lax.broadcasted_iota(jnp.int32, (1, LANES), 1)
    first = jnp.where(lane < LANES // 2, 1.0, 0.0)
    return first.astype(BF16), (1.0 - first).astype(BF16)


def both_heads(block, halves):
    return jnp.concatenate([block * halves[0], block * halves[1]], axis=0)


def merge_heads(stacked):
    keys = stacked.shape[0] // 2
    lane = lax.broadcasted_iota(jnp.int32, (keys, LANES), 1)
    return jnp.where(lane < LANES // 2, stacked[:keys], stacked[keys:])


def softmax(scores):
    raised = jnp.exp(scores - jnp.max(scores, axis=-1, keepdims=True))
    return raised * (1.0 / jnp.sum(raised, axis=-1, keepdims=True))


def attend(lens, pack, packed, probs, mixed_slots, parts):
    halves = lane_halves()
    keys = SLOT * parts

    def image(j, carry):
        rows = pl.ds(pl.multiple_of(j * SLOT, SLOT), SLOT)
        size = lens[pack, j]
        place = lax.bitwise_and(
            lax.broadcasted_iota(jnp.int32, (SLOT, 2 * keys), 1), SLOT - 1
        )
        valid = place < size
        for g in range(PAIRS):
            cols = slice(g * LANES, (g + 1) * LANES)
            kk = jnp.concatenate([packed[1 + 2 * m, rows, cols] for m in range(parts)], axis=0)
            vv = jnp.concatenate([packed[2 + 2 * m, rows, cols] for m in range(parts)], axis=0)
            scores = dot_nt(packed[0, rows, cols], both_heads(kk, halves))
            scores = jnp.where(valid, scores, -1e30)
            prob = jnp.concatenate(
                [softmax(scores[:, :keys]), softmax(scores[:, keys:])], axis=1
            ).astype(BF16)
            probs[j, g] = prob
            mixed_slots[rows, cols] = dot(prob, both_heads(vv, halves)).astype(BF16)
        return carry

    lax.fori_loop(0, IMGS, image, 0)


def attend_back(packed, probs, d_mixed_slots, d_packed, parts):
    halves = lane_halves()
    keys = SLOT * parts

    def image(j, carry):
        rows = pl.ds(pl.multiple_of(j * SLOT, SLOT), SLOT)
        for g in range(PAIRS):
            cols = slice(g * LANES, (g + 1) * LANES)
            q = packed[0, rows, cols]
            kk = jnp.concatenate([packed[1 + 2 * m, rows, cols] for m in range(parts)], axis=0)
            vv = jnp.concatenate([packed[2 + 2 * m, rows, cols] for m in range(parts)], axis=0)
            d_out = d_mixed_slots[rows, cols]
            low = probs[j, g]
            prob = low.astype(F32)
            d_prob = dot_nt(d_out, both_heads(vv, halves))
            weighted = prob * d_prob
            d_scores = []
            for half in (slice(0, keys), slice(keys, 2 * keys)):
                centre = jnp.sum(weighted[:, half], axis=-1, keepdims=True)
                d_scores.append(weighted[:, half] - prob[:, half] * centre)
            d_scores = jnp.concatenate(d_scores, axis=1).astype(BF16)
            d_q = dot(d_scores, both_heads(kk, halves)) * 0.125
            d_packed[0, rows, cols] = d_q.astype(BF16)
            d_k = merge_heads(dot_tn(d_scores, q)).astype(BF16)
            d_v = merge_heads(dot_tn(low, d_out)).astype(BF16)
            for m in range(parts):
                part = slice(m * SLOT, (m + 1) * SLOT)
                d_packed[1 + 2 * m, rows, cols] = d_k[part]
                d_packed[2 + 2 * m, rows, cols] = d_v[part]
        return carry

    lax.fori_loop(0, IMGS, image, 0)


def blocks_of(i):
    return slice(i * D, (i + 1) * D)


ATT_STATE = (
    sds((5, CAP, D), BF16),
    sds((5, PAD, D), BF16),
    sds((IMGS, PAIRS, SLOT, 4 * SLOT), BF16),
    sds((CAP, D), BF16),
    sds((CAP, D), BF16),
    sds((CAP, D), F32),
    sds((CAP, D), F32),
)
FFN_STATE = (
    sds((CAP, D), BF16),
    sds((CAP, FF), BF16),
    sds((CAP, FF), BF16),
    sds((CAP, D), BF16),
)
ATT_GRADS = (
    sds((5, CAP, D), BF16),
    sds((CAP, D), BF16),
    sds((10, D), F32),
)
FFN_GRADS = (
    sds((CAP, FF), BF16),
    sds((CAP, D), BF16),
    sds((4, D), F32),
    sds((1, FF), F32),
)
ROWS = sds((CAP, D), BF16)


def full(shape):
    return pl.BlockSpec(shape, lambda i: (0,) * len(shape))


def lead(count, shape):
    return pl.BlockSpec((count, *shape), lambda i: (0,) * (1 + len(shape)))


def slot_of(index, shape):
    return pl.BlockSpec((None, *shape), lambda i: (index,) + (0,) * len(shape))


def unset(shapes):
    def kernel(*refs):
        del refs

    return pl.pallas_call(
        kernel, out_shape=shapes, out_specs=tuple(ANY for _ in shapes), name="unset"
    )()


def encoder_attention_kernel(
    lens, which, x, matrix, e, out, normed, packed, probs, mixed, branch, q_source, k_source, flat, mixed_slots
):
    del q_source, k_source
    pack = which[0]
    values = x[...].astype(F32)
    centred, _ = normalize(values)
    normed[0] = (centred * row(e, 0) + row(e, 1)).astype(BF16)
    flat[0] = ((dot(normed[0], matrix[:, blocks_of(0)]) + row(e, 2)).astype(BF16) * 0.125).astype(BF16)
    flat[1] = dot(normed[0], matrix[:, blocks_of(1)]).astype(BF16)
    flat[2] = (dot(normed[0], matrix[:, blocks_of(2)]) + row(e, 3)).astype(BF16)
    regroup = regroup_matrix(lens, pack)
    for m in range(3):
        packed[m] = dot(regroup, flat[m]).astype(BF16)
    attend(lens, pack, packed, probs, mixed_slots, 1)
    mixed[...] = dot(ungroup_matrix(lens, pack), mixed_slots[...]).astype(BF16)
    total = dot_nt(mixed[...], matrix[:, blocks_of(3)]) + row(e, 4)
    branch[...] = total.astype(BF16)
    out[...] = (values + row(e, 5) * total).astype(BF16)


def encoder_attention(lens, which, x, matrices, e):
    return pl.pallas_call(
        encoder_attention_kernel,
        grid=(1,),
        in_specs=[SMEM, SMEM, full((CAP, D)), slot_of(0, (D, FF)), full((6, D))],
        out_specs=(
            full((CAP, D)),
            lead(1, (CAP, D)),
            lead(3, (PAD, D)),
            full((IMGS, PAIRS, SLOT, 2 * SLOT)),
            full((CAP, D)),
            full((CAP, D)),
            ANY,
            ANY,
        ),
        out_shape=(ROWS, *ATT_STATE),
        scratch_shapes=[pltpu.VMEM((3, CAP, D), BF16), pltpu.VMEM((PAD, D), BF16)],
        compiler_params=params(),
        name="encoder_attention",
    )(lens, which, x, matrices, e)


def encoder_attention_back_kernel(
    lens, which, g_in, x, matrix, e, packed, probs, branch, d_x, d_flat, d_branch, vectors, d_slots, d_packed
):
    pack = which[0]
    g = g_in[...].astype(F32)
    vectors[5:6] = colsum(g * branch[...].astype(F32))
    d_branch[...] = (g * row(e, 5)).astype(BF16)
    vectors[4:5] = colsum(d_branch[...].astype(F32))
    d_mixed = dot(d_branch[...], matrix[:, blocks_of(3)]).astype(BF16)
    d_slots[...] = dot(regroup_matrix(lens, pack), d_mixed).astype(BF16)
    attend_back(packed, probs, d_slots, d_packed, 1)
    ungroup = ungroup_matrix(lens, pack)
    for m in range(3):
        d_flat[m] = dot(ungroup, d_packed[m]).astype(BF16)
    vectors[2:3] = colsum(d_flat[0].astype(F32))
    vectors[3:4] = colsum(d_flat[2].astype(F32))
    d_normed = dot_nt(d_flat[0], matrix[:, blocks_of(0)])
    for m in (1, 2):
        d_normed += dot_nt(d_flat[m], matrix[:, blocks_of(m)])
    normed, inverse = normalize(x[...].astype(F32))
    vectors[0:1] = colsum(d_normed * normed)
    vectors[1:2] = colsum(d_normed)
    vectors[6:10] = jnp.zeros((4, D), F32)
    d_x[...] = (g + norm_back(d_normed, row(e, 0), normed, inverse)).astype(BF16)


def encoder_attention_back(lens, which, g, x, matrices, e, state):
    return pl.pallas_call(
        encoder_attention_back_kernel,
        grid=(1,),
        in_specs=[
            SMEM,
            SMEM,
            full((CAP, D)),
            full((CAP, D)),
            slot_of(0, (D, FF)),
            full((6, D)),
            lead(3, (PAD, D)),
            full((IMGS, PAIRS, SLOT, 2 * SLOT)),
            full((CAP, D)),
        ],
        out_specs=(full((CAP, D)), lead(3, (CAP, D)), full((CAP, D)), full((10, D))),
        out_shape=(ROWS, *ATT_GRADS),
        scratch_shapes=[pltpu.VMEM((PAD, D), BF16), pltpu.VMEM((3, PAD, D), BF16)],
        compiler_params=params(),
        name="encoder_attention_back",
    )(lens, which, g, x, matrices, e, state[1], state[2], state[4])


def table_rows(indices, table):
    places = lax.broadcasted_iota(jnp.int32, (indices.shape[0], table.shape[0]), 1)
    chosen = jnp.where(places == indices[...], 1.0, 0.0).astype(BF16)
    values = table[...]
    top = values.astype(BF16)
    values = values - top.astype(F32)
    middle = values.astype(BF16)
    bottom = (values - middle.astype(F32)).astype(BF16)
    return (dot(chosen, top) + dot(chosen, middle)) + dot(chosen, bottom)


def regressor_attention_kernel(
    lens, which, latents, queries, vis, mask, table, matrix, e,
    out, normed, packed, probs, mixed, branch, q_source, k_source, flat, mixed_slots,
):
    pack = which[0]
    residual = queries[...].astype(F32)
    q_source[...] = residual + table_rows(mask, table)
    centred, _ = normalize(q_source[...])
    normed[0] = (centred * row(e, 0) + row(e, 1)).astype(BF16)
    normed[3] = (centred * row(e, 2) + row(e, 3)).astype(BF16)
    centred, _ = normalize(residual)
    normed[4] = (centred * row(e, 4) + row(e, 5)).astype(BF16)
    incoming = latents[...].astype(F32)
    k_source[...] = incoming + table_rows(vis, table)
    centred, _ = normalize(k_source[...])
    normed[1] = (centred * row(e, 2) + row(e, 3)).astype(BF16)
    centred, _ = normalize(incoming)
    normed[2] = (centred * row(e, 4) + row(e, 5)).astype(BF16)
    flat[0] = ((dot(normed[0], matrix[:, blocks_of(0)]) + row(e, 6)).astype(BF16) * 0.125).astype(BF16)
    for m in (1, 3):
        flat[m] = dot(normed[m], matrix[:, blocks_of(1)]).astype(BF16)
    for m in (2, 4):
        flat[m] = (dot(normed[m], matrix[:, blocks_of(2)]) + row(e, 7)).astype(BF16)
    regroup = regroup_matrix(lens, pack)
    for m in range(5):
        packed[m] = dot(regroup, flat[m]).astype(BF16)
    attend(lens, pack, packed, probs, mixed_slots, 2)
    mixed[...] = dot(ungroup_matrix(lens, pack), mixed_slots[...]).astype(BF16)
    total = dot_nt(mixed[...], matrix[:, blocks_of(3)]) + row(e, 8)
    branch[...] = total.astype(BF16)
    out[...] = (residual + row(e, 9) * total).astype(BF16)


def regressor_attention(lens, which, latents, queries, vis, mask, table, matrices, e):
    return pl.pallas_call(
        regressor_attention_kernel,
        grid=(1,),
        in_specs=[
            SMEM,
            SMEM,
            full((CAP, D)),
            full((CAP, D)),
            full((CAP, 1)),
            full((CAP, 1)),
            full(table.shape),
            slot_of(0, (D, FF)),
            full((10, D)),
        ],
        out_specs=(
            full((CAP, D)),
            lead(5, (CAP, D)),
            lead(5, (PAD, D)),
            full((IMGS, PAIRS, SLOT, 4 * SLOT)),
            full((CAP, D)),
            full((CAP, D)),
            full((CAP, D)),
            full((CAP, D)),
        ),
        out_shape=(ROWS, *ATT_STATE),
        scratch_shapes=[pltpu.VMEM((5, CAP, D), BF16), pltpu.VMEM((PAD, D), BF16)],
        compiler_params=params(),
        name="regressor_attention",
    )(lens, which, latents, queries, vis, mask, table, matrices, e)


def regressor_attention_back_kernel(
    lens, which, g_in, latents, queries, q_source, k_source, matrix, e, packed, probs, branch,
    d_latents, d_queries, d_flat, d_branch, vectors, d_slots, d_packed,
):
    pack = which[0]
    g = g_in[...].astype(F32)
    vectors[9:10] = colsum(g * branch[...].astype(F32))
    d_branch[...] = (g * row(e, 9)).astype(BF16)
    vectors[8:9] = colsum(d_branch[...].astype(F32))
    d_mixed = dot(d_branch[...], matrix[:, blocks_of(3)]).astype(BF16)
    d_slots[...] = dot(regroup_matrix(lens, pack), d_mixed).astype(BF16)
    attend_back(packed, probs, d_slots, d_packed, 2)
    ungroup = ungroup_matrix(lens, pack)
    for m in range(5):
        d_flat[m] = dot(ungroup, d_packed[m]).astype(BF16)
    vectors[6:7] = colsum(d_flat[0].astype(F32))
    vectors[7:8] = colsum(d_flat[2].astype(F32)) + colsum(d_flat[4].astype(F32))
    normed, inverse = normalize(q_source[...])
    grad = dot_nt(d_flat[0], matrix[:, blocks_of(0)])
    vectors[0:1] = colsum(grad * normed)
    vectors[1:2] = colsum(grad)
    total = g + norm_back(grad, row(e, 0), normed, inverse)
    grad = dot_nt(d_flat[3], matrix[:, blocks_of(1)])
    k_gain = colsum(grad * normed)
    k_offset = colsum(grad)
    total += norm_back(grad, row(e, 2), normed, inverse)
    normed, inverse = normalize(queries[...].astype(F32))
    grad = dot_nt(d_flat[4], matrix[:, blocks_of(2)])
    v_gain = colsum(grad * normed)
    v_offset = colsum(grad)
    total += norm_back(grad, row(e, 4), normed, inverse)
    d_queries[...] = total.astype(BF16)
    normed, inverse = normalize(k_source[...])
    grad = dot_nt(d_flat[1], matrix[:, blocks_of(1)])
    vectors[2:3] = k_gain + colsum(grad * normed)
    vectors[3:4] = k_offset + colsum(grad)
    total = norm_back(grad, row(e, 2), normed, inverse)
    normed, inverse = normalize(latents[...].astype(F32))
    grad = dot_nt(d_flat[2], matrix[:, blocks_of(2)])
    vectors[4:5] = v_gain + colsum(grad * normed)
    vectors[5:6] = v_offset + colsum(grad)
    total += norm_back(grad, row(e, 4), normed, inverse)
    d_latents[...] = total.astype(BF16)


def regressor_attention_back(lens, which, g, latents, queries, matrices, e, state):
    return pl.pallas_call(
        regressor_attention_back_kernel,
        grid=(1,),
        in_specs=[
            SMEM,
            SMEM,
            full((CAP, D)),
            full((CAP, D)),
            full((CAP, D)),
            full((CAP, D)),
            full((CAP, D)),
            slot_of(0, (D, FF)),
            full((10, D)),
            lead(5, (PAD, D)),
            full((IMGS, PAIRS, SLOT, 4 * SLOT)),
            full((CAP, D)),
        ],
        out_specs=(
            full((CAP, D)),
            full((CAP, D)),
            lead(5, (CAP, D)),
            full((CAP, D)),
            full((10, D)),
        ),
        out_shape=(ROWS, ROWS, *ATT_GRADS),
        scratch_shapes=[pltpu.VMEM((PAD, D), BF16), pltpu.VMEM((5, PAD, D), BF16)],
        compiler_params=params(),
        name="regressor_attention_back",
    )(lens, which, g, latents, queries, state[5], state[6], matrices, e, state[1], state[2], state[4])


def feed_forward_kernel(x, up, down, r, c, out, normed, active, slope, branch, total):
    step = pl.program_id(0)

    @pl.when(step == 0)
    def _():
        centred, _ = normalize(x[...].astype(F32))
        normed[...] = (centred * row(r, 0) + row(r, 1)).astype(BF16)
        total[...] = jnp.zeros_like(total)

    value, steep = gelu_parts(dot(normed[...], up[...]) + c[...])
    active[...] = value.astype(BF16)
    slope[...] = steep.astype(BF16)
    total[...] += dot(active[...], down[...])

    @pl.when(step == pl.num_programs(0) - 1)
    def _():
        summed = total[...] + row(r, 2)
        branch[...] = summed.astype(BF16)
        out[...] = (x[...].astype(F32) + row(r, 3) * summed).astype(BF16)


HIDDEN = pl.BlockSpec((CAP, HB), lambda i: (0, i))
UP = pl.BlockSpec((None, D, HB), lambda i: (1, 0, i))
DOWN = pl.BlockSpec((HB, D), lambda i: (i, 0))
OFFSET = pl.BlockSpec((1, HB), lambda i: (0, i))


def feed_forward(x, matrices, down, r, c):
    return pl.pallas_call(
        feed_forward_kernel,
        grid=(FF // HB,),
        in_specs=[full((CAP, D)), UP, DOWN, full((4, D)), OFFSET],
        out_specs=(full((CAP, D)), full((CAP, D)), HIDDEN, HIDDEN, full((CAP, D))),
        out_shape=(ROWS, *FFN_STATE),
        scratch_shapes=[pltpu.VMEM((CAP, D), F32)],
        compiler_params=params(),
        name="feed_forward",
    )(x, matrices, down, r, c)


def feed_forward_back_kernel(
    several, *refs
):
    g_refs, (x, branch, slope, up, down, r, d_x, d_hidden, d_branch, vectors, d_offset, g, total) = (
        refs[:several],
        refs[several:],
    )
    step = pl.program_id(0)

    @pl.when(step == 0)
    def _():
        g[...] = g_refs[0][...].astype(F32)
        for more in g_refs[1:]:
            g[...] += more[...].astype(F32)
        d_branch[...] = (g[...] * row(r, 3)).astype(BF16)
        vectors[2:3] = colsum(d_branch[...].astype(F32))
        vectors[3:4] = colsum(g[...] * branch[...].astype(F32))
        total[...] = jnp.zeros_like(total)

    d_active = dot_nt(d_branch[...], down[...])
    d_hidden[...] = (d_active * slope[...].astype(F32)).astype(BF16)
    d_offset[...] = colsum(d_hidden[...].astype(F32))
    total[...] += dot_nt(d_hidden[...], up[...])

    @pl.when(step == pl.num_programs(0) - 1)
    def _():
        d_normed = total[...]
        normed, inverse = normalize(x[...].astype(F32))
        vectors[0:1] = colsum(d_normed * normed)
        vectors[1:2] = colsum(d_normed)
        d_x[...] = (g[...] + norm_back(d_normed, row(r, 0), normed, inverse)).astype(BF16)


def feed_forward_back(g, x, state, matrices, down, r):
    return pl.pallas_call(
        functools.partial(feed_forward_back_kernel, len(g)),
        grid=(FF // HB,),
        in_specs=[full((CAP, D)) for _ in g]
        + [full((CAP, D)), full((CAP, D)), HIDDEN, UP, DOWN, full((4, D))],
        out_specs=(full((CAP, D)), HIDDEN, full((CAP, D)), full((4, D)), OFFSET),
        out_shape=(ROWS, *FFN_GRADS),
        scratch_shapes=[pltpu.VMEM((CAP, D), F32), pltpu.VMEM((CAP, D), F32)],
        compiler_params=params(),
        name="feed_forward_back",
    )(*g, x, state[3], state[2], matrices, down, r)


BLOCKS = FF // D
SHARE = BLOCKS + BLOCKS // 2


def weight_grads_kernel(parts, n1, n2, p1, p2, m1, m2, b1, b2, k1, k2, h1, h2, a1, a2, c1, c2, out):
    step = pl.program_id(0)

    @pl.when(step < 3)
    def _():
        place = 0 if parts == 1 else step
        total = dot_tn(n1[place], p1[step]) + dot_tn(n2[place], p2[step])
        out[...] = total.astype(BF16)
        if parts == 2:

            @pl.when(step > 0)
            def _():
                more = dot_tn(n1[step + 2], p1[step + 2]) + dot_tn(n2[step + 2], p2[step + 2])
                out[...] = (total + more).astype(BF16)

    @pl.when(step == 3)
    def _():
        out[...] = (dot_tn(b1[...], m1[...]) + dot_tn(b2[...], m2[...])).astype(BF16)

    @pl.when((step >= 4) & (step < 8))
    def _():
        out[...] = (dot_tn(k1[...], h1[...]) + dot_tn(k2[...], h2[...])).astype(BF16)

    @pl.when(step >= 8)
    def _():
        out[...] = (dot_tn(a1[...], c1[...]) + dot_tn(a2[...], c2[...])).astype(BF16)


def grad_place(step):
    tail = jnp.maximum(step - 2 * BLOCKS, 0)
    late = jnp.where(step >= 2 * BLOCKS, 1, 0)
    section = (1 - late) * (step // BLOCKS) + late * (tail // 2)
    block = (1 - late) * (step % BLOCKS) + late * (BLOCKS + tail % 2)
    return section, block, 0, 0


def weight_grads(parts, kept, grads):
    att, ffn = [k[2] for k in kept], [k[3] for k in kept]
    att_grads, ffn_grads = [g[2] for g in grads], [g[3] for g in grads]
    have = 1 if parts == 1 else 5
    made = 3 if parts == 1 else 5
    rows = full((CAP, D))
    up_part = pl.BlockSpec((CAP, D), lambda i: (0, jnp.clip(i - BLOCKS, 0, BLOCKS - 1)))
    down_part = pl.BlockSpec((CAP, D), lambda i: (0, jnp.clip(i - 2 * BLOCKS, 0, BLOCKS - 1)))
    return pl.pallas_call(
        functools.partial(weight_grads_kernel, parts),
        grid=(3 * BLOCKS,),
        in_specs=[lead(have, (CAP, D))] * 2
        + [lead(made, (CAP, D))] * 2
        + [rows] * 6
        + [up_part] * 2
        + [down_part] * 2
        + [rows] * 2,
        out_specs=pl.BlockSpec((None, None, D, D), grad_place),
        out_shape=sds((2, SHARE, D, D), BF16),
        compiler_params=params(),
        name="weight_grads",
    )(
        att[0][0], att[1][0], att_grads[0][0], att_grads[1][0],
        att[0][3], att[1][3], att_grads[0][1], att_grads[1][1],
        ffn[0][0], ffn[1][0], ffn_grads[0][0], ffn_grads[1][0],
        ffn[0][1], ffn[1][1], ffn_grads[0][1], ffn_grads[1][1],
    )


MESH = pl.DeviceIdType.MESH


def gather_weights_kernel(matrix, down, matrices, downs, send, receive, local):
    dp, section = lax.axis_index("dp"), lax.axis_index("section")
    odd = lax.rem(section, 2)
    partner = (dp, section + 1 - 2 * odd)
    barrier = pltpu.get_barrier_semaphore()
    pl.semaphore_signal(barrier, inc=1, device_id=partner, device_id_type=MESH)
    pl.semaphore_wait(barrier, 1)
    half = down.shape[0]
    places = (
        (matrix.at[0], matrices.at[odd]),
        (down, downs.at[pl.ds(pl.multiple_of(odd * half, half), half)]),
    )
    copies = []
    for i, (source, target) in enumerate(places):
        away = pltpu.make_async_remote_copy(
            source, target, send.at[i], receive.at[i], device_id=partner, device_id_type=MESH
        )
        away.start()
        here = pltpu.make_async_copy(source, target, local.at[i])
        here.start()
        copies += [away, here]
    for copy in copies:
        copy.wait()


def gather_weights(matrix, down):
    vmem = pl.BlockSpec(memory_space=pltpu.VMEM)
    return pl.pallas_call(
        gather_weights_kernel,
        in_specs=[vmem, vmem],
        out_specs=(ANY, ANY),
        out_shape=(
            sds((2, *matrix.shape[1:]), matrix.dtype),
            sds((2 * down.shape[0], down.shape[1]), down.dtype),
        ),
        scratch_shapes=[pltpu.SemaphoreType.DMA((2,)) for _ in range(3)],
        compiler_params=params(collective_id=1, has_side_effects=True),
        name="gather_weights",
    )(matrix, down)


RING = 8
SEGMENT = D // RING
PART = SEGMENT // 2
CHAIN = SHARE // 2
VECTORS = 24


def ring_place(d):
    odd = lax.rem(d, 2)
    return (1 - odd) * lax.div(d, 2) + odd * (RING - 1 - lax.div(d, 2))


def ring_device(place):
    place = lax.rem(place + RING, RING)
    late = lax.div(place, RING // 2)
    return (1 - late) * 2 * place + late * (2 * (RING - 1 - place) + 1)


def reduce_kernel(
    grads, swapping, vectors, out_matrix, out_down, swapped, out_vectors,
    mine, partner_part, landing, final, stage, v_sum, v_in,
    pair_send, pair_receive, own_sem, ring_send, ring_receive, last_send, last_receive, out_sem,
    v_send, v_receive, swap_send, swap_receive,
):
    d, section = lax.axis_index("dp"), lax.axis_index("section")
    odd = lax.rem(section, 2)
    place = ring_place(d)
    across = (d, section + 2 - 4 * lax.div(section, 2))
    pair = (d, section + 1 - 2 * odd)
    ways = ((ring_device(place + 1), section), (ring_device(place - 1), section))

    def flipped(bit):
        return d + bit - 2 * bit * lax.rem(lax.div(d, bit), 2)

    levels = (pair, (flipped(1), section), (flipped(2), section), (flipped(4), section), across)
    barrier = pltpu.get_barrier_semaphore()
    for other in (*ways, *levels):
        pl.semaphore_signal(barrier, inc=1, device_id=other, device_id_type=MESH)
    pl.semaphore_wait(barrier, len(ways) + len(levels))

    def rows_of(step, way):
        segment = lax.rem(place + (step if way else -step) + 2 * RING, RING)
        return pl.ds(pl.multiple_of(segment * SEGMENT + way * PART, 8), PART)

    def remote(source, target, send, receive, device):
        return pltpu.make_async_remote_copy(source, target, send, receive, device_id=device, device_id_type=MESH)

    swap = remote(swapping, swapped, swap_send, swap_receive, across)
    swap.start()
    own = pltpu.make_async_copy(grads.at[odd], mine, own_sem)
    own.start()

    def pair_copy(step, way):
        rows = rows_of(step, way)
        return remote(
            grads.at[1 - odd, :, rows, :], partner_part.at[:, rows, :],
            pair_send.at[step, way], pair_receive.at[step, way], pair,
        )

    def start_pair(step, carry):
        for way in range(2):
            pair_copy(step, way).start()
        return carry

    lax.fori_loop(0, RING, start_pair, 0)

    def vector_copy(level):
        return remote(v_sum.at[level], v_in.at[level], v_send.at[level], v_receive.at[level], levels[level])

    def vector_next(level):
        vector_copy(level).wait()
        if level + 1 < len(levels):
            v_sum[level + 1] = v_sum[level] + v_in[level]
            vector_copy(level + 1).start()

    v_sum[0] = vectors[...]
    vector_copy(0).start()

    def blocks(chain):
        return pl.ds(chain * CHAIN, CHAIN)

    def ring_copy(step, way, chain):
        rows = rows_of(step, way)
        return remote(
            mine.at[blocks(chain), rows, :], landing.at[blocks(chain), rows, :],
            ring_send.at[step, way, chain], ring_receive.at[step, way, chain], ways[way],
        )

    def incoming(step, way, chain):
        rows = rows_of(step + 1, way)
        return remote(
            mine.at[blocks(chain), rows, :], landing.at[blocks(chain), rows, :],
            ring_send.at[step, way, chain], ring_receive.at[step, way, chain], ways[way],
        )

    own.wait()
    for way in range(2):
        pair_copy(0, way).wait_recv()
        rows = rows_of(0, way)
        for chain in range(2):
            part = (blocks(chain), rows, slice(None))
            mine[part] = (mine[part].astype(F32) + partner_part[part].astype(F32)).astype(BF16)
            ring_copy(0, way, chain).start()
    vector_next(0)

    def total_of(part):
        return (
            mine[part].astype(F32) + partner_part[part].astype(F32) + landing[part].astype(F32)
        ).astype(BF16)

    def reduce_step(step, carry):
        for chain in range(2):
            for way in range(2):
                if chain == 0:
                    pair_copy(step, way).wait_recv()
                incoming(step - 1, way, chain).wait_recv()
                part = (blocks(chain), rows_of(step, way), slice(None))
                mine[part] = total_of(part)
                ring_copy(step, way, chain).start()
        return carry

    lax.fori_loop(1, RING - 1, reduce_step, 0)
    vector_next(1)

    def last_copy(step, way, chain):
        rows = rows_of(step + RING - 1, way)
        return remote(
            final.at[blocks(chain), rows, :], final.at[blocks(chain), rows, :],
            last_send.at[step, way, chain], last_receive.at[step, way, chain], ways[way],
        )

    def last_incoming(step, way, chain):
        rows = rows_of(step + RING, way)
        return remote(
            final.at[blocks(chain), rows, :], final.at[blocks(chain), rows, :],
            last_send.at[step, way, chain], last_receive.at[step, way, chain], ways[way],
        )

    def out_copies(step, way, chain):
        rows = rows_of(step + RING - 1, way)
        copies = []
        for i in range(CHAIN):
            block = chain * CHAIN + i
            if block < BLOCKS:
                target = out_matrix.at[0, rows, pl.ds(block * D, D)]
            else:
                segment = lax.rem(place + (step + RING - 1 if way else 1 - step - RING) + 4 * RING, RING)
                start = (block - BLOCKS) * D + segment * SEGMENT + way * PART
                target = out_down.at[pl.ds(pl.multiple_of(start, 8), PART), :]
            copies.append(pltpu.make_async_copy(stage.at[way, chain, i], target, out_sem.at[way, chain, i]))
        return copies

    def write_out(step, way, chain, first):
        if not first:
            for copy in out_copies(step - 1, way, chain):
                copy.wait()
        stage[way, chain] = final[blocks(chain), rows_of(step + RING - 1, way), :].astype(F32)
        for copy in out_copies(step, way, chain):
            copy.start()

    for chain in range(2):
        for way in range(2):
            if chain == 0:
                pair_copy(RING - 1, way).wait_recv()
            incoming(RING - 2, way, chain).wait_recv()
            part = (blocks(chain), rows_of(RING - 1, way), slice(None))
            final[part] = total_of(part)
            last_copy(0, way, chain).start()
    vector_next(2)
    for chain in range(2):
        for way in range(2):
            write_out(0, way, chain, True)

    def gather_step(step, carry):
        for chain in range(2):
            for way in range(2):
                last_incoming(step - 1, way, chain).wait_recv()
                last_copy(step, way, chain).start()
                write_out(step, way, chain, False)
        return carry

    lax.fori_loop(1, 3, gather_step, 0)
    vector_next(3)
    lax.fori_loop(3, 5, gather_step, 0)
    vector_next(4)
    out_vectors[0] = v_sum[len(levels) - 1]
    out_vectors[1] = v_in[len(levels) - 1]
    lax.fori_loop(5, RING - 1, gather_step, 0)
    for chain in range(2):
        for way in range(2):
            last_incoming(RING - 2, way, chain).wait_recv()
            write_out(RING - 1, way, chain, False)
    for chain in range(2):
        for way in range(2):
            for copy in out_copies(RING - 1, way, chain):
                copy.wait()

    def all_sent(step, carry):
        for way in range(2):
            for chain in range(2):
                ring_copy(step, way, chain).wait_send()
                last_copy(step, way, chain).wait_send()
        return carry

    lax.fori_loop(0, RING - 1, all_sent, 0)

    def pair_sent(step, carry):
        for way in range(2):
            pair_copy(step, way).wait_send()
        return carry

    lax.fori_loop(0, RING, pair_sent, 0)
    swap.wait()


def reduce_grads(grads, swapping, vectors):
    share = (SHARE, D, D)
    vmem = pl.BlockSpec(memory_space=pltpu.VMEM)
    dma = pltpu.SemaphoreType.DMA
    return pl.pallas_call(
        reduce_kernel,
        in_specs=[ANY, ANY, vmem],
        out_specs=(ANY, ANY, ANY, vmem),
        out_shape=(
            sds((1, D, FF), F32),
            sds((FF // 2, D), F32),
            sds(swapping.shape, swapping.dtype),
            sds((2, VECTORS, D), F32),
        ),
        scratch_shapes=[
            pltpu.VMEM(share, BF16),
            pltpu.VMEM(share, BF16),
            pltpu.VMEM(share, BF16),
            pltpu.VMEM(share, BF16),
            pltpu.VMEM((2, 2, CHAIN, PART, D), F32),
            pltpu.VMEM((5, VECTORS, D), F32),
            pltpu.VMEM((5, VECTORS, D), F32),
            dma((RING, 2)),
            dma((RING, 2)),
            dma,
            dma((RING - 1, 2, 2)),
            dma((RING - 1, 2, 2)),
            dma((RING - 1, 2, 2)),
            dma((RING - 1, 2, 2)),
            dma((2, 2, CHAIN)),
            dma((5,)),
            dma((5,)),
            dma,
            dma,
        ],
        compiler_params=params(56, collective_id=2, has_side_effects=True),
        name="reduce_grads",
    )(grads, swapping, vectors)


def plain_reduce_grads(grads, swapping, vectors):
    odd = lax.rem(lax.axis_index("section"), 2)
    pair = [(0, 1), (1, 0), (2, 3), (3, 2)]
    theirs = lax.dynamic_index_in_dim(grads, 1 - odd, 0, keepdims=False)
    mine = lax.dynamic_index_in_dim(grads, odd, 0, keepdims=False)
    total = lax.psum(mine + lax.ppermute(theirs, "section", pair), "dp").astype(F32)
    vectors = lax.psum(vectors + lax.ppermute(vectors, "section", pair), "dp")
    matrix = jnp.swapaxes(total[:BLOCKS], 0, 1).reshape(1, D, FF)
    return (
        matrix,
        total[BLOCKS:].reshape(FF // 2, D),
        swap_layers(swapping),
        jnp.stack([vectors, swap_layers(vectors)]),
    )


def swap_layers(block):
    return lax.ppermute(block, "section", [(0, 2), (1, 3), (2, 0), (3, 1)])


def to_regressor(block):
    return lax.ppermute(block, "section", [(0, 2), (1, 3)])


def to_encoder(block):
    return lax.ppermute(block, "section", [(2, 0), (3, 1)])


def body(
    vis_embed, latent_cot, reg_queries, out_cot, section_matrix, down_weight, enc_vectors, reg_vectors,
    mlp_vectors, hidden_bias, pos_table, image_lengths, vis_index, mask_index,
):
    section = lax.axis_index("section")
    odd = lax.rem(section, 2)
    is_reg = section >= 2
    layer = jnp.where(is_reg, 1, 0)
    matrices, down = gather_weights(section_matrix, down_weight)
    r = lax.dynamic_index_in_dim(mlp_vectors, layer, 0, keepdims=False)
    c = lax.dynamic_slice_in_dim(hidden_bias, layer, 1, 0)
    packs = [(odd + 2 * i).reshape(1).astype(jnp.int32) for i in range(2)]
    vis = [lax.dynamic_slice_in_dim(vis_index, (odd + 2 * i) * CAP, CAP)[:, None] for i in range(2)]
    mask = [lax.dynamic_slice_in_dim(mask_index, (odd + 2 * i) * CAP, CAP)[:, None] for i in range(2)]

    outgoing = jnp.where(is_reg, jnp.stack([vis_embed, latent_cot]), jnp.stack([reg_queries, out_cot]))
    incoming = swap_layers(outgoing)

    def attention_out(result):
        return result[0], tuple(result[1:])

    def enc_forward(i, x):
        mid, att = attention_out(encoder_attention(image_lengths, packs[i], x, matrices, enc_vectors))
        out, ffn = attention_out(feed_forward(mid, matrices, down, r, c))
        return mid, out, att, ffn

    def reg_forward(i, latents, queries):
        mid, att = attention_out(
            regressor_attention(
                image_lengths, packs[i], latents, queries, vis[i], mask[i], pos_table, matrices, reg_vectors
            )
        )
        out, ffn = attention_out(feed_forward(mid, matrices, down, r, c))
        return mid, out, att, ffn

    def no_forward():
        made = unset((ROWS, ROWS, *ATT_STATE, *FFN_STATE))
        split = 2 + len(ATT_STATE)
        return made[0], made[1], tuple(made[2:split]), tuple(made[split:])

    def enc_back(i, g, x, kept):
        mid, _, att, ffn = kept
        d_mid, *ffn_grads = feed_forward_back(g, mid, ffn, matrices, down, r)
        d_x, *att_grads = encoder_attention_back(image_lengths, packs[i], d_mid, x, matrices, enc_vectors, att)
        return d_x, d_x, tuple(att_grads), tuple(ffn_grads)

    def reg_back(i, g, latents, queries, kept):
        mid, _, att, ffn = kept
        d_mid, *ffn_grads = feed_forward_back(g, mid, ffn, matrices, down, r)
        d_latents, d_queries, *att_grads = regressor_attention_back(
            image_lengths, packs[i], d_mid, latents, queries, matrices, reg_vectors, att
        )
        return d_latents, d_queries, tuple(att_grads), tuple(ffn_grads)

    def no_back():
        made = unset((ROWS, ROWS, *ATT_GRADS, *FFN_GRADS))
        split = 2 + len(ATT_GRADS)
        return made[0], made[1], tuple(made[2:split]), tuple(made[split:])

    x = [vis_embed, incoming[0]]
    lat_cot = [latent_cot, incoming[1]]
    queries = [incoming[0], reg_queries]
    cot = [incoming[1], out_cot]

    first = lax.cond(is_reg, no_forward, lambda: enc_forward(0, x[0]))
    latents1 = to_regressor(first[1])
    second = lax.cond(is_reg, lambda: reg_forward(0, latents1, queries[0]), lambda: enc_forward(1, x[1]))
    latents2 = to_regressor(second[1])
    reg_grads1 = lax.cond(is_reg, lambda: reg_back(0, [cot[0]], latents1, queries[0], second), no_back)
    d_latents1 = to_encoder(reg_grads1[0])
    enc_grads1, third = lax.cond(
        is_reg,
        lambda: (no_back(), reg_forward(1, latents2, queries[1])),
        lambda: (enc_back(0, [lat_cot[0], d_latents1], x[0], first), no_forward()),
    )
    reg_grads2 = lax.cond(is_reg, lambda: reg_back(1, [cot[1]], latents2, queries[1], third), no_back)
    d_latents2 = to_encoder(reg_grads2[0])

    def total_vectors(grads1, grads2):
        att, ffn = grads1[2][2] + grads2[2][2], grads1[3][2] + grads2[3][2]
        offset = (grads1[3][3] + grads2[3][3]).reshape(BLOCKS, D)
        return jnp.concatenate([att, ffn, offset, jnp.zeros((VECTORS - 18, D), F32)])

    def last_reg():
        return (
            *no_back(),
            weight_grads(2, (second, third), (reg_grads1, reg_grads2)),
            total_vectors(reg_grads1, reg_grads2),
            jnp.stack([second[1], reg_grads1[1]]),
        )

    def last_enc():
        grads2 = enc_back(1, [lat_cot[1], d_latents2], x[1], second)
        return (
            *grads2,
            weight_grads(1, (first, second), (enc_grads1, grads2)),
            total_vectors(enc_grads1, grads2),
            jnp.stack([grads2[0], grads2[0]]),
        )

    last = lax.cond(is_reg, last_reg, last_enc)
    grads, vectors, swapping = last[4:]
    reduce = reduce_grads if lax.axis_size("dp") == RING else plain_reduce_grads
    matrix_grad, down_grad, swapped, vectors = reduce(grads, swapping, vectors)

    def pick(reg, enc):
        return jnp.where(is_reg, reg, enc)

    latents = pick(latents2, first[1])
    regressed = pick(third[1], swapped[0])
    vis_grad = pick(swapped[0], enc_grads1[0])
    query_grad = pick(reg_grads2[1], swapped[1])
    enc_total, reg_total = pick(vectors[1], vectors[0]), pick(vectors[0], vectors[1])
    return (
        latents,
        regressed,
        vis_grad,
        query_grad,
        matrix_grad,
        down_grad,
        enc_total[:6],
        reg_total[:10],
        jnp.stack([enc_total[10:14], reg_total[10:14]]),
        jnp.stack([enc_total[14:18].reshape(FF), reg_total[14:18].reshape(FF)]),
    )


def solution(mesh):
    rows = P(("dp", "section"), None)
    in_specs = (
        rows, rows, rows, rows, P("section", None, None), P("section", None),
        P(), P(), P(), P(), P(), P("dp", None), P("dp"), P("dp"),
    )
    out_specs = (rows, rows, rows, rows, P("section", None, None), P("section", None), P(), P(), P(), P())
    return jax.shard_map(body, mesh=mesh, in_specs=in_specs, out_specs=out_specs, check_vma=False)
```

```python
import functools

import jax
import jax.numpy as jnp
from jax import lax
from jax.experimental import pallas as pl
from jax.experimental.pallas import tpu as pltpu
from jax.sharding import PartitionSpec as P

F32 = jnp.float32
BF16 = jnp.bfloat16
CAP = 384
IMGS = 4
SLOT = 128
PAD = IMGS * SLOT
D = 768
FF = 3072
LANES = 128
PAIRS = D // LANES
BLOCKS = FF // D
VECTORS = 24
EPS = 1e-06
MIB = 1 << 20
ANY = pl.BlockSpec(memory_space=pl.ANY)
SMEM = pl.BlockSpec(memory_space=pltpu.SMEM)


def params(limit=48, **more):
    return pltpu.CompilerParams(vmem_limit_bytes=limit * MIB, **more)


def sds(shape, dtype):
    return jax.ShapeDtypeStruct(shape, dtype)


def dot(a, b):
    return jnp.dot(a, b, preferred_element_type=F32)


def dot_nt(a, b):
    return lax.dot_general(a, b, (((1,), (1,)), ((), ())), preferred_element_type=F32)


def dot_tn(a, b):
    return lax.dot_general(a, b, (((0,), (0,)), ((), ())), preferred_element_type=F32)


def row(ref, i):
    return ref[i : i + 1, :]


def colsum(values):
    return jnp.sum(values, axis=0, keepdims=True)


def normalize(values):
    centred = values - jnp.mean(values, axis=-1, keepdims=True)
    spread = jnp.mean(centred * centred, axis=-1, keepdims=True)
    inverse = lax.rsqrt(spread + EPS)
    return centred * inverse, inverse


def norm_back(gradient, gain, normed, inverse):
    scaled = gradient * gain
    level = jnp.mean(scaled, axis=-1, keepdims=True)
    slope = jnp.mean(scaled * normed, axis=-1, keepdims=True)
    return inverse * (scaled - level - normed * slope)


def gelu_parts(t):
    e = jnp.exp(-0.5 * t * t)
    k = 1.0 / (1.0 + (0.3275911 * 0.7071067811865476) * jnp.abs(t))
    poly = k * (
        0.127414796
        + k * (-0.142248368 + k * (0.7107068705 + k * (-0.7265760135 + k * 0.5307027145)))
    )
    tail = poly * e
    phi = jnp.where(t >= 0.0, 1.0 - tail, tail)
    return t * phi, phi + t * (e * 0.3989422804014327)


CHUNK = 64


def over_rows(body, carry=0, chunk=CHUNK):
    def step(i, carry):
        return body(pl.ds(pl.multiple_of(i * chunk, chunk), chunk), carry)

    return lax.fori_loop(0, CAP // chunk, step, carry)


def each_rows(body, chunk=CHUNK):
    def step(rows, carry):
        body(rows)
        return carry

    over_rows(step, 0, chunk)


def zero_row():
    return jnp.zeros((1, D), F32)


def group_matrices(lens, pack, regroup, ungroup):
    def image(j, start):
        size = lens[pack, j]
        slots = pl.ds(pl.multiple_of(j * SLOT, SLOT), SLOT)
        place = lax.broadcasted_iota(jnp.int32, (SLOT, CAP), 0)
        rows = lax.broadcasted_iota(jnp.int32, (SLOT, CAP), 1)
        hit = (place + start == rows) & (place < size)
        regroup[slots, :] = jnp.where(hit, 1.0, 0.0).astype(BF16)
        place = lax.broadcasted_iota(jnp.int32, (CAP, SLOT), 1)
        rows = lax.broadcasted_iota(jnp.int32, (CAP, SLOT), 0)
        hit = (place + start == rows) & (place < size)
        ungroup[:, slots] = jnp.where(hit, 1.0, 0.0).astype(BF16)
        return start + size

    lax.fori_loop(0, IMGS, image, jnp.int32(0))


def lane_halves():
    lane = lax.broadcasted_iota(jnp.int32, (1, LANES), 1)
    first = jnp.where(lane < LANES // 2, 1.0, 0.0)
    return first.astype(BF16), (1.0 - first).astype(BF16)


def both_heads(block, halves):
    return jnp.concatenate([block * halves[0], block * halves[1]], axis=0)


def merge_heads(stacked):
    keys = stacked.shape[0] // 2
    lane = lax.broadcasted_iota(jnp.int32, (keys, LANES), 1)
    return jnp.where(lane < LANES // 2, stacked[:keys], stacked[keys:])


def softmax(scores):
    raised = jnp.exp(scores - jnp.max(scores, axis=0, keepdims=True))
    return (raised * (1.0 / jnp.sum(raised, axis=0, keepdims=True))).astype(BF16)


def keys_of(packed, first, parts, rows, cols, halves):
    return both_heads(
        jnp.concatenate([packed[first + 2 * m, rows, cols] for m in range(parts)], axis=0), halves
    )


def attend(lens, pack, packed, probs, mixed_slots, parts, done):
    halves = lane_halves()
    keys = SLOT * parts

    def image(j, carry):
        rows = pl.ds(pl.multiple_of(j * SLOT, SLOT), SLOT)
        size = lens[pack, j]
        valid = lax.bitwise_and(lax.broadcasted_iota(jnp.int32, (keys, SLOT), 0), SLOT - 1) < size
        for g in range(PAIRS):
            cols = slice(g * LANES, (g + 1) * LANES)
            scores = dot_nt(keys_of(packed, 1, parts, rows, cols, halves), packed[0, rows, cols])
            low = jnp.concatenate(
                [softmax(jnp.where(valid, part, -1e30)) for part in (scores[:keys], scores[keys:])], axis=0
            )
            probs[j, g] = low
            mixed_slots[rows, cols] = dot_tn(low, keys_of(packed, 2, parts, rows, cols, halves)).astype(BF16)
        done(j)
        return carry

    lax.fori_loop(0, IMGS, image, 0)


def attend_back(packed, probs, mixed_slots, d_mixed_slots, d_packed, parts, ready):
    halves = lane_halves()
    keys = SLOT * parts
    less = both_heads(jnp.full((keys, LANES), -1.0, BF16), halves)

    def image(j, carry):
        ready(j)
        rows = pl.ds(pl.multiple_of(j * SLOT, SLOT), SLOT)
        for g in range(PAIRS):
            cols = slice(g * LANES, (g + 1) * LANES)
            d_out = d_mixed_slots[rows, cols]
            centre = (d_out.astype(F32) * mixed_slots[rows, cols].astype(F32)).astype(BF16)
            low = probs[j, g]
            d_prob = dot_nt(
                jnp.concatenate([keys_of(packed, 2, parts, rows, cols, halves), less], axis=1),
                jnp.concatenate([d_out, centre], axis=1),
            )
            d_scores = (low.astype(F32) * d_prob).astype(BF16)
            d_q = dot_tn(d_scores, keys_of(packed, 1, parts, rows, cols, halves)) * 0.125
            d_packed[0, rows, cols] = d_q.astype(BF16)
            q = packed[0, rows, cols]
            zero = jnp.zeros_like(q)
            sides = jnp.concatenate(
                [jnp.concatenate([q, zero], axis=1), jnp.concatenate([zero, d_out], axis=1)], axis=0
            )
            d_kv = dot(jnp.concatenate([d_scores, low], axis=1), sides)
            d_k = merge_heads(d_kv[:, :LANES]).astype(BF16)
            d_v = merge_heads(d_kv[:, LANES:]).astype(BF16)
            for m in range(parts):
                part = slice(m * SLOT, (m + 1) * SLOT)
                d_packed[1 + 2 * m, rows, cols] = d_k[part]
                d_packed[2 + 2 * m, rows, cols] = d_v[part]
        return carry

    lax.fori_loop(0, IMGS, image, 0)


SQUARE = (D, D)
ROWS = sds((CAP, D), BF16)
STATE = (
    sds((5, CAP, D), BF16),
    sds((5, PAD, D), BF16),
    sds((IMGS, PAIRS, 4 * SLOT, SLOT), BF16),
    sds((CAP, D), BF16),
    sds((CAP, D), BF16),
    sds((2, CAP, D), F32),
    sds((CAP, D), BF16),
    sds((CAP, FF), BF16),
    sds((CAP, FF), BF16),
    sds((CAP, D), BF16),
    sds((PAD, D), BF16),
)
GRADS = (
    sds((5, CAP, D), BF16),
    sds((CAP, D), BF16),
    sds((CAP, FF), BF16),
    sds((CAP, D), BF16),
)
TOTALS = sds((VECTORS, D), F32)
FFN_AT = 10
HIDDEN_AT = FFN_AT + 4


def full(shape):
    return pl.BlockSpec(shape, lambda i: (0,) * len(shape))


def lead(count, shape):
    return pl.BlockSpec((count, *shape), lambda i: (0,) * (1 + len(shape)))


VMEM = pl.BlockSpec(memory_space=pltpu.VMEM)


def unset(shapes):
    def kernel(*refs):
        del refs

    return pl.pallas_call(
        kernel, out_shape=shapes, out_specs=tuple(ANY for _ in shapes), name="unset"
    )()


class Copies:
    def __init__(self, semaphores):
        self.semaphores, self.used, self.open = semaphores, 0, []

    def take(self, count=1):
        self.used += count
        return self.used - count

    def start(self, source, target):
        copy = pltpu.make_async_copy(source, target, self.semaphores.at[self.take()])
        copy.start()
        return copy

    def leave(self, source, target):
        self.open.append(self.start(source, target))

    def finish(self):
        for copy in self.open:
            copy.wait()


def columns(i):
    return slice(i * D, (i + 1) * D)


class Weights:
    def __init__(self, copies, weights, held):
        self.copies, self.weights, self.held, self.started = copies, weights, held, {}

    def target(self, i):
        kind, block = divmod(i, BLOCKS)
        held = self.held[kind]
        return held.at[columns(block), :] if kind == 2 else held.at[:, columns(block)]

    def start(self, *order):
        for i in order:
            self.started[i] = self.copies.start(self.weights.at[i], self.target(i))

    def wait(self, *which):
        for i in which:
            self.started[i].wait()


WEIGHT_SCRATCH = [pltpu.VMEM((D, FF), BF16), pltpu.VMEM((D, FF), BF16), pltpu.VMEM((FF, D), BF16)]
ALL_BLOCKS = range(BLOCKS)
UPS = [BLOCKS + i for i in ALL_BLOCKS]
DOWNS = [2 * BLOCKS + i for i in ALL_BLOCKS]


def feed_forward(copies, weights, mid, r, c, out, state, kept):
    normed, active, slope, branch = state

    def norm(rows):
        centred, _ = normalize(mid[rows, :].astype(F32))
        normed[rows, :] = (centred * row(r, 0) + row(r, 1)).astype(BF16)

    each_rows(norm)
    copies.leave(normed, kept[0])
    _, up, down = weights.held
    for i in ALL_BLOCKS:
        weights.wait(BLOCKS + i)
        value, steep = gelu_parts(dot(normed[...], up[:, columns(i)]) + c[:, columns(i)])
        active[:, columns(i)] = value.astype(BF16)
        slope[:, columns(i)] = steep.astype(BF16)
        copies.leave(active.at[:, columns(i)], kept[1].at[:, columns(i)])
        copies.leave(slope.at[:, columns(i)], kept[2].at[:, columns(i)])
    weights.wait(*DOWNS)
    summed = dot(active[...], down[...]) + row(r, 2)
    branch[...] = summed.astype(BF16)
    out[...] = (mid[...].astype(F32) + row(r, 3) * summed).astype(BF16)
    copies.leave(branch, kept[3])


def feed_forward_back(copies, weights, ready, grads, mid, r, refs, totals, kept, residual):
    slope, branch, d_hidden, d_branch, work = refs
    ready("branch")

    def enter(rows, carry):
        g = grads[0][rows, :].astype(F32)
        for more in grads[1:]:
            g += more[rows, :].astype(F32)
        residual[rows, :] = g
        low = (g * row(r, 3)).astype(BF16)
        d_branch[rows, :] = low
        return carry[0] + colsum(low.astype(F32)), carry[1] + colsum(g * branch[rows, :].astype(F32))

    sums = over_rows(enter, (zero_row(), zero_row()))
    totals[FFN_AT + 2 : FFN_AT + 3], totals[FFN_AT + 3 : FFN_AT + 4] = sums
    copies.leave(d_branch, kept[1])
    for i in ALL_BLOCKS:
        weights.wait(2 * BLOCKS + i)
        ready(i)
        d_active = dot_nt(d_branch[...], weights.held[2][columns(i), :])
        d_hidden[:, columns(i)] = (d_active * slope[:, columns(i)].astype(F32)).astype(BF16)
        copies.leave(d_hidden.at[:, columns(i)], kept[0].at[:, columns(i)])
        at = HIDDEN_AT + i
        totals[at : at + 1] = over_rows(
            lambda rows, sums, i=i: sums + colsum(d_hidden[rows, columns(i)].astype(F32)), zero_row()
        )
    weights.wait(*UPS)
    work[...] = dot_nt(d_hidden[...], weights.held[1][...])

    def leave(rows, carry):
        grad = work[rows, :]
        normed, inverse = normalize(mid[rows, :].astype(F32))
        moved = residual[rows, :] + norm_back(grad, row(r, 0), normed, inverse)
        residual[rows, :] = moved.astype(BF16).astype(F32)
        return carry[0] + colsum(grad * normed), carry[1] + colsum(grad)

    totals[FFN_AT : FFN_AT + 1], totals[FFN_AT + 1 : FFN_AT + 2] = over_rows(leave, (zero_row(), zero_row()))


def attention(copies, lens, pack, parts, refs, kept):
    flat, packed, probs, mixed, mixed_slots, regroup, ungroup = refs
    group_matrices(lens, pack, regroup, ungroup)
    for m in range(1 + 2 * parts):
        packed[m] = dot(regroup[...], flat[m]).astype(BF16)
        copies.leave(packed.at[m], kept[1].at[m])
    first = copies.take(IMGS)

    def probs_copy(j):
        target = kept[2].at[j, :, pl.ds(0, 2 * SLOT * parts), :]
        return pltpu.make_async_copy(probs.at[j], target, copies.semaphores.at[first + j])

    attend(lens, pack, packed, probs, mixed_slots, parts, lambda j: probs_copy(j).start())
    copies.leave(mixed_slots, kept[10])
    mixed[...] = dot(ungroup[...], mixed_slots[...]).astype(BF16)
    copies.leave(mixed, kept[3])
    copies.open += [probs_copy(j) for j in range(IMGS)]


def state_scratch(parts):
    rows = pltpu.VMEM((CAP, D), BF16)
    wide = pltpu.VMEM((CAP, FF), BF16)
    count = 1 + 2 * parts
    return [
        *WEIGHT_SCRATCH,
        pltpu.VMEM((count, CAP, D), BF16),
        pltpu.VMEM((PAD, D), BF16),
        pltpu.VMEM((PAD, CAP), BF16),
        pltpu.VMEM((CAP, PAD), BF16),
        pltpu.VMEM((5 if parts == 2 else 1, CAP, D), BF16),
        pltpu.VMEM((count, PAD, D), BF16),
        pltpu.VMEM((IMGS, PAIRS, 2 * SLOT * parts, SLOT), BF16),
        rows,
        rows,
        pltpu.VMEM((2, CAP, D), F32),
        rows,
        wide,
        wide,
        rows,
        pltpu.SemaphoreType.DMA((64,)),
    ]


def encoder_forward_kernel(lens, which, x, e, r, c, given, mid, out, *refs):
    kept, scratch = refs[: len(STATE)], refs[len(STATE) :]
    (
        *held, flat, mixed_slots, regroup, ungroup, normed, packed, probs, mixed, branch, _, f_normed, active,
        slope, f_branch, semaphores,
    ) = scratch
    copies = Copies(semaphores)
    weights = Weights(copies, given, held)
    weights.start(*ALL_BLOCKS, *UPS, *DOWNS)

    def norm(rows):
        centred, _ = normalize(x[rows, :].astype(F32))
        normed[0, rows, :] = (centred * row(e, 0) + row(e, 1)).astype(BF16)

    each_rows(norm)
    copies.leave(normed.at[0], kept[0].at[0])
    weights.wait(0)
    qkvo = weights.held[0]
    flat[0] = ((dot(normed[0], qkvo[:, columns(0)]) + row(e, 2)).astype(BF16) * 0.125).astype(BF16)
    weights.wait(1)
    flat[1] = dot(normed[0], qkvo[:, columns(1)]).astype(BF16)
    weights.wait(2)
    flat[2] = (dot(normed[0], qkvo[:, columns(2)]) + row(e, 3)).astype(BF16)
    attention(copies, lens, which[0], 1, (flat, packed, probs, mixed, mixed_slots, regroup, ungroup), kept)
    weights.wait(3)
    summed = dot_nt(mixed[...], qkvo[:, columns(3)]) + row(e, 4)
    branch[...] = summed.astype(BF16)
    copies.leave(branch, kept[4])
    mid[...] = (x[...].astype(F32) + row(e, 5) * summed).astype(BF16)
    feed_forward(copies, weights, mid, r, c, out, (f_normed, active, slope, f_branch), kept[6:])
    copies.finish()


def encoder_forward(lens, which, x, e, r, c, weights):
    made = pl.pallas_call(
        encoder_forward_kernel,
        in_specs=[SMEM, SMEM, VMEM, VMEM, VMEM, VMEM, ANY],
        out_specs=(VMEM, VMEM, *(ANY for _ in STATE)),
        out_shape=(ROWS, ROWS, *STATE),
        scratch_shapes=state_scratch(1),
        compiler_params=params(56),
        name="encoder_forward",
    )(lens, which, x, e, r, c, weights)
    return made[0], made[1], tuple(made[2:])


def table_rows(indices, table):
    places = lax.broadcasted_iota(jnp.int32, (indices.shape[0], table.shape[0]), 1)
    chosen = jnp.where(places == indices[...], 1.0, 0.0).astype(BF16)
    values = table[...]
    top = values.astype(BF16)
    values = values - top.astype(F32)
    middle = values.astype(BF16)
    bottom = (values - middle.astype(F32)).astype(BF16)
    return (dot(chosen, top) + dot(chosen, middle)) + dot(chosen, bottom)


def regressor_forward_kernel(lens, which, latents, queries, vis, mask, table, e, r, c, given, mid, out, *refs):
    kept, scratch = refs[: len(STATE)], refs[len(STATE) :]
    (
        *held, flat, mixed_slots, regroup, ungroup, normed, packed, probs, mixed, branch, sources, f_normed,
        active, slope, f_branch, semaphores,
    ) = scratch
    copies = Copies(semaphores)
    weights = Weights(copies, given, held)
    weights.start(*ALL_BLOCKS, *UPS, *DOWNS)
    for half, indices in enumerate((mask, vis)):
        sources[half] = table_rows(indices, table)

    def norms(rows):
        residual = queries[rows, :].astype(F32)
        source = residual + sources[0, rows, :]
        sources[0, rows, :] = source
        centred, _ = normalize(source)
        normed[0, rows, :] = (centred * row(e, 0) + row(e, 1)).astype(BF16)
        normed[3, rows, :] = (centred * row(e, 2) + row(e, 3)).astype(BF16)
        centred, _ = normalize(residual)
        normed[4, rows, :] = (centred * row(e, 4) + row(e, 5)).astype(BF16)
        incoming = latents[rows, :].astype(F32)
        source = incoming + sources[1, rows, :]
        sources[1, rows, :] = source
        centred, _ = normalize(source)
        normed[1, rows, :] = (centred * row(e, 2) + row(e, 3)).astype(BF16)
        centred, _ = normalize(incoming)
        normed[2, rows, :] = (centred * row(e, 4) + row(e, 5)).astype(BF16)

    each_rows(norms)
    copies.leave(normed, kept[0])
    copies.leave(sources, kept[5])
    weights.wait(0)
    qkvo = weights.held[0]
    flat[0] = ((dot(normed[0], qkvo[:, columns(0)]) + row(e, 6)).astype(BF16) * 0.125).astype(BF16)
    weights.wait(1)
    for m in (1, 3):
        flat[m] = dot(normed[m], qkvo[:, columns(1)]).astype(BF16)
    weights.wait(2)
    for m in (2, 4):
        flat[m] = (dot(normed[m], qkvo[:, columns(2)]) + row(e, 7)).astype(BF16)
    attention(copies, lens, which[0], 2, (flat, packed, probs, mixed, mixed_slots, regroup, ungroup), kept)
    weights.wait(3)
    summed = dot_nt(mixed[...], qkvo[:, columns(3)]) + row(e, 8)
    branch[...] = summed.astype(BF16)
    copies.leave(branch, kept[4])
    mid[...] = (queries[...].astype(F32) + row(e, 9) * summed).astype(BF16)
    feed_forward(copies, weights, mid, r, c, out, (f_normed, active, slope, f_branch), kept[6:])
    copies.finish()


def regressor_forward(lens, which, latents, queries, vis, mask, table, e, r, c, weights):
    made = pl.pallas_call(
        regressor_forward_kernel,
        in_specs=[SMEM, SMEM, *(VMEM for _ in range(8)), ANY],
        out_specs=(VMEM, VMEM, *(ANY for _ in STATE)),
        out_shape=(ROWS, ROWS, *STATE),
        scratch_shapes=state_scratch(2),
        compiler_params=params(56),
        name="regressor_forward",
    )(lens, which, latents, queries, vis, mask, table, e, r, c, weights)
    return made[0], made[1], tuple(made[2:])


def back_scratch(parts):
    rows = pltpu.VMEM((CAP, D), BF16)
    wide = pltpu.VMEM((CAP, FF), BF16)
    count = 1 + 2 * parts
    return [
        *WEIGHT_SCRATCH,
        wide,
        rows,
        wide,
        rows,
        pltpu.VMEM((count, PAD, D), BF16),
        pltpu.VMEM((IMGS, PAIRS, 2 * SLOT * parts, SLOT), BF16),
        rows,
        pltpu.VMEM((PAD, D), BF16),
        pltpu.VMEM((PAD, D), BF16),
        pltpu.VMEM((PAD, CAP), BF16),
        pltpu.VMEM((CAP, PAD), BF16),
        pltpu.VMEM((count, PAD, D), BF16),
        rows,
        pltpu.VMEM((2, CAP, D), F32),
        pltpu.VMEM((count, CAP, D), BF16),
        pltpu.VMEM((3 if parts == 2 else 1, CAP, D), F32),
        pltpu.VMEM((CAP, D), F32),
        pltpu.SemaphoreType.DMA((64,)),
    ]


def layer_back(parts, lens, pack, grads, mid, e, r, given, state, totals, kept, scratch):
    (
        *held, slope, f_branch, d_hidden, d_f_branch, packed, probs, branch, mixed_slots, d_slots, regroup, ungroup, d_packed,
        d_branch, sources, d_flat, work, residual, semaphores,
    ) = scratch
    copies = Copies(semaphores)
    weights = Weights(copies, given, held)
    parts_in = {"branch": copies.start(state[3], f_branch)}
    for i in ALL_BLOCKS:
        weights.start(2 * BLOCKS + i)
        parts_in[i] = copies.start(state[2].at[:, columns(i)], slope.at[:, columns(i)])
    weights.start(*UPS, 3)
    in_branch = copies.start(state[4], branch)
    in_packed = copies.start(state[0].at[pl.ds(0, 1 + 2 * parts)], packed)
    in_mixed = copies.start(state[6], mixed_slots)
    first = copies.take(IMGS)

    def probs_copy(j):
        source = state[1].at[j, :, pl.ds(0, 2 * SLOT * parts), :]
        return pltpu.make_async_copy(source, probs.at[j], semaphores.at[first + j])

    for j in range(IMGS):
        probs_copy(j).start()
    weights.start(0, 1, 2)
    in_sources = copies.start(state[5], sources) if parts == 2 else None
    totals[...] = jnp.zeros_like(totals)
    group_matrices(lens, pack, regroup, ungroup)
    feed_forward_back(
        copies, weights, lambda name: parts_in[name].wait(), grads, mid, r,
        (slope, f_branch, d_hidden, d_f_branch, work.at[0]), totals, kept[2:], residual,
    )
    in_branch.wait()
    last = 1 + 4 * parts

    def enter(rows, carry):
        g = residual[rows, :]
        low = (g * row(e, last)).astype(BF16)
        d_branch[rows, :] = low
        return carry[0] + colsum(low.astype(F32)), carry[1] + colsum(g * branch[rows, :].astype(F32))

    totals[last - 1 : last], totals[last : last + 1] = over_rows(enter, (zero_row(), zero_row()))
    copies.leave(d_branch, kept[1])
    weights.wait(3)
    d_mixed = dot(d_branch[...], weights.held[0][:, columns(3)]).astype(BF16)
    d_slots[...] = dot(regroup[...], d_mixed).astype(BF16)
    in_packed.wait()
    in_mixed.wait()
    attend_back(packed, probs, mixed_slots, d_slots, d_packed, parts, lambda j: probs_copy(j).wait())
    for m in range(1 + 2 * parts):
        d_flat[m] = dot(ungroup[...], d_packed[m]).astype(BF16)
        copies.leave(d_flat.at[m], kept[0].at[m])
    weights.wait(0, 1, 2)
    if in_sources is not None:
        in_sources.wait()
    return copies, weights.held[0]


def encoder_back_kernel(
    lens, which, g1, g2, x, mid, e, r, weights, s1, s2, s3, s4, s5, s6, s7, d_x, totals, k1, k2, k3, k4, *scratch
):
    *_, d_flat, work, residual, _ = scratch
    copies, qkvo = layer_back(
        1, lens, which[0], (g1, g2), mid, e, r, weights, (s1, s2, s3, s4, s5, s6, s7), totals, (k1, k2, k3, k4), scratch
    )
    d_normed = dot_nt(d_flat[0], qkvo[:, columns(0)])
    for m in (1, 2):
        d_normed += dot_nt(d_flat[m], qkvo[:, columns(m)])
    work[0] = d_normed

    def leave(rows, carry):
        grad = work[0, rows, :]
        normed, inverse = normalize(x[rows, :].astype(F32))
        d_x[rows, :] = (residual[rows, :] + norm_back(grad, row(e, 0), normed, inverse)).astype(BF16)
        terms = (grad * normed, grad, d_flat[0, rows, :].astype(F32), d_flat[2, rows, :].astype(F32))
        return tuple(total + colsum(term) for total, term in zip(carry, terms))

    sums = over_rows(leave, (zero_row(),) * 4)
    for i, total in enumerate(sums):
        totals[i : i + 1] = total
    copies.finish()


def back_state(state):
    return state[1], state[2], state[8], state[9], state[4], state[5], state[10]


def encoder_back(lens, which, g1, g2, x, mid, e, r, weights, state):
    made = pl.pallas_call(
        encoder_back_kernel,
        in_specs=[SMEM, SMEM, *(VMEM for _ in range(6)), *(ANY for _ in range(8))],
        out_specs=(VMEM, VMEM, *(ANY for _ in GRADS)),
        out_shape=(ROWS, TOTALS, *GRADS),
        scratch_shapes=back_scratch(1),
        compiler_params=params(56),
        name="encoder_back",
    )(lens, which, g1, g2, x, mid, e, r, weights, *back_state(state))
    return made[0], made[0], made[1], tuple(made[2:])


def regressor_back_kernel(
    lens, which, g, latents, queries, mid, e, r, weights, s1, s2, s3, s4, s5, s6, s7,
    d_latents, d_queries, totals, k1, k2, k3, k4, *scratch,
):
    *_, sources, d_flat, work, residual, _ = scratch
    copies, qkvo = layer_back(
        2, lens, which[0], (g,), mid, e, r, weights, (s1, s2, s3, s4, s5, s6, s7), totals, (k1, k2, k3, k4), scratch
    )

    def add(carry, terms):
        return tuple(total + colsum(term) for total, term in zip(carry, terms))

    for i, (m, block) in enumerate(((0, 0), (3, 1), (4, 2))):
        work[i] = dot_nt(d_flat[m], qkvo[:, columns(block)])

    def masked(rows, carry):
        normed, inverse = normalize(sources[0, rows, :])
        q_grad, k_grad, v_grad = (work[i, rows, :] for i in range(3))
        both = norm_back(q_grad, row(e, 0), normed, inverse) + norm_back(k_grad, row(e, 2), normed, inverse)
        v_normed, inverse = normalize(queries[rows, :].astype(F32))
        both += norm_back(v_grad, row(e, 4), v_normed, inverse)
        d_queries[rows, :] = (residual[rows, :] + both).astype(BF16)
        bias = d_flat[0, rows, :].astype(F32), d_flat[4, rows, :].astype(F32)
        return add(carry, (q_grad * normed, q_grad, k_grad * normed, k_grad, v_grad * v_normed, v_grad, *bias))

    sums = over_rows(masked, (zero_row(),) * 8)
    for i, (m, block) in enumerate(((1, 1), (2, 2))):
        work[i] = dot_nt(d_flat[m], qkvo[:, columns(block)])

    def visible(rows, carry):
        normed, inverse = normalize(sources[1, rows, :])
        k_grad, v_grad = (work[i, rows, :] for i in range(2))
        total = norm_back(k_grad, row(e, 2), normed, inverse)
        v_normed, inverse = normalize(latents[rows, :].astype(F32))
        d_latents[rows, :] = (total + norm_back(v_grad, row(e, 4), v_normed, inverse)).astype(BF16)
        bias = d_flat[2, rows, :].astype(F32)
        return add(carry, (k_grad * normed, k_grad, v_grad * v_normed, v_grad, bias))

    more = over_rows(visible, (*sums[2:6], sums[7]))
    for i, total in enumerate((*sums[:2], *more[:4], sums[6], more[4])):
        totals[i : i + 1] = total
    copies.finish()


def regressor_back(lens, which, g, latents, queries, mid, e, r, weights, state):
    made = pl.pallas_call(
        regressor_back_kernel,
        in_specs=[SMEM, SMEM, *(VMEM for _ in range(6)), *(ANY for _ in range(8))],
        out_specs=(VMEM, VMEM, VMEM, *(ANY for _ in GRADS)),
        out_shape=(ROWS, ROWS, TOTALS, *GRADS),
        scratch_shapes=back_scratch(2),
        compiler_params=params(56),
        name="regressor_back",
    )(lens, which, g, latents, queries, mid, e, r, weights, *back_state(state))
    return made[0], made[1], made[2], tuple(made[3:])


SHARE = BLOCKS + BLOCKS // 2


def weight_grads_kernel(parts, packs, *refs):
    step = pl.program_id(0)
    *base, out = refs[8 * packs :]
    inputs = [refs[8 * i : 8 * i + 8] for i in range(packs)]

    def put(terms):
        total = base[0][...].astype(F32) if base else None
        for term in terms:
            total = term if total is None else total + term
        out[...] = total.astype(BF16)

    @pl.when((step < 3) if parts == 1 else (step == 0))
    def _():
        put(dot_tn(n[0], p[step]) for n, p, *_ in inputs)

    if parts == 2:

        @pl.when((step == 1) | (step == 2))
        def _():
            put(dot_tn(n[step + more], p[step + more]) for n, p, *_ in inputs for more in (0, 2))

    @pl.when(step == 3)
    def _():
        put(dot_tn(b[...], m[...]) for _, _, m, b, *_ in inputs)

    @pl.when((step >= 4) & (step < 8))
    def _():
        put(dot_tn(n[...], h[...]) for *_, n, h, _, _ in inputs)

    @pl.when(step >= 8)
    def _():
        put(dot_tn(a[...], b[...]) for *_, a, b in inputs)


def grad_place(step):
    tail = jnp.maximum(step - 2 * BLOCKS, 0)
    late = jnp.where(step >= 2 * BLOCKS, 1, 0)
    section = (1 - late) * (step // BLOCKS) + late * (tail // 2)
    block = (1 - late) * (step % BLOCKS) + late * (BLOCKS + tail % 2)
    return section, block, 0, 0


def weight_grads(parts, states, grads, base=()):
    have = 1 if parts == 1 else 5
    made = 3 if parts == 1 else 5
    rows = full((CAP, D))
    up_part = pl.BlockSpec((CAP, D), lambda i: (0, jnp.clip(i - BLOCKS, 0, BLOCKS - 1)))
    down_part = pl.BlockSpec((CAP, D), lambda i: (0, jnp.clip(i - 2 * BLOCKS, 0, BLOCKS - 1)))
    placed = pl.BlockSpec((None, None, D, D), grad_place)
    one = [lead(have, (CAP, D)), lead(made, (CAP, D)), rows, rows, rows, up_part, down_part, rows]
    operands = []
    for s, g in zip(states, grads):
        operands += [s[0], g[0], s[3], g[1], s[6], g[2], s[7], g[3]]
    return pl.pallas_call(
        functools.partial(weight_grads_kernel, parts, len(states)),
        grid=(3 * BLOCKS,),
        in_specs=one * len(states) + [placed for _ in base],
        out_specs=placed,
        out_shape=sds((2, SHARE, D, D), BF16),
        compiler_params=params(),
        name="weight_grads",
    )(*operands, *base)


MESH = pl.DeviceIdType.MESH


def gather_weights_kernel(matrix, down, weights, send, receive, local):
    dp, section = lax.axis_index("dp"), lax.axis_index("section")
    odd = lax.rem(section, 2)
    partner = (dp, section + 1 - 2 * odd)
    barrier = pltpu.get_barrier_semaphore()
    pl.semaphore_signal(barrier, inc=1, device_id=partner, device_id_type=MESH)
    pl.semaphore_wait(barrier, 1)
    places = [(matrix.at[0, :, pl.ds(i * D, D)], odd * BLOCKS + i) for i in range(BLOCKS)]
    places += [(down.at[pl.ds(i * D, D), :], 2 * BLOCKS + odd * (BLOCKS // 2) + i) for i in range(BLOCKS // 2)]
    copies = []
    for i, (source, place) in enumerate(places):
        away = pltpu.make_async_remote_copy(
            source, weights.at[place], send.at[i], receive.at[i], device_id=partner, device_id_type=MESH
        )
        away.start()
        here = pltpu.make_async_copy(source, weights.at[place], local.at[i])
        here.start()
        copies += [away, here]
    for copy in copies:
        copy.wait()


def gather_weights(matrix, down):
    vmem = pl.BlockSpec(memory_space=pltpu.VMEM)
    return pl.pallas_call(
        gather_weights_kernel,
        in_specs=[vmem, vmem],
        out_specs=ANY,
        out_shape=sds((3 * BLOCKS, D, D), matrix.dtype),
        scratch_shapes=[pltpu.SemaphoreType.DMA((SHARE,)) for _ in range(3)],
        compiler_params=params(collective_id=1, has_side_effects=True),
        name="gather_weights",
    )(matrix, down)


RING = 8
SEGMENT = D // RING
PART = SEGMENT // 2
CHAIN = SHARE // 2


def ring_place(d):
    odd = lax.rem(d, 2)
    return (1 - odd) * lax.div(d, 2) + odd * (RING - 1 - lax.div(d, 2))


def ring_device(place):
    place = lax.rem(place + RING, RING)
    late = lax.div(place, RING // 2)
    return (1 - late) * 2 * place + late * (2 * (RING - 1 - place) + 1)


def reduce_kernel(
    grads, swapping, vectors, out_matrix, out_down, swapped, out_vectors,
    mine, partner_part, landing, final, stage, v_sum, v_in,
    pair_send, pair_receive, own_sem, ring_send, ring_receive, last_send, last_receive, out_sem,
    v_send, v_receive, swap_send, swap_receive,
):
    d, section = lax.axis_index("dp"), lax.axis_index("section")
    odd = lax.rem(section, 2)
    place = ring_place(d)
    across = (d, section + 2 - 4 * lax.div(section, 2))
    pair = (d, section + 1 - 2 * odd)
    ways = ((ring_device(place + 1), section), (ring_device(place - 1), section))

    def flipped(bit):
        return d + bit - 2 * bit * lax.rem(lax.div(d, bit), 2)

    levels = (pair, (flipped(1), section), (flipped(2), section), (flipped(4), section), across)
    barrier = pltpu.get_barrier_semaphore()
    for other in (*ways, *levels):
        pl.semaphore_signal(barrier, inc=1, device_id=other, device_id_type=MESH)
    pl.semaphore_wait(barrier, len(ways) + len(levels))

    def rows_of(step, way):
        segment = lax.rem(place + (step if way else -step) + 2 * RING, RING)
        return pl.ds(pl.multiple_of(segment * SEGMENT + way * PART, 8), PART)

    def remote(source, target, send, receive, device):
        return pltpu.make_async_remote_copy(source, target, send, receive, device_id=device, device_id_type=MESH)

    swap = remote(swapping, swapped, swap_send, swap_receive, across)
    swap.start()
    own = pltpu.make_async_copy(grads.at[odd], mine, own_sem)
    own.start()

    def pair_copy(step, way):
        rows = rows_of(step, way)
        return remote(
            grads.at[1 - odd, :, rows, :], partner_part.at[:, rows, :],
            pair_send.at[step, way], pair_receive.at[step, way], pair,
        )

    def start_pair(step, carry):
        for way in range(2):
            pair_copy(step, way).start()
        return carry

    lax.fori_loop(0, RING, start_pair, 0)

    def vector_copy(level):
        return remote(v_sum.at[level], v_in.at[level], v_send.at[level], v_receive.at[level], levels[level])

    def vector_next(level):
        vector_copy(level).wait()
        if level + 1 < len(levels):
            v_sum[level + 1] = v_sum[level] + v_in[level]
            vector_copy(level + 1).start()

    v_sum[0] = vectors[...]
    vector_copy(0).start()

    def blocks(chain):
        return pl.ds(chain * CHAIN, CHAIN)

    def ring_copy(step, way, chain):
        rows = rows_of(step, way)
        return remote(
            mine.at[blocks(chain), rows, :], landing.at[blocks(chain), rows, :],
            ring_send.at[step, way, chain], ring_receive.at[step, way, chain], ways[way],
        )

    def incoming(step, way, chain):
        rows = rows_of(step + 1, way)
        return remote(
            mine.at[blocks(chain), rows, :], landing.at[blocks(chain), rows, :],
            ring_send.at[step, way, chain], ring_receive.at[step, way, chain], ways[way],
        )

    own.wait()
    for way in range(2):
        pair_copy(0, way).wait_recv()
        rows = rows_of(0, way)
        for chain in range(2):
            part = (blocks(chain), rows, slice(None))
            mine[part] = (mine[part].astype(F32) + partner_part[part].astype(F32)).astype(BF16)
            ring_copy(0, way, chain).start()
    vector_next(0)

    def total_of(part):
        return (
            mine[part].astype(F32) + partner_part[part].astype(F32) + landing[part].astype(F32)
        ).astype(BF16)

    def reduce_step(step, carry):
        for chain in range(2):
            for way in range(2):
                if chain == 0:
                    pair_copy(step, way).wait_recv()
                incoming(step - 1, way, chain).wait_recv()
                part = (blocks(chain), rows_of(step, way), slice(None))
                mine[part] = total_of(part)
                ring_copy(step, way, chain).start()
        return carry

    lax.fori_loop(1, RING - 1, reduce_step, 0)
    vector_next(1)

    def last_copy(step, way, chain):
        rows = rows_of(step + RING - 1, way)
        return remote(
            final.at[blocks(chain), rows, :], final.at[blocks(chain), rows, :],
            last_send.at[step, way, chain], last_receive.at[step, way, chain], ways[way],
        )

    def last_incoming(step, way, chain):
        rows = rows_of(step + RING, way)
        return remote(
            final.at[blocks(chain), rows, :], final.at[blocks(chain), rows, :],
            last_send.at[step, way, chain], last_receive.at[step, way, chain], ways[way],
        )

    def out_copies(step, way, chain):
        rows = rows_of(step + RING - 1, way)
        copies = []
        for i in range(CHAIN):
            block = chain * CHAIN + i
            if block < BLOCKS:
                target = out_matrix.at[0, rows, pl.ds(block * D, D)]
            else:
                segment = lax.rem(place + (step + RING - 1 if way else 1 - step - RING) + 4 * RING, RING)
                start = (block - BLOCKS) * D + segment * SEGMENT + way * PART
                target = out_down.at[pl.ds(pl.multiple_of(start, 8), PART), :]
            copies.append(pltpu.make_async_copy(stage.at[way, chain, i], target, out_sem.at[way, chain, i]))
        return copies

    def write_out(step, way, chain, first):
        if not first:
            for copy in out_copies(step - 1, way, chain):
                copy.wait()
        stage[way, chain] = final[blocks(chain), rows_of(step + RING - 1, way), :].astype(F32)
        for copy in out_copies(step, way, chain):
            copy.start()

    for chain in range(2):
        for way in range(2):
            if chain == 0:
                pair_copy(RING - 1, way).wait_recv()
            incoming(RING - 2, way, chain).wait_recv()
            part = (blocks(chain), rows_of(RING - 1, way), slice(None))
            final[part] = total_of(part)
            last_copy(0, way, chain).start()
    vector_next(2)
    for chain in range(2):
        for way in range(2):
            write_out(0, way, chain, True)

    def gather_step(step, carry):
        for chain in range(2):
            for way in range(2):
                last_incoming(step - 1, way, chain).wait_recv()
                last_copy(step, way, chain).start()
                write_out(step, way, chain, False)
        return carry

    lax.fori_loop(1, 3, gather_step, 0)
    vector_next(3)
    lax.fori_loop(3, 5, gather_step, 0)
    vector_next(4)
    out_vectors[0] = v_sum[len(levels) - 1]
    out_vectors[1] = v_in[len(levels) - 1]
    lax.fori_loop(5, RING - 1, gather_step, 0)
    for chain in range(2):
        for way in range(2):
            last_incoming(RING - 2, way, chain).wait_recv()
            write_out(RING - 1, way, chain, False)
    for chain in range(2):
        for way in range(2):
            for copy in out_copies(RING - 1, way, chain):
                copy.wait()

    def all_sent(step, carry):
        for way in range(2):
            for chain in range(2):
                ring_copy(step, way, chain).wait_send()
                last_copy(step, way, chain).wait_send()
        return carry

    lax.fori_loop(0, RING - 1, all_sent, 0)

    def pair_sent(step, carry):
        for way in range(2):
            pair_copy(step, way).wait_send()
        return carry

    lax.fori_loop(0, RING, pair_sent, 0)
    swap.wait()


def reduce_grads(grads, swapping, vectors):
    share = (SHARE, D, D)
    vmem = pl.BlockSpec(memory_space=pltpu.VMEM)
    dma = pltpu.SemaphoreType.DMA
    return pl.pallas_call(
        reduce_kernel,
        in_specs=[ANY, ANY, vmem],
        out_specs=(ANY, ANY, ANY, vmem),
        out_shape=(
            sds((1, D, FF), F32),
            sds((FF // 2, D), F32),
            sds(swapping.shape, swapping.dtype),
            sds((2, VECTORS, D), F32),
        ),
        scratch_shapes=[
            pltpu.VMEM(share, BF16),
            pltpu.VMEM(share, BF16),
            pltpu.VMEM(share, BF16),
            pltpu.VMEM(share, BF16),
            pltpu.VMEM((2, 2, CHAIN, PART, D), F32),
            pltpu.VMEM((5, VECTORS, D), F32),
            pltpu.VMEM((5, VECTORS, D), F32),
            dma((RING, 2)),
            dma((RING, 2)),
            dma,
            dma((RING - 1, 2, 2)),
            dma((RING - 1, 2, 2)),
            dma((RING - 1, 2, 2)),
            dma((RING - 1, 2, 2)),
            dma((2, 2, CHAIN)),
            dma((5,)),
            dma((5,)),
            dma,
            dma,
        ],
        compiler_params=params(56, collective_id=2, has_side_effects=True),
        name="reduce_grads",
    )(grads, swapping, vectors)


def plain_reduce_grads(grads, swapping, vectors):
    odd = lax.rem(lax.axis_index("section"), 2)
    pair = [(0, 1), (1, 0), (2, 3), (3, 2)]
    theirs = lax.dynamic_index_in_dim(grads, 1 - odd, 0, keepdims=False)
    mine = lax.dynamic_index_in_dim(grads, odd, 0, keepdims=False)
    total = lax.psum(mine + lax.ppermute(theirs, "section", pair), "dp").astype(F32)
    vectors = lax.psum(vectors + lax.ppermute(vectors, "section", pair), "dp")
    matrix = jnp.swapaxes(total[:BLOCKS], 0, 1).reshape(1, D, FF)
    return (
        matrix,
        total[BLOCKS:].reshape(FF // 2, D),
        swap_layers(swapping),
        jnp.stack([vectors, swap_layers(vectors)]),
    )


def swap_layers(block):
    return lax.ppermute(block, "section", [(0, 2), (1, 3), (2, 0), (3, 1)])


def to_regressor(block):
    return lax.ppermute(block, "section", [(0, 2), (1, 3)])


def to_encoder(block):
    return lax.ppermute(block, "section", [(2, 0), (3, 1)])


def body(
    vis_embed, latent_cot, reg_queries, out_cot, section_matrix, down_weight, enc_vectors, reg_vectors,
    mlp_vectors, hidden_bias, pos_table, image_lengths, vis_index, mask_index,
):
    section = lax.axis_index("section")
    odd = lax.rem(section, 2)
    is_reg = section >= 2
    layer = jnp.where(is_reg, 1, 0)
    weights = gather_weights(section_matrix, down_weight)
    r = lax.dynamic_index_in_dim(mlp_vectors, layer, 0, keepdims=False)
    c = lax.dynamic_slice_in_dim(hidden_bias, layer, 1, 0)
    packs = [(odd + 2 * i).reshape(1).astype(jnp.int32) for i in range(2)]
    vis = [lax.dynamic_slice_in_dim(vis_index, (odd + 2 * i) * CAP, CAP)[:, None] for i in range(2)]
    mask = [lax.dynamic_slice_in_dim(mask_index, (odd + 2 * i) * CAP, CAP)[:, None] for i in range(2)]

    incoming = swap_layers(jnp.where(is_reg, vis_embed, reg_queries))
    x = [vis_embed, incoming]
    queries = [incoming, reg_queries]

    def enc_forward(i):
        return encoder_forward(image_lengths, packs[i], x[i], enc_vectors, r, c, weights)

    def reg_forward(i, latents):
        return regressor_forward(
            image_lengths, packs[i], latents, queries[i], vis[i], mask[i], pos_table, reg_vectors, r, c, weights
        )

    def no_forward():
        made = unset((ROWS, ROWS, *STATE))
        return made[0], made[1], tuple(made[2:])

    def enc_back(i, d_latents, kept):
        return encoder_back(
            image_lengths, packs[i], lat_cot[i], d_latents, x[i], kept[0], enc_vectors, r, weights, kept[2]
        )

    def reg_back(i, latents, kept):
        return regressor_back(
            image_lengths, packs[i], cot[i], latents, queries[i], kept[0], reg_vectors, r, weights, kept[2]
        )

    def no_back():
        made = unset((ROWS, ROWS, TOTALS, *GRADS))
        return made[0], made[1], made[2], tuple(made[3:])

    def on_encoder(work, otherwise):
        return lax.cond(is_reg, otherwise, work)

    def on_regressor(work, otherwise):
        return lax.cond(is_reg, work, otherwise)

    enc1 = on_encoder(lambda: enc_forward(0), no_forward)
    latents1 = to_regressor(enc1[1])
    swapped_cot = swap_layers(jnp.where(is_reg, latent_cot, out_cot))
    lat_cot = [latent_cot, swapped_cot]
    cot = [swapped_cot, out_cot]
    enc2 = on_encoder(lambda: enc_forward(1), no_forward)
    latents2 = to_regressor(enc2[1])

    def reg_first():
        state = reg_forward(0, latents1)
        return state, reg_back(0, latents1, state)

    reg1, reg_grads1 = on_regressor(reg_first, lambda: (no_forward(), no_back()))
    d_latents1 = to_encoder(reg_grads1[0])
    reg2 = on_regressor(lambda: reg_forward(1, latents2), no_forward)
    reg_grads2 = on_regressor(lambda: reg_back(1, latents2, reg2), no_back)
    d_latents2 = to_encoder(reg_grads2[0])
    share = sds((2, SHARE, D, D), BF16)

    def enc_back1():
        grads = enc_back(0, d_latents1, enc1)
        return grads, weight_grads(1, (enc1[2],), (grads[3],))

    enc_grads1, enc_share = on_encoder(enc_back1, lambda: (no_back(), unset((share,))[0]))

    def reg_last():
        return (
            weight_grads(2, (reg1[2], reg2[2]), (reg_grads1[3], reg_grads2[3])),
            reg_grads1[2] + reg_grads2[2],
            jnp.stack([reg1[1], reg_grads1[1]]),
        )

    def enc_last():
        grads = enc_back(1, d_latents2, enc2)
        return (
            weight_grads(1, (enc2[2],), (grads[3],), (enc_share,)),
            enc_grads1[2] + grads[2],
            jnp.stack([grads[0], grads[0]]),
        )

    grads, vectors, swapping = lax.cond(is_reg, reg_last, enc_last)
    reduce = reduce_grads if lax.axis_size("dp") == RING else plain_reduce_grads
    matrix_grad, down_grad, swapped, vectors = reduce(grads, swapping, vectors)

    def pick(reg, enc):
        return jnp.where(is_reg, reg, enc)

    latents = pick(latents2, enc1[1])
    regressed = pick(reg2[1], swapped[0])
    vis_grad = pick(swapped[0], enc_grads1[0])
    query_grad = pick(reg_grads2[1], swapped[1])
    enc_total, reg_total = pick(vectors[1], vectors[0]), pick(vectors[0], vectors[1])
    return (
        latents,
        regressed,
        vis_grad,
        query_grad,
        matrix_grad,
        down_grad,
        enc_total[:6],
        reg_total[:10],
        jnp.stack([enc_total[FFN_AT:HIDDEN_AT], reg_total[FFN_AT:HIDDEN_AT]]),
        jnp.stack([t[HIDDEN_AT : HIDDEN_AT + BLOCKS].reshape(FF) for t in (enc_total, reg_total)]),
    )


def solution(mesh):
    rows = P(("dp", "section"), None)
    in_specs = (
        rows, rows, rows, rows, P("section", None, None), P("section", None),
        P(), P(), P(), P(), P(), P("dp", None), P("dp"), P("dp"),
    )
    out_specs = (rows, rows, rows, rows, P("section", None, None), P("section", None), P(), P(), P(), P())
    return jax.shard_map(body, mesh=mesh, in_specs=in_specs, out_specs=out_specs, check_vma=False)
```

```python
import functools

import jax
import jax.numpy as jnp
from jax import lax
from jax.experimental import pallas as pl
from jax.experimental.pallas import tpu as pltpu
from jax.sharding import PartitionSpec as P

F32 = jnp.float32
BF16 = jnp.bfloat16
CAP = 384
IMGS = 4
SLOT = 128
PAD = IMGS * SLOT
D = 768
FF = 3072
LANES = 128
PAIRS = D // LANES
BLOCKS = FF // D
VECTORS = 24
EPS = 1e-06
MIB = 1 << 20
ANY = pl.BlockSpec(memory_space=pl.ANY)
SMEM = pl.BlockSpec(memory_space=pltpu.SMEM)


def params(limit=48, **more):
    return pltpu.CompilerParams(vmem_limit_bytes=limit * MIB, **more)


def sds(shape, dtype):
    return jax.ShapeDtypeStruct(shape, dtype)


def dot(a, b):
    return jnp.dot(a, b, preferred_element_type=F32)


def dot_nt(a, b):
    return lax.dot_general(a, b, (((1,), (1,)), ((), ())), preferred_element_type=F32)


def dot_tn(a, b):
    return lax.dot_general(a, b, (((0,), (0,)), ((), ())), preferred_element_type=F32)


def row(ref, i):
    return ref[i : i + 1, :]


def colsum(values):
    return jnp.sum(values, axis=0, keepdims=True)


def normalize(values):
    centred = values - jnp.mean(values, axis=-1, keepdims=True)
    spread = jnp.mean(centred * centred, axis=-1, keepdims=True)
    inverse = lax.rsqrt(spread + EPS)
    return centred * inverse, inverse


def norm_back(gradient, gain, normed, inverse):
    scaled = gradient * gain
    level = jnp.mean(scaled, axis=-1, keepdims=True)
    slope = jnp.mean(scaled * normed, axis=-1, keepdims=True)
    return inverse * (scaled - level - normed * slope)


def gelu_parts(t):
    e = jnp.exp(-0.5 * t * t)
    k = 1.0 / (1.0 + (0.3275911 * 0.7071067811865476) * jnp.abs(t))
    poly = k * (
        0.127414796
        + k * (-0.142248368 + k * (0.7107068705 + k * (-0.7265760135 + k * 0.5307027145)))
    )
    tail = poly * e
    phi = jnp.where(t >= 0.0, 1.0 - tail, tail)
    return t * phi, phi + t * (e * 0.3989422804014327)


def group_matrices(lens, pack, regroup, ungroup):
    def image(j, start):
        size = lens[pack, j]
        slots = pl.ds(pl.multiple_of(j * SLOT, SLOT), SLOT)
        place = lax.broadcasted_iota(jnp.int32, (SLOT, CAP), 0)
        rows = lax.broadcasted_iota(jnp.int32, (SLOT, CAP), 1)
        hit = (place + start == rows) & (place < size)
        regroup[slots, :] = jnp.where(hit, 1.0, 0.0).astype(BF16)
        place = lax.broadcasted_iota(jnp.int32, (CAP, SLOT), 1)
        rows = lax.broadcasted_iota(jnp.int32, (CAP, SLOT), 0)
        hit = (place + start == rows) & (place < size)
        ungroup[:, slots] = jnp.where(hit, 1.0, 0.0).astype(BF16)
        return start + size

    lax.fori_loop(0, IMGS, image, jnp.int32(0))


def lane_halves():
    lane = lax.broadcasted_iota(jnp.int32, (1, LANES), 1)
    first = jnp.where(lane < LANES // 2, 1.0, 0.0)
    return first.astype(BF16), (1.0 - first).astype(BF16)


def both_heads(block, halves):
    return jnp.concatenate([block * halves[0], block * halves[1]], axis=0)


def merge_heads(stacked):
    keys = stacked.shape[0] // 2
    lane = lax.broadcasted_iota(jnp.int32, (keys, LANES), 1)
    return jnp.where(lane < LANES // 2, stacked[:keys], stacked[keys:])


def softmax(scores):
    raised = jnp.exp(scores - jnp.max(scores, axis=0, keepdims=True))
    return (raised * (1.0 / jnp.sum(raised, axis=0, keepdims=True))).astype(BF16)


def keys_of(packed, first, parts, rows, cols, halves):
    return both_heads(
        jnp.concatenate([packed[first + 2 * m, rows, cols] for m in range(parts)], axis=0), halves
    )


def attend(lens, pack, packed, probs, mixed_slots, parts, done):
    halves = lane_halves()
    keys = SLOT * parts
    place = lax.bitwise_and(lax.broadcasted_iota(jnp.int32, (keys, SLOT), 0), SLOT - 1)
    for j in range(IMGS):
        rows = slice(j * SLOT, (j + 1) * SLOT)
        valid = place < lens[pack, j]
        for g in range(PAIRS):
            cols = slice(g * LANES, (g + 1) * LANES)
            scores = dot_nt(keys_of(packed, 1, parts, rows, cols, halves), packed[0, rows, cols])
            low = jnp.concatenate(
                [softmax(jnp.where(valid, part, -1e30)) for part in (scores[:keys], scores[keys:])], axis=0
            )
            probs[j, g] = low
            mixed_slots[rows, cols] = dot_tn(low, keys_of(packed, 2, parts, rows, cols, halves)).astype(BF16)
        done(j)


def attend_back(packed, probs, mixed_slots, d_mixed_slots, parts, ready):
    halves = lane_halves()
    keys = SLOT * parts
    less = both_heads(jnp.full((keys, LANES), -1.0, BF16), halves)

    def image(j, carry):
        ready(j)
        rows = pl.ds(pl.multiple_of(j * SLOT, SLOT), SLOT)
        for g in range(PAIRS):
            cols = slice(g * LANES, (g + 1) * LANES)
            d_out = d_mixed_slots[rows, cols]
            centre = (d_out.astype(F32) * mixed_slots[rows, cols].astype(F32)).astype(BF16)
            low = probs[j, g]
            d_prob = dot_nt(
                jnp.concatenate([keys_of(packed, 2, parts, rows, cols, halves), less], axis=1),
                jnp.concatenate([d_out, centre], axis=1),
            )
            d_scores = (low.astype(F32) * d_prob).astype(BF16)
            q = packed[0, rows, cols]
            zero = jnp.zeros_like(q)
            sides = jnp.concatenate(
                [jnp.concatenate([q, zero], axis=1), jnp.concatenate([zero, d_out], axis=1)], axis=0
            )
            d_kv = dot(jnp.concatenate([d_scores, low], axis=1), sides)
            d_q = dot_tn(d_scores, keys_of(packed, 1, parts, rows, cols, halves)) * 0.125
            packed[0, rows, cols] = d_q.astype(BF16)
            for side in range(2):
                merged = merge_heads(d_kv[:, side * LANES : (side + 1) * LANES]).astype(BF16)
                for m in range(parts):
                    packed[1 + side + 2 * m, rows, cols] = merged[m * SLOT : (m + 1) * SLOT]
        return carry

    lax.fori_loop(0, IMGS, image, 0)


ROWS = sds((CAP, D), BF16)
WIDE = sds((CAP, FF), BF16)
TOTALS = sds((VECTORS, D), F32)
FFN_AT = 10
HIDDEN_AT = FFN_AT + 4
ENC_STATE = (
    ROWS,
    sds((3, PAD, D), BF16),
    sds((IMGS, PAIRS, 2 * SLOT, SLOT), BF16),
    sds((PAD, D), BF16),
    ROWS,
    ROWS,
    ROWS,
    WIDE,
    WIDE,
    ROWS,
)
REG_BEFORE = (
    sds((3, CAP, D), BF16),
    sds((3, PAD, D), BF16),
    sds((2, CAP, D), F32),
)
REG_STATE = (
    sds((2, CAP, D), BF16),
    sds((5, CAP, D), BF16),
    ROWS,
    ROWS,
    ROWS,
    WIDE,
    WIDE,
    ROWS,
)


def full(shape):
    return pl.BlockSpec(shape, lambda i: (0,) * len(shape))


VMEM = pl.BlockSpec(memory_space=pltpu.VMEM)


def scratch(shape):
    return pltpu.VMEM(shape.shape, shape.dtype)


def unset(shapes):
    def kernel(*refs):
        del refs

    return pl.pallas_call(
        kernel, out_shape=shapes, out_specs=tuple(ANY for _ in shapes), name="unset"
    )()


class Copies:
    def __init__(self, semaphores):
        self.semaphores, self.used, self.open = semaphores, 0, []

    def take(self, count=1):
        self.used += count
        return self.used - count

    def start(self, source, target):
        copy = pltpu.make_async_copy(source, target, self.semaphores.at[self.take()])
        copy.start()
        return copy

    def leave(self, source, target):
        self.open.append(self.start(source, target))

    def finish(self):
        for copy in self.open:
            copy.wait()


COPIES = pltpu.SemaphoreType.DMA((80,))


def columns(i):
    return slice(i * D, (i + 1) * D)


class Weights:
    def __init__(self, copies, weights, held):
        self.copies, self.weights, self.held, self.started = copies, weights, held, {}

    def target(self, i):
        kind, block = divmod(i, BLOCKS)
        held = self.held[kind]
        return held.at[columns(block), :] if kind == 2 else held.at[:, columns(block)]

    def start(self, *order):
        for i in order:
            self.started[i] = self.copies.start(self.weights.at[i], self.target(i))

    def wait(self, *which):
        for i in which:
            self.started[i].wait()


WEIGHT_SCRATCH = [pltpu.VMEM((D, FF), BF16), pltpu.VMEM((D, FF), BF16), pltpu.VMEM((FF, D), BF16)]
ALL_BLOCKS = range(BLOCKS)
UPS = [BLOCKS + i for i in ALL_BLOCKS]
DOWNS = [2 * BLOCKS + i for i in ALL_BLOCKS]


def feed_forward(weights, mid, r, c, out, state, made):
    normed, active, slope, branch = state
    values = mid[...].astype(F32)
    centred, _ = normalize(values)
    normed[...] = (centred * row(r, 0) + row(r, 1)).astype(BF16)
    made("normed")
    _, up, down = weights.held
    for i in ALL_BLOCKS:
        weights.wait(BLOCKS + i)
        value, steep = gelu_parts(dot(normed[...], up[:, columns(i)]) + c[:, columns(i)])
        active[:, columns(i)] = value.astype(BF16)
        slope[:, columns(i)] = steep.astype(BF16)
        made(i)
    weights.wait(*DOWNS)
    summed = dot(active[...], down[...]) + row(r, 2)
    branch[...] = summed.astype(BF16)
    out[...] = (values + row(r, 3) * summed).astype(BF16)
    made("branch")


def feed_forward_back(weights, ready, g, mid, r, refs, totals, residual, made):
    slope, branch, d_branch = refs
    _, up, down = weights.held
    d_branch[...] = (g * row(r, 3)).astype(BF16)
    made("branch")
    totals[FFN_AT + 2 : FFN_AT + 3] = colsum(d_branch[...].astype(F32))
    ready("branch")
    totals[FFN_AT + 3 : FFN_AT + 4] = colsum(g * branch[...].astype(F32))
    for i in ALL_BLOCKS:
        weights.wait(2 * BLOCKS + i)
        ready(i)
        d_active = dot_nt(d_branch[...], down[columns(i), :])
        d_hidden = (d_active * slope[:, columns(i)].astype(F32)).astype(BF16)
        slope[:, columns(i)] = d_hidden
        made(i)
        totals[HIDDEN_AT + i : HIDDEN_AT + i + 1] = colsum(d_hidden.astype(F32))
    weights.wait(*UPS)
    d_normed = dot_nt(slope[...], up[...])
    normed, inverse = normalize(mid[...].astype(F32))
    totals[FFN_AT : FFN_AT + 1] = colsum(d_normed * normed)
    totals[FFN_AT + 1 : FFN_AT + 2] = colsum(d_normed)
    residual[...] = (g + norm_back(d_normed, row(r, 0), normed, inverse)).astype(BF16).astype(F32)


def attention_back(parts, weights, e, refs, totals, ready, made):
    residual, branch, d_branch, regroup, ungroup, packed, probs, mixed_slots, d_slots, d_flat = refs
    last = 1 + 4 * parts
    g = residual[...]
    ready("branch")
    d_branch[...] = (g * row(e, last)).astype(BF16)
    made("branch")
    totals[last : last + 1] = colsum(g * branch[...].astype(F32))
    totals[last - 1 : last] = colsum(d_branch[...].astype(F32))
    weights.wait(3)
    d_mixed = dot(d_branch[...], weights.held[0][:, columns(3)]).astype(BF16)
    d_slots[...] = dot(regroup[...], d_mixed).astype(BF16)
    ready("packed")
    attend_back(packed, probs, mixed_slots, d_slots, parts, ready)
    for m in range(1 + 2 * parts):
        d_flat[m] = dot(ungroup[...], packed[m]).astype(BF16)
        made(m)


def nothing(name):
    del name


def encoder_forward_kernel(lens, which, x, e, r, c, given, mid, out, *refs):
    kept, scratch = refs[: len(ENC_STATE)], refs[len(ENC_STATE) :]
    *held, flat, regroup, ungroup, semaphores = scratch[: 3 + 4]
    state = scratch[3 + 4 :]
    normed, packed, probs, mixed_slots, mixed, branch, *ffn = state
    pack = which[0]
    copies = Copies(semaphores)
    weights = Weights(copies, given, held)
    weights.start(*ALL_BLOCKS, *UPS, *DOWNS)
    values = x[...].astype(F32)
    centred, _ = normalize(values)
    normed[...] = (centred * row(e, 0) + row(e, 1)).astype(BF16)
    copies.leave(normed, kept[0])
    group_matrices(lens, pack, regroup, ungroup)
    qkvo = weights.held[0]
    weights.wait(0)
    flat[0] = ((dot(normed[...], qkvo[:, columns(0)]) + row(e, 2)).astype(BF16) * 0.125).astype(BF16)
    weights.wait(1)
    flat[1] = dot(normed[...], qkvo[:, columns(1)]).astype(BF16)
    weights.wait(2)
    flat[2] = (dot(normed[...], qkvo[:, columns(2)]) + row(e, 3)).astype(BF16)
    for m in range(3):
        packed[m] = dot(regroup[...], flat[m]).astype(BF16)
        copies.leave(packed.at[m], kept[1].at[m])
    attend(lens, pack, packed, probs, mixed_slots, 1, lambda j: copies.leave(probs.at[j], kept[2].at[j]))
    copies.leave(mixed_slots, kept[3])
    mixed[...] = dot(ungroup[...], mixed_slots[...]).astype(BF16)
    copies.leave(mixed, kept[4])
    weights.wait(3)
    summed = dot_nt(mixed[...], qkvo[:, columns(3)]) + row(e, 4)
    branch[...] = summed.astype(BF16)
    copies.leave(branch, kept[5])
    mid[...] = (values + row(e, 5) * summed).astype(BF16)

    def made(name):
        if name == "normed":
            copies.leave(ffn[0], kept[6])
        elif name == "branch":
            copies.leave(ffn[3], kept[9])
        else:
            for k in (1, 2):
                copies.leave(ffn[k].at[:, columns(name)], kept[6 + k].at[:, columns(name)])

    feed_forward(weights, mid, r, c, out, ffn, made)
    copies.finish()


def encoder_forward(lens, which, x, e, r, c, weights):
    made = pl.pallas_call(
        encoder_forward_kernel,
        in_specs=[SMEM, SMEM, VMEM, VMEM, VMEM, VMEM, ANY],
        out_specs=(VMEM, VMEM, *(ANY for _ in ENC_STATE)),
        out_shape=(ROWS, ROWS, *ENC_STATE),
        scratch_shapes=[
            *WEIGHT_SCRATCH,
            pltpu.VMEM((3, CAP, D), BF16),
            pltpu.VMEM((PAD, CAP), BF16),
            pltpu.VMEM((CAP, PAD), BF16),
            COPIES,
            *map(scratch, ENC_STATE),
        ],
        compiler_params=params(58),
        name="encoder_forward",
    )(lens, which, x, e, r, c, weights)
    return made[0], made[1], tuple(made[2:])


def encoder_back_kernel(more, lens, which, g1, g2, x, mid, e, r, given, *refs):
    state, refs = refs[: len(ENC_STATE)], refs[len(ENC_STATE) :]
    base, refs = refs[:more], refs[more:]
    d_x, totals, share, *held, regroup, ungroup, d_slots, d_branch, d_f_branch, d_flat, residual, blocks, semaphores = (
        refs[: 3 + 3 + 9]
    )
    normed, packed, probs, mixed_slots, mixed, branch, f_normed, active, slope, f_branch = refs[3 + 3 + 9 :]
    copies = Copies(semaphores)
    weights = Weights(copies, given, held)
    coming = {"branch": copies.start(state[9], f_branch)}
    for i in ALL_BLOCKS:
        weights.start(2 * BLOCKS + i)
        coming[i] = copies.start(state[8].at[:, columns(i)], slope.at[:, columns(i)])
    weights.start(*UPS, 3)
    later = {"branch": copies.start(state[5], branch)}
    later["packed"] = copies.start(state[1], packed)
    later["mixed"] = copies.start(state[3], mixed_slots)
    probs_in = [copies.start(state[2].at[j], probs.at[j]) for j in range(IMGS)]
    late = [copies.start(state[i], ref) for i, ref in ((6, f_normed), (7, active), (0, normed), (4, mixed))]
    weights.start(0, 1, 2)

    slots = blocks.shape[0]
    order = [(1, i) for i in ALL_BLOCKS] + [(i // 2, BLOCKS + i % 2) for i in ALL_BLOCKS] + [(0, i) for i in ALL_BLOCKS]
    first = copies.take(2 * len(order))

    def base_copy(i):
        return pltpu.make_async_copy(base[0].at[order[i]], blocks.at[i % slots], semaphores.at[first + 2 * i])

    def out_copy(i):
        return pltpu.make_async_copy(blocks.at[i % slots], share.at[order[i]], semaphores.at[first + 2 * i + 1])

    if more:
        for i in range(slots):
            base_copy(i).start()

    def put(i, product):
        if more:
            base_copy(i).wait()
            product = product + blocks[i % slots].astype(F32)
        elif i >= slots:
            out_copy(i - slots).wait()
        blocks[i % slots] = product.astype(BF16)
        out_copy(i).start()
        ahead = i + slots // 2
        if more and slots <= ahead < len(order):
            out_copy(ahead - slots).wait()
            base_copy(ahead).start()

    totals[...] = jnp.zeros_like(totals)
    group_matrices(lens, which[0], regroup, ungroup)
    g = g1[...].astype(F32) + g2[...].astype(F32)
    feed_forward_back(
        weights, lambda name: coming[name].wait(), g, mid, r, (slope, f_branch, d_f_branch), totals, residual, nothing
    )
    for copy in late:
        copy.wait()
    count = 0
    for i in ALL_BLOCKS:
        put(count, dot_tn(f_normed[...], slope[:, columns(i)]))
        count += 1
    for i in ALL_BLOCKS:
        put(count, dot_tn(active[:, columns(i)], d_f_branch[...]))
        count += 1

    def ready(name):
        if name == "branch":
            later["branch"].wait()
        elif name == "packed":
            later["packed"].wait()
            later["mixed"].wait()
            for copy in probs_in:
                copy.wait()

    attention_back(
        1, weights, e, (residual, branch, d_branch, regroup, ungroup, packed, probs, mixed_slots, d_slots, d_flat),
        totals, ready, nothing,
    )
    for i in ALL_BLOCKS:
        put(count, dot_tn(normed[...], d_flat[i]) if i < 3 else dot_tn(d_branch[...], mixed[...]))
        count += 1
    weights.wait(0, 1, 2)
    qkvo = weights.held[0]
    d_normed = dot_nt(d_flat[0], qkvo[:, columns(0)])
    for m in (1, 2):
        d_normed += dot_nt(d_flat[m], qkvo[:, columns(m)])
    values, inverse = normalize(x[...].astype(F32))
    totals[0:1] = colsum(d_normed * values)
    totals[1:2] = colsum(d_normed)
    totals[2:3] = colsum(d_flat[0].astype(F32))
    totals[3:4] = colsum(d_flat[2].astype(F32))
    d_x[...] = (residual[...] + norm_back(d_normed, row(e, 0), values, inverse)).astype(BF16)
    for i in range(count - slots, count):
        out_copy(i).wait()


def encoder_back(lens, which, g1, g2, x, mid, e, r, weights, state, base=()):
    return pl.pallas_call(
        functools.partial(encoder_back_kernel, len(base)),
        in_specs=[SMEM, SMEM, *(VMEM for _ in range(6)), ANY, *(ANY for _ in ENC_STATE), *(ANY for _ in base)],
        out_specs=(VMEM, VMEM, ANY),
        out_shape=(ROWS, TOTALS, sds((2, SHARE, D, D), BF16)),
        scratch_shapes=[
            *WEIGHT_SCRATCH,
            pltpu.VMEM((PAD, CAP), BF16),
            pltpu.VMEM((CAP, PAD), BF16),
            pltpu.VMEM((PAD, D), BF16),
            scratch(ROWS),
            scratch(ROWS),
            pltpu.VMEM((3, CAP, D), BF16),
            pltpu.VMEM((CAP, D), F32),
            pltpu.VMEM((BLOCKS, D, D), BF16),
            COPIES,
            *map(scratch, ENC_STATE),
        ],
        compiler_params=params(58),
        name="encoder_back",
    )(lens, which, g1, g2, x, mid, e, r, weights, *state, *base)


def table_rows(indices, table):
    places = lax.broadcasted_iota(jnp.int32, (indices.shape[0], table.shape[0]), 1)
    chosen = jnp.where(places == indices[...], 1.0, 0.0).astype(BF16)
    values = table[...]
    top = values.astype(BF16)
    values = values - top.astype(F32)
    middle = values.astype(BF16)
    bottom = (values - middle.astype(F32)).astype(BF16)
    return (dot(chosen, top) + dot(chosen, middle)) + dot(chosen, bottom)


def regressor_before_kernel(lens, which, queries, vis, mask, table, e, given, normed, packed, sources, held, flat, regroup, ungroup, semaphores):
    copies = Copies(semaphores)
    weights = Weights(copies, given, [held])
    weights.start(0, 1, 2)
    group_matrices(lens, which[0], regroup, ungroup)
    sources[1] = table_rows(vis, table)
    residual = queries[...].astype(F32)
    source = residual + table_rows(mask, table)
    sources[0] = source
    centred, _ = normalize(source)
    normed[0] = (centred * row(e, 0) + row(e, 1)).astype(BF16)
    normed[1] = (centred * row(e, 2) + row(e, 3)).astype(BF16)
    centred, _ = normalize(residual)
    normed[2] = (centred * row(e, 4) + row(e, 5)).astype(BF16)
    weights.wait(0, 1, 2)
    flat[0] = ((dot(normed[0], held[:, columns(0)]) + row(e, 6)).astype(BF16) * 0.125).astype(BF16)
    flat[1] = dot(normed[1], held[:, columns(1)]).astype(BF16)
    flat[2] = (dot(normed[2], held[:, columns(2)]) + row(e, 7)).astype(BF16)
    for m in range(3):
        packed[m] = dot(regroup[...], flat[m]).astype(BF16)


def regressor_before(lens, which, queries, vis, mask, table, e, weights):
    return pl.pallas_call(
        regressor_before_kernel,
        in_specs=[SMEM, SMEM, *(VMEM for _ in range(5)), ANY],
        out_specs=(VMEM, VMEM, VMEM),
        out_shape=REG_BEFORE,
        scratch_shapes=[
            pltpu.VMEM((D, FF), BF16),
            pltpu.VMEM((3, CAP, D), BF16),
            pltpu.VMEM((PAD, CAP), BF16),
            pltpu.VMEM((CAP, PAD), BF16),
            COPIES,
        ],
        compiler_params=params(48),
        name="regressor_before",
    )(lens, which, queries, vis, mask, table, e, weights)


def regressor_kernel(
    lens, which, latents, queries, cot, e, r, c, given, packed_before, sources_before,
    regressed, d_latents, d_queries, totals, *refs,
):
    kept, refs = refs[: len(REG_STATE)], refs[len(REG_STATE) :]
    (
        *held, regroup, ungroup, packed, probs, mixed_slots, d_slots, sources, branch, slope, f_branch, mid, residual,
        flat, semaphores, normed, d_flat, mixed, d_branch, f_normed, _, active, d_f_branch,
    ) = refs
    pack = which[0]
    copies = Copies(semaphores)
    weights = Weights(copies, given, held)
    in_sources = copies.start(sources_before, sources)
    weights.start(1, 2)
    in_packed = [copies.start(packed_before.at[i], packed.at[m]) for i, m in enumerate((0, 3, 4))]
    weights.start(3, *UPS, *DOWNS, 0)
    qkvo = weights.held[0]
    group_matrices(lens, pack, regroup, ungroup)
    incoming = latents[...].astype(F32)
    centred, _ = normalize(incoming)
    normed[1] = (centred * row(e, 4) + row(e, 5)).astype(BF16)
    in_sources.wait()
    k_source = incoming + sources[1]
    sources[1] = k_source
    centred, _ = normalize(k_source)
    normed[0] = (centred * row(e, 2) + row(e, 3)).astype(BF16)
    copies.leave(normed, kept[0])
    weights.wait(1)
    flat[0] = dot(normed[0], qkvo[:, columns(1)]).astype(BF16)
    weights.wait(2)
    flat[1] = (dot(normed[1], qkvo[:, columns(2)]) + row(e, 7)).astype(BF16)
    for m in range(2):
        packed[1 + m] = dot(regroup[...], flat[m]).astype(BF16)
    for copy in in_packed:
        copy.wait()
    attend(lens, pack, packed, probs, mixed_slots, 2, nothing)
    mixed[...] = dot(ungroup[...], mixed_slots[...]).astype(BF16)
    copies.leave(mixed, kept[2])
    weights.wait(3)
    summed = dot_nt(mixed[...], qkvo[:, columns(3)]) + row(e, 8)
    branch[...] = summed.astype(BF16)
    mid[...] = (queries[...].astype(F32) + row(e, 9) * summed).astype(BF16)

    def forward_made(name):
        if name == "normed":
            copies.leave(f_normed, kept[4])
        elif name != "branch":
            copies.leave(active.at[:, columns(name)], kept[6].at[:, columns(name)])

    feed_forward(weights, mid, r, c, regressed, (f_normed, active, slope, f_branch), forward_made)

    totals[...] = jnp.zeros_like(totals)
    waited = Weights(copies, given, held)
    waited.wait = nothing_more

    def back_made(name):
        if name == "branch":
            copies.leave(d_f_branch, kept[7])
        else:
            copies.leave(slope.at[:, columns(name)], kept[5].at[:, columns(name)])

    feed_forward_back(
        waited, nothing, cot[...].astype(F32), mid, r, (slope, f_branch, d_f_branch), totals, residual, back_made
    )

    def attention_made(name):
        if name == "branch":
            copies.leave(d_branch, kept[3])
        else:
            copies.leave(d_flat.at[name], kept[1].at[name])

    attention_back(
        2, waited, e, (residual, branch, d_branch, regroup, ungroup, packed, probs, mixed_slots, d_slots, d_flat),
        totals, nothing, attention_made,
    )
    weights.wait(0)
    totals[6:7] = colsum(d_flat[0].astype(F32))
    totals[7:8] = colsum(d_flat[2].astype(F32)) + colsum(d_flat[4].astype(F32))
    values, inverse = normalize(sources[0])
    grad = dot_nt(d_flat[0], qkvo[:, columns(0)])
    totals[0:1] = colsum(grad * values)
    totals[1:2] = colsum(grad)
    total = residual[...] + norm_back(grad, row(e, 0), values, inverse)
    grad = dot_nt(d_flat[3], qkvo[:, columns(1)])
    k_gain = colsum(grad * values)
    k_offset = colsum(grad)
    total += norm_back(grad, row(e, 2), values, inverse)
    values, inverse = normalize(queries[...].astype(F32))
    grad = dot_nt(d_flat[4], qkvo[:, columns(2)])
    v_gain = colsum(grad * values)
    v_offset = colsum(grad)
    total += norm_back(grad, row(e, 4), values, inverse)
    d_queries[...] = total.astype(BF16)
    values, inverse = normalize(sources[1])
    grad = dot_nt(d_flat[1], qkvo[:, columns(1)])
    totals[2:3] = k_gain + colsum(grad * values)
    totals[3:4] = k_offset + colsum(grad)
    total = norm_back(grad, row(e, 2), values, inverse)
    values, inverse = normalize(latents[...].astype(F32))
    grad = dot_nt(d_flat[2], qkvo[:, columns(2)])
    totals[4:5] = v_gain + colsum(grad * values)
    totals[5:6] = v_offset + colsum(grad)
    total += norm_back(grad, row(e, 4), values, inverse)
    d_latents[...] = total.astype(BF16)
    copies.finish()


def nothing_more(*which):
    del which


def regressor(lens, which, latents, queries, cot, e, r, c, weights, before):
    made = pl.pallas_call(
        regressor_kernel,
        in_specs=[SMEM, SMEM, *(VMEM for _ in range(6)), ANY, ANY, ANY],
        out_specs=(VMEM, VMEM, VMEM, VMEM, *(ANY for _ in REG_STATE)),
        out_shape=(ROWS, ROWS, ROWS, TOTALS, *REG_STATE),
        scratch_shapes=[
            *WEIGHT_SCRATCH,
            pltpu.VMEM((PAD, CAP), BF16),
            pltpu.VMEM((CAP, PAD), BF16),
            pltpu.VMEM((5, PAD, D), BF16),
            pltpu.VMEM((IMGS, PAIRS, 4 * SLOT, SLOT), BF16),
            pltpu.VMEM((PAD, D), BF16),
            pltpu.VMEM((PAD, D), BF16),
            pltpu.VMEM((2, CAP, D), F32),
            scratch(ROWS),
            scratch(WIDE),
            scratch(ROWS),
            scratch(ROWS),
            pltpu.VMEM((CAP, D), F32),
            pltpu.VMEM((2, CAP, D), BF16),
            COPIES,
            *(scratch(s) if i != 5 else pltpu.VMEM((8, LANES), BF16) for i, s in enumerate(REG_STATE)),
        ],
        compiler_params=params(60),
        name="regressor",
    )(lens, which, latents, queries, cot, e, r, c, weights, before[1], before[2])
    return (*made[:4], tuple(made[4:]))


SHARE = BLOCKS + BLOCKS // 2


def weight_grads_kernel(packs, *refs):
    step = pl.program_id(0)
    out = refs[9 * packs]
    inputs = [refs[9 * i : 9 * i + 9] for i in range(packs)]

    def put(terms):
        total = None
        for term in terms:
            total = term if total is None else total + term
        out[...] = total.astype(BF16)

    @pl.when(step == 0)
    def _():
        put(dot_tn(n[0], p[0]) for n, _, p, *_ in inputs)

    @pl.when((step == 1) | (step == 2))
    def _():
        put(
            dot_tn(m[step + first], p[step + more])
            for n, v, p, *_ in inputs
            for m, first, more in ((v, -1, 0), (n, 0, 2))
        )

    @pl.when(step == 3)
    def _():
        put(dot_tn(b[...], m[...]) for _, _, _, m, b, *_ in inputs)

    @pl.when((step >= 4) & (step < 8))
    def _():
        put(dot_tn(n[...], h[...]) for *_, n, h, _, _ in inputs)

    @pl.when(step >= 8)
    def _():
        put(dot_tn(a[...], b[...]) for *_, a, b in inputs)


def grad_place(step):
    tail = jnp.maximum(step - 2 * BLOCKS, 0)
    late = jnp.where(step >= 2 * BLOCKS, 1, 0)
    section = (1 - late) * (step // BLOCKS) + late * (tail // 2)
    block = (1 - late) * (step % BLOCKS) + late * (BLOCKS + tail % 2)
    return section, block, 0, 0


def weight_grads(before, states):
    rows = full((CAP, D))
    up_part = pl.BlockSpec((CAP, D), lambda i: (0, jnp.clip(i - BLOCKS, 0, BLOCKS - 1)))
    down_part = pl.BlockSpec((CAP, D), lambda i: (0, jnp.clip(i - 2 * BLOCKS, 0, BLOCKS - 1)))
    one = [full((3, CAP, D)), full((2, CAP, D)), full((5, CAP, D)), rows, rows, rows, up_part, down_part, rows]
    operands = []
    for b, s in zip(before, states):
        operands += [b[0], *s]
    return pl.pallas_call(
        functools.partial(weight_grads_kernel, len(states)),
        grid=(3 * BLOCKS,),
        in_specs=one * len(states),
        out_specs=pl.BlockSpec((None, None, D, D), grad_place),
        out_shape=sds((2, SHARE, D, D), BF16),
        compiler_params=params(),
        name="weight_grads",
    )(*operands)


MESH = pl.DeviceIdType.MESH


def gather_weights_kernel(matrix, down, weights, send, receive, local):
    dp, section = lax.axis_index("dp"), lax.axis_index("section")
    odd = lax.rem(section, 2)
    partner = (dp, section + 1 - 2 * odd)
    barrier = pltpu.get_barrier_semaphore()
    pl.semaphore_signal(barrier, inc=1, device_id=partner, device_id_type=MESH)
    pl.semaphore_wait(barrier, 1)
    places = [(matrix.at[0, :, pl.ds(i * D, D)], odd * BLOCKS + i) for i in range(BLOCKS)]
    places += [(down.at[pl.ds(i * D, D), :], 2 * BLOCKS + odd * (BLOCKS // 2) + i) for i in range(BLOCKS // 2)]
    copies = []
    for i, (source, place) in enumerate(places):
        away = pltpu.make_async_remote_copy(
            source, weights.at[place], send.at[i], receive.at[i], device_id=partner, device_id_type=MESH
        )
        away.start()
        here = pltpu.make_async_copy(source, weights.at[place], local.at[i])
        here.start()
        copies += [away, here]
    for copy in copies:
        copy.wait()


def gather_weights(matrix, down):
    vmem = pl.BlockSpec(memory_space=pltpu.VMEM)
    return pl.pallas_call(
        gather_weights_kernel,
        in_specs=[vmem, vmem],
        out_specs=ANY,
        out_shape=sds((3 * BLOCKS, D, D), matrix.dtype),
        scratch_shapes=[pltpu.SemaphoreType.DMA((SHARE,)) for _ in range(3)],
        compiler_params=params(collective_id=1, has_side_effects=True),
        name="gather_weights",
    )(matrix, down)


RING = 8
SEGMENT = D // RING
PART = SEGMENT // 2
CHAIN = SHARE // 2


def ring_place(d):
    odd = lax.rem(d, 2)
    return (1 - odd) * lax.div(d, 2) + odd * (RING - 1 - lax.div(d, 2))


def ring_device(place):
    place = lax.rem(place + RING, RING)
    late = lax.div(place, RING // 2)
    return (1 - late) * 2 * place + late * (2 * (RING - 1 - place) + 1)


def reduce_kernel(
    grads, swapping, vectors, out_matrix, out_down, swapped, out_vectors,
    mine, partner_part, landing, final, stage, v_sum, v_in,
    pair_send, pair_receive, own_sem, ring_send, ring_receive, last_send, last_receive, out_sem,
    v_send, v_receive, swap_send, swap_receive,
):
    d, section = lax.axis_index("dp"), lax.axis_index("section")
    odd = lax.rem(section, 2)
    place = ring_place(d)
    across = (d, section + 2 - 4 * lax.div(section, 2))
    pair = (d, section + 1 - 2 * odd)
    ways = ((ring_device(place + 1), section), (ring_device(place - 1), section))

    def flipped(bit):
        return d + bit - 2 * bit * lax.rem(lax.div(d, bit), 2)

    levels = (pair, (flipped(1), section), (flipped(2), section), (flipped(4), section), across)
    barrier = pltpu.get_barrier_semaphore()
    for other in (*ways, *levels):
        pl.semaphore_signal(barrier, inc=1, device_id=other, device_id_type=MESH)
    pl.semaphore_wait(barrier, len(ways) + len(levels))

    def rows_of(step, way):
        segment = lax.rem(place + (step if way else -step) + 2 * RING, RING)
        return pl.ds(pl.multiple_of(segment * SEGMENT + way * PART, 8), PART)

    def remote(source, target, send, receive, device):
        return pltpu.make_async_remote_copy(source, target, send, receive, device_id=device, device_id_type=MESH)

    swap = remote(swapping, swapped, swap_send, swap_receive, across)
    swap.start()
    own = pltpu.make_async_copy(grads.at[odd], mine, own_sem)
    own.start()

    def pair_copy(step, way):
        rows = rows_of(step, way)
        return remote(
            grads.at[1 - odd, :, rows, :], partner_part.at[:, rows, :],
            pair_send.at[step, way], pair_receive.at[step, way], pair,
        )

    def start_pair(step, carry):
        for way in range(2):
            pair_copy(step, way).start()
        return carry

    lax.fori_loop(0, RING, start_pair, 0)

    def vector_copy(level):
        return remote(v_sum.at[level], v_in.at[level], v_send.at[level], v_receive.at[level], levels[level])

    def vector_next(level):
        vector_copy(level).wait()
        if level + 1 < len(levels):
            v_sum[level + 1] = v_sum[level] + v_in[level]
            vector_copy(level + 1).start()

    v_sum[0] = vectors[...]
    vector_copy(0).start()

    def blocks(chain):
        return pl.ds(chain * CHAIN, CHAIN)

    def ring_copy(step, way, chain):
        rows = rows_of(step, way)
        return remote(
            mine.at[blocks(chain), rows, :], landing.at[blocks(chain), rows, :],
            ring_send.at[step, way, chain], ring_receive.at[step, way, chain], ways[way],
        )

    def incoming(step, way, chain):
        rows = rows_of(step + 1, way)
        return remote(
            mine.at[blocks(chain), rows, :], landing.at[blocks(chain), rows, :],
            ring_send.at[step, way, chain], ring_receive.at[step, way, chain], ways[way],
        )

    own.wait()
    for way in range(2):
        pair_copy(0, way).wait_recv()
        rows = rows_of(0, way)
        for chain in range(2):
            part = (blocks(chain), rows, slice(None))
            mine[part] = (mine[part].astype(F32) + partner_part[part].astype(F32)).astype(BF16)
            ring_copy(0, way, chain).start()
    vector_next(0)

    def total_of(part):
        return (
            mine[part].astype(F32) + partner_part[part].astype(F32) + landing[part].astype(F32)
        ).astype(BF16)

    def reduce_step(step, carry):
        for chain in range(2):
            for way in range(2):
                if chain == 0:
                    pair_copy(step, way).wait_recv()
                incoming(step - 1, way, chain).wait_recv()
                part = (blocks(chain), rows_of(step, way), slice(None))
                mine[part] = total_of(part)
                ring_copy(step, way, chain).start()
        return carry

    lax.fori_loop(1, RING - 1, reduce_step, 0)
    vector_next(1)

    def last_copy(step, way, chain):
        rows = rows_of(step + RING - 1, way)
        return remote(
            final.at[blocks(chain), rows, :], final.at[blocks(chain), rows, :],
            last_send.at[step, way, chain], last_receive.at[step, way, chain], ways[way],
        )

    def last_incoming(step, way, chain):
        rows = rows_of(step + RING, way)
        return remote(
            final.at[blocks(chain), rows, :], final.at[blocks(chain), rows, :],
            last_send.at[step, way, chain], last_receive.at[step, way, chain], ways[way],
        )

    def out_copies(step, way, chain):
        rows = rows_of(step + RING - 1, way)
        copies = []
        for i in range(CHAIN):
            block = chain * CHAIN + i
            if block < BLOCKS:
                target = out_matrix.at[0, rows, pl.ds(block * D, D)]
            else:
                segment = lax.rem(place + (step + RING - 1 if way else 1 - step - RING) + 4 * RING, RING)
                start = (block - BLOCKS) * D + segment * SEGMENT + way * PART
                target = out_down.at[pl.ds(pl.multiple_of(start, 8), PART), :]
            copies.append(pltpu.make_async_copy(stage.at[way, chain, i], target, out_sem.at[way, chain, i]))
        return copies

    def write_out(step, way, chain, first):
        if not first:
            for copy in out_copies(step - 1, way, chain):
                copy.wait()
        stage[way, chain] = final[blocks(chain), rows_of(step + RING - 1, way), :].astype(F32)
        for copy in out_copies(step, way, chain):
            copy.start()

    for chain in range(2):
        for way in range(2):
            if chain == 0:
                pair_copy(RING - 1, way).wait_recv()
            incoming(RING - 2, way, chain).wait_recv()
            part = (blocks(chain), rows_of(RING - 1, way), slice(None))
            final[part] = total_of(part)
            last_copy(0, way, chain).start()
    vector_next(2)
    for chain in range(2):
        for way in range(2):
            write_out(0, way, chain, True)

    def gather_step(step, carry):
        for chain in range(2):
            for way in range(2):
                last_incoming(step - 1, way, chain).wait_recv()
                last_copy(step, way, chain).start()
                write_out(step, way, chain, False)
        return carry

    lax.fori_loop(1, 3, gather_step, 0)
    vector_next(3)
    lax.fori_loop(3, 5, gather_step, 0)
    vector_next(4)
    out_vectors[0] = v_sum[len(levels) - 1]
    out_vectors[1] = v_in[len(levels) - 1]
    lax.fori_loop(5, RING - 1, gather_step, 0)
    for chain in range(2):
        for way in range(2):
            last_incoming(RING - 2, way, chain).wait_recv()
            write_out(RING - 1, way, chain, False)
    for chain in range(2):
        for way in range(2):
            for copy in out_copies(RING - 1, way, chain):
                copy.wait()

    def all_sent(step, carry):
        for way in range(2):
            for chain in range(2):
                ring_copy(step, way, chain).wait_send()
                last_copy(step, way, chain).wait_send()
        return carry

    lax.fori_loop(0, RING - 1, all_sent, 0)

    def pair_sent(step, carry):
        for way in range(2):
            pair_copy(step, way).wait_send()
        return carry

    lax.fori_loop(0, RING, pair_sent, 0)
    swap.wait()


def reduce_grads(grads, swapping, vectors):
    share = (SHARE, D, D)
    vmem = pl.BlockSpec(memory_space=pltpu.VMEM)
    dma = pltpu.SemaphoreType.DMA
    return pl.pallas_call(
        reduce_kernel,
        in_specs=[ANY, ANY, vmem],
        out_specs=(ANY, ANY, ANY, vmem),
        out_shape=(
            sds((1, D, FF), F32),
            sds((FF // 2, D), F32),
            sds(swapping.shape, swapping.dtype),
            sds((2, VECTORS, D), F32),
        ),
        scratch_shapes=[
            pltpu.VMEM(share, BF16),
            pltpu.VMEM(share, BF16),
            pltpu.VMEM(share, BF16),
            pltpu.VMEM(share, BF16),
            pltpu.VMEM((2, 2, CHAIN, PART, D), F32),
            pltpu.VMEM((5, VECTORS, D), F32),
            pltpu.VMEM((5, VECTORS, D), F32),
            dma((RING, 2)),
            dma((RING, 2)),
            dma,
            dma((RING - 1, 2, 2)),
            dma((RING - 1, 2, 2)),
            dma((RING - 1, 2, 2)),
            dma((RING - 1, 2, 2)),
            dma((2, 2, CHAIN)),
            dma((5,)),
            dma((5,)),
            dma,
            dma,
        ],
        compiler_params=params(56, collective_id=2, has_side_effects=True),
        name="reduce_grads",
    )(grads, swapping, vectors)


def plain_reduce_grads(grads, swapping, vectors):
    odd = lax.rem(lax.axis_index("section"), 2)
    pair = [(0, 1), (1, 0), (2, 3), (3, 2)]
    theirs = lax.dynamic_index_in_dim(grads, 1 - odd, 0, keepdims=False)
    mine = lax.dynamic_index_in_dim(grads, odd, 0, keepdims=False)
    total = lax.psum(mine + lax.ppermute(theirs, "section", pair), "dp").astype(F32)
    vectors = lax.psum(vectors + lax.ppermute(vectors, "section", pair), "dp")
    matrix = jnp.swapaxes(total[:BLOCKS], 0, 1).reshape(1, D, FF)
    return (
        matrix,
        total[BLOCKS:].reshape(FF // 2, D),
        swap_layers(swapping),
        jnp.stack([vectors, swap_layers(vectors)]),
    )


def swap_layers(block):
    return lax.ppermute(block, "section", [(0, 2), (1, 3), (2, 0), (3, 1)])


def to_regressor(block):
    return lax.ppermute(block, "section", [(0, 2), (1, 3)])


def to_encoder(block):
    return lax.ppermute(block, "section", [(2, 0), (3, 1)])


def body(
    vis_embed, latent_cot, reg_queries, out_cot, section_matrix, down_weight, enc_vectors, reg_vectors,
    mlp_vectors, hidden_bias, pos_table, image_lengths, vis_index, mask_index,
):
    section = lax.axis_index("section")
    odd = lax.rem(section, 2)
    is_reg = section >= 2
    layer = jnp.where(is_reg, 1, 0)
    weights = gather_weights(section_matrix, down_weight)
    r = lax.dynamic_index_in_dim(mlp_vectors, layer, 0, keepdims=False)
    c = lax.dynamic_slice_in_dim(hidden_bias, layer, 1, 0)
    packs = [(odd + 2 * i).reshape(1).astype(jnp.int32) for i in range(2)]
    vis = [lax.dynamic_slice_in_dim(vis_index, (odd + 2 * i) * CAP, CAP)[:, None] for i in range(2)]
    mask = [lax.dynamic_slice_in_dim(mask_index, (odd + 2 * i) * CAP, CAP)[:, None] for i in range(2)]

    incoming = swap_layers(jnp.where(is_reg, vis_embed, reg_queries))
    x = [vis_embed, incoming]
    queries = [incoming, reg_queries]

    def on_encoder(work, otherwise):
        return lax.cond(is_reg, otherwise, work)

    def on_regressor(work, otherwise):
        return lax.cond(is_reg, work, otherwise)

    def enc_forward(i):
        return encoder_forward(image_lengths, packs[i], x[i], enc_vectors, r, c, weights)

    def no_enc_forward():
        made = unset((ROWS, ROWS, *ENC_STATE))
        return made[0], made[1], tuple(made[2:])

    def enc_back(i, d_latents, kept, base=()):
        return encoder_back(
            image_lengths, packs[i], lat_cot[i], d_latents, x[i], kept[0], enc_vectors, r, weights, kept[2], base
        )

    def reg_before():
        return tuple(
            tuple(regressor_before(image_lengths, packs[i], queries[i], vis[i], mask[i], pos_table, reg_vectors, weights))
            for i in range(2)
        )

    def no_reg_before():
        made = unset((*REG_BEFORE, *REG_BEFORE))
        return tuple(made[: len(REG_BEFORE)]), tuple(made[len(REG_BEFORE) :])

    def reg_work(i, latents):
        return lambda: regressor(
            image_lengths, packs[i], latents, queries[i], cot[i], reg_vectors, r, c, weights, before[i]
        )

    def no_reg_work():
        made = unset((ROWS, ROWS, ROWS, TOTALS, *REG_STATE))
        return (*made[:4], tuple(made[4:]))

    share = sds((2, SHARE, D, D), BF16)
    enc1 = on_encoder(lambda: enc_forward(0), no_enc_forward)
    latents1 = to_regressor(enc1[1])
    before = on_regressor(reg_before, no_reg_before)
    swapped_cot = swap_layers(jnp.where(is_reg, latent_cot, out_cot))
    lat_cot = [latent_cot, swapped_cot]
    cot = [swapped_cot, out_cot]
    enc2 = on_encoder(lambda: enc_forward(1), no_enc_forward)
    latents2 = to_regressor(enc2[1])
    reg1 = on_regressor(reg_work(0, latents1), no_reg_work)
    d_latents1 = to_encoder(reg1[1])
    reg2 = on_regressor(reg_work(1, latents2), no_reg_work)
    d_latents2 = to_encoder(reg2[1])
    enc_grads1 = on_encoder(
        lambda: tuple(enc_back(0, d_latents1, enc1)), lambda: tuple(unset((ROWS, TOTALS, share)))
    )

    def reg_last():
        return (
            weight_grads(before, (reg1[4], reg2[4])),
            reg1[3] + reg2[3],
            jnp.stack([reg1[0], reg1[2]]),
        )

    def enc_last():
        d_x, totals, grads = enc_back(1, d_latents2, enc2, (enc_grads1[2],))
        return grads, enc_grads1[1] + totals, jnp.stack([d_x, d_x])

    grads, vectors, swapping = lax.cond(is_reg, reg_last, enc_last)
    reduce = reduce_grads if lax.axis_size("dp") == RING else plain_reduce_grads
    matrix_grad, down_grad, swapped, vectors = reduce(grads, swapping, vectors)

    def pick(reg, enc):
        return jnp.where(is_reg, reg, enc)

    latents = pick(latents2, enc1[1])
    regressed = pick(reg2[0], swapped[0])
    vis_grad = pick(swapped[0], enc_grads1[0])
    query_grad = pick(reg2[2], swapped[1])
    enc_total, reg_total = pick(vectors[1], vectors[0]), pick(vectors[0], vectors[1])
    return (
        latents,
        regressed,
        vis_grad,
        query_grad,
        matrix_grad,
        down_grad,
        enc_total[:6],
        reg_total[:10],
        jnp.stack([enc_total[FFN_AT:HIDDEN_AT], reg_total[FFN_AT:HIDDEN_AT]]),
        jnp.stack([t[HIDDEN_AT : HIDDEN_AT + BLOCKS].reshape(FF) for t in (enc_total, reg_total)]),
    )


def solution(mesh):
    rows = P(("dp", "section"), None)
    in_specs = (
        rows, rows, rows, rows, P("section", None, None), P("section", None),
        P(), P(), P(), P(), P(), P("dp", None), P("dp"), P("dp"),
    )
    out_specs = (rows, rows, rows, rows, P("section", None, None), P("section", None), P(), P(), P(), P())
    return jax.shard_map(body, mesh=mesh, in_specs=in_specs, out_specs=out_specs, check_vma=False)
```

```python
import functools

import jax
import jax.numpy as jnp
from jax import lax
from jax.experimental import pallas as pl
from jax.experimental.pallas import tpu as pltpu
from jax.sharding import PartitionSpec as P

F32 = jnp.float32
BF16 = jnp.bfloat16
CAP = 384
IMGS = 4
SLOT = 128
PAD = IMGS * SLOT
D = 768
FF = 3072
LANES = 128
PAIRS = D // LANES
BLOCKS = FF // D
VECTORS = 24
EPS = 1e-06
MIB = 1 << 20
ANY = pl.BlockSpec(memory_space=pl.ANY)
SMEM = pl.BlockSpec(memory_space=pltpu.SMEM)


def params(limit=48, **more):
    return pltpu.CompilerParams(vmem_limit_bytes=limit * MIB, **more)


def sds(shape, dtype):
    return jax.ShapeDtypeStruct(shape, dtype)


def dot(a, b):
    return jnp.dot(a, b, preferred_element_type=F32)


def dot_nt(a, b):
    return lax.dot_general(a, b, (((1,), (1,)), ((), ())), preferred_element_type=F32)


def dot_tn(a, b):
    return lax.dot_general(a, b, (((0,), (0,)), ((), ())), preferred_element_type=F32)


def row(ref, i):
    return ref[i : i + 1, :]


def colsum(values):
    return jnp.sum(values, axis=0, keepdims=True)


def normalize(values):
    centred = values - jnp.mean(values, axis=-1, keepdims=True)
    spread = jnp.mean(centred * centred, axis=-1, keepdims=True)
    inverse = lax.rsqrt(spread + EPS)
    return centred * inverse, inverse


def norm_back(gradient, gain, normed, inverse):
    scaled = gradient * gain
    level = jnp.mean(scaled, axis=-1, keepdims=True)
    slope = jnp.mean(scaled * normed, axis=-1, keepdims=True)
    return inverse * (scaled - level - normed * slope)


def gelu_parts(t):
    e = jnp.exp(-0.5 * t * t)
    k = 1.0 / (1.0 + (0.3275911 * 0.7071067811865476) * jnp.abs(t))
    poly = k * (
        0.127414796
        + k * (-0.142248368 + k * (0.7107068705 + k * (-0.7265760135 + k * 0.5307027145)))
    )
    tail = poly * e
    phi = jnp.where(t >= 0.0, 1.0 - tail, tail)
    return t * phi, phi + t * (e * 0.3989422804014327)


def group_matrices(lens, pack, regroup, ungroup):
    def image(j, start):
        size = lens[pack, j]
        slots = pl.ds(pl.multiple_of(j * SLOT, SLOT), SLOT)
        place = lax.broadcasted_iota(jnp.int32, (SLOT, CAP), 0)
        rows = lax.broadcasted_iota(jnp.int32, (SLOT, CAP), 1)
        hit = (place + start == rows) & (place < size)
        regroup[slots, :] = jnp.where(hit, 1.0, 0.0).astype(BF16)
        place = lax.broadcasted_iota(jnp.int32, (CAP, SLOT), 1)
        rows = lax.broadcasted_iota(jnp.int32, (CAP, SLOT), 0)
        hit = (place + start == rows) & (place < size)
        ungroup[:, slots] = jnp.where(hit, 1.0, 0.0).astype(BF16)
        return start + size

    lax.fori_loop(0, IMGS, image, jnp.int32(0))


def lane_halves():
    lane = lax.broadcasted_iota(jnp.int32, (1, LANES), 1)
    first = jnp.where(lane < LANES // 2, 1.0, 0.0)
    return first.astype(BF16), (1.0 - first).astype(BF16)


def both_heads(block, halves):
    return jnp.concatenate([block * halves[0], block * halves[1]], axis=0)


def merge_heads(stacked):
    keys = stacked.shape[0] // 2
    lane = lax.broadcasted_iota(jnp.int32, (keys, LANES), 1)
    return jnp.where(lane < LANES // 2, stacked[:keys], stacked[keys:])


def softmax(scores):
    raised = jnp.exp(scores - jnp.max(scores, axis=0, keepdims=True))
    return (raised * (1.0 / jnp.sum(raised, axis=0, keepdims=True))).astype(BF16)


def keys_of(packed, first, parts, rows, cols, halves):
    return both_heads(
        jnp.concatenate([packed[first + 2 * m, rows, cols] for m in range(parts)], axis=0), halves
    )


def attend(lens, pack, packed, probs, mixed_slots, parts, done):
    halves = lane_halves()
    keys = SLOT * parts
    place = lax.bitwise_and(lax.broadcasted_iota(jnp.int32, (keys, SLOT), 0), SLOT - 1)
    for j in range(IMGS):
        rows = slice(j * SLOT, (j + 1) * SLOT)
        valid = place < lens[pack, j]
        for g in range(PAIRS):
            cols = slice(g * LANES, (g + 1) * LANES)
            scores = dot_nt(keys_of(packed, 1, parts, rows, cols, halves), packed[0, rows, cols])
            low = jnp.concatenate(
                [softmax(jnp.where(valid, part, -1e30)) for part in (scores[:keys], scores[keys:])], axis=0
            )
            probs[j, g] = low
            mixed_slots[rows, cols] = dot_tn(low, keys_of(packed, 2, parts, rows, cols, halves)).astype(BF16)
        done(j)


def attend_back(packed, probs, mixed_slots, d_mixed_slots, parts, ready):
    halves = lane_halves()
    keys = SLOT * parts
    less = both_heads(jnp.full((keys, LANES), -1.0, BF16), halves)

    def image(j, carry):
        ready(j)
        rows = pl.ds(pl.multiple_of(j * SLOT, SLOT), SLOT)
        for g in range(PAIRS):
            cols = slice(g * LANES, (g + 1) * LANES)
            d_out = d_mixed_slots[rows, cols]
            centre = (d_out.astype(F32) * mixed_slots[rows, cols].astype(F32)).astype(BF16)
            low = probs[j, g]
            d_prob = dot_nt(
                jnp.concatenate([keys_of(packed, 2, parts, rows, cols, halves), less], axis=1),
                jnp.concatenate([d_out, centre], axis=1),
            )
            d_scores = (low.astype(F32) * d_prob).astype(BF16)
            q = packed[0, rows, cols]
            zero = jnp.zeros_like(q)
            sides = jnp.concatenate(
                [jnp.concatenate([q, zero], axis=1), jnp.concatenate([zero, d_out], axis=1)], axis=0
            )
            d_kv = dot(jnp.concatenate([d_scores, low], axis=1), sides)
            d_q = dot_tn(d_scores, keys_of(packed, 1, parts, rows, cols, halves)) * 0.125
            packed[0, rows, cols] = d_q.astype(BF16)
            for side in range(2):
                merged = merge_heads(d_kv[:, side * LANES : (side + 1) * LANES]).astype(BF16)
                for m in range(parts):
                    packed[1 + side + 2 * m, rows, cols] = merged[m * SLOT : (m + 1) * SLOT]
        return carry

    lax.fori_loop(0, IMGS, image, 0)


ROWS = sds((CAP, D), BF16)
WIDE = sds((CAP, FF), BF16)
TOTALS = sds((VECTORS, D), F32)
FFN_AT = 10
HIDDEN_AT = FFN_AT + 4
ENC_STATE = (
    ROWS,
    sds((3, PAD, D), BF16),
    sds((IMGS, PAIRS, 2 * SLOT, SLOT), BF16),
    sds((PAD, D), BF16),
    ROWS,
    ROWS,
    ROWS,
    WIDE,
    WIDE,
    ROWS,
)
REG_BEFORE = (
    sds((3, CAP, D), BF16),
    sds((3, PAD, D), BF16),
    sds((2, CAP, D), F32),
)
REG_STATE = (
    sds((2, CAP, D), BF16),
    sds((5, CAP, D), BF16),
    ROWS,
    ROWS,
    ROWS,
    WIDE,
    WIDE,
    ROWS,
)


def full(shape):
    return pl.BlockSpec(shape, lambda i: (0,) * len(shape))


VMEM = pl.BlockSpec(memory_space=pltpu.VMEM)


def scratch(shape):
    return pltpu.VMEM(shape.shape, shape.dtype)


def unset(shapes):
    def kernel(*refs):
        del refs

    return pl.pallas_call(
        kernel, out_shape=shapes, out_specs=tuple(ANY for _ in shapes), name="unset"
    )()


class Copies:
    def __init__(self, semaphores):
        self.semaphores, self.used, self.open = semaphores, 0, []

    def take(self, count=1):
        self.used += count
        return self.used - count

    def start(self, source, target):
        copy = pltpu.make_async_copy(source, target, self.semaphores.at[self.take()])
        copy.start()
        return copy

    def leave(self, source, target):
        self.open.append(self.start(source, target))

    def finish(self):
        for copy in self.open:
            copy.wait()


COPIES = pltpu.SemaphoreType.DMA((80,))


def columns(i):
    return slice(i * D, (i + 1) * D)


class Weights:
    def __init__(self, copies, weights, held):
        self.copies, self.weights, self.held, self.started = copies, weights, held, {}

    def target(self, i):
        kind, block = divmod(i, BLOCKS)
        held = self.held[kind]
        return held.at[columns(block), :] if kind == 2 else held.at[:, columns(block)]

    def start(self, *order):
        for i in order:
            self.started[i] = self.copies.start(self.weights.at[i], self.target(i))

    def wait(self, *which):
        for i in which:
            self.started[i].wait()


WEIGHT_SCRATCH = [pltpu.VMEM((D, FF), BF16), pltpu.VMEM((D, FF), BF16), pltpu.VMEM((FF, D), BF16)]
ALL_BLOCKS = range(BLOCKS)
UPS = [BLOCKS + i for i in ALL_BLOCKS]
DOWNS = [2 * BLOCKS + i for i in ALL_BLOCKS]


def feed_forward(weights, mid, r, c, out, state, made):
    normed, active, slope, branch = state
    values = mid[...].astype(F32)
    centred, _ = normalize(values)
    normed[...] = (centred * row(r, 0) + row(r, 1)).astype(BF16)
    made("normed")
    _, up, down = weights.held
    for i in ALL_BLOCKS:
        weights.wait(BLOCKS + i)
        value, steep = gelu_parts(dot(normed[...], up[:, columns(i)]) + c[:, columns(i)])
        active[:, columns(i)] = value.astype(BF16)
        slope[:, columns(i)] = steep.astype(BF16)
        made(i)
    weights.wait(*DOWNS)
    summed = dot(active[...], down[...]) + row(r, 2)
    branch[...] = summed.astype(BF16)
    out[...] = (values + row(r, 3) * summed).astype(BF16)
    made("branch")


def feed_forward_back(weights, ready, g, mid, r, refs, totals, residual, made):
    slope, branch, d_branch = refs
    _, up, down = weights.held
    d_branch[...] = (g * row(r, 3)).astype(BF16)
    made("branch")
    add_row(totals, FFN_AT + 2, colsum(d_branch[...].astype(F32)))
    ready("branch")
    add_row(totals, FFN_AT + 3, colsum(g * branch[...].astype(F32)))
    for i in ALL_BLOCKS:
        weights.wait(2 * BLOCKS + i)
        ready(i)
        d_active = dot_nt(d_branch[...], down[columns(i), :])
        d_hidden = (d_active * slope[:, columns(i)].astype(F32)).astype(BF16)
        slope[:, columns(i)] = d_hidden
        made(i)
        add_row(totals, HIDDEN_AT + i, colsum(d_hidden.astype(F32)))
    weights.wait(*UPS)
    d_normed = dot_nt(slope[...], up[...])
    normed, inverse = normalize(mid[...].astype(F32))
    add_row(totals, FFN_AT, colsum(d_normed * normed))
    add_row(totals, FFN_AT + 1, colsum(d_normed))
    residual[...] = (g + norm_back(d_normed, row(r, 0), normed, inverse)).astype(BF16).astype(F32)


def attention_back(parts, weights, e, refs, totals, ready, made):
    residual, branch, d_branch, regroup, ungroup, packed, probs, mixed_slots, d_slots, d_flat = refs
    last = 1 + 4 * parts
    g = residual[...]
    ready("branch")
    d_branch[...] = (g * row(e, last)).astype(BF16)
    made("branch")
    add_row(totals, last, colsum(g * branch[...].astype(F32)))
    add_row(totals, last - 1, colsum(d_branch[...].astype(F32)))
    weights.wait(3)
    d_mixed = dot(d_branch[...], weights.held[0][:, columns(3)]).astype(BF16)
    d_slots[...] = dot(regroup[...], d_mixed).astype(BF16)
    ready("packed")
    attend_back(packed, probs, mixed_slots, d_slots, parts, ready)
    for m in range(1 + 2 * parts):
        d_flat[m] = dot(ungroup[...], packed[m]).astype(BF16)
        made(m)


def add_row(totals, i, value):
    totals[i : i + 1] += value


def nothing(name):
    del name


def wide(i):
    return pl.ds(pl.multiple_of(i * D, D), D)


class Shares:
    def __init__(self, copies, blocks, share):
        self.semaphores, self.blocks, self.share = copies.semaphores, blocks, share
        self.first = copies.take(3 * BLOCKS)

    def copy(self, kind, i):
        section, block = (lax.div(i, 2), BLOCKS + lax.rem(i, 2)) if kind == 1 else (1 - kind // 2, i)
        semaphore = self.semaphores.at[self.first + kind * BLOCKS + i]
        return pltpu.make_async_copy(self.blocks.at[i], self.share.at[section, block], semaphore)

    def put(self, kind, i, product):
        if kind:
            self.copy(kind - 1, i).wait()
        self.blocks[i] = product.astype(BF16)
        self.copy(kind, i).start()

    def feed_forward(self, normed, d_hidden, active, d_branch):
        def up_block(i, carry):
            self.put(0, i, dot_tn(normed[...], d_hidden[:, wide(i)]))
            return carry

        def down_block(i, carry):
            self.put(1, i, dot_tn(active[:, wide(i)], d_branch[...]))
            return carry

        lax.fori_loop(0, BLOCKS, up_block, 0)
        lax.fori_loop(0, BLOCKS, down_block, 0)

    def finish(self):
        for i in ALL_BLOCKS:
            self.copy(2, i).wait()


def encoder_forward_kernel(lens, which, x, e, r, c, given, mid, out, *refs):
    kept, scratch = refs[: len(ENC_STATE)], refs[len(ENC_STATE) :]
    *held, flat, regroup, ungroup, semaphores = scratch[: 3 + 4]
    state = scratch[3 + 4 :]
    normed, packed, probs, mixed_slots, mixed, branch, *ffn = state
    pack = which[0]
    copies = Copies(semaphores)
    weights = Weights(copies, given, held)
    weights.start(*ALL_BLOCKS, *UPS, *DOWNS)
    values = x[...].astype(F32)
    centred, _ = normalize(values)
    normed[...] = (centred * row(e, 0) + row(e, 1)).astype(BF16)
    copies.leave(normed, kept[0])
    group_matrices(lens, pack, regroup, ungroup)
    qkvo = weights.held[0]
    weights.wait(0)
    flat[0] = ((dot(normed[...], qkvo[:, columns(0)]) + row(e, 2)).astype(BF16) * 0.125).astype(BF16)
    weights.wait(1)
    flat[1] = dot(normed[...], qkvo[:, columns(1)]).astype(BF16)
    weights.wait(2)
    flat[2] = (dot(normed[...], qkvo[:, columns(2)]) + row(e, 3)).astype(BF16)
    for m in range(3):
        packed[m] = dot(regroup[...], flat[m]).astype(BF16)
        copies.leave(packed.at[m], kept[1].at[m])
    attend(lens, pack, packed, probs, mixed_slots, 1, lambda j: copies.leave(probs.at[j], kept[2].at[j]))
    copies.leave(mixed_slots, kept[3])
    mixed[...] = dot(ungroup[...], mixed_slots[...]).astype(BF16)
    copies.leave(mixed, kept[4])
    weights.wait(3)
    summed = dot_nt(mixed[...], qkvo[:, columns(3)]) + row(e, 4)
    branch[...] = summed.astype(BF16)
    copies.leave(branch, kept[5])
    mid[...] = (values + row(e, 5) * summed).astype(BF16)

    def made(name):
        if name == "normed":
            copies.leave(ffn[0], kept[6])
        elif name == "branch":
            copies.leave(ffn[3], kept[9])
        else:
            for k in (1, 2):
                copies.leave(ffn[k].at[:, columns(name)], kept[6 + k].at[:, columns(name)])

    feed_forward(weights, mid, r, c, out, ffn, made)
    copies.finish()


def encoder_forward(lens, which, x, e, r, c, weights):
    made = pl.pallas_call(
        encoder_forward_kernel,
        in_specs=[SMEM, SMEM, VMEM, VMEM, VMEM, VMEM, ANY],
        out_specs=(VMEM, VMEM, *(ANY for _ in ENC_STATE)),
        out_shape=(ROWS, ROWS, *ENC_STATE),
        scratch_shapes=[
            *WEIGHT_SCRATCH,
            pltpu.VMEM((3, CAP, D), BF16),
            pltpu.VMEM((PAD, CAP), BF16),
            pltpu.VMEM((CAP, PAD), BF16),
            COPIES,
            *map(scratch, ENC_STATE),
        ],
        compiler_params=params(58),
        name="encoder_forward",
    )(lens, which, x, e, r, c, weights)
    return made[0], made[1], tuple(made[2:])


def encoder_back_kernel(lens, which, g1, g2, x, mid, e, r, so_far, given, *refs):
    state, refs = refs[: len(ENC_STATE)], refs[len(ENC_STATE) :]
    d_x, totals, share, *held, regroup, ungroup, d_slots, d_branch, d_f_branch, d_flat, residual, blocks, semaphores = (
        refs[: 3 + 3 + 9]
    )
    normed, packed, probs, mixed_slots, mixed, branch, f_normed, active, slope, f_branch = refs[3 + 3 + 9 :]
    copies = Copies(semaphores)
    weights = Weights(copies, given, held)
    coming = {"branch": copies.start(state[9], f_branch)}
    for i in ALL_BLOCKS:
        weights.start(2 * BLOCKS + i)
        coming[i] = copies.start(state[8].at[:, columns(i)], slope.at[:, columns(i)])
    weights.start(*UPS, 3)
    later = {"branch": copies.start(state[5], branch)}
    later["packed"] = copies.start(state[1], packed)
    later["mixed"] = copies.start(state[3], mixed_slots)
    probs_in = [copies.start(state[2].at[j], probs.at[j]) for j in range(IMGS)]
    late = [copies.start(state[i], ref) for i, ref in ((6, f_normed), (7, active), (0, normed), (4, mixed))]
    weights.start(0, 1, 2)
    shares = Shares(copies, blocks, share)
    totals[...] = so_far[...]
    group_matrices(lens, which[0], regroup, ungroup)
    g = g1[...].astype(F32) + g2[...].astype(F32)
    feed_forward_back(
        weights, lambda name: coming[name].wait(), g, mid, r, (slope, f_branch, d_f_branch), totals, residual, nothing
    )
    for copy in late:
        copy.wait()
    shares.feed_forward(f_normed, slope, active, d_f_branch)

    def ready(name):
        if name == "branch":
            later["branch"].wait()
        elif name == "packed":
            later["packed"].wait()
            later["mixed"].wait()
            for copy in probs_in:
                copy.wait()

    attention_back(
        1, weights, e, (residual, branch, d_branch, regroup, ungroup, packed, probs, mixed_slots, d_slots, d_flat),
        totals, ready, nothing,
    )

    def first_block(i, carry):
        shares.put(2, i, dot_tn(normed[...], d_flat[i]))
        return carry

    lax.fori_loop(0, 3, first_block, 0)
    shares.put(2, 3, dot_tn(d_branch[...], mixed[...]))
    weights.wait(0, 1, 2)
    qkvo = weights.held[0]
    d_normed = dot_nt(d_flat[0], qkvo[:, columns(0)])
    for m in (1, 2):
        d_normed += dot_nt(d_flat[m], qkvo[:, columns(m)])
    values, inverse = normalize(x[...].astype(F32))
    add_row(totals, 0, colsum(d_normed * values))
    add_row(totals, 1, colsum(d_normed))
    add_row(totals, 2, colsum(d_flat[0].astype(F32)))
    add_row(totals, 3, colsum(d_flat[2].astype(F32)))
    d_x[...] = (residual[...] + norm_back(d_normed, row(e, 0), values, inverse)).astype(BF16)
    shares.finish()


def encoder_back(lens, which, g1, g2, x, mid, e, r, so_far, weights, state):
    return pl.pallas_call(
        encoder_back_kernel,
        in_specs=[SMEM, SMEM, *(VMEM for _ in range(7)), ANY, *(ANY for _ in ENC_STATE)],
        out_specs=(VMEM, VMEM, ANY),
        out_shape=(ROWS, TOTALS, sds((2, SHARE, D, D), BF16)),
        scratch_shapes=[
            *WEIGHT_SCRATCH,
            pltpu.VMEM((PAD, CAP), BF16),
            pltpu.VMEM((CAP, PAD), BF16),
            pltpu.VMEM((PAD, D), BF16),
            scratch(ROWS),
            scratch(ROWS),
            pltpu.VMEM((3, CAP, D), BF16),
            pltpu.VMEM((CAP, D), F32),
            pltpu.VMEM((BLOCKS, D, D), BF16),
            COPIES,
            *map(scratch, ENC_STATE),
        ],
        compiler_params=params(58),
        name="encoder_back",
    )(lens, which, g1, g2, x, mid, e, r, so_far, weights, *state)


def table_rows(indices, table):
    places = lax.broadcasted_iota(jnp.int32, (indices.shape[0], table.shape[0]), 1)
    chosen = jnp.where(places == indices[...], 1.0, 0.0).astype(BF16)
    values = table[...]
    top = values.astype(BF16)
    values = values - top.astype(F32)
    middle = values.astype(BF16)
    bottom = (values - middle.astype(F32)).astype(BF16)
    return (dot(chosen, top) + dot(chosen, middle)) + dot(chosen, bottom)


def regressor_before_kernel(lens, which, queries, vis, mask, table, e, given, normed, packed, sources, held, flat, regroup, ungroup, semaphores):
    copies = Copies(semaphores)
    weights = Weights(copies, given, [held])
    weights.start(0, 1, 2)
    group_matrices(lens, which[0], regroup, ungroup)
    sources[1] = table_rows(vis, table)
    residual = queries[...].astype(F32)
    source = residual + table_rows(mask, table)
    sources[0] = source
    centred, _ = normalize(source)
    normed[0] = (centred * row(e, 0) + row(e, 1)).astype(BF16)
    normed[1] = (centred * row(e, 2) + row(e, 3)).astype(BF16)
    centred, _ = normalize(residual)
    normed[2] = (centred * row(e, 4) + row(e, 5)).astype(BF16)
    weights.wait(0, 1, 2)
    flat[0] = ((dot(normed[0], held[:, columns(0)]) + row(e, 6)).astype(BF16) * 0.125).astype(BF16)
    flat[1] = dot(normed[1], held[:, columns(1)]).astype(BF16)
    flat[2] = (dot(normed[2], held[:, columns(2)]) + row(e, 7)).astype(BF16)
    for m in range(3):
        packed[m] = dot(regroup[...], flat[m]).astype(BF16)


def regressor_before(lens, which, queries, vis, mask, table, e, weights):
    return pl.pallas_call(
        regressor_before_kernel,
        in_specs=[SMEM, SMEM, *(VMEM for _ in range(5)), ANY],
        out_specs=(VMEM, VMEM, VMEM),
        out_shape=REG_BEFORE,
        scratch_shapes=[
            pltpu.VMEM((D, FF), BF16),
            pltpu.VMEM((3, CAP, D), BF16),
            pltpu.VMEM((PAD, CAP), BF16),
            pltpu.VMEM((CAP, PAD), BF16),
            COPIES,
        ],
        compiler_params=params(48),
        name="regressor_before",
    )(lens, which, queries, vis, mask, table, e, weights)


def regressor_kernel(
    lens, which, latents, queries, cot, e, r, c, so_far, given, packed_before, sources_before,
    regressed, d_latents, d_queries, totals, *refs,
):
    kept, refs = refs[: len(REG_STATE)], refs[len(REG_STATE) :]
    (
        *held, regroup, ungroup, packed, probs, mixed_slots, d_slots, sources, branch, slope, f_branch, mid, residual,
        flat, semaphores, normed, d_flat, mixed, d_branch, f_normed, _, active, d_f_branch,
    ) = refs
    pack = which[0]
    copies = Copies(semaphores)
    weights = Weights(copies, given, held)
    in_sources = copies.start(sources_before, sources)
    weights.start(1, 2)
    in_packed = [copies.start(packed_before.at[i], packed.at[m]) for i, m in enumerate((0, 3, 4))]
    weights.start(3, *UPS, *DOWNS, 0)
    qkvo = weights.held[0]
    group_matrices(lens, pack, regroup, ungroup)
    incoming = latents[...].astype(F32)
    centred, _ = normalize(incoming)
    normed[1] = (centred * row(e, 4) + row(e, 5)).astype(BF16)
    in_sources.wait()
    k_source = incoming + sources[1]
    sources[1] = k_source
    centred, _ = normalize(k_source)
    normed[0] = (centred * row(e, 2) + row(e, 3)).astype(BF16)
    copies.leave(normed, kept[0])
    weights.wait(1)
    flat[0] = dot(normed[0], qkvo[:, columns(1)]).astype(BF16)
    weights.wait(2)
    flat[1] = (dot(normed[1], qkvo[:, columns(2)]) + row(e, 7)).astype(BF16)
    for m in range(2):
        packed[1 + m] = dot(regroup[...], flat[m]).astype(BF16)
    for copy in in_packed:
        copy.wait()
    attend(lens, pack, packed, probs, mixed_slots, 2, nothing)
    mixed[...] = dot(ungroup[...], mixed_slots[...]).astype(BF16)
    copies.leave(mixed, kept[2])
    weights.wait(3)
    summed = dot_nt(mixed[...], qkvo[:, columns(3)]) + row(e, 8)
    branch[...] = summed.astype(BF16)
    mid[...] = (queries[...].astype(F32) + row(e, 9) * summed).astype(BF16)

    def forward_made(name):
        if name == "normed":
            copies.leave(f_normed, kept[4])
        elif name != "branch":
            copies.leave(active.at[:, columns(name)], kept[6].at[:, columns(name)])

    feed_forward(weights, mid, r, c, regressed, (f_normed, active, slope, f_branch), forward_made)

    totals[...] = so_far[...]
    waited = Weights(copies, given, held)
    waited.wait = nothing_more

    def back_made(name):
        if name == "branch":
            copies.leave(d_f_branch, kept[7])
        else:
            copies.leave(slope.at[:, columns(name)], kept[5].at[:, columns(name)])

    feed_forward_back(
        waited, nothing, cot[...].astype(F32), mid, r, (slope, f_branch, d_f_branch), totals, residual, back_made
    )

    def attention_made(name):
        if name == "branch":
            copies.leave(d_branch, kept[3])
        else:
            copies.leave(d_flat.at[name], kept[1].at[name])

    attention_back(
        2, waited, e, (residual, branch, d_branch, regroup, ungroup, packed, probs, mixed_slots, d_slots, d_flat),
        totals, nothing, attention_made,
    )
    weights.wait(0)
    add_row(totals, 6, colsum(d_flat[0].astype(F32)))
    add_row(totals, 7, colsum(d_flat[2].astype(F32)) + colsum(d_flat[4].astype(F32)))
    values, inverse = normalize(sources[0])
    grad = dot_nt(d_flat[0], qkvo[:, columns(0)])
    add_row(totals, 0, colsum(grad * values))
    add_row(totals, 1, colsum(grad))
    total = residual[...] + norm_back(grad, row(e, 0), values, inverse)
    grad = dot_nt(d_flat[3], qkvo[:, columns(1)])
    k_gain = colsum(grad * values)
    k_offset = colsum(grad)
    total += norm_back(grad, row(e, 2), values, inverse)
    values, inverse = normalize(queries[...].astype(F32))
    grad = dot_nt(d_flat[4], qkvo[:, columns(2)])
    v_gain = colsum(grad * values)
    v_offset = colsum(grad)
    total += norm_back(grad, row(e, 4), values, inverse)
    d_queries[...] = total.astype(BF16)
    values, inverse = normalize(sources[1])
    grad = dot_nt(d_flat[1], qkvo[:, columns(1)])
    add_row(totals, 2, k_gain + colsum(grad * values))
    add_row(totals, 3, k_offset + colsum(grad))
    total = norm_back(grad, row(e, 2), values, inverse)
    values, inverse = normalize(latents[...].astype(F32))
    grad = dot_nt(d_flat[2], qkvo[:, columns(2)])
    add_row(totals, 4, v_gain + colsum(grad * values))
    add_row(totals, 5, v_offset + colsum(grad))
    total += norm_back(grad, row(e, 4), values, inverse)
    d_latents[...] = total.astype(BF16)
    copies.finish()


def nothing_more(*which):
    del which


def regressor(lens, which, latents, queries, cot, e, r, c, so_far, weights, before):
    made = pl.pallas_call(
        regressor_kernel,
        in_specs=[SMEM, SMEM, *(VMEM for _ in range(7)), ANY, ANY, ANY],
        out_specs=(VMEM, VMEM, VMEM, VMEM, *(ANY for _ in REG_STATE)),
        out_shape=(ROWS, ROWS, ROWS, TOTALS, *REG_STATE),
        scratch_shapes=[
            *WEIGHT_SCRATCH,
            pltpu.VMEM((PAD, CAP), BF16),
            pltpu.VMEM((CAP, PAD), BF16),
            pltpu.VMEM((5, PAD, D), BF16),
            pltpu.VMEM((IMGS, PAIRS, 4 * SLOT, SLOT), BF16),
            pltpu.VMEM((PAD, D), BF16),
            pltpu.VMEM((PAD, D), BF16),
            pltpu.VMEM((2, CAP, D), F32),
            scratch(ROWS),
            scratch(WIDE),
            scratch(ROWS),
            scratch(ROWS),
            pltpu.VMEM((CAP, D), F32),
            pltpu.VMEM((2, CAP, D), BF16),
            COPIES,
            *(scratch(s) if i != 5 else pltpu.VMEM((8, LANES), BF16) for i, s in enumerate(REG_STATE)),
        ],
        compiler_params=params(60),
        name="regressor",
    )(lens, which, latents, queries, cot, e, r, c, so_far, weights, before[1], before[2])
    return (*made[:4], tuple(made[4:]))


SHARE = BLOCKS + BLOCKS // 2


def weight_grads_kernel(*refs):
    sources, share, held, blocks, semaphores = refs[:9], refs[9], refs[10:19], refs[19], refs[20]
    copies = Copies(semaphores)
    order = (5, 6, 7, 8, 0, 1, 2, 3, 4)
    started = {i: copies.start(sources[i], held[i]) for i in order}
    before, normed, d_flat, mixed, d_branch, f_normed, d_hidden, active, d_f_branch = held
    shares = Shares(copies, blocks, share)
    for i in order[:4]:
        started[i].wait()
    shares.feed_forward(f_normed, d_hidden, active, d_f_branch)
    for i in order[4:]:
        started[i].wait()
    shares.put(2, 0, dot_tn(before[0], d_flat[0]))

    def pair_block(i, carry):
        shares.put(2, i, dot_tn(normed[i - 1], d_flat[i]) + dot_tn(before[i], d_flat[i + 2]))
        return carry

    lax.fori_loop(1, 3, pair_block, 0)
    shares.put(2, 3, dot_tn(d_branch[...], mixed[...]))
    shares.finish()


def weight_grads(before, state):
    return pl.pallas_call(
        weight_grads_kernel,
        in_specs=[ANY] * 9,
        out_specs=ANY,
        out_shape=sds((2, SHARE, D, D), BF16),
        scratch_shapes=[
            scratch(REG_BEFORE[0]),
            *map(scratch, REG_STATE),
            pltpu.VMEM((BLOCKS, D, D), BF16),
            COPIES,
        ],
        compiler_params=params(),
        name="weight_grads",
    )(before[0], *state)


MESH = pl.DeviceIdType.MESH


def gather_weights_kernel(matrix, down, weights, send, receive, local):
    dp, section = lax.axis_index("dp"), lax.axis_index("section")
    odd = lax.rem(section, 2)
    partner = (dp, section + 1 - 2 * odd)
    barrier = pltpu.get_barrier_semaphore()
    pl.semaphore_signal(barrier, inc=1, device_id=partner, device_id_type=MESH)
    pl.semaphore_wait(barrier, 1)
    places = [(matrix.at[0, :, pl.ds(i * D, D)], odd * BLOCKS + i) for i in range(BLOCKS)]
    places += [(down.at[pl.ds(i * D, D), :], 2 * BLOCKS + odd * (BLOCKS // 2) + i) for i in range(BLOCKS // 2)]
    copies = []
    for i, (source, place) in enumerate(places):
        away = pltpu.make_async_remote_copy(
            source, weights.at[place], send.at[i], receive.at[i], device_id=partner, device_id_type=MESH
        )
        away.start()
        here = pltpu.make_async_copy(source, weights.at[place], local.at[i])
        here.start()
        copies += [away, here]
    for copy in copies:
        copy.wait()


def gather_weights(matrix, down):
    vmem = pl.BlockSpec(memory_space=pltpu.VMEM)
    return pl.pallas_call(
        gather_weights_kernel,
        in_specs=[vmem, vmem],
        out_specs=ANY,
        out_shape=sds((3 * BLOCKS, D, D), matrix.dtype),
        scratch_shapes=[pltpu.SemaphoreType.DMA((SHARE,)) for _ in range(3)],
        compiler_params=params(collective_id=1, has_side_effects=True),
        name="gather_weights",
    )(matrix, down)


RING = 8
SEGMENT = D // RING
PART = SEGMENT // 2
CHAIN = SHARE // 2


def ring_place(d):
    odd = lax.rem(d, 2)
    return (1 - odd) * lax.div(d, 2) + odd * (RING - 1 - lax.div(d, 2))


def ring_device(place):
    place = lax.rem(place + RING, RING)
    late = lax.div(place, RING // 2)
    return (1 - late) * 2 * place + late * (2 * (RING - 1 - place) + 1)


def reduce_kernel(
    grads1, grads2, swapping1, swapping2, vectors, out, swapped1, swapped2, out_vectors,
    mine, partner_part, landing, final, v_sum, v_in,
    out_sem, pair_send, pair_receive, own_sem, ring_send, ring_receive, last_send, last_receive,
    v_send, v_receive, swap_send, swap_receive,
):
    d, section = lax.axis_index("dp"), lax.axis_index("section")
    odd = lax.rem(section, 2)
    place = ring_place(d)
    across = (d, section + 2 - 4 * lax.div(section, 2))
    pair = (d, section + 1 - 2 * odd)
    ways = ((ring_device(place + 1), section), (ring_device(place - 1), section))
    packs = (grads1, grads2)

    def flipped(bit):
        return d + bit - 2 * bit * lax.rem(lax.div(d, bit), 2)

    levels = (pair, (flipped(1), section), (flipped(2), section), (flipped(4), section), across)
    barrier = pltpu.get_barrier_semaphore()
    for other in (*ways, *levels):
        pl.semaphore_signal(barrier, inc=1, device_id=other, device_id_type=MESH)
    own = [pltpu.make_async_copy(grads.at[odd], mine.at[k], own_sem.at[k]) for k, grads in enumerate(packs)]
    for copy in own:
        copy.start()
    pl.semaphore_wait(barrier, len(ways) + len(levels))

    def rows_of(step, way):
        segment = lax.rem(place + (step if way else -step) + 2 * RING, RING)
        return pl.ds(pl.multiple_of(segment * SEGMENT + way * PART, 8), PART)

    def remote(source, target, send, receive, device):
        return pltpu.make_async_remote_copy(source, target, send, receive, device_id=device, device_id_type=MESH)

    def pair_copy(step, way, k):
        rows = rows_of(step, way)
        return remote(
            packs[k].at[1 - odd, :, rows, :], partner_part.at[k, :, rows, :],
            pair_send.at[step, way, k], pair_receive.at[step, way, k], pair,
        )

    def start_pair(step, carry):
        for way in range(2):
            for k in range(2):
                pair_copy(step, way, k).start()
        return carry

    lax.fori_loop(0, RING, start_pair, 0)
    swaps = [
        remote(source, target, swap_send.at[k], swap_receive.at[k], across)
        for k, (source, target) in enumerate(((swapping1, swapped1), (swapping2, swapped2)))
    ]
    for swap in swaps:
        swap.start()

    def vector_copy(level):
        return remote(v_sum.at[level], v_in.at[level], v_send.at[level], v_receive.at[level], levels[level])

    def vector_next(level):
        vector_copy(level).wait()
        if level + 1 < len(levels):
            v_sum[level + 1] = v_sum[level] + v_in[level]
            vector_copy(level + 1).start()

    v_sum[0] = vectors[...]
    vector_copy(0).start()

    def blocks(chain):
        return pl.ds(chain * CHAIN, CHAIN)

    def ring_copy(step, way, chain):
        rows = rows_of(step, way)
        return remote(
            mine.at[0, blocks(chain), rows, :], landing.at[blocks(chain), rows, :],
            ring_send.at[step, way, chain], ring_receive.at[step, way, chain], ways[way],
        )

    def incoming(step, way, chain):
        rows = rows_of(step + 1, way)
        return remote(
            mine.at[0, blocks(chain), rows, :], landing.at[blocks(chain), rows, :],
            ring_send.at[step, way, chain], ring_receive.at[step, way, chain], ways[way],
        )

    def own_total(chain, rows):
        part = (blocks(chain), rows, slice(None))
        both = [ref[(k, *part)].astype(F32) for ref in (mine, partner_part) for k in range(2)]
        return (both[0] + both[1]) + (both[2] + both[3])

    def total_of(chain, rows):
        return (own_total(chain, rows) + landing[blocks(chain), rows, :].astype(F32)).astype(BF16)

    def pair_here(step, way):
        for k in range(2):
            pair_copy(step, way, k).wait_recv()

    for copy in own:
        copy.wait()
    for way in range(2):
        pair_here(0, way)
        rows = rows_of(0, way)
        for chain in range(2):
            mine[0, blocks(chain), rows, :] = own_total(chain, rows).astype(BF16)
            ring_copy(0, way, chain).start()
    vector_next(0)

    def reduce_step(step, carry):
        for chain in range(2):
            for way in range(2):
                if chain == 0:
                    pair_here(step, way)
                incoming(step - 1, way, chain).wait_recv()
                rows = rows_of(step, way)
                mine[0, blocks(chain), rows, :] = total_of(chain, rows)
                ring_copy(step, way, chain).start()
        return carry

    lax.fori_loop(1, RING - 1, reduce_step, 0)
    vector_next(1)

    def last_copy(step, way, chain, arriving=0):
        rows = rows_of(step + RING - 1 + arriving, way)
        return remote(
            final.at[blocks(chain), rows, :], final.at[blocks(chain), rows, :],
            last_send.at[step, way, chain], last_receive.at[step, way, chain], ways[way],
        )

    def out_copy(step, way, chain):
        part = (blocks(chain), rows_of(step + RING - 1, way), slice(None))
        return pltpu.make_async_copy(final.at[part], out.at[part], out_sem.at[step, way, chain])

    for chain in range(2):
        for way in range(2):
            if chain == 0:
                pair_here(RING - 1, way)
            incoming(RING - 2, way, chain).wait_recv()
            rows = rows_of(RING - 1, way)
            final[blocks(chain), rows, :] = total_of(chain, rows)
            last_copy(0, way, chain).start()
            out_copy(0, way, chain).start()
    vector_next(2)

    def gather_step(step, carry):
        for chain in range(2):
            for way in range(2):
                last_copy(step - 1, way, chain, 1).wait_recv()
                last_copy(step, way, chain).start()
                out_copy(step, way, chain).start()
        return carry

    lax.fori_loop(1, 3, gather_step, 0)
    vector_next(3)
    lax.fori_loop(3, 5, gather_step, 0)
    vector_next(4)
    out_vectors[0] = v_sum[len(levels) - 1]
    out_vectors[1] = v_in[len(levels) - 1]
    lax.fori_loop(5, RING - 1, gather_step, 0)

    def all_sent(step, carry):
        for way in range(2):
            for chain in range(2):
                ring_copy(step, way, chain).wait_send()
        return carry

    def pair_sent(step, carry):
        for way in range(2):
            for k in range(2):
                pair_copy(step, way, k).wait_send()
        return carry

    lax.fori_loop(0, RING - 1, all_sent, 0)
    lax.fori_loop(0, RING, pair_sent, 0)
    for swap in swaps:
        swap.wait()
    for chain in range(2):
        for way in range(2):
            last_copy(RING - 2, way, chain, 1).wait_recv()
            out_copy(RING - 1, way, chain).start()

    def last_sent(step, carry):
        for way in range(2):
            for chain in range(2):
                last_copy(step, way, chain).wait_send()
        return carry

    def written(step, carry):
        for way in range(2):
            for chain in range(2):
                out_copy(step, way, chain).wait()
        return carry

    lax.fori_loop(0, RING - 1, last_sent, 0)
    lax.fori_loop(0, RING, written, 0)


def reduce_grads(grads, swapping, vectors):
    share = (SHARE, D, D)
    dma = pltpu.SemaphoreType.DMA
    return pl.pallas_call(
        reduce_kernel,
        in_specs=[ANY, ANY, ANY, ANY, VMEM],
        out_specs=(ANY, ANY, ANY, VMEM),
        out_shape=(sds(share, BF16), ROWS, ROWS, sds((2, VECTORS, D), F32)),
        scratch_shapes=[
            pltpu.VMEM((2, *share), BF16),
            pltpu.VMEM((2, *share), BF16),
            pltpu.VMEM(share, BF16),
            pltpu.VMEM(share, BF16),
            pltpu.VMEM((5, VECTORS, D), F32),
            pltpu.VMEM((5, VECTORS, D), F32),
            dma((RING, 2, 2)),
            dma((RING, 2, 2)),
            dma((RING, 2, 2)),
            dma((2,)),
            dma((RING - 1, 2, 2)),
            dma((RING - 1, 2, 2)),
            dma((RING - 1, 2, 2)),
            dma((RING - 1, 2, 2)),
            dma((5,)),
            dma((5,)),
            dma((2,)),
            dma((2,)),
        ],
        compiler_params=params(56, collective_id=2, has_side_effects=True),
        name="reduce_grads",
    )(*grads, *swapping, vectors)


def spread_kernel(total, matrix, down):
    step = pl.program_id(0)

    @pl.when(step < BLOCKS)
    def _():
        matrix[...] = total[...].astype(F32)

    @pl.when(step >= BLOCKS)
    def _():
        down[...] = total[...].astype(F32)


def spread(total):
    return pl.pallas_call(
        spread_kernel,
        grid=(SHARE,),
        in_specs=[pl.BlockSpec((None, D, D), lambda i: (i, 0, 0))],
        out_specs=(
            pl.BlockSpec((None, D, D), lambda i: (0, 0, jnp.minimum(i, BLOCKS - 1))),
            pl.BlockSpec((D, D), lambda i: (jnp.maximum(i - BLOCKS, 0), 0)),
        ),
        out_shape=(sds((1, D, FF), F32), sds((FF // 2, D), F32)),
        compiler_params=params(60),
        name="spread",
    )(total)


def plain_reduce_grads(grads, swapping, vectors):
    odd = lax.rem(lax.axis_index("section"), 2)
    pair = [(0, 1), (1, 0), (2, 3), (3, 2)]
    grads = grads[0] + grads[1]
    theirs = lax.dynamic_index_in_dim(grads, 1 - odd, 0, keepdims=False)
    mine = lax.dynamic_index_in_dim(grads, odd, 0, keepdims=False)
    total = lax.psum(mine + lax.ppermute(theirs, "section", pair), "dp")
    vectors = lax.psum(vectors + lax.ppermute(vectors, "section", pair), "dp")
    return total, *map(swap_layers, swapping), jnp.stack([vectors, swap_layers(vectors)])


def swap_layers(block):
    return lax.ppermute(block, "section", [(0, 2), (1, 3), (2, 0), (3, 1)])


def to_regressor(block):
    return lax.ppermute(block, "section", [(0, 2), (1, 3)])


def to_encoder(block):
    return lax.ppermute(block, "section", [(2, 0), (3, 1)])


def body(
    vis_embed, latent_cot, reg_queries, out_cot, section_matrix, down_weight, enc_vectors, reg_vectors,
    mlp_vectors, hidden_bias, pos_table, image_lengths, vis_index, mask_index,
):
    section = lax.axis_index("section")
    odd = lax.rem(section, 2)
    is_reg = section >= 2
    layer = jnp.where(is_reg, 1, 0)
    weights = gather_weights(section_matrix, down_weight)
    r = lax.dynamic_index_in_dim(mlp_vectors, layer, 0, keepdims=False)
    c = lax.dynamic_slice_in_dim(hidden_bias, layer, 1, 0)
    packs = [(odd + 2 * i).reshape(1).astype(jnp.int32) for i in range(2)]
    vis = [lax.dynamic_slice_in_dim(vis_index, (odd + 2 * i) * CAP, CAP)[:, None] for i in range(2)]
    mask = [lax.dynamic_slice_in_dim(mask_index, (odd + 2 * i) * CAP, CAP)[:, None] for i in range(2)]

    incoming = swap_layers(jnp.where(is_reg, vis_embed, reg_queries))
    x = [vis_embed, incoming]
    queries = [incoming, reg_queries]

    def on_encoder(work, otherwise):
        return lax.cond(is_reg, otherwise, work)

    def on_regressor(work, otherwise):
        return lax.cond(is_reg, work, otherwise)

    def enc_forward(i):
        return encoder_forward(image_lengths, packs[i], x[i], enc_vectors, r, c, weights)

    def no_enc_forward():
        made = unset((ROWS, ROWS, *ENC_STATE))
        return made[0], made[1], tuple(made[2:])

    def enc_back(i, d_latents, kept, so_far):
        return encoder_back(
            image_lengths, packs[i], lat_cot[i], d_latents, x[i], kept[0], enc_vectors, r, so_far, weights, kept[2]
        )

    def reg_before():
        return tuple(
            tuple(regressor_before(image_lengths, packs[i], queries[i], vis[i], mask[i], pos_table, reg_vectors, weights))
            for i in range(2)
        )

    def no_reg_before():
        made = unset((*REG_BEFORE, *REG_BEFORE))
        return tuple(made[: len(REG_BEFORE)]), tuple(made[len(REG_BEFORE) :])

    def reg_work(i, latents, so_far):
        return lambda: regressor(
            image_lengths, packs[i], latents, queries[i], cot[i], reg_vectors, r, c, so_far, weights, before[i]
        )

    def no_reg_work():
        made = unset((ROWS, ROWS, ROWS, TOTALS, *REG_STATE))
        return (*made[:4], tuple(made[4:]))

    none = jnp.zeros((VECTORS, D), F32)
    enc1 = on_encoder(lambda: enc_forward(0), no_enc_forward)
    latents1 = to_regressor(enc1[1])
    before = on_regressor(reg_before, no_reg_before)
    swapped_cot = swap_layers(jnp.where(is_reg, latent_cot, out_cot))
    lat_cot = [latent_cot, swapped_cot]
    cot = [swapped_cot, out_cot]
    enc2 = on_encoder(lambda: enc_forward(1), no_enc_forward)
    latents2 = to_regressor(enc2[1])
    reg1 = on_regressor(reg_work(0, latents1, none), no_reg_work)
    d_latents1 = to_encoder(reg1[1])
    reg2 = on_regressor(reg_work(1, latents2, reg1[3]), no_reg_work)
    d_latents2 = to_encoder(reg2[1])
    shares1, enc_totals, vis_grad1 = lax.cond(
        is_reg,
        lambda: (weight_grads(before[0], reg1[4]), *unset((TOTALS, ROWS))),
        lambda: enc_back(0, d_latents1, enc1, none)[::-1],
    )
    shares2, vectors, swapping = lax.cond(
        is_reg,
        lambda: (weight_grads(before[1], reg2[4]), reg2[3], reg1[0]),
        lambda: enc_back(1, d_latents2, enc2, enc_totals)[::-1],
    )
    reduce = reduce_grads if lax.axis_size("dp") == RING else plain_reduce_grads
    total, swapped1, swapped2, vectors = reduce((shares1, shares2), (swapping, reg1[2]), vectors)
    matrix_grad, down_grad = spread(total)

    def pick(reg, enc):
        return jnp.where(is_reg, reg, enc)

    latents = pick(latents2, enc1[1])
    regressed = pick(reg2[0], swapped1)
    vis_grad = pick(swapped1, vis_grad1)
    query_grad = pick(reg2[2], swapped2)
    enc_total, reg_total = pick(vectors[1], vectors[0]), pick(vectors[0], vectors[1])
    return (
        latents,
        regressed,
        vis_grad,
        query_grad,
        matrix_grad,
        down_grad,
        enc_total[:6],
        reg_total[:10],
        jnp.stack([enc_total[FFN_AT:HIDDEN_AT], reg_total[FFN_AT:HIDDEN_AT]]),
        jnp.stack([t[HIDDEN_AT : HIDDEN_AT + BLOCKS].reshape(FF) for t in (enc_total, reg_total)]),
    )


def solution(mesh):
    rows = P(("dp", "section"), None)
    in_specs = (
        rows, rows, rows, rows, P("section", None, None), P("section", None),
        P(), P(), P(), P(), P(), P("dp", None), P("dp"), P("dp"),
    )
    out_specs = (rows, rows, rows, rows, P("section", None, None), P("section", None), P(), P(), P(), P())
    return jax.shard_map(body, mesh=mesh, in_specs=in_specs, out_specs=out_specs, check_vma=False)
```

```python
import functools

import jax
import jax.numpy as jnp
from jax import lax
from jax.experimental import pallas as pl
from jax.experimental.pallas import tpu as pltpu
from jax.sharding import PartitionSpec as P

F32 = jnp.float32
BF16 = jnp.bfloat16
CAP = 384
IMGS = 4
SLOT = 128
PAD = IMGS * SLOT
D = 768
FF = 3072
LANES = 128
PAIRS = D // LANES
BLOCKS = FF // D
VECTORS = 24
EPS = 1e-06
MIB = 1 << 20
ANY = pl.BlockSpec(memory_space=pl.ANY)
SMEM = pl.BlockSpec(memory_space=pltpu.SMEM)


def params(limit=48, **more):
    return pltpu.CompilerParams(vmem_limit_bytes=limit * MIB, **more)


def sds(shape, dtype):
    return jax.ShapeDtypeStruct(shape, dtype)


def dot(a, b):
    return jnp.dot(a, b, preferred_element_type=F32)


def dot_nt(a, b):
    return lax.dot_general(a, b, (((1,), (1,)), ((), ())), preferred_element_type=F32)


def dot_tn(a, b):
    return lax.dot_general(a, b, (((0,), (0,)), ((), ())), preferred_element_type=F32)


def row(ref, i):
    return ref[i : i + 1, :]


def colsum(values):
    return jnp.sum(values, axis=0, keepdims=True)


def normalize(values):
    centred = values - jnp.mean(values, axis=-1, keepdims=True)
    spread = jnp.mean(centred * centred, axis=-1, keepdims=True)
    inverse = lax.rsqrt(spread + EPS)
    return centred * inverse, inverse


def norm_back(gradient, gain, normed, inverse):
    return scaled_norm_back(gradient * gain, normed, inverse)


def scaled_norm_back(scaled, normed, inverse):
    level = jnp.mean(scaled, axis=-1, keepdims=True)
    slope = jnp.mean(scaled * normed, axis=-1, keepdims=True)
    return inverse * (scaled - level - normed * slope)


def gelu_parts(t):
    e = jnp.exp(-0.5 * t * t)
    k = 1.0 / (1.0 + (0.3275911 * 0.7071067811865476) * jnp.abs(t))
    poly = k * (
        0.127414796
        + k * (-0.142248368 + k * (0.7107068705 + k * (-0.7265760135 + k * 0.5307027145)))
    )
    tail = poly * e
    phi = jnp.where(t >= 0.0, 1.0 - tail, tail)
    return t * phi, phi + t * (e * 0.3989422804014327)


def group_matrices(lens, pack, regroup, ungroup):
    def image(j, start):
        size = lens[pack, j]
        slots = pl.ds(pl.multiple_of(j * SLOT, SLOT), SLOT)
        place = lax.broadcasted_iota(jnp.int32, (SLOT, CAP), 0)
        rows = lax.broadcasted_iota(jnp.int32, (SLOT, CAP), 1)
        hit = (place + start == rows) & (place < size)
        regroup[slots, :] = jnp.where(hit, 1.0, 0.0).astype(BF16)
        place = lax.broadcasted_iota(jnp.int32, (CAP, SLOT), 1)
        rows = lax.broadcasted_iota(jnp.int32, (CAP, SLOT), 0)
        hit = (place + start == rows) & (place < size)
        ungroup[:, slots] = jnp.where(hit, 1.0, 0.0).astype(BF16)
        return start + size

    lax.fori_loop(0, IMGS, image, jnp.int32(0))


def lane_halves():
    lane = lax.broadcasted_iota(jnp.int32, (1, LANES), 1)
    first = jnp.where(lane < LANES // 2, 1.0, 0.0)
    return first.astype(BF16), (1.0 - first).astype(BF16)


def both_heads(block, halves):
    return jnp.concatenate([block * halves[0], block * halves[1]], axis=0)


def merge_heads(stacked):
    keys = stacked.shape[0] // 2
    lane = lax.broadcasted_iota(jnp.int32, (keys, LANES), 1)
    return jnp.where(lane < LANES // 2, stacked[:keys], stacked[keys:])


def softmax(scores):
    raised = jnp.exp(scores - jnp.max(scores, axis=0, keepdims=True))
    return (raised * (1.0 / jnp.sum(raised, axis=0, keepdims=True))).astype(BF16)


def keys_of(packed, first, parts, rows, cols, halves):
    return both_heads(
        jnp.concatenate([packed[first + 2 * m, rows, cols] for m in range(parts)], axis=0), halves
    )


def attend(lens, pack, packed, probs, mixed_slots, parts, done):
    halves = lane_halves()
    keys = SLOT * parts
    place = lax.bitwise_and(lax.broadcasted_iota(jnp.int32, (keys, SLOT), 0), SLOT - 1)
    for j in range(IMGS):
        rows = slice(j * SLOT, (j + 1) * SLOT)
        valid = place < lens[pack, j]
        for g in range(PAIRS):
            cols = slice(g * LANES, (g + 1) * LANES)
            scores = dot_nt(keys_of(packed, 1, parts, rows, cols, halves), packed[0, rows, cols])
            low = jnp.concatenate(
                [softmax(jnp.where(valid, part, -1e30)) for part in (scores[:keys], scores[keys:])], axis=0
            )
            probs[j, g] = low
            mixed_slots[rows, cols] = dot_tn(low, keys_of(packed, 2, parts, rows, cols, halves)).astype(BF16)
        done(j)


def attend_back(packed, probs, mixed_slots, d_mixed_slots, parts, ready, beside):
    halves = lane_halves()
    keys = SLOT * parts
    less = both_heads(jnp.full((keys, LANES), -1.0, BF16), halves)

    def image(j, carry):
        ready(j)
        rows = pl.ds(pl.multiple_of(j * SLOT, SLOT), SLOT)
        after = beside(j)
        for g in range(PAIRS):
            cols = slice(g * LANES, (g + 1) * LANES)
            d_out = d_mixed_slots[rows, cols]
            centre = (d_out.astype(F32) * mixed_slots[rows, cols].astype(F32)).astype(BF16)
            low = probs[j, g]
            d_prob = dot_nt(
                jnp.concatenate([keys_of(packed, 2, parts, rows, cols, halves), less], axis=1),
                jnp.concatenate([d_out, centre], axis=1),
            )
            d_scores = (low.astype(F32) * d_prob).astype(BF16)
            q = packed[0, rows, cols]
            zero = jnp.zeros_like(q)
            sides = jnp.concatenate(
                [jnp.concatenate([q, zero], axis=1), jnp.concatenate([zero, d_out], axis=1)], axis=0
            )
            d_kv = dot(jnp.concatenate([d_scores, low], axis=1), sides)
            d_q = dot_tn(d_scores, keys_of(packed, 1, parts, rows, cols, halves)) * 0.125
            packed[0, rows, cols] = d_q.astype(BF16)
            for side in range(2):
                merged = merge_heads(d_kv[:, side * LANES : (side + 1) * LANES]).astype(BF16)
                for m in range(parts):
                    packed[1 + side + 2 * m, rows, cols] = merged[m * SLOT : (m + 1) * SLOT]
        if after is not None:
            after()
        return carry

    lax.fori_loop(0, IMGS, image, 0)


ROWS = sds((CAP, D), BF16)
WIDE = sds((CAP, FF), BF16)
TOTALS = sds((VECTORS, D), F32)
FFN_AT = 10
HIDDEN_AT = FFN_AT + 4
ENC_STATE = (
    ROWS,
    sds((3, PAD, D), BF16),
    sds((IMGS, PAIRS, 2 * SLOT, SLOT), BF16),
    sds((PAD, D), BF16),
    ROWS,
    ROWS,
    ROWS,
    WIDE,
    WIDE,
    ROWS,
)
REG_BEFORE = (
    sds((3, CAP, D), BF16),
    sds((3, PAD, D), BF16),
    sds((2, CAP, D), F32),
)
REG_STATE = (
    sds((2, CAP, D), BF16),
    sds((5, CAP, D), BF16),
    ROWS,
    ROWS,
    ROWS,
    WIDE,
    WIDE,
    ROWS,
)


def full(shape):
    return pl.BlockSpec(shape, lambda i: (0,) * len(shape))


VMEM = pl.BlockSpec(memory_space=pltpu.VMEM)


def scratch(shape):
    return pltpu.VMEM(shape.shape, shape.dtype)


def unset(shapes):
    def kernel(*refs):
        del refs

    return pl.pallas_call(
        kernel, out_shape=shapes, out_specs=tuple(ANY for _ in shapes), name="unset"
    )()


class Copies:
    def __init__(self, semaphores):
        self.semaphores, self.used, self.open = semaphores, 0, []

    def take(self, count=1):
        self.used += count
        return self.used - count

    def start(self, source, target):
        copy = pltpu.make_async_copy(source, target, self.semaphores.at[self.take()])
        copy.start()
        return copy

    def leave(self, source, target):
        self.open.append(self.start(source, target))

    def halves(self, *pairs):
        first = self.take(2 * len(pairs))

        def copies(i):
            rows = half_rows(i)
            return [
                pltpu.make_async_copy(source.at[rows, :], target.at[rows, :], self.semaphores.at[first + 2 * k + i])
                for k, (source, target) in enumerate(pairs)
            ]

        def start(i):
            for copy in copies(i):
                copy.start()

        self.open += copies(0) + copies(1)
        return start

    def finish(self):
        for copy in self.open:
            copy.wait()


COPIES = pltpu.SemaphoreType.DMA((80,))


def columns(i):
    return slice(i * D, (i + 1) * D)


class Weights:
    def __init__(self, copies, weights, held):
        self.copies, self.weights, self.held, self.started = copies, weights, held, {}

    def target(self, i):
        kind, block = divmod(i, BLOCKS)
        held = self.held[kind]
        return held.at[columns(block), :] if kind == 2 else held.at[:, columns(block)]

    def start(self, *order):
        for i in order:
            self.started[i] = self.copies.start(self.weights.at[i], self.target(i))

    def wait(self, *which):
        for i in which:
            self.started[i].wait()


WEIGHT_SCRATCH = [pltpu.VMEM((D, FF), BF16), pltpu.VMEM((D, FF), BF16), pltpu.VMEM((FF, D), BF16)]
ALL_BLOCKS = range(BLOCKS)
UPS = [BLOCKS + i for i in ALL_BLOCKS]
DOWNS = [2 * BLOCKS + i for i in ALL_BLOCKS]


def wide(i):
    return pl.ds(pl.multiple_of(i * D, D), D)


HALF = CAP // 2


def half_rows(i):
    return pl.ds(pl.multiple_of(i * HALF, HALF), HALF)


def feed_forward(weights, mid, r, c, out, state, made):
    normed, active, slope, branch = state
    centred, _ = normalize(mid[...].astype(F32))
    normed[...] = (centred * row(r, 0) + row(r, 1)).astype(BF16)
    made("normed")
    _, up, down = weights.held
    weights.wait(*UPS, *DOWNS)

    def part(i, carry):
        rows = half_rows(i)
        value, steep = gelu_parts(dot(normed[rows, :], up[...]) + c[...])
        active[rows, :] = value.astype(BF16)
        slope[rows, :] = steep.astype(BF16)
        made(i)
        summed = dot(active[rows, :], down[...]) + row(r, 2)
        branch[rows, :] = summed.astype(BF16)
        out[rows, :] = (mid[rows, :].astype(F32) + row(r, 3) * summed).astype(BF16)
        return carry

    lax.fori_loop(0, 2, part, 0)
    made("branch")


def feed_forward_back(weights, ready, g, mid, r, refs, totals, residual, made):
    slope, branch, d_branch = refs
    _, up, down = weights.held
    d_branch[...] = (g * row(r, 3)).astype(BF16)
    made("branch")
    add_row(totals, FFN_AT + 2, colsum(d_branch[...].astype(F32)))
    ready("branch")
    add_row(totals, FFN_AT + 3, colsum(g * branch[...].astype(F32)))
    for i in ALL_BLOCKS:
        weights.wait(2 * BLOCKS + i)
        ready(i)
        d_active = dot_nt(d_branch[...], down[columns(i), :])
        d_hidden = (d_active * slope[:, columns(i)].astype(F32)).astype(BF16)
        slope[:, columns(i)] = d_hidden
        made(i)
        add_row(totals, HIDDEN_AT + i, colsum(d_hidden.astype(F32)))
    weights.wait(*UPS)
    d_normed = dot_nt(slope[...], up[...])
    normed, inverse = normalize(mid[...].astype(F32))
    add_row(totals, FFN_AT, colsum(d_normed * normed))
    add_row(totals, FFN_AT + 1, colsum(d_normed))
    residual[...] = (g + norm_back(d_normed, row(r, 0), normed, inverse)).astype(BF16).astype(F32)


def attention_back(parts, weights, e, refs, totals, ready, made, beside):
    residual, branch, d_branch, regroup, ungroup, packed, probs, mixed_slots, d_slots, d_flat = refs
    last = 1 + 4 * parts
    g = residual[...]
    ready("branch")
    d_branch[...] = (g * row(e, last)).astype(BF16)
    made("branch")
    add_row(totals, last, colsum(g * branch[...].astype(F32)))
    add_row(totals, last - 1, colsum(d_branch[...].astype(F32)))
    weights.wait(3)
    d_mixed = dot(d_branch[...], weights.held[0][:, columns(3)]).astype(BF16)
    d_slots[...] = dot(regroup[...], d_mixed).astype(BF16)
    ready("packed")
    attend_back(packed, probs, mixed_slots, d_slots, parts, ready, beside)
    for m in range(1 + 2 * parts):
        d_flat[m] = dot(ungroup[...], packed[m]).astype(BF16)
        made(m)


def add_row(totals, i, value):
    totals[i : i + 1] += value


def nothing(name):
    del name


class Shares:
    def __init__(self, copies, blocks, share):
        self.semaphores, self.blocks, self.share = copies.semaphores, blocks, share
        self.first = copies.take(3 * BLOCKS)

    def copy(self, kind, i):
        section, block = (lax.div(i, 2), BLOCKS + lax.rem(i, 2)) if kind == 2 else (kind, i)
        place = kind * BLOCKS + i
        return pltpu.make_async_copy(
            self.blocks.at[place], self.share.at[section, block], self.semaphores.at[self.first + place]
        )

    def put(self, kind, i, product):
        self.blocks[kind * BLOCKS + i] = product.astype(BF16)
        self.copy(kind, i).start()

    def feed_forward(self, normed, d_hidden, active, d_branch):
        def step(i):
            self.blocks[BLOCKS + i] = dot_tn(normed[...], d_hidden[:, wide(i)]).astype(BF16)
            self.blocks[2 * BLOCKS + i] = dot_tn(active[:, wide(i)], d_branch[...]).astype(BF16)

            def after():
                for kind in (1, 2):
                    self.copy(kind, i).start()

            return after

        return step

    def finish(self):
        for kind in range(3):
            for i in ALL_BLOCKS:
                self.copy(kind, i).wait()


def encoder_forward_kernel(lens, which, x, e, r, c, given, mid, out, *refs):
    kept, scratch = refs[: len(ENC_STATE)], refs[len(ENC_STATE) :]
    *held, flat, regroup, ungroup, semaphores = scratch[: 3 + 4]
    state = scratch[3 + 4 :]
    normed, packed, probs, mixed_slots, mixed, branch, *ffn = state
    pack = which[0]
    copies = Copies(semaphores)
    weights = Weights(copies, given, held)
    weights.start(*ALL_BLOCKS, *UPS, *DOWNS)
    values = x[...].astype(F32)
    centred, _ = normalize(values)
    normed[...] = (centred * row(e, 0) + row(e, 1)).astype(BF16)
    copies.leave(normed, kept[0])
    group_matrices(lens, pack, regroup, ungroup)
    qkvo = weights.held[0]
    weights.wait(0)
    flat[0] = ((dot(normed[...], qkvo[:, columns(0)]) + row(e, 2)).astype(BF16) * 0.125).astype(BF16)
    weights.wait(1)
    flat[1] = dot(normed[...], qkvo[:, columns(1)]).astype(BF16)
    weights.wait(2)
    flat[2] = (dot(normed[...], qkvo[:, columns(2)]) + row(e, 3)).astype(BF16)
    for m in range(3):
        packed[m] = dot(regroup[...], flat[m]).astype(BF16)
        copies.leave(packed.at[m], kept[1].at[m])
    attend(lens, pack, packed, probs, mixed_slots, 1, lambda j: copies.leave(probs.at[j], kept[2].at[j]))
    copies.leave(mixed_slots, kept[3])
    mixed[...] = dot(ungroup[...], mixed_slots[...]).astype(BF16)
    copies.leave(mixed, kept[4])
    weights.wait(3)
    summed = dot_nt(mixed[...], qkvo[:, columns(3)]) + row(e, 4)
    branch[...] = summed.astype(BF16)
    copies.leave(branch, kept[5])
    mid[...] = (values + row(e, 5) * summed).astype(BF16)

    half_made = copies.halves((ffn[1], kept[7]), (ffn[2], kept[8]))

    def made(name):
        if isinstance(name, str):
            source, target = (ffn[0], kept[6]) if name == "normed" else (ffn[3], kept[9])
            copies.leave(source, target)
        else:
            half_made(name)

    feed_forward(weights, mid, r, c, out, ffn, made)
    copies.finish()


def encoder_forward(lens, which, x, e, r, c, weights):
    made = pl.pallas_call(
        encoder_forward_kernel,
        in_specs=[SMEM, SMEM, VMEM, VMEM, VMEM, VMEM, ANY],
        out_specs=(VMEM, VMEM, *(ANY for _ in ENC_STATE)),
        out_shape=(ROWS, ROWS, *ENC_STATE),
        scratch_shapes=[
            *WEIGHT_SCRATCH,
            pltpu.VMEM((3, CAP, D), BF16),
            pltpu.VMEM((PAD, CAP), BF16),
            pltpu.VMEM((CAP, PAD), BF16),
            COPIES,
            *map(scratch, ENC_STATE),
        ],
        compiler_params=params(58),
        name="encoder_forward",
    )(lens, which, x, e, r, c, weights)
    return made[0], made[1], tuple(made[2:])


def encoder_back_kernel(lens, which, g1, g2, x, mid, e, r, so_far, given, *refs):
    state, refs = refs[: len(ENC_STATE)], refs[len(ENC_STATE) :]
    d_x, totals, share, *held, regroup, ungroup, d_slots, d_branch, d_f_branch, d_flat, residual, blocks, semaphores = (
        refs[: 3 + 3 + 9]
    )
    normed, packed, probs, mixed_slots, mixed, branch, f_normed, active, slope, f_branch = refs[3 + 3 + 9 :]
    copies = Copies(semaphores)
    weights = Weights(copies, given, held)
    coming = {"branch": copies.start(state[9], f_branch)}
    for i in ALL_BLOCKS:
        weights.start(2 * BLOCKS + i)
        coming[i] = copies.start(state[8].at[:, columns(i)], slope.at[:, columns(i)])
    weights.start(*UPS, 3)
    later = {"branch": copies.start(state[5], branch)}
    later["packed"] = copies.start(state[1], packed)
    later["mixed"] = copies.start(state[3], mixed_slots)
    probs_in = [copies.start(state[2].at[j], probs.at[j]) for j in range(IMGS)]
    late = [copies.start(state[i], ref) for i, ref in ((6, f_normed), (7, active), (0, normed), (4, mixed))]
    weights.start(0, 1, 2)
    shares = Shares(copies, blocks, share)
    totals[...] = so_far[...]
    group_matrices(lens, which[0], regroup, ungroup)
    g = g1[...].astype(F32) + g2[...].astype(F32)
    feed_forward_back(
        weights, lambda name: coming[name].wait(), g, mid, r, (slope, f_branch, d_f_branch), totals, residual, nothing
    )
    for copy in late:
        copy.wait()

    def ready(name):
        if name == "branch":
            later["branch"].wait()
        elif name == "packed":
            later["packed"].wait()
            later["mixed"].wait()
            for copy in probs_in:
                copy.wait()

    attention_back(
        1, weights, e, (residual, branch, d_branch, regroup, ungroup, packed, probs, mixed_slots, d_slots, d_flat),
        totals, ready, nothing, shares.feed_forward(f_normed, slope, active, d_f_branch),
    )

    def first_block(i, carry):
        shares.put(0, i, dot_tn(normed[...], d_flat[i]))
        return carry

    lax.fori_loop(0, 3, first_block, 0)
    shares.put(0, 3, dot_tn(d_branch[...], mixed[...]))
    weights.wait(0, 1, 2)
    qkvo = weights.held[0]
    d_normed = dot_nt(d_flat[0], qkvo[:, columns(0)])
    for m in (1, 2):
        d_normed += dot_nt(d_flat[m], qkvo[:, columns(m)])
    values, inverse = normalize(x[...].astype(F32))
    add_row(totals, 0, colsum(d_normed * values))
    add_row(totals, 1, colsum(d_normed))
    add_row(totals, 2, colsum(d_flat[0].astype(F32)))
    add_row(totals, 3, colsum(d_flat[2].astype(F32)))
    d_x[...] = (residual[...] + norm_back(d_normed, row(e, 0), values, inverse)).astype(BF16)
    shares.finish()


def encoder_back(lens, which, g1, g2, x, mid, e, r, so_far, weights, state):
    return pl.pallas_call(
        encoder_back_kernel,
        in_specs=[SMEM, SMEM, *(VMEM for _ in range(7)), ANY, *(ANY for _ in ENC_STATE)],
        out_specs=(VMEM, VMEM, ANY),
        out_shape=(ROWS, TOTALS, sds((2, SHARE, D, D), BF16)),
        scratch_shapes=[
            *WEIGHT_SCRATCH,
            pltpu.VMEM((PAD, CAP), BF16),
            pltpu.VMEM((CAP, PAD), BF16),
            pltpu.VMEM((PAD, D), BF16),
            scratch(ROWS),
            scratch(ROWS),
            pltpu.VMEM((3, CAP, D), BF16),
            pltpu.VMEM((CAP, D), F32),
            pltpu.VMEM((3 * BLOCKS, D, D), BF16),
            COPIES,
            *map(scratch, ENC_STATE),
        ],
        compiler_params=params(58),
        name="encoder_back",
    )(lens, which, g1, g2, x, mid, e, r, so_far, weights, *state)


def table_rows(indices, table):
    places = lax.broadcasted_iota(jnp.int32, (indices.shape[0], table.shape[0]), 1)
    chosen = jnp.where(places == indices[...], 1.0, 0.0).astype(BF16)
    values = table[...]
    top = values.astype(BF16)
    values = values - top.astype(F32)
    middle = values.astype(BF16)
    bottom = (values - middle.astype(F32)).astype(BF16)
    return (dot(chosen, top) + dot(chosen, middle)) + dot(chosen, bottom)


def regressor_before_kernel(lens, which, queries, vis, mask, table, e, given, normed, packed, sources, held, flat, regroup, ungroup, semaphores):
    copies = Copies(semaphores)
    weights = Weights(copies, given, [held])
    weights.start(0, 1, 2)
    group_matrices(lens, which[0], regroup, ungroup)
    sources[1] = table_rows(vis, table)
    residual = queries[...].astype(F32)
    source = residual + table_rows(mask, table)
    sources[0] = source
    centred, _ = normalize(source)
    normed[0] = (centred * row(e, 0) + row(e, 1)).astype(BF16)
    normed[1] = (centred * row(e, 2) + row(e, 3)).astype(BF16)
    centred, _ = normalize(residual)
    normed[2] = (centred * row(e, 4) + row(e, 5)).astype(BF16)
    weights.wait(0, 1, 2)
    flat[0] = ((dot(normed[0], held[:, columns(0)]) + row(e, 6)).astype(BF16) * 0.125).astype(BF16)
    flat[1] = dot(normed[1], held[:, columns(1)]).astype(BF16)
    flat[2] = (dot(normed[2], held[:, columns(2)]) + row(e, 7)).astype(BF16)
    for m in range(3):
        packed[m] = dot(regroup[...], flat[m]).astype(BF16)


def regressor_before(lens, which, queries, vis, mask, table, e, weights):
    return pl.pallas_call(
        regressor_before_kernel,
        in_specs=[SMEM, SMEM, *(VMEM for _ in range(5)), ANY],
        out_specs=(VMEM, VMEM, VMEM),
        out_shape=REG_BEFORE,
        scratch_shapes=[
            pltpu.VMEM((D, FF), BF16),
            pltpu.VMEM((3, CAP, D), BF16),
            pltpu.VMEM((PAD, CAP), BF16),
            pltpu.VMEM((CAP, PAD), BF16),
            COPIES,
        ],
        compiler_params=params(48),
        name="regressor_before",
    )(lens, which, queries, vis, mask, table, e, weights)


def regressor_kernel(
    lens, which, latents, queries, cot, e, r, c, so_far, given, packed_before, sources_before,
    regressed, d_latents, d_queries, totals, *refs,
):
    kept, refs = refs[: len(REG_STATE)], refs[len(REG_STATE) :]
    (
        *held, regroup, ungroup, packed, probs, mixed_slots, d_slots, sources, branch, slope, f_branch, mid, residual,
        flat, semaphores, normed, d_flat, mixed, d_branch, f_normed, _, active, d_f_branch,
    ) = refs
    pack = which[0]
    copies = Copies(semaphores)
    weights = Weights(copies, given, held)
    in_sources = copies.start(sources_before, sources)
    weights.start(1, 2)
    in_packed = [copies.start(packed_before.at[i], packed.at[m]) for i, m in enumerate((0, 3, 4))]
    weights.start(3, *UPS, *DOWNS, 0)
    qkvo = weights.held[0]
    group_matrices(lens, pack, regroup, ungroup)
    incoming = latents[...].astype(F32)
    centred, _ = normalize(incoming)
    normed[1] = (centred * row(e, 4) + row(e, 5)).astype(BF16)
    in_sources.wait()
    k_source = incoming + sources[1]
    sources[1] = k_source
    centred, _ = normalize(k_source)
    normed[0] = (centred * row(e, 2) + row(e, 3)).astype(BF16)
    copies.leave(normed, kept[0])
    weights.wait(1)
    flat[0] = dot(normed[0], qkvo[:, columns(1)]).astype(BF16)
    weights.wait(2)
    flat[1] = (dot(normed[1], qkvo[:, columns(2)]) + row(e, 7)).astype(BF16)
    for m in range(2):
        packed[1 + m] = dot(regroup[...], flat[m]).astype(BF16)
    for copy in in_packed:
        copy.wait()
    attend(lens, pack, packed, probs, mixed_slots, 2, nothing)
    mixed[...] = dot(ungroup[...], mixed_slots[...]).astype(BF16)
    copies.leave(mixed, kept[2])
    weights.wait(3)
    summed = dot_nt(mixed[...], qkvo[:, columns(3)]) + row(e, 8)
    branch[...] = summed.astype(BF16)
    mid[...] = (queries[...].astype(F32) + row(e, 9) * summed).astype(BF16)

    half_made = copies.halves((active, kept[6]))

    def forward_made(name):
        if not isinstance(name, str):
            half_made(name)
        elif name == "normed":
            copies.leave(f_normed, kept[4])

    feed_forward(weights, mid, r, c, regressed, (f_normed, active, slope, f_branch), forward_made)

    totals[...] = so_far[...]
    waited = Weights(copies, given, held)
    waited.wait = nothing_more

    def back_made(name):
        if name == "branch":
            copies.leave(d_f_branch, kept[7])
        else:
            copies.leave(slope.at[:, columns(name)], kept[5].at[:, columns(name)])

    feed_forward_back(
        waited, nothing, cot[...].astype(F32), mid, r, (slope, f_branch, d_f_branch), totals, residual, back_made
    )

    def attention_made(name):
        if name == "branch":
            copies.leave(d_branch, kept[3])
        else:
            copies.leave(d_flat.at[name], kept[1].at[name])

    attention_back(
        2, waited, e, (residual, branch, d_branch, regroup, ungroup, packed, probs, mixed_slots, d_slots, d_flat),
        totals, nothing, attention_made, nothing,
    )
    weights.wait(0)
    add_row(totals, 6, colsum(d_flat[0].astype(F32)))
    add_row(totals, 7, colsum(d_flat[2].astype(F32)) + colsum(d_flat[4].astype(F32)))
    values, inverse = normalize(sources[0])
    grad = dot_nt(d_flat[0], qkvo[:, columns(0)])
    add_row(totals, 0, colsum(grad * values))
    add_row(totals, 1, colsum(grad))
    scaled = grad * row(e, 0)
    grad = dot_nt(d_flat[3], qkvo[:, columns(1)])
    k_gain = colsum(grad * values)
    k_offset = colsum(grad)
    scaled += grad * row(e, 2)
    total = residual[...] + scaled_norm_back(scaled, values, inverse)
    values, inverse = normalize(queries[...].astype(F32))
    grad = dot_nt(d_flat[4], qkvo[:, columns(2)])
    v_gain = colsum(grad * values)
    v_offset = colsum(grad)
    total += norm_back(grad, row(e, 4), values, inverse)
    d_queries[...] = total.astype(BF16)
    values, inverse = normalize(sources[1])
    grad = dot_nt(d_flat[1], qkvo[:, columns(1)])
    add_row(totals, 2, k_gain + colsum(grad * values))
    add_row(totals, 3, k_offset + colsum(grad))
    total = norm_back(grad, row(e, 2), values, inverse)
    values, inverse = normalize(latents[...].astype(F32))
    grad = dot_nt(d_flat[2], qkvo[:, columns(2)])
    add_row(totals, 4, v_gain + colsum(grad * values))
    add_row(totals, 5, v_offset + colsum(grad))
    total += norm_back(grad, row(e, 4), values, inverse)
    d_latents[...] = total.astype(BF16)
    copies.finish()


def nothing_more(*which):
    del which


def regressor(lens, which, latents, queries, cot, e, r, c, so_far, weights, before):
    made = pl.pallas_call(
        regressor_kernel,
        in_specs=[SMEM, SMEM, *(VMEM for _ in range(7)), ANY, ANY, ANY],
        out_specs=(VMEM, VMEM, VMEM, VMEM, *(ANY for _ in REG_STATE)),
        out_shape=(ROWS, ROWS, ROWS, TOTALS, *REG_STATE),
        scratch_shapes=[
            *WEIGHT_SCRATCH,
            pltpu.VMEM((PAD, CAP), BF16),
            pltpu.VMEM((CAP, PAD), BF16),
            pltpu.VMEM((5, PAD, D), BF16),
            pltpu.VMEM((IMGS, PAIRS, 4 * SLOT, SLOT), BF16),
            pltpu.VMEM((PAD, D), BF16),
            pltpu.VMEM((PAD, D), BF16),
            pltpu.VMEM((2, CAP, D), F32),
            scratch(ROWS),
            scratch(WIDE),
            scratch(ROWS),
            scratch(ROWS),
            pltpu.VMEM((CAP, D), F32),
            pltpu.VMEM((2, CAP, D), BF16),
            COPIES,
            *(scratch(s) if i != 5 else pltpu.VMEM((8, LANES), BF16) for i, s in enumerate(REG_STATE)),
        ],
        compiler_params=params(60),
        name="regressor",
    )(lens, which, latents, queries, cot, e, r, c, so_far, weights, before[1], before[2])
    return (*made[:4], tuple(made[4:]))


SHARE = BLOCKS + BLOCKS // 2


def weight_grads_kernel(*refs):
    sources, share, held, blocks, semaphores = refs[:9], refs[9], refs[10:19], refs[19], refs[20]
    copies = Copies(semaphores)
    order = (5, 6, 7, 8, 0, 1, 2, 3, 4)
    started = {i: copies.start(sources[i], held[i]) for i in order}
    before, normed, d_flat, mixed, d_branch, f_normed, d_hidden, active, d_f_branch = held
    shares = Shares(copies, blocks, share)
    for i in order[:4]:
        started[i].wait()
    work = shares.feed_forward(f_normed, d_hidden, active, d_f_branch)

    def ffn_blocks(i, carry):
        work(i)()
        return carry

    lax.fori_loop(0, BLOCKS, ffn_blocks, 0)
    for i in order[4:]:
        started[i].wait()
    shares.put(0, 0, dot_tn(before[0], d_flat[0]))

    def pair_block(i, carry):
        shares.put(0, i, dot_tn(normed[i - 1], d_flat[i]) + dot_tn(before[i], d_flat[i + 2]))
        return carry

    lax.fori_loop(1, 3, pair_block, 0)
    shares.put(0, 3, dot_tn(d_branch[...], mixed[...]))
    shares.finish()


def weight_grads(before, state):
    return pl.pallas_call(
        weight_grads_kernel,
        in_specs=[ANY] * 9,
        out_specs=ANY,
        out_shape=sds((2, SHARE, D, D), BF16),
        scratch_shapes=[
            scratch(REG_BEFORE[0]),
            *map(scratch, REG_STATE),
            pltpu.VMEM((3 * BLOCKS, D, D), BF16),
            COPIES,
        ],
        compiler_params=params(),
        name="weight_grads",
    )(before[0], *state)


MESH = pl.DeviceIdType.MESH


def gather_weights_kernel(matrix, down, weights, send, receive, local):
    dp, section = lax.axis_index("dp"), lax.axis_index("section")
    odd = lax.rem(section, 2)
    partner = (dp, section + 1 - 2 * odd)
    barrier = pltpu.get_barrier_semaphore()
    pl.semaphore_signal(barrier, inc=1, device_id=partner, device_id_type=MESH)
    pl.semaphore_wait(barrier, 1)
    places = [(matrix.at[0, :, pl.ds(i * D, D)], odd * BLOCKS + i) for i in range(BLOCKS)]
    places += [(down.at[pl.ds(i * D, D), :], 2 * BLOCKS + odd * (BLOCKS // 2) + i) for i in range(BLOCKS // 2)]
    copies = []
    for i, (source, place) in enumerate(places):
        away = pltpu.make_async_remote_copy(
            source, weights.at[place], send.at[i], receive.at[i], device_id=partner, device_id_type=MESH
        )
        away.start()
        here = pltpu.make_async_copy(source, weights.at[place], local.at[i])
        here.start()
        copies += [away, here]
    for copy in copies:
        copy.wait()


def gather_weights(matrix, down):
    vmem = pl.BlockSpec(memory_space=pltpu.VMEM)
    return pl.pallas_call(
        gather_weights_kernel,
        in_specs=[vmem, vmem],
        out_specs=ANY,
        out_shape=sds((3 * BLOCKS, D, D), matrix.dtype),
        scratch_shapes=[pltpu.SemaphoreType.DMA((SHARE,)) for _ in range(3)],
        compiler_params=params(collective_id=1, has_side_effects=True),
        name="gather_weights",
    )(matrix, down)


RING = 8
SEGMENT = D // RING
PART = SEGMENT // 2
CHAIN = SHARE // 2


def ring_place(d):
    odd = lax.rem(d, 2)
    return (1 - odd) * lax.div(d, 2) + odd * (RING - 1 - lax.div(d, 2))


def ring_device(place):
    place = lax.rem(place + RING, RING)
    late = lax.div(place, RING // 2)
    return (1 - late) * 2 * place + late * (2 * (RING - 1 - place) + 1)


def reduce_kernel(
    grads1, grads2, swapping1, swapping2, vectors, out, swapped1, swapped2, out_vectors,
    mine, partner_part, landing, final, v_sum, v_in,
    out_sem, pair_send, pair_receive, own_sem, ring_send, ring_receive, last_send, last_receive,
    v_send, v_receive, swap_send, swap_receive,
):
    d, section = lax.axis_index("dp"), lax.axis_index("section")
    odd = lax.rem(section, 2)
    place = ring_place(d)
    across = (d, section + 2 - 4 * lax.div(section, 2))
    pair = (d, section + 1 - 2 * odd)
    ways = ((ring_device(place + 1), section), (ring_device(place - 1), section))
    packs = (grads1, grads2)

    def flipped(bit):
        return d + bit - 2 * bit * lax.rem(lax.div(d, bit), 2)

    levels = (pair, (flipped(1), section), (flipped(2), section), (flipped(4), section), across)
    barrier = pltpu.get_barrier_semaphore()
    for other in (*ways, *levels):
        pl.semaphore_signal(barrier, inc=1, device_id=other, device_id_type=MESH)

    def rows_of(step, way):
        segment = lax.rem(place + (step if way else -step) + 2 * RING, RING)
        return pl.ds(pl.multiple_of(segment * SEGMENT + way * PART, 8), PART)

    def own_copy(step, way, k):
        rows = rows_of(step, way)
        return pltpu.make_async_copy(
            packs[k].at[odd, :, rows, :], mine.at[k, :, rows, :], own_sem.at[step, way, k]
        )

    pl.semaphore_wait(barrier, len(ways) + len(levels))

    def remote(source, target, send, receive, device):
        return pltpu.make_async_remote_copy(source, target, send, receive, device_id=device, device_id_type=MESH)

    def pair_copy(step, way, k):
        rows = rows_of(step, way)
        return remote(
            packs[k].at[1 - odd, :, rows, :], partner_part.at[k, :, rows, :],
            pair_send.at[step, way, k], pair_receive.at[step, way, k], pair,
        )

    def start_inputs(step):
        for way in range(2):
            for k in range(2):
                pair_copy(step, way, k).start()
                own_copy(step, way, k).start()

    start_inputs(0)
    start_inputs(1)
    swaps = [
        remote(source, target, swap_send.at[k], swap_receive.at[k], across)
        for k, (source, target) in enumerate(((swapping1, swapped1), (swapping2, swapped2)))
    ]
    for swap in swaps:
        swap.start()

    def vector_copy(level):
        return remote(v_sum.at[level], v_in.at[level], v_send.at[level], v_receive.at[level], levels[level])

    def vector_next(level):
        vector_copy(level).wait()
        if level + 1 < len(levels):
            v_sum[level + 1] = v_sum[level] + v_in[level]
            vector_copy(level + 1).start()

    v_sum[0] = vectors[...]
    vector_copy(0).start()

    def blocks(chain):
        return pl.ds(chain * CHAIN, CHAIN)

    def ring_copy(step, way, chain):
        rows = rows_of(step, way)
        return remote(
            mine.at[0, blocks(chain), rows, :], landing.at[blocks(chain), rows, :],
            ring_send.at[step, way, chain], ring_receive.at[step, way, chain], ways[way],
        )

    def incoming(step, way, chain):
        rows = rows_of(step + 1, way)
        return remote(
            mine.at[0, blocks(chain), rows, :], landing.at[blocks(chain), rows, :],
            ring_send.at[step, way, chain], ring_receive.at[step, way, chain], ways[way],
        )

    def own_total(chain, rows):
        part = (blocks(chain), rows, slice(None))
        both = [ref[(k, *part)].astype(F32) for ref in (mine, partner_part) for k in range(2)]
        return (both[0] + both[1]) + (both[2] + both[3])

    def total_of(chain, rows):
        return (own_total(chain, rows) + landing[blocks(chain), rows, :].astype(F32)).astype(BF16)

    def pair_here(step, way):
        for k in range(2):
            own_copy(step, way, k).wait()
            pair_copy(step, way, k).wait_recv()

    for way in range(2):
        pair_here(0, way)
        rows = rows_of(0, way)
        for chain in range(2):
            mine[0, blocks(chain), rows, :] = own_total(chain, rows).astype(BF16)
            ring_copy(0, way, chain).start()
    start_inputs(2)
    vector_next(0)

    def reduce_step(step, carry):
        for chain in range(2):
            for way in range(2):
                if chain == 0:
                    pair_here(step, way)
                incoming(step - 1, way, chain).wait_recv()
                rows = rows_of(step, way)
                mine[0, blocks(chain), rows, :] = total_of(chain, rows)
                ring_copy(step, way, chain).start()

        @pl.when(step + 2 < RING)
        def _():
            start_inputs(step + 2)

        return carry

    lax.fori_loop(1, RING - 1, reduce_step, 0)
    vector_next(1)

    def last_copy(step, way, chain, arriving=0):
        rows = rows_of(step + RING - 1 + arriving, way)
        return remote(
            final.at[blocks(chain), rows, :], final.at[blocks(chain), rows, :],
            last_send.at[step, way, chain], last_receive.at[step, way, chain], ways[way],
        )

    def out_copy(step, way, chain):
        part = (blocks(chain), rows_of(step + RING - 1, way), slice(None))
        return pltpu.make_async_copy(final.at[part], out.at[part], out_sem.at[step, way, chain])

    for chain in range(2):
        for way in range(2):
            if chain == 0:
                pair_here(RING - 1, way)
            incoming(RING - 2, way, chain).wait_recv()
            rows = rows_of(RING - 1, way)
            final[blocks(chain), rows, :] = total_of(chain, rows)
            last_copy(0, way, chain).start()
            out_copy(0, way, chain).start()
    vector_next(2)

    def gather_step(step, carry):
        for chain in range(2):
            for way in range(2):
                last_copy(step - 1, way, chain, 1).wait_recv()
                last_copy(step, way, chain).start()
                out_copy(step, way, chain).start()
        return carry

    lax.fori_loop(1, 3, gather_step, 0)
    vector_next(3)
    lax.fori_loop(3, 5, gather_step, 0)
    vector_next(4)
    out_vectors[0] = v_sum[len(levels) - 1]
    out_vectors[1] = v_in[len(levels) - 1]
    lax.fori_loop(5, RING - 1, gather_step, 0)

    def all_sent(step, carry):
        for way in range(2):
            for chain in range(2):
                ring_copy(step, way, chain).wait_send()
        return carry

    def pair_sent(step, carry):
        for way in range(2):
            for k in range(2):
                pair_copy(step, way, k).wait_send()
        return carry

    lax.fori_loop(0, RING - 1, all_sent, 0)
    lax.fori_loop(0, RING, pair_sent, 0)
    for swap in swaps:
        swap.wait()
    for chain in range(2):
        for way in range(2):
            last_copy(RING - 2, way, chain, 1).wait_recv()
            out_copy(RING - 1, way, chain).start()

    def last_sent(step, carry):
        for way in range(2):
            for chain in range(2):
                last_copy(step, way, chain).wait_send()
        return carry

    def written(step, carry):
        for way in range(2):
            for chain in range(2):
                out_copy(step, way, chain).wait()
        return carry

    lax.fori_loop(0, RING - 1, last_sent, 0)
    lax.fori_loop(0, RING, written, 0)


def reduce_grads(grads, swapping, vectors):
    share = (SHARE, D, D)
    dma = pltpu.SemaphoreType.DMA
    return pl.pallas_call(
        reduce_kernel,
        in_specs=[ANY, ANY, ANY, ANY, VMEM],
        out_specs=(ANY, ANY, ANY, VMEM),
        out_shape=(sds(share, BF16), ROWS, ROWS, sds((2, VECTORS, D), F32)),
        scratch_shapes=[
            pltpu.VMEM((2, *share), BF16),
            pltpu.VMEM((2, *share), BF16),
            pltpu.VMEM(share, BF16),
            pltpu.VMEM(share, BF16),
            pltpu.VMEM((5, VECTORS, D), F32),
            pltpu.VMEM((5, VECTORS, D), F32),
            dma((RING, 2, 2)),
            dma((RING, 2, 2)),
            dma((RING, 2, 2)),
            dma((RING, 2, 2)),
            dma((RING - 1, 2, 2)),
            dma((RING - 1, 2, 2)),
            dma((RING - 1, 2, 2)),
            dma((RING - 1, 2, 2)),
            dma((5,)),
            dma((5,)),
            dma((2,)),
            dma((2,)),
        ],
        compiler_params=params(56, collective_id=2, has_side_effects=True),
        name="reduce_grads",
    )(*grads, *swapping, vectors)


def spread_kernel(total, matrix, down, low, wide, low_sem, wide_sem):
    low_copies = [pltpu.make_async_copy(total.at[i], low.at[i], low_sem.at[i]) for i in range(SHARE)]
    for copy in low_copies:
        copy.start()
    copies = []
    for i in range(SHARE):
        low_copies[i].wait()
        wide[i] = low[i].astype(F32)
        target = matrix.at[0, :, columns(i)] if i < BLOCKS else down.at[columns(i - BLOCKS), :]
        copies.append(pltpu.make_async_copy(wide.at[i], target, wide_sem.at[i]))
        copies[i].start()
    for copy in copies:
        copy.wait()


def spread(total):
    return pl.pallas_call(
        spread_kernel,
        in_specs=[ANY],
        out_specs=(ANY, ANY),
        out_shape=(sds((1, D, FF), F32), sds((FF // 2, D), F32)),
        scratch_shapes=[
            pltpu.VMEM((SHARE, D, D), BF16),
            pltpu.VMEM((SHARE, D, D), F32),
            pltpu.SemaphoreType.DMA((SHARE,)),
            pltpu.SemaphoreType.DMA((SHARE,)),
        ],
        compiler_params=params(60),
        name="spread",
    )(total)


def plain_reduce_grads(grads, swapping, vectors):
    odd = lax.rem(lax.axis_index("section"), 2)
    pair = [(0, 1), (1, 0), (2, 3), (3, 2)]
    grads = grads[0] + grads[1]
    theirs = lax.dynamic_index_in_dim(grads, 1 - odd, 0, keepdims=False)
    mine = lax.dynamic_index_in_dim(grads, odd, 0, keepdims=False)
    total = lax.psum(mine + lax.ppermute(theirs, "section", pair), "dp")
    vectors = lax.psum(vectors + lax.ppermute(vectors, "section", pair), "dp")
    return total, *map(swap_layers, swapping), jnp.stack([vectors, swap_layers(vectors)])


def swap_layers(block):
    return lax.ppermute(block, "section", [(0, 2), (1, 3), (2, 0), (3, 1)])


def to_regressor(block):
    return lax.ppermute(block, "section", [(0, 2), (1, 3)])


def to_encoder(block):
    return lax.ppermute(block, "section", [(2, 0), (3, 1)])


def body(
    vis_embed, latent_cot, reg_queries, out_cot, section_matrix, down_weight, enc_vectors, reg_vectors,
    mlp_vectors, hidden_bias, pos_table, image_lengths, vis_index, mask_index,
):
    section = lax.axis_index("section")
    odd = lax.rem(section, 2)
    is_reg = section >= 2
    layer = jnp.where(is_reg, 1, 0)
    weights = gather_weights(section_matrix, down_weight)
    r = lax.dynamic_index_in_dim(mlp_vectors, layer, 0, keepdims=False)
    c = lax.dynamic_slice_in_dim(hidden_bias, layer, 1, 0)
    packs = [(odd + 2 * i).reshape(1).astype(jnp.int32) for i in range(2)]
    vis = [lax.dynamic_slice_in_dim(vis_index, (odd + 2 * i) * CAP, CAP)[:, None] for i in range(2)]
    mask = [lax.dynamic_slice_in_dim(mask_index, (odd + 2 * i) * CAP, CAP)[:, None] for i in range(2)]

    incoming = swap_layers(jnp.where(is_reg, vis_embed, reg_queries))
    x = [vis_embed, incoming]
    queries = [incoming, reg_queries]

    def on_encoder(work, otherwise):
        return lax.cond(is_reg, otherwise, work)

    def on_regressor(work, otherwise):
        return lax.cond(is_reg, work, otherwise)

    def enc_forward(i):
        return encoder_forward(image_lengths, packs[i], x[i], enc_vectors, r, c, weights)

    def no_enc_forward():
        made = unset((ROWS, ROWS, *ENC_STATE))
        return made[0], made[1], tuple(made[2:])

    def enc_back(i, d_latents, kept, so_far):
        return encoder_back(
            image_lengths, packs[i], lat_cot[i], d_latents, x[i], kept[0], enc_vectors, r, so_far, weights, kept[2]
        )

    def reg_before():
        return tuple(
            tuple(regressor_before(image_lengths, packs[i], queries[i], vis[i], mask[i], pos_table, reg_vectors, weights))
            for i in range(2)
        )

    def no_reg_before():
        made = unset((*REG_BEFORE, *REG_BEFORE))
        return tuple(made[: len(REG_BEFORE)]), tuple(made[len(REG_BEFORE) :])

    def reg_work(i, latents, so_far):
        return lambda: regressor(
            image_lengths, packs[i], latents, queries[i], cot[i], reg_vectors, r, c, so_far, weights, before[i]
        )

    def no_reg_work():
        made = unset((ROWS, ROWS, ROWS, TOTALS, *REG_STATE))
        return (*made[:4], tuple(made[4:]))

    none = jnp.zeros((VECTORS, D), F32)
    enc1 = on_encoder(lambda: enc_forward(0), no_enc_forward)
    latents1 = to_regressor(enc1[1])
    before = on_regressor(reg_before, no_reg_before)
    swapped_cot = swap_layers(jnp.where(is_reg, latent_cot, out_cot))
    lat_cot = [latent_cot, swapped_cot]
    cot = [swapped_cot, out_cot]
    enc2 = on_encoder(lambda: enc_forward(1), no_enc_forward)
    latents2 = to_regressor(enc2[1])
    reg1 = on_regressor(reg_work(0, latents1, none), no_reg_work)
    d_latents1 = to_encoder(reg1[1])
    reg2 = on_regressor(reg_work(1, latents2, reg1[3]), no_reg_work)
    d_latents2 = to_encoder(reg2[1])
    shares1, enc_totals, vis_grad1 = lax.cond(
        is_reg,
        lambda: (weight_grads(before[0], reg1[4]), *unset((TOTALS, ROWS))),
        lambda: enc_back(0, d_latents1, enc1, none)[::-1],
    )
    shares2, vectors, swapping = lax.cond(
        is_reg,
        lambda: (weight_grads(before[1], reg2[4]), reg2[3], reg1[0]),
        lambda: enc_back(1, d_latents2, enc2, enc_totals)[::-1],
    )
    reduce = reduce_grads if lax.axis_size("dp") == RING else plain_reduce_grads
    total, swapped1, swapped2, vectors = reduce((shares1, shares2), (swapping, reg1[2]), vectors)
    matrix_grad, down_grad = spread(total)

    def pick(reg, enc):
        return jnp.where(is_reg, reg, enc)

    latents = pick(latents2, enc1[1])
    regressed = pick(reg2[0], swapped1)
    vis_grad = pick(swapped1, vis_grad1)
    query_grad = pick(reg2[2], swapped2)
    enc_total, reg_total = pick(vectors[1], vectors[0]), pick(vectors[0], vectors[1])
    return (
        latents,
        regressed,
        vis_grad,
        query_grad,
        matrix_grad,
        down_grad,
        enc_total[:6],
        reg_total[:10],
        jnp.stack([enc_total[FFN_AT:HIDDEN_AT], reg_total[FFN_AT:HIDDEN_AT]]),
        jnp.stack([t[HIDDEN_AT : HIDDEN_AT + BLOCKS].reshape(FF) for t in (enc_total, reg_total)]),
    )


def solution(mesh):
    rows = P(("dp", "section"), None)
    in_specs = (
        rows, rows, rows, rows, P("section", None, None), P("section", None),
        P(), P(), P(), P(), P(), P("dp", None), P("dp"), P("dp"),
    )
    out_specs = (rows, rows, rows, rows, P("section", None, None), P("section", None), P(), P(), P(), P())
    return jax.shard_map(body, mesh=mesh, in_specs=in_specs, out_specs=out_specs, check_vma=False)
```

```python
import functools

import jax
import jax.numpy as jnp
from jax import lax
from jax.experimental import pallas as pl
from jax.experimental.pallas import tpu as pltpu
from jax.sharding import PartitionSpec as P

F32 = jnp.float32
BF16 = jnp.bfloat16
CAP = 384
IMGS = 4
SLOT = 128
PAD = IMGS * SLOT
D = 768
FF = 3072
LANES = 128
PAIRS = D // LANES
BLOCKS = FF // D
VECTORS = 24
EPS = 1e-06
MIB = 1 << 20
ANY = pl.BlockSpec(memory_space=pl.ANY)
SMEM = pl.BlockSpec(memory_space=pltpu.SMEM)


def params(limit=48, **more):
    return pltpu.CompilerParams(vmem_limit_bytes=limit * MIB, **more)


def sds(shape, dtype):
    return jax.ShapeDtypeStruct(shape, dtype)


def dot(a, b):
    return jnp.dot(a, b, preferred_element_type=F32)


def dot_nt(a, b):
    return lax.dot_general(a, b, (((1,), (1,)), ((), ())), preferred_element_type=F32)


def dot_tn(a, b):
    return lax.dot_general(a, b, (((0,), (0,)), ((), ())), preferred_element_type=F32)


def row(ref, i):
    return ref[i : i + 1, :]


def colsum(values):
    return jnp.sum(values, axis=0, keepdims=True)


def normalize(values):
    centred = values - jnp.mean(values, axis=-1, keepdims=True)
    spread = jnp.mean(centred * centred, axis=-1, keepdims=True)
    inverse = lax.rsqrt(spread + EPS)
    return centred * inverse, inverse


def norm_back(gradient, gain, normed, inverse):
    return scaled_norm_back(gradient * gain, normed, inverse)


def scaled_norm_back(scaled, normed, inverse):
    level = jnp.mean(scaled, axis=-1, keepdims=True)
    slope = jnp.mean(scaled * normed, axis=-1, keepdims=True)
    return inverse * (scaled - level - normed * slope)


def gelu_parts(t):
    e = jnp.exp(-0.5 * t * t)
    k = 1.0 / (1.0 + (0.3275911 * 0.7071067811865476) * jnp.abs(t))
    poly = k * (
        0.127414796
        + k * (-0.142248368 + k * (0.7107068705 + k * (-0.7265760135 + k * 0.5307027145)))
    )
    tail = poly * e
    phi = jnp.where(t >= 0.0, 1.0 - tail, tail)
    return t * phi, phi + t * (e * 0.3989422804014327)


def group_matrices(lens, pack, regroup, ungroup):
    def image(j, start):
        size = lens[pack, j]
        slots = pl.ds(pl.multiple_of(j * SLOT, SLOT), SLOT)
        place = lax.broadcasted_iota(jnp.int32, (SLOT, CAP), 0)
        rows = lax.broadcasted_iota(jnp.int32, (SLOT, CAP), 1)
        hit = (place + start == rows) & (place < size)
        regroup[slots, :] = jnp.where(hit, 1.0, 0.0).astype(BF16)
        place = lax.broadcasted_iota(jnp.int32, (CAP, SLOT), 1)
        rows = lax.broadcasted_iota(jnp.int32, (CAP, SLOT), 0)
        hit = (place + start == rows) & (place < size)
        ungroup[:, slots] = jnp.where(hit, 1.0, 0.0).astype(BF16)
        return start + size

    lax.fori_loop(0, IMGS, image, jnp.int32(0))


def lane_halves():
    lane = lax.broadcasted_iota(jnp.int32, (1, LANES), 1)
    first = jnp.where(lane < LANES // 2, 1.0, 0.0)
    return first.astype(BF16), (1.0 - first).astype(BF16)


def both_heads(block, halves):
    return jnp.concatenate([block * halves[0], block * halves[1]], axis=0)


def merge_heads(stacked):
    keys = stacked.shape[0] // 2
    lane = lax.broadcasted_iota(jnp.int32, (keys, LANES), 1)
    return jnp.where(lane < LANES // 2, stacked[:keys], stacked[keys:])


def softmax(scores):
    raised = jnp.exp(scores - jnp.max(scores, axis=0, keepdims=True))
    return (raised * (1.0 / jnp.sum(raised, axis=0, keepdims=True))).astype(BF16)


def keys_of(packed, first, parts, rows, cols, halves):
    return both_heads(
        jnp.concatenate([packed[first + 2 * m, rows, cols] for m in range(parts)], axis=0), halves
    )


def attend(lens, pack, packed, probs, mixed_slots, parts, done):
    halves = lane_halves()
    keys = SLOT * parts
    place = lax.bitwise_and(lax.broadcasted_iota(jnp.int32, (keys, SLOT), 0), SLOT - 1)
    for j in range(IMGS):
        rows = slice(j * SLOT, (j + 1) * SLOT)
        valid = place < lens[pack, j]
        for g in range(PAIRS):
            cols = slice(g * LANES, (g + 1) * LANES)
            scores = dot_nt(keys_of(packed, 1, parts, rows, cols, halves), packed[0, rows, cols])
            low = jnp.concatenate(
                [softmax(jnp.where(valid, part, -1e30)) for part in (scores[:keys], scores[keys:])], axis=0
            )
            probs[j, g] = low
            mixed_slots[rows, cols] = dot_tn(low, keys_of(packed, 2, parts, rows, cols, halves)).astype(BF16)
        done(j)


def attend_back(packed, probs, mixed_slots, d_mixed_slots, parts, ready, beside):
    halves = lane_halves()
    keys = SLOT * parts
    less = both_heads(jnp.full((keys, LANES), -1.0, BF16), halves)

    def image(j, carry):
        ready(j)
        rows = pl.ds(pl.multiple_of(j * SLOT, SLOT), SLOT)
        after = beside(j)
        for g in range(PAIRS):
            cols = slice(g * LANES, (g + 1) * LANES)
            d_out = d_mixed_slots[rows, cols]
            centre = (d_out.astype(F32) * mixed_slots[rows, cols].astype(F32)).astype(BF16)
            low = probs[j, g]
            d_prob = dot_nt(
                jnp.concatenate([keys_of(packed, 2, parts, rows, cols, halves), less], axis=1),
                jnp.concatenate([d_out, centre], axis=1),
            )
            d_scores = (low.astype(F32) * d_prob).astype(BF16)
            q = packed[0, rows, cols]
            zero = jnp.zeros_like(q)
            sides = jnp.concatenate(
                [jnp.concatenate([q, zero], axis=1), jnp.concatenate([zero, d_out], axis=1)], axis=0
            )
            d_kv = dot(jnp.concatenate([d_scores, low], axis=1), sides)
            d_q = dot_tn(d_scores, keys_of(packed, 1, parts, rows, cols, halves)) * 0.125
            packed[0, rows, cols] = d_q.astype(BF16)
            for side in range(2):
                merged = merge_heads(d_kv[:, side * LANES : (side + 1) * LANES]).astype(BF16)
                for m in range(parts):
                    packed[1 + side + 2 * m, rows, cols] = merged[m * SLOT : (m + 1) * SLOT]
        if after is not None:
            after()
        return carry

    lax.fori_loop(0, IMGS, image, 0)


ROWS = sds((CAP, D), BF16)
WIDE = sds((CAP, FF), BF16)
TOTALS = sds((VECTORS, D), F32)
FFN_AT = 10
HIDDEN_AT = FFN_AT + 4
ENC_STATE = (
    ROWS,
    sds((3, PAD, D), BF16),
    sds((IMGS, PAIRS, 2 * SLOT, SLOT), BF16),
    sds((PAD, D), BF16),
    ROWS,
    ROWS,
    ROWS,
    WIDE,
    WIDE,
    ROWS,
)
REG_BEFORE = (
    sds((3, CAP, D), BF16),
    sds((3, PAD, D), BF16),
    sds((2, CAP, D), F32),
)
REG_STATE = (
    sds((2, CAP, D), BF16),
    sds((5, CAP, D), BF16),
    ROWS,
    ROWS,
    ROWS,
    WIDE,
    WIDE,
    ROWS,
)


def full(shape):
    return pl.BlockSpec(shape, lambda i: (0,) * len(shape))


VMEM = pl.BlockSpec(memory_space=pltpu.VMEM)


def scratch(shape):
    return pltpu.VMEM(shape.shape, shape.dtype)


def unset(shapes):
    def kernel(*refs):
        del refs

    return pl.pallas_call(
        kernel, out_shape=shapes, out_specs=tuple(ANY for _ in shapes), name="unset"
    )()


class Copies:
    def __init__(self, semaphores):
        self.semaphores, self.used, self.open = semaphores, 0, []

    def take(self, count=1):
        self.used += count
        return self.used - count

    def start(self, source, target):
        copy = pltpu.make_async_copy(source, target, self.semaphores.at[self.take()])
        copy.start()
        return copy

    def leave(self, source, target):
        self.open.append(self.start(source, target))

    def halves(self, *pairs):
        first = self.take(2 * len(pairs))

        def copies(i):
            rows = half_rows(i)
            return [
                pltpu.make_async_copy(source.at[rows, :], target.at[rows, :], self.semaphores.at[first + 2 * k + i])
                for k, (source, target) in enumerate(pairs)
            ]

        def start(i):
            for copy in copies(i):
                copy.start()

        self.open += copies(0) + copies(1)
        return start

    def finish(self):
        for copy in self.open:
            copy.wait()


COPIES = pltpu.SemaphoreType.DMA((80,))


def columns(i):
    return slice(i * D, (i + 1) * D)


class Weights:
    def __init__(self, copies, weights, held):
        self.copies, self.weights, self.held, self.started = copies, weights, held, {}

    def target(self, i):
        kind, block = divmod(i, BLOCKS)
        held = self.held[kind]
        return held.at[columns(block), :] if kind == 2 else held.at[:, columns(block)]

    def start(self, *order):
        for i in order:
            self.started[i] = self.copies.start(self.weights.at[i], self.target(i))

    def wait(self, *which):
        for i in which:
            self.started[i].wait()


WEIGHT_SCRATCH = [pltpu.VMEM((D, FF), BF16), pltpu.VMEM((D, FF), BF16), pltpu.VMEM((FF, D), BF16)]
ALL_BLOCKS = range(BLOCKS)
UPS = [BLOCKS + i for i in ALL_BLOCKS]
DOWNS = [2 * BLOCKS + i for i in ALL_BLOCKS]


def wide(i):
    return pl.ds(pl.multiple_of(i * D, D), D)


HALF = CAP // 2


def half_rows(i):
    return pl.ds(pl.multiple_of(i * HALF, HALF), HALF)


def feed_forward(weights, mid, r, c, out, state, made):
    normed, active, slope, branch = state
    centred, _ = normalize(mid[...].astype(F32))
    normed[...] = (centred * row(r, 0) + row(r, 1)).astype(BF16)
    made("normed")
    _, up, down = weights.held
    weights.wait(*UPS, *DOWNS)

    def part(i, carry):
        rows = half_rows(i)
        value, steep = gelu_parts(dot(normed[rows, :], up[...]) + c[...])
        active[rows, :] = value.astype(BF16)
        slope[rows, :] = steep.astype(BF16)
        made(i)
        summed = dot(active[rows, :], down[...]) + row(r, 2)
        branch[rows, :] = summed.astype(BF16)
        out[rows, :] = (mid[rows, :].astype(F32) + row(r, 3) * summed).astype(BF16)
        return carry

    lax.fori_loop(0, 2, part, 0)
    made("branch")


def feed_forward_back(weights, ready, g, mid, r, refs, totals, residual, made):
    slope, branch, d_branch = refs
    _, up, down = weights.held
    d_branch[...] = (g * row(r, 3)).astype(BF16)
    made("branch")
    add_row(totals, FFN_AT + 2, colsum(d_branch[...].astype(F32)))
    ready("branch")
    add_row(totals, FFN_AT + 3, colsum(g * branch[...].astype(F32)))
    for i in ALL_BLOCKS:
        weights.wait(2 * BLOCKS + i)
        ready(i)
        d_active = dot_nt(d_branch[...], down[columns(i), :])
        d_hidden = (d_active * slope[:, columns(i)].astype(F32)).astype(BF16)
        slope[:, columns(i)] = d_hidden
        made(i)
        add_row(totals, HIDDEN_AT + i, colsum(d_hidden.astype(F32)))
    weights.wait(*UPS)
    d_normed = dot_nt(slope[...], up[...])
    normed, inverse = normalize(mid[...].astype(F32))
    add_row(totals, FFN_AT, colsum(d_normed * normed))
    add_row(totals, FFN_AT + 1, colsum(d_normed))
    residual[...] = (g + norm_back(d_normed, row(r, 0), normed, inverse)).astype(BF16).astype(F32)


def attention_back(parts, weights, e, refs, totals, ready, made, beside):
    residual, branch, d_branch, regroup, ungroup, packed, probs, mixed_slots, d_slots, d_flat = refs
    last = 1 + 4 * parts
    g = residual[...]
    ready("branch")
    d_branch[...] = (g * row(e, last)).astype(BF16)
    made("branch")
    add_row(totals, last, colsum(g * branch[...].astype(F32)))
    add_row(totals, last - 1, colsum(d_branch[...].astype(F32)))
    weights.wait(3)
    d_mixed = dot(d_branch[...], weights.held[0][:, columns(3)]).astype(BF16)
    d_slots[...] = dot(regroup[...], d_mixed).astype(BF16)
    ready("packed")
    attend_back(packed, probs, mixed_slots, d_slots, parts, ready, beside)
    for m in range(1 + 2 * parts):
        d_flat[m] = dot(ungroup[...], packed[m]).astype(BF16)
        made(m)


def add_row(totals, i, value):
    totals[i : i + 1] += value


def nothing(name):
    del name


class Shares:
    def __init__(self, copies, blocks, share):
        self.semaphores, self.blocks, self.share = copies.semaphores, blocks, share
        self.first = copies.take(3 * BLOCKS)

    def copy(self, kind, i):
        section, block = (lax.div(i, 2), BLOCKS + lax.rem(i, 2)) if kind == 2 else (kind, i)
        place = kind * BLOCKS + i
        return pltpu.make_async_copy(
            self.blocks.at[place], self.share.at[section, block], self.semaphores.at[self.first + place]
        )

    def put(self, kind, i, product):
        self.blocks[kind * BLOCKS + i] = product.astype(BF16)
        self.copy(kind, i).start()

    def feed_forward(self, normed, d_hidden, active, d_branch):
        def step(i):
            self.blocks[BLOCKS + i] = dot_tn(normed[...], d_hidden[:, wide(i)]).astype(BF16)
            self.blocks[2 * BLOCKS + i] = dot_tn(active[:, wide(i)], d_branch[...]).astype(BF16)

            def after():
                for kind in (1, 2):
                    self.copy(kind, i).start()

            return after

        return step

    def finish(self):
        for kind in range(3):
            for i in ALL_BLOCKS:
                self.copy(kind, i).wait()


def encoder_forward_kernel(lens, which, x, e, r, c, given, mid, out, *refs):
    kept, scratch = refs[: len(ENC_STATE)], refs[len(ENC_STATE) :]
    *held, flat, regroup, ungroup, semaphores = scratch[: 3 + 4]
    state = scratch[3 + 4 :]
    normed, packed, probs, mixed_slots, mixed, branch, *ffn = state
    pack = which[0]
    copies = Copies(semaphores)
    weights = Weights(copies, given, held)
    weights.start(*ALL_BLOCKS, *UPS, *DOWNS)
    values = x[...].astype(F32)
    centred, _ = normalize(values)
    normed[...] = (centred * row(e, 0) + row(e, 1)).astype(BF16)
    copies.leave(normed, kept[0])
    group_matrices(lens, pack, regroup, ungroup)
    qkvo = weights.held[0]
    weights.wait(0)
    flat[0] = ((dot(normed[...], qkvo[:, columns(0)]) + row(e, 2)).astype(BF16) * 0.125).astype(BF16)
    weights.wait(1)
    flat[1] = dot(normed[...], qkvo[:, columns(1)]).astype(BF16)
    weights.wait(2)
    flat[2] = (dot(normed[...], qkvo[:, columns(2)]) + row(e, 3)).astype(BF16)
    for m in range(3):
        packed[m] = dot(regroup[...], flat[m]).astype(BF16)
        copies.leave(packed.at[m], kept[1].at[m])
    attend(lens, pack, packed, probs, mixed_slots, 1, lambda j: copies.leave(probs.at[j], kept[2].at[j]))
    copies.leave(mixed_slots, kept[3])
    mixed[...] = dot(ungroup[...], mixed_slots[...]).astype(BF16)
    copies.leave(mixed, kept[4])
    weights.wait(3)
    summed = dot_nt(mixed[...], qkvo[:, columns(3)]) + row(e, 4)
    branch[...] = summed.astype(BF16)
    copies.leave(branch, kept[5])
    mid[...] = (values + row(e, 5) * summed).astype(BF16)

    half_made = copies.halves((ffn[1], kept[7]), (ffn[2], kept[8]))

    def made(name):
        if isinstance(name, str):
            source, target = (ffn[0], kept[6]) if name == "normed" else (ffn[3], kept[9])
            copies.leave(source, target)
        else:
            half_made(name)

    feed_forward(weights, mid, r, c, out, ffn, made)
    copies.finish()


def encoder_forward(lens, which, x, e, r, c, weights):
    made = pl.pallas_call(
        encoder_forward_kernel,
        in_specs=[SMEM, SMEM, VMEM, VMEM, VMEM, VMEM, ANY],
        out_specs=(VMEM, VMEM, *(ANY for _ in ENC_STATE)),
        out_shape=(ROWS, ROWS, *ENC_STATE),
        scratch_shapes=[
            *WEIGHT_SCRATCH,
            pltpu.VMEM((3, CAP, D), BF16),
            pltpu.VMEM((PAD, CAP), BF16),
            pltpu.VMEM((CAP, PAD), BF16),
            COPIES,
            *map(scratch, ENC_STATE),
        ],
        compiler_params=params(58),
        name="encoder_forward",
    )(lens, which, x, e, r, c, weights)
    return made[0], made[1], tuple(made[2:])


def encoder_back_kernel(lens, which, g1, g2, x, mid, e, r, so_far, given, *refs):
    state, refs = refs[: len(ENC_STATE)], refs[len(ENC_STATE) :]
    d_x, totals, share, *held, regroup, ungroup, d_slots, d_branch, d_f_branch, d_flat, residual, blocks, semaphores = (
        refs[: 3 + 3 + 9]
    )
    normed, packed, probs, mixed_slots, mixed, branch, f_normed, active, slope, f_branch = refs[3 + 3 + 9 :]
    copies = Copies(semaphores)
    weights = Weights(copies, given, held)
    coming = {"branch": copies.start(state[9], f_branch)}
    for i in ALL_BLOCKS:
        weights.start(2 * BLOCKS + i)
        coming[i] = copies.start(state[8].at[:, columns(i)], slope.at[:, columns(i)])
    weights.start(*UPS, 3)
    later = {"branch": copies.start(state[5], branch)}
    later["packed"] = copies.start(state[1], packed)
    later["mixed"] = copies.start(state[3], mixed_slots)
    probs_in = [copies.start(state[2].at[j], probs.at[j]) for j in range(IMGS)]
    late = [copies.start(state[i], ref) for i, ref in ((6, f_normed), (7, active), (0, normed), (4, mixed))]
    weights.start(0, 1, 2)
    shares = Shares(copies, blocks, share)
    totals[...] = so_far[...]
    group_matrices(lens, which[0], regroup, ungroup)
    g = g1[...].astype(F32) + g2[...].astype(F32)
    feed_forward_back(
        weights, lambda name: coming[name].wait(), g, mid, r, (slope, f_branch, d_f_branch), totals, residual, nothing
    )
    for copy in late:
        copy.wait()

    def ready(name):
        if name == "branch":
            later["branch"].wait()
        elif name == "packed":
            later["packed"].wait()
            later["mixed"].wait()
            for copy in probs_in:
                copy.wait()

    attention_back(
        1, weights, e, (residual, branch, d_branch, regroup, ungroup, packed, probs, mixed_slots, d_slots, d_flat),
        totals, ready, nothing, shares.feed_forward(f_normed, slope, active, d_f_branch),
    )

    def first_block(i, carry):
        shares.put(0, i, dot_tn(normed[...], d_flat[i]))
        return carry

    lax.fori_loop(0, 3, first_block, 0)
    shares.put(0, 3, dot_tn(d_branch[...], mixed[...]))
    weights.wait(0, 1, 2)
    qkvo = weights.held[0]
    d_normed = dot_nt(d_flat[0], qkvo[:, columns(0)])
    for m in (1, 2):
        d_normed += dot_nt(d_flat[m], qkvo[:, columns(m)])
    values, inverse = normalize(x[...].astype(F32))
    add_row(totals, 0, colsum(d_normed * values))
    add_row(totals, 1, colsum(d_normed))
    add_row(totals, 2, colsum(d_flat[0].astype(F32)))
    add_row(totals, 3, colsum(d_flat[2].astype(F32)))
    d_x[...] = (residual[...] + norm_back(d_normed, row(e, 0), values, inverse)).astype(BF16)
    shares.finish()


def encoder_back(lens, which, g1, g2, x, mid, e, r, so_far, weights, state):
    return pl.pallas_call(
        encoder_back_kernel,
        in_specs=[SMEM, SMEM, *(VMEM for _ in range(7)), ANY, *(ANY for _ in ENC_STATE)],
        out_specs=(VMEM, VMEM, ANY),
        out_shape=(ROWS, TOTALS, sds((2, SHARE, D, D), BF16)),
        scratch_shapes=[
            *WEIGHT_SCRATCH,
            pltpu.VMEM((PAD, CAP), BF16),
            pltpu.VMEM((CAP, PAD), BF16),
            pltpu.VMEM((PAD, D), BF16),
            scratch(ROWS),
            scratch(ROWS),
            pltpu.VMEM((3, CAP, D), BF16),
            pltpu.VMEM((CAP, D), F32),
            pltpu.VMEM((3 * BLOCKS, D, D), BF16),
            COPIES,
            *map(scratch, ENC_STATE),
        ],
        compiler_params=params(58),
        name="encoder_back",
    )(lens, which, g1, g2, x, mid, e, r, so_far, weights, *state)


def table_rows(indices, table):
    places = lax.broadcasted_iota(jnp.int32, (indices.shape[0], table.shape[0]), 1)
    chosen = jnp.where(places == indices[...], 1.0, 0.0).astype(BF16)
    values = table[...]
    top = values.astype(BF16)
    values = values - top.astype(F32)
    middle = values.astype(BF16)
    bottom = (values - middle.astype(F32)).astype(BF16)
    return (dot(chosen, top) + dot(chosen, middle)) + dot(chosen, bottom)


def regressor_before_kernel(lens, which, queries, vis, mask, table, e, given, normed, packed, sources, held, flat, regroup, ungroup, semaphores):
    copies = Copies(semaphores)
    weights = Weights(copies, given, [held])
    weights.start(0, 1, 2)
    group_matrices(lens, which[0], regroup, ungroup)
    sources[1] = table_rows(vis, table)
    residual = queries[...].astype(F32)
    source = residual + table_rows(mask, table)
    sources[0] = source
    centred, _ = normalize(source)
    normed[0] = (centred * row(e, 0) + row(e, 1)).astype(BF16)
    normed[1] = (centred * row(e, 2) + row(e, 3)).astype(BF16)
    centred, _ = normalize(residual)
    normed[2] = (centred * row(e, 4) + row(e, 5)).astype(BF16)
    weights.wait(0, 1, 2)
    flat[0] = ((dot(normed[0], held[:, columns(0)]) + row(e, 6)).astype(BF16) * 0.125).astype(BF16)
    flat[1] = dot(normed[1], held[:, columns(1)]).astype(BF16)
    flat[2] = (dot(normed[2], held[:, columns(2)]) + row(e, 7)).astype(BF16)
    for m in range(3):
        packed[m] = dot(regroup[...], flat[m]).astype(BF16)


def regressor_before(lens, which, queries, vis, mask, table, e, weights):
    return pl.pallas_call(
        regressor_before_kernel,
        in_specs=[SMEM, SMEM, *(VMEM for _ in range(5)), ANY],
        out_specs=(VMEM, VMEM, VMEM),
        out_shape=REG_BEFORE,
        scratch_shapes=[
            pltpu.VMEM((D, FF), BF16),
            pltpu.VMEM((3, CAP, D), BF16),
            pltpu.VMEM((PAD, CAP), BF16),
            pltpu.VMEM((CAP, PAD), BF16),
            COPIES,
        ],
        compiler_params=params(48),
        name="regressor_before",
    )(lens, which, queries, vis, mask, table, e, weights)


def regressor_kernel(
    lens, which, latents, queries, cot, e, r, c, so_far, given, packed_before, sources_before,
    regressed, d_latents, d_queries, totals, *refs,
):
    kept, refs = refs[: len(REG_STATE)], refs[len(REG_STATE) :]
    (
        *held, regroup, ungroup, packed, probs, mixed_slots, d_slots, sources, branch, slope, f_branch, mid, residual,
        flat, semaphores, normed, d_flat, mixed, d_branch, f_normed, _, active, d_f_branch,
    ) = refs
    pack = which[0]
    copies = Copies(semaphores)
    weights = Weights(copies, given, held)
    in_sources = copies.start(sources_before, sources)
    weights.start(1, 2)
    in_packed = [copies.start(packed_before.at[i], packed.at[m]) for i, m in enumerate((0, 3, 4))]
    weights.start(3, *UPS, *DOWNS, 0)
    qkvo = weights.held[0]
    group_matrices(lens, pack, regroup, ungroup)
    incoming = latents[...].astype(F32)
    centred, _ = normalize(incoming)
    normed[1] = (centred * row(e, 4) + row(e, 5)).astype(BF16)
    in_sources.wait()
    k_source = incoming + sources[1]
    sources[1] = k_source
    centred, _ = normalize(k_source)
    normed[0] = (centred * row(e, 2) + row(e, 3)).astype(BF16)
    copies.leave(normed, kept[0])
    weights.wait(1)
    flat[0] = dot(normed[0], qkvo[:, columns(1)]).astype(BF16)
    weights.wait(2)
    flat[1] = (dot(normed[1], qkvo[:, columns(2)]) + row(e, 7)).astype(BF16)
    for m in range(2):
        packed[1 + m] = dot(regroup[...], flat[m]).astype(BF16)
    for copy in in_packed:
        copy.wait()
    attend(lens, pack, packed, probs, mixed_slots, 2, nothing)
    mixed[...] = dot(ungroup[...], mixed_slots[...]).astype(BF16)
    copies.leave(mixed, kept[2])
    weights.wait(3)
    summed = dot_nt(mixed[...], qkvo[:, columns(3)]) + row(e, 8)
    branch[...] = summed.astype(BF16)
    mid[...] = (queries[...].astype(F32) + row(e, 9) * summed).astype(BF16)

    half_made = copies.halves((active, kept[6]))

    def forward_made(name):
        if not isinstance(name, str):
            half_made(name)
        elif name == "normed":
            copies.leave(f_normed, kept[4])

    feed_forward(weights, mid, r, c, regressed, (f_normed, active, slope, f_branch), forward_made)

    totals[...] = so_far[...]
    waited = Weights(copies, given, held)
    waited.wait = nothing_more

    def back_made(name):
        if name == "branch":
            copies.leave(d_f_branch, kept[7])
        else:
            copies.leave(slope.at[:, columns(name)], kept[5].at[:, columns(name)])

    feed_forward_back(
        waited, nothing, cot[...].astype(F32), mid, r, (slope, f_branch, d_f_branch), totals, residual, back_made
    )

    def attention_made(name):
        if name == "branch":
            copies.leave(d_branch, kept[3])
        else:
            copies.leave(d_flat.at[name], kept[1].at[name])

    attention_back(
        2, waited, e, (residual, branch, d_branch, regroup, ungroup, packed, probs, mixed_slots, d_slots, d_flat),
        totals, nothing, attention_made, nothing,
    )
    weights.wait(0)
    add_row(totals, 6, colsum(d_flat[0].astype(F32)))
    add_row(totals, 7, colsum(d_flat[2].astype(F32)) + colsum(d_flat[4].astype(F32)))
    values, inverse = normalize(sources[0])
    grad = dot_nt(d_flat[0], qkvo[:, columns(0)])
    add_row(totals, 0, colsum(grad * values))
    add_row(totals, 1, colsum(grad))
    scaled = grad * row(e, 0)
    grad = dot_nt(d_flat[3], qkvo[:, columns(1)])
    k_gain = colsum(grad * values)
    k_offset = colsum(grad)
    scaled += grad * row(e, 2)
    total = residual[...] + scaled_norm_back(scaled, values, inverse)
    values, inverse = normalize(queries[...].astype(F32))
    grad = dot_nt(d_flat[4], qkvo[:, columns(2)])
    v_gain = colsum(grad * values)
    v_offset = colsum(grad)
    total += norm_back(grad, row(e, 4), values, inverse)
    d_queries[...] = total.astype(BF16)
    values, inverse = normalize(sources[1])
    grad = dot_nt(d_flat[1], qkvo[:, columns(1)])
    add_row(totals, 2, k_gain + colsum(grad * values))
    add_row(totals, 3, k_offset + colsum(grad))
    total = norm_back(grad, row(e, 2), values, inverse)
    values, inverse = normalize(latents[...].astype(F32))
    grad = dot_nt(d_flat[2], qkvo[:, columns(2)])
    add_row(totals, 4, v_gain + colsum(grad * values))
    add_row(totals, 5, v_offset + colsum(grad))
    total += norm_back(grad, row(e, 4), values, inverse)
    d_latents[...] = total.astype(BF16)
    copies.finish()


def nothing_more(*which):
    del which


def regressor(lens, which, latents, queries, cot, e, r, c, so_far, weights, before):
    made = pl.pallas_call(
        regressor_kernel,
        in_specs=[SMEM, SMEM, *(VMEM for _ in range(7)), ANY, ANY, ANY],
        out_specs=(VMEM, VMEM, VMEM, VMEM, *(ANY for _ in REG_STATE)),
        out_shape=(ROWS, ROWS, ROWS, TOTALS, *REG_STATE),
        scratch_shapes=[
            *WEIGHT_SCRATCH,
            pltpu.VMEM((PAD, CAP), BF16),
            pltpu.VMEM((CAP, PAD), BF16),
            pltpu.VMEM((5, PAD, D), BF16),
            pltpu.VMEM((IMGS, PAIRS, 4 * SLOT, SLOT), BF16),
            pltpu.VMEM((PAD, D), BF16),
            pltpu.VMEM((PAD, D), BF16),
            pltpu.VMEM((2, CAP, D), F32),
            scratch(ROWS),
            scratch(WIDE),
            scratch(ROWS),
            scratch(ROWS),
            pltpu.VMEM((CAP, D), F32),
            pltpu.VMEM((2, CAP, D), BF16),
            COPIES,
            *(scratch(s) if i != 5 else pltpu.VMEM((8, LANES), BF16) for i, s in enumerate(REG_STATE)),
        ],
        compiler_params=params(60),
        name="regressor",
    )(lens, which, latents, queries, cot, e, r, c, so_far, weights, before[1], before[2])
    return (*made[:4], tuple(made[4:]))


SHARE = BLOCKS + BLOCKS // 2


def weight_grads_kernel(*refs):
    sources, share, held, blocks, semaphores = refs[:9], refs[9], refs[10:19], refs[19], refs[20]
    copies = Copies(semaphores)
    order = (5, 6, 7, 8, 0, 1, 2, 3, 4)
    started = {i: copies.start(sources[i], held[i]) for i in order}
    before, normed, d_flat, mixed, d_branch, f_normed, d_hidden, active, d_f_branch = held
    shares = Shares(copies, blocks, share)
    for i in order[:4]:
        started[i].wait()
    work = shares.feed_forward(f_normed, d_hidden, active, d_f_branch)

    def ffn_blocks(i, carry):
        work(i)()
        return carry

    lax.fori_loop(0, BLOCKS, ffn_blocks, 0)
    for i in order[4:]:
        started[i].wait()
    shares.put(0, 0, dot_tn(before[0], d_flat[0]))

    def pair_block(i, carry):
        shares.put(0, i, dot_tn(normed[i - 1], d_flat[i]) + dot_tn(before[i], d_flat[i + 2]))
        return carry

    lax.fori_loop(1, 3, pair_block, 0)
    shares.put(0, 3, dot_tn(d_branch[...], mixed[...]))
    shares.finish()


def weight_grads(before, state):
    return pl.pallas_call(
        weight_grads_kernel,
        in_specs=[ANY] * 9,
        out_specs=ANY,
        out_shape=sds((2, SHARE, D, D), BF16),
        scratch_shapes=[
            scratch(REG_BEFORE[0]),
            *map(scratch, REG_STATE),
            pltpu.VMEM((3 * BLOCKS, D, D), BF16),
            COPIES,
        ],
        compiler_params=params(),
        name="weight_grads",
    )(before[0], *state)


MESH = pl.DeviceIdType.MESH


def gather_weights_kernel(matrix, down, weights, send, receive, local):
    dp, section = lax.axis_index("dp"), lax.axis_index("section")
    odd = lax.rem(section, 2)
    partner = (dp, section + 1 - 2 * odd)
    barrier = pltpu.get_barrier_semaphore()
    pl.semaphore_signal(barrier, inc=1, device_id=partner, device_id_type=MESH)
    pl.semaphore_wait(barrier, 1)
    places = [(matrix.at[0, :, pl.ds(i * D, D)], odd * BLOCKS + i) for i in range(BLOCKS)]
    places += [(down.at[pl.ds(i * D, D), :], 2 * BLOCKS + odd * (BLOCKS // 2) + i) for i in range(BLOCKS // 2)]
    copies = []
    for i, (source, place) in enumerate(places):
        away = pltpu.make_async_remote_copy(
            source, weights.at[place], send.at[i], receive.at[i], device_id=partner, device_id_type=MESH
        )
        away.start()
        here = pltpu.make_async_copy(source, weights.at[place], local.at[i])
        here.start()
        copies += [away, here]
    for copy in copies:
        copy.wait()


def gather_weights(matrix, down):
    vmem = pl.BlockSpec(memory_space=pltpu.VMEM)
    return pl.pallas_call(
        gather_weights_kernel,
        in_specs=[vmem, vmem],
        out_specs=ANY,
        out_shape=sds((3 * BLOCKS, D, D), matrix.dtype),
        scratch_shapes=[pltpu.SemaphoreType.DMA((SHARE,)) for _ in range(3)],
        compiler_params=params(collective_id=1, has_side_effects=True),
        name="gather_weights",
    )(matrix, down)


RING = 8
SEGMENT = D // RING
PART = SEGMENT // 2
CHAIN = SHARE // 2


def ring_place(d):
    odd = lax.rem(d, 2)
    return (1 - odd) * lax.div(d, 2) + odd * (RING - 1 - lax.div(d, 2))


def ring_device(place):
    place = lax.rem(place + RING, RING)
    late = lax.div(place, RING // 2)
    return (1 - late) * 2 * place + late * (2 * (RING - 1 - place) + 1)


def reduce_kernel(
    grads1, grads2, swapping1, swapping2, vectors, out, swapped1, swapped2, out_vectors,
    mine, partner_part, landing, final, v_sum, v_in,
    out_sem, pair_send, pair_receive, own_sem, ring_send, ring_receive, last_send, last_receive,
    v_send, v_receive, swap_send, swap_receive,
):
    d, section = lax.axis_index("dp"), lax.axis_index("section")
    odd = lax.rem(section, 2)
    place = ring_place(d)
    across = (d, section + 2 - 4 * lax.div(section, 2))
    pair = (d, section + 1 - 2 * odd)
    ways = ((ring_device(place + 1), section), (ring_device(place - 1), section))
    packs = (grads1, grads2)

    def flipped(bit):
        return d + bit - 2 * bit * lax.rem(lax.div(d, bit), 2)

    levels = (pair, (flipped(1), section), (flipped(2), section), (flipped(4), section), across)
    barrier = pltpu.get_barrier_semaphore()
    for other in (*ways, *levels):
        pl.semaphore_signal(barrier, inc=1, device_id=other, device_id_type=MESH)

    def rows_of(step, way):
        segment = lax.rem(place + (step if way else -step) + 2 * RING, RING)
        return pl.ds(pl.multiple_of(segment * SEGMENT + way * PART, 8), PART)

    def own_copy(step, way, k):
        rows = rows_of(step, way)
        return pltpu.make_async_copy(
            packs[k].at[odd, :, rows, :], mine.at[k, :, rows, :], own_sem.at[step, way, k]
        )

    pl.semaphore_wait(barrier, len(ways) + len(levels))

    def remote(source, target, send, receive, device):
        return pltpu.make_async_remote_copy(source, target, send, receive, device_id=device, device_id_type=MESH)

    def pair_copy(step, way, k):
        rows = rows_of(step, way)
        return remote(
            packs[k].at[1 - odd, :, rows, :], partner_part.at[k, :, rows, :],
            pair_send.at[step, way, k], pair_receive.at[step, way, k], pair,
        )

    def start_inputs(step):
        for way in range(2):
            for k in range(2):
                pair_copy(step, way, k).start()
                own_copy(step, way, k).start()

    start_inputs(0)
    start_inputs(1)
    swaps = [
        remote(source, target, swap_send.at[k], swap_receive.at[k], across)
        for k, (source, target) in enumerate(((swapping1, swapped1), (swapping2, swapped2)))
    ]
    for swap in swaps:
        swap.start()

    def vector_copy(level):
        return remote(v_sum.at[level], v_in.at[level], v_send.at[level], v_receive.at[level], levels[level])

    def vector_next(level):
        vector_copy(level).wait()
        if level + 1 < len(levels):
            v_sum[level + 1] = v_sum[level] + v_in[level]
            vector_copy(level + 1).start()

    v_sum[0] = vectors[...]
    vector_copy(0).start()

    def blocks(chain):
        return pl.ds(chain * CHAIN, CHAIN)

    def ring_copy(step, way, chain):
        rows = rows_of(step, way)
        return remote(
            mine.at[0, blocks(chain), rows, :], landing.at[blocks(chain), rows, :],
            ring_send.at[step, way, chain], ring_receive.at[step, way, chain], ways[way],
        )

    def incoming(step, way, chain):
        rows = rows_of(step + 1, way)
        return remote(
            mine.at[0, blocks(chain), rows, :], landing.at[blocks(chain), rows, :],
            ring_send.at[step, way, chain], ring_receive.at[step, way, chain], ways[way],
        )

    def own_total(chain, rows):
        part = (blocks(chain), rows, slice(None))
        both = [ref[(k, *part)].astype(F32) for ref in (mine, partner_part) for k in range(2)]
        return (both[0] + both[1]) + (both[2] + both[3])

    def total_of(chain, rows):
        return (own_total(chain, rows) + landing[blocks(chain), rows, :].astype(F32)).astype(BF16)

    def pair_here(step, way):
        for k in range(2):
            own_copy(step, way, k).wait()
            pair_copy(step, way, k).wait_recv()

    for way in range(2):
        pair_here(0, way)
        rows = rows_of(0, way)
        for chain in range(2):
            mine[0, blocks(chain), rows, :] = own_total(chain, rows).astype(BF16)
            ring_copy(0, way, chain).start()
    start_inputs(2)
    vector_next(0)

    def reduce_step(step, carry):
        for chain in range(2):
            for way in range(2):
                if chain == 0:
                    pair_here(step, way)
                incoming(step - 1, way, chain).wait_recv()
                rows = rows_of(step, way)
                mine[0, blocks(chain), rows, :] = total_of(chain, rows)
                ring_copy(step, way, chain).start()

        @pl.when(step + 2 < RING)
        def _():
            start_inputs(step + 2)

        return carry

    lax.fori_loop(1, RING - 1, reduce_step, 0)
    vector_next(1)

    def last_copy(step, way, chain, arriving=0):
        rows = rows_of(step + RING - 1 + arriving, way)
        return remote(
            final.at[blocks(chain), rows, :], final.at[blocks(chain), rows, :],
            last_send.at[step, way, chain], last_receive.at[step, way, chain], ways[way],
        )

    def out_copy(step, way, chain):
        part = (blocks(chain), rows_of(step + RING - 1, way), slice(None))
        return pltpu.make_async_copy(final.at[part], out.at[part], out_sem.at[step, way, chain])

    for chain in range(2):
        for way in range(2):
            if chain == 0:
                pair_here(RING - 1, way)
            incoming(RING - 2, way, chain).wait_recv()
            rows = rows_of(RING - 1, way)
            final[blocks(chain), rows, :] = total_of(chain, rows)
            last_copy(0, way, chain).start()
            out_copy(0, way, chain).start()
    vector_next(2)

    def gather_step(step, carry):
        for chain in range(2):
            for way in range(2):
                last_copy(step - 1, way, chain, 1).wait_recv()
                last_copy(step, way, chain).start()
                out_copy(step, way, chain).start()
        return carry

    lax.fori_loop(1, 3, gather_step, 0)
    vector_next(3)
    lax.fori_loop(3, 5, gather_step, 0)
    vector_next(4)
    out_vectors[0] = v_sum[len(levels) - 1]
    out_vectors[1] = v_in[len(levels) - 1]
    lax.fori_loop(5, RING - 1, gather_step, 0)

    def all_sent(step, carry):
        for way in range(2):
            for chain in range(2):
                ring_copy(step, way, chain).wait_send()
        return carry

    def pair_sent(step, carry):
        for way in range(2):
            for k in range(2):
                pair_copy(step, way, k).wait_send()
        return carry

    lax.fori_loop(0, RING - 1, all_sent, 0)
    lax.fori_loop(0, RING, pair_sent, 0)
    for swap in swaps:
        swap.wait()
    for chain in range(2):
        for way in range(2):
            last_copy(RING - 2, way, chain, 1).wait_recv()
            out_copy(RING - 1, way, chain).start()

    def last_sent(step, carry):
        for way in range(2):
            for chain in range(2):
                last_copy(step, way, chain).wait_send()
        return carry

    def written(step, carry):
        for way in range(2):
            for chain in range(2):
                out_copy(step, way, chain).wait()
        return carry

    lax.fori_loop(0, RING - 1, last_sent, 0)
    lax.fori_loop(0, RING, written, 0)


def reduce_grads(grads, swapping, vectors):
    share = (SHARE, D, D)
    dma = pltpu.SemaphoreType.DMA
    return pl.pallas_call(
        reduce_kernel,
        in_specs=[ANY, ANY, ANY, ANY, VMEM],
        out_specs=(ANY, ANY, ANY, VMEM),
        out_shape=(sds(share, BF16), ROWS, ROWS, sds((2, VECTORS, D), F32)),
        scratch_shapes=[
            pltpu.VMEM((2, *share), BF16),
            pltpu.VMEM((2, *share), BF16),
            pltpu.VMEM(share, BF16),
            pltpu.VMEM(share, BF16),
            pltpu.VMEM((5, VECTORS, D), F32),
            pltpu.VMEM((5, VECTORS, D), F32),
            dma((RING, 2, 2)),
            dma((RING, 2, 2)),
            dma((RING, 2, 2)),
            dma((RING, 2, 2)),
            dma((RING - 1, 2, 2)),
            dma((RING - 1, 2, 2)),
            dma((RING - 1, 2, 2)),
            dma((RING - 1, 2, 2)),
            dma((5,)),
            dma((5,)),
            dma((2,)),
            dma((2,)),
        ],
        compiler_params=params(56, collective_id=2, has_side_effects=True),
        name="reduce_grads",
    )(*grads, *swapping, vectors)


def spread_kernel(layer, total, vectors, *refs):
    of_encoder, of_regressor, refs = refs[:4], refs[4:8], refs[8:]
    matrix, down, *picked, enc, reg, mlp, hidden, low, wide_rows, rows, low_sem, wide_sem, rows_sem, picked_sem = refs
    low_copies = [pltpu.make_async_copy(total.at[i], low.at[i], low_sem.at[i]) for i in range(SHARE)]
    for copy in low_copies:
        copy.start()
    for which, sources in enumerate((of_encoder, of_regressor)):

        @pl.when(layer[0] == which)
        def _(sources=sources):
            for k, source in enumerate(sources):
                pltpu.make_async_copy(source, rows.at[k], rows_sem.at[k]).start()

    copies = []
    for which in range(2):

        @pl.when(layer[0] == which)
        def _(which=which):
            enc[...] = vectors[which, :6]
            reg[...] = vectors[1 - which, :FFN_AT]
            for block, of in enumerate((which, 1 - which)):
                mlp[block] = vectors[of, FFN_AT:HIDDEN_AT]
                for i in ALL_BLOCKS:
                    hidden[block : block + 1, columns(i)] = vectors[of, HIDDEN_AT + i : HIDDEN_AT + i + 1]

    for i in range(SHARE):
        low_copies[i].wait()
        wide_rows[i] = low[i].astype(F32)
        target = matrix.at[0, :, columns(i)] if i < BLOCKS else down.at[columns(i - BLOCKS), :]
        copies.append(pltpu.make_async_copy(wide_rows.at[i], target, wide_sem.at[i]))
        copies[i].start()
    for k, target in enumerate(picked):
        pltpu.make_async_copy(of_encoder[k], rows.at[k], rows_sem.at[k]).wait()
        copies.append(pltpu.make_async_copy(rows.at[k], target, picked_sem.at[k]))
        copies[-1].start()
    for copy in copies:
        copy.wait()


def spread(layer, total, vectors, of_encoder, of_regressor):
    dma = pltpu.SemaphoreType.DMA
    return pl.pallas_call(
        spread_kernel,
        in_specs=[SMEM, ANY, VMEM, *(ANY for _ in range(8))],
        out_specs=(*(ANY for _ in range(6)), *(VMEM for _ in range(4))),
        out_shape=(
            sds((1, D, FF), F32),
            sds((FF // 2, D), F32),
            *(ROWS for _ in range(4)),
            sds((6, D), F32),
            sds((FFN_AT, D), F32),
            sds((2, 4, D), F32),
            sds((2, FF), F32),
        ),
        scratch_shapes=[
            pltpu.VMEM((SHARE, D, D), BF16),
            pltpu.VMEM((SHARE, D, D), F32),
            pltpu.VMEM((4, CAP, D), BF16),
            dma((SHARE,)),
            dma((SHARE,)),
            dma((4,)),
            dma((4,)),
        ],
        compiler_params=params(60),
        name="spread",
    )(layer, total, vectors, *of_encoder, *of_regressor)


def plain_reduce_grads(grads, swapping, vectors):
    odd = lax.rem(lax.axis_index("section"), 2)
    pair = [(0, 1), (1, 0), (2, 3), (3, 2)]
    grads = grads[0] + grads[1]
    theirs = lax.dynamic_index_in_dim(grads, 1 - odd, 0, keepdims=False)
    mine = lax.dynamic_index_in_dim(grads, odd, 0, keepdims=False)
    total = lax.psum(mine + lax.ppermute(theirs, "section", pair), "dp")
    vectors = lax.psum(vectors + lax.ppermute(vectors, "section", pair), "dp")
    return total, *map(swap_layers, swapping), jnp.stack([vectors, swap_layers(vectors)])


def swap_layers(block):
    return lax.ppermute(block, "section", [(0, 2), (1, 3), (2, 0), (3, 1)])


def to_regressor(block):
    return lax.ppermute(block, "section", [(0, 2), (1, 3)])


def to_encoder(block):
    return lax.ppermute(block, "section", [(2, 0), (3, 1)])


def body(
    vis_embed, latent_cot, reg_queries, out_cot, section_matrix, down_weight, enc_vectors, reg_vectors,
    mlp_vectors, hidden_bias, pos_table, image_lengths, vis_index, mask_index,
):
    section = lax.axis_index("section")
    odd = lax.rem(section, 2)
    is_reg = section >= 2
    layer = jnp.where(is_reg, 1, 0)
    weights = gather_weights(section_matrix, down_weight)
    r = lax.dynamic_index_in_dim(mlp_vectors, layer, 0, keepdims=False)
    c = lax.dynamic_slice_in_dim(hidden_bias, layer, 1, 0)
    packs = [(odd + 2 * i).reshape(1).astype(jnp.int32) for i in range(2)]
    vis = [lax.dynamic_slice_in_dim(vis_index, (odd + 2 * i) * CAP, CAP)[:, None] for i in range(2)]
    mask = [lax.dynamic_slice_in_dim(mask_index, (odd + 2 * i) * CAP, CAP)[:, None] for i in range(2)]

    incoming = swap_layers(jnp.where(is_reg, vis_embed, reg_queries))
    x = [vis_embed, incoming]
    queries = [incoming, reg_queries]

    def on_encoder(work, otherwise):
        return lax.cond(is_reg, otherwise, work)

    def on_regressor(work, otherwise):
        return lax.cond(is_reg, work, otherwise)

    def enc_forward(i):
        return encoder_forward(image_lengths, packs[i], x[i], enc_vectors, r, c, weights)

    def no_enc_forward():
        made = unset((ROWS, ROWS, *ENC_STATE))
        return made[0], made[1], tuple(made[2:])

    def enc_back(i, d_latents, kept, so_far):
        return encoder_back(
            image_lengths, packs[i], lat_cot[i], d_latents, x[i], kept[0], enc_vectors, r, so_far, weights, kept[2]
        )

    def reg_before():
        return tuple(
            tuple(regressor_before(image_lengths, packs[i], queries[i], vis[i], mask[i], pos_table, reg_vectors, weights))
            for i in range(2)
        )

    def no_reg_before():
        made = unset((*REG_BEFORE, *REG_BEFORE))
        return tuple(made[: len(REG_BEFORE)]), tuple(made[len(REG_BEFORE) :])

    def reg_work(i, latents, so_far):
        return lambda: regressor(
            image_lengths, packs[i], latents, queries[i], cot[i], reg_vectors, r, c, so_far, weights, before[i]
        )

    def no_reg_work():
        made = unset((ROWS, ROWS, ROWS, TOTALS, *REG_STATE))
        return (*made[:4], tuple(made[4:]))

    none = jnp.zeros((VECTORS, D), F32)
    enc1 = on_encoder(lambda: enc_forward(0), no_enc_forward)
    latents1 = to_regressor(enc1[1])
    before = on_regressor(reg_before, no_reg_before)
    swapped_cot = swap_layers(jnp.where(is_reg, latent_cot, out_cot))
    lat_cot = [latent_cot, swapped_cot]
    cot = [swapped_cot, out_cot]
    enc2 = on_encoder(lambda: enc_forward(1), no_enc_forward)
    latents2 = to_regressor(enc2[1])
    reg1 = on_regressor(reg_work(0, latents1, none), no_reg_work)
    d_latents1 = to_encoder(reg1[1])
    reg2 = on_regressor(reg_work(1, latents2, reg1[3]), no_reg_work)
    d_latents2 = to_encoder(reg2[1])
    shares1, enc_totals, vis_grad1 = lax.cond(
        is_reg,
        lambda: (weight_grads(before[0], reg1[4]), *unset((TOTALS, ROWS))),
        lambda: enc_back(0, d_latents1, enc1, none)[::-1],
    )
    shares2, vectors, swapping = lax.cond(
        is_reg,
        lambda: (weight_grads(before[1], reg2[4]), reg2[3], reg1[0]),
        lambda: enc_back(1, d_latents2, enc2, enc_totals)[::-1],
    )
    reduce = reduce_grads if lax.axis_size("dp") == RING else plain_reduce_grads
    total, swapped1, swapped2, vectors = reduce((shares1, shares2), (swapping, reg1[2]), vectors)
    matrix_grad, down_grad, *others = spread(
        layer.reshape(1).astype(jnp.int32),
        total,
        vectors,
        (enc1[1], swapped1, vis_grad1, swapped2),
        (latents2, reg2[0], swapped1, reg2[2]),
    )
    return (*others[:4], matrix_grad, down_grad, *others[4:])


def solution(mesh):
    rows = P(("dp", "section"), None)
    in_specs = (
        rows, rows, rows, rows, P("section", None, None), P("section", None),
        P(), P(), P(), P(), P(), P("dp", None), P("dp"), P("dp"),
    )
    out_specs = (rows, rows, rows, rows, P("section", None, None), P("section", None), P(), P(), P(), P())
    return jax.shard_map(body, mesh=mesh, in_specs=in_specs, out_specs=out_specs, check_vma=False)
```

```python
import functools

import jax
import jax.numpy as jnp
from jax import lax
from jax.experimental import pallas as pl
from jax.experimental.pallas import tpu as pltpu
from jax.sharding import PartitionSpec as P

F32 = jnp.float32
BF16 = jnp.bfloat16
CAP = 384
IMGS = 4
SLOT = 128
PAD = IMGS * SLOT
D = 768
FF = 3072
LANES = 128
PAIRS = D // LANES
BLOCKS = FF // D
VECTORS = 24
EPS = 1e-06
MIB = 1 << 20
ANY = pl.BlockSpec(memory_space=pl.ANY)
SMEM = pl.BlockSpec(memory_space=pltpu.SMEM)


def params(limit=48, **more):
    return pltpu.CompilerParams(vmem_limit_bytes=limit * MIB, **more)


def sds(shape, dtype):
    return jax.ShapeDtypeStruct(shape, dtype)


def dot(a, b):
    return jnp.dot(a, b, preferred_element_type=F32)


def dot_nt(a, b):
    return lax.dot_general(a, b, (((1,), (1,)), ((), ())), preferred_element_type=F32)


def dot_tn(a, b):
    return lax.dot_general(a, b, (((0,), (0,)), ((), ())), preferred_element_type=F32)


def row(ref, i):
    return ref[i : i + 1, :]


def colsum(values):
    return jnp.sum(values, axis=0, keepdims=True)


def normalize(values):
    centred = values - jnp.mean(values, axis=-1, keepdims=True)
    spread = jnp.mean(centred * centred, axis=-1, keepdims=True)
    inverse = lax.rsqrt(spread + EPS)
    return centred * inverse, inverse


def norm_back(gradient, gain, normed, inverse):
    return scaled_norm_back(gradient * gain, normed, inverse)


def scaled_norm_back(scaled, normed, inverse):
    level = jnp.mean(scaled, axis=-1, keepdims=True)
    slope = jnp.mean(scaled * normed, axis=-1, keepdims=True)
    return inverse * (scaled - level - normed * slope)


def gelu_parts(t):
    e = jnp.exp(-0.5 * t * t)
    k = 1.0 / (1.0 + (0.3275911 * 0.7071067811865476) * jnp.abs(t))
    poly = k * (
        0.127414796
        + k * (-0.142248368 + k * (0.7107068705 + k * (-0.7265760135 + k * 0.5307027145)))
    )
    tail = poly * e
    phi = jnp.where(t >= 0.0, 1.0 - tail, tail)
    return t * phi, phi + t * (e * 0.3989422804014327)


def group_matrices(lens, pack, regroup, ungroup):
    def image(j, start):
        size = lens[pack, j]
        slots = pl.ds(pl.multiple_of(j * SLOT, SLOT), SLOT)
        place = lax.broadcasted_iota(jnp.int32, (SLOT, CAP), 0)
        rows = lax.broadcasted_iota(jnp.int32, (SLOT, CAP), 1)
        hit = (place + start == rows) & (place < size)
        regroup[slots, :] = jnp.where(hit, 1.0, 0.0).astype(BF16)
        place = lax.broadcasted_iota(jnp.int32, (CAP, SLOT), 1)
        rows = lax.broadcasted_iota(jnp.int32, (CAP, SLOT), 0)
        hit = (place + start == rows) & (place < size)
        ungroup[:, slots] = jnp.where(hit, 1.0, 0.0).astype(BF16)
        return start + size

    lax.fori_loop(0, IMGS, image, jnp.int32(0))


def lane_halves():
    lane = lax.broadcasted_iota(jnp.int32, (1, LANES), 1)
    first = jnp.where(lane < LANES // 2, 1.0, 0.0)
    return first.astype(BF16), (1.0 - first).astype(BF16)


def both_heads(block, halves):
    return jnp.concatenate([block * halves[0], block * halves[1]], axis=0)


def merge_heads(stacked):
    keys = stacked.shape[0] // 2
    lane = lax.broadcasted_iota(jnp.int32, (keys, LANES), 1)
    return jnp.where(lane < LANES // 2, stacked[:keys], stacked[keys:])


def softmax(scores):
    raised = jnp.exp(scores - jnp.max(scores, axis=0, keepdims=True))
    return (raised * (1.0 / jnp.sum(raised, axis=0, keepdims=True))).astype(BF16)


def keys_of(packed, first, parts, rows, cols, halves):
    return both_heads(
        jnp.concatenate([packed[first + 2 * m, rows, cols] for m in range(parts)], axis=0), halves
    )


def attend(lens, pack, packed, probs, mixed_slots, parts, done):
    halves = lane_halves()
    keys = SLOT * parts
    place = lax.bitwise_and(lax.broadcasted_iota(jnp.int32, (keys, SLOT), 0), SLOT - 1)
    for j in range(IMGS):
        rows = slice(j * SLOT, (j + 1) * SLOT)
        valid = place < lens[pack, j]
        for g in range(PAIRS):
            cols = slice(g * LANES, (g + 1) * LANES)
            scores = dot_nt(keys_of(packed, 1, parts, rows, cols, halves), packed[0, rows, cols])
            low = jnp.concatenate(
                [softmax(jnp.where(valid, part, -1e30)) for part in (scores[:keys], scores[keys:])], axis=0
            )
            probs[j, g] = low
            mixed_slots[rows, cols] = dot_tn(low, keys_of(packed, 2, parts, rows, cols, halves)).astype(BF16)
        done(j)


def attend_back(packed, probs, mixed_slots, d_mixed_slots, parts, ready, beside):
    halves = lane_halves()
    keys = SLOT * parts
    less = both_heads(jnp.full((keys, LANES), -1.0, BF16), halves)

    def image(j, carry):
        ready(j)
        rows = pl.ds(pl.multiple_of(j * SLOT, SLOT), SLOT)
        after = beside(j)
        for g in range(PAIRS):
            cols = slice(g * LANES, (g + 1) * LANES)
            d_out = d_mixed_slots[rows, cols]
            centre = (d_out.astype(F32) * mixed_slots[rows, cols].astype(F32)).astype(BF16)
            low = probs[j, g]
            d_prob = dot_nt(
                jnp.concatenate([keys_of(packed, 2, parts, rows, cols, halves), less], axis=1),
                jnp.concatenate([d_out, centre], axis=1),
            )
            d_scores = (low.astype(F32) * d_prob).astype(BF16)
            q = packed[0, rows, cols]
            zero = jnp.zeros_like(q)
            sides = jnp.concatenate(
                [jnp.concatenate([q, zero], axis=1), jnp.concatenate([zero, d_out], axis=1)], axis=0
            )
            d_kv = dot(jnp.concatenate([d_scores, low], axis=1), sides)
            d_q = dot_tn(d_scores, keys_of(packed, 1, parts, rows, cols, halves)) * 0.125
            packed[0, rows, cols] = d_q.astype(BF16)
            for side in range(2):
                merged = merge_heads(d_kv[:, side * LANES : (side + 1) * LANES]).astype(BF16)
                for m in range(parts):
                    packed[1 + side + 2 * m, rows, cols] = merged[m * SLOT : (m + 1) * SLOT]
        if after is not None:
            after()
        return carry

    lax.fori_loop(0, IMGS, image, 0)


ROWS = sds((CAP, D), BF16)
WIDE = sds((CAP, FF), BF16)
TOTALS = sds((VECTORS, D), F32)
FFN_AT = 10
HIDDEN_AT = FFN_AT + 4
ENC_STATE = (
    ROWS,
    sds((3, PAD, D), BF16),
    sds((IMGS, PAIRS, 2 * SLOT, SLOT), BF16),
    sds((PAD, D), BF16),
    ROWS,
    ROWS,
    ROWS,
    WIDE,
    WIDE,
    ROWS,
)
REG_BEFORE = (
    sds((3, CAP, D), BF16),
    sds((3, PAD, D), BF16),
    sds((2, CAP, D), F32),
)
REG_STATE = (
    sds((2, CAP, D), BF16),
    sds((5, CAP, D), BF16),
    ROWS,
    ROWS,
    ROWS,
    WIDE,
    WIDE,
    ROWS,
)


def full(shape):
    return pl.BlockSpec(shape, lambda i: (0,) * len(shape))


VMEM = pl.BlockSpec(memory_space=pltpu.VMEM)


def scratch(shape):
    return pltpu.VMEM(shape.shape, shape.dtype)


def unset(shapes):
    def kernel(*refs):
        del refs

    return pl.pallas_call(
        kernel, out_shape=shapes, out_specs=tuple(ANY for _ in shapes), name="unset"
    )()


class Copies:
    def __init__(self, semaphores):
        self.semaphores, self.used, self.open = semaphores, 0, []

    def take(self, count=1):
        self.used += count
        return self.used - count

    def start(self, source, target):
        copy = pltpu.make_async_copy(source, target, self.semaphores.at[self.take()])
        copy.start()
        return copy

    def leave(self, source, target):
        self.open.append(self.start(source, target))

    def halves(self, *pairs):
        first = self.take(2 * len(pairs))

        def copies(i):
            rows = half_rows(i)
            return [
                pltpu.make_async_copy(source.at[rows, :], target.at[rows, :], self.semaphores.at[first + 2 * k + i])
                for k, (source, target) in enumerate(pairs)
            ]

        def start(i):
            for copy in copies(i):
                copy.start()

        self.open += copies(0) + copies(1)
        return start

    def finish(self):
        for copy in self.open:
            copy.wait()


COPIES = pltpu.SemaphoreType.DMA((80,))


def columns(i):
    return slice(i * D, (i + 1) * D)


class Weights:
    def __init__(self, copies, weights, held):
        self.copies, self.weights, self.held, self.started = copies, weights, held, {}

    def target(self, i):
        kind, block = divmod(i, BLOCKS)
        held = self.held[kind]
        return held.at[columns(block), :] if kind == 2 else held.at[:, columns(block)]

    def start(self, *order):
        for i in order:
            self.started[i] = self.copies.start(self.weights.at[i], self.target(i))

    def wait(self, *which):
        for i in which:
            self.started[i].wait()


WEIGHT_SCRATCH = [pltpu.VMEM((D, FF), BF16), pltpu.VMEM((D, FF), BF16), pltpu.VMEM((FF, D), BF16)]
ALL_BLOCKS = range(BLOCKS)
UPS = [BLOCKS + i for i in ALL_BLOCKS]
DOWNS = [2 * BLOCKS + i for i in ALL_BLOCKS]


def wide(i):
    return pl.ds(pl.multiple_of(i * D, D), D)


HALF = CAP // 2


def half_rows(i):
    return pl.ds(pl.multiple_of(i * HALF, HALF), HALF)


def feed_forward(weights, mid, r, c, out, state, made):
    normed, active, slope, branch = state
    centred, _ = normalize(mid[...].astype(F32))
    normed[...] = (centred * row(r, 0) + row(r, 1)).astype(BF16)
    made("normed")
    _, up, down = weights.held
    weights.wait(*UPS, *DOWNS)

    def part(i, carry):
        rows = half_rows(i)
        value, steep = gelu_parts(dot(normed[rows, :], up[...]) + c[...])
        active[rows, :] = value.astype(BF16)
        slope[rows, :] = steep.astype(BF16)
        made(i)
        summed = dot(active[rows, :], down[...]) + row(r, 2)
        branch[rows, :] = summed.astype(BF16)
        out[rows, :] = (mid[rows, :].astype(F32) + row(r, 3) * summed).astype(BF16)
        return carry

    lax.fori_loop(0, 2, part, 0)
    made("branch")


def feed_forward_back(weights, ready, g, mid, r, refs, totals, residual, made):
    slope, branch, d_branch = refs
    _, up, down = weights.held
    d_branch[...] = (g * row(r, 3)).astype(BF16)
    made("branch")
    add_row(totals, FFN_AT + 2, colsum(d_branch[...].astype(F32)))
    ready("branch")
    add_row(totals, FFN_AT + 3, colsum(g * branch[...].astype(F32)))
    for i in ALL_BLOCKS:
        weights.wait(2 * BLOCKS + i)
        ready(i)
        d_active = dot_nt(d_branch[...], down[columns(i), :])
        d_hidden = (d_active * slope[:, columns(i)].astype(F32)).astype(BF16)
        slope[:, columns(i)] = d_hidden
        made(i)
        add_row(totals, HIDDEN_AT + i, colsum(d_hidden.astype(F32)))
    weights.wait(*UPS)
    d_normed = dot_nt(slope[...], up[...])
    normed, inverse = normalize(mid[...].astype(F32))
    add_row(totals, FFN_AT, colsum(d_normed * normed))
    add_row(totals, FFN_AT + 1, colsum(d_normed))
    residual[...] = (g + norm_back(d_normed, row(r, 0), normed, inverse)).astype(BF16).astype(F32)


def attention_back(parts, weights, e, refs, totals, ready, made, beside):
    residual, branch, d_branch, regroup, ungroup, packed, probs, mixed_slots, d_slots, d_flat = refs
    last = 1 + 4 * parts
    g = residual[...]
    ready("branch")
    d_branch[...] = (g * row(e, last)).astype(BF16)
    made("branch")
    add_row(totals, last, colsum(g * branch[...].astype(F32)))
    add_row(totals, last - 1, colsum(d_branch[...].astype(F32)))
    weights.wait(3)
    d_mixed = dot(d_branch[...], weights.held[0][:, columns(3)]).astype(BF16)
    d_slots[...] = dot(regroup[...], d_mixed).astype(BF16)
    ready("packed")
    attend_back(packed, probs, mixed_slots, d_slots, parts, ready, beside)
    for m in range(1 + 2 * parts):
        d_flat[m] = dot(ungroup[...], packed[m]).astype(BF16)
        made(m)


def add_row(totals, i, value):
    totals[i : i + 1] += value


def nothing(name):
    del name


class Shares:
    def __init__(self, copies, blocks, share):
        self.semaphores, self.blocks, self.share = copies.semaphores, blocks, share
        self.first = copies.take(3 * BLOCKS)

    def copy(self, kind, i):
        section, block = (lax.div(i, 2), BLOCKS + lax.rem(i, 2)) if kind == 2 else (kind, i)
        place = kind * BLOCKS + i
        return pltpu.make_async_copy(
            self.blocks.at[place], self.share.at[section, block], self.semaphores.at[self.first + place]
        )

    def put(self, kind, i, product):
        self.blocks[kind * BLOCKS + i] = product.astype(BF16)
        self.copy(kind, i).start()

    def feed_forward(self, normed, d_hidden, active, d_branch):
        def step(i):
            self.blocks[BLOCKS + i] = dot_tn(normed[...], d_hidden[:, wide(i)]).astype(BF16)
            self.blocks[2 * BLOCKS + i] = dot_tn(active[:, wide(i)], d_branch[...]).astype(BF16)

            def after():
                for kind in (1, 2):
                    self.copy(kind, i).start()

            return after

        return step

    def finish(self):
        for kind in range(3):
            for i in ALL_BLOCKS:
                self.copy(kind, i).wait()


def encoder_forward_kernel(lens, which, x, e, r, c, given, mid, out, *refs):
    kept, scratch = refs[: len(ENC_STATE)], refs[len(ENC_STATE) :]
    *held, flat, regroup, ungroup, semaphores = scratch[: 3 + 4]
    state = scratch[3 + 4 :]
    normed, packed, probs, mixed_slots, mixed, branch, *ffn = state
    pack = which[0]
    copies = Copies(semaphores)
    weights = Weights(copies, given, held)
    weights.start(*ALL_BLOCKS, *UPS, *DOWNS)
    values = x[...].astype(F32)
    centred, _ = normalize(values)
    normed[...] = (centred * row(e, 0) + row(e, 1)).astype(BF16)
    copies.leave(normed, kept[0])
    group_matrices(lens, pack, regroup, ungroup)
    qkvo = weights.held[0]
    weights.wait(0)
    flat[0] = ((dot(normed[...], qkvo[:, columns(0)]) + row(e, 2)).astype(BF16) * 0.125).astype(BF16)
    weights.wait(1)
    flat[1] = dot(normed[...], qkvo[:, columns(1)]).astype(BF16)
    weights.wait(2)
    flat[2] = (dot(normed[...], qkvo[:, columns(2)]) + row(e, 3)).astype(BF16)
    for m in range(3):
        packed[m] = dot(regroup[...], flat[m]).astype(BF16)
        copies.leave(packed.at[m], kept[1].at[m])
    attend(lens, pack, packed, probs, mixed_slots, 1, lambda j: copies.leave(probs.at[j], kept[2].at[j]))
    copies.leave(mixed_slots, kept[3])
    mixed[...] = dot(ungroup[...], mixed_slots[...]).astype(BF16)
    copies.leave(mixed, kept[4])
    weights.wait(3)
    summed = dot_nt(mixed[...], qkvo[:, columns(3)]) + row(e, 4)
    branch[...] = summed.astype(BF16)
    copies.leave(branch, kept[5])
    mid[...] = (values + row(e, 5) * summed).astype(BF16)

    half_made = copies.halves((ffn[1], kept[7]), (ffn[2], kept[8]))

    def made(name):
        if isinstance(name, str):
            source, target = (ffn[0], kept[6]) if name == "normed" else (ffn[3], kept[9])
            copies.leave(source, target)
        else:
            half_made(name)

    feed_forward(weights, mid, r, c, out, ffn, made)
    copies.finish()


def encoder_forward(lens, which, x, e, r, c, weights):
    made = pl.pallas_call(
        encoder_forward_kernel,
        in_specs=[SMEM, SMEM, VMEM, VMEM, VMEM, VMEM, ANY],
        out_specs=(VMEM, VMEM, *(ANY for _ in ENC_STATE)),
        out_shape=(ROWS, ROWS, *ENC_STATE),
        scratch_shapes=[
            *WEIGHT_SCRATCH,
            pltpu.VMEM((3, CAP, D), BF16),
            pltpu.VMEM((PAD, CAP), BF16),
            pltpu.VMEM((CAP, PAD), BF16),
            COPIES,
            *map(scratch, ENC_STATE),
        ],
        compiler_params=params(58),
        name="encoder_forward",
    )(lens, which, x, e, r, c, weights)
    return made[0], made[1], tuple(made[2:])


def encoder_back_kernel(lens, which, g1, g2, x, mid, e, r, so_far, given, *refs):
    state, refs = refs[: len(ENC_STATE)], refs[len(ENC_STATE) :]
    d_x, totals, share, *held, regroup, ungroup, d_slots, d_branch, d_f_branch, d_flat, residual, blocks, semaphores = (
        refs[: 3 + 3 + 9]
    )
    normed, packed, probs, mixed_slots, mixed, branch, f_normed, active, slope, f_branch = refs[3 + 3 + 9 :]
    copies = Copies(semaphores)
    weights = Weights(copies, given, held)
    coming = {"branch": copies.start(state[9], f_branch)}
    for i in ALL_BLOCKS:
        weights.start(2 * BLOCKS + i)
        coming[i] = copies.start(state[8].at[:, columns(i)], slope.at[:, columns(i)])
    weights.start(*UPS, 3)
    later = {"branch": copies.start(state[5], branch)}
    later["packed"] = copies.start(state[1], packed)
    later["mixed"] = copies.start(state[3], mixed_slots)
    probs_in = [copies.start(state[2].at[j], probs.at[j]) for j in range(IMGS)]
    late = [copies.start(state[i], ref) for i, ref in ((6, f_normed), (7, active), (0, normed), (4, mixed))]
    weights.start(0, 1, 2)
    shares = Shares(copies, blocks, share)
    totals[...] = so_far[...]
    group_matrices(lens, which[0], regroup, ungroup)
    g = g1[...].astype(F32) + g2[...].astype(F32)
    feed_forward_back(
        weights, lambda name: coming[name].wait(), g, mid, r, (slope, f_branch, d_f_branch), totals, residual, nothing
    )
    for copy in late:
        copy.wait()

    def ready(name):
        if name == "branch":
            later["branch"].wait()
        elif name == "packed":
            later["packed"].wait()
            later["mixed"].wait()
            for copy in probs_in:
                copy.wait()

    attention_back(
        1, weights, e, (residual, branch, d_branch, regroup, ungroup, packed, probs, mixed_slots, d_slots, d_flat),
        totals, ready, nothing, shares.feed_forward(f_normed, slope, active, d_f_branch),
    )

    def first_block(i, carry):
        shares.put(0, i, dot_tn(normed[...], d_flat[i]))
        return carry

    lax.fori_loop(0, 3, first_block, 0)
    shares.put(0, 3, dot_tn(d_branch[...], mixed[...]))
    weights.wait(0, 1, 2)
    qkvo = weights.held[0]
    d_normed = dot_nt(d_flat[0], qkvo[:, columns(0)])
    for m in (1, 2):
        d_normed += dot_nt(d_flat[m], qkvo[:, columns(m)])
    values, inverse = normalize(x[...].astype(F32))
    add_row(totals, 0, colsum(d_normed * values))
    add_row(totals, 1, colsum(d_normed))
    add_row(totals, 2, colsum(d_flat[0].astype(F32)))
    add_row(totals, 3, colsum(d_flat[2].astype(F32)))
    d_x[...] = (residual[...] + norm_back(d_normed, row(e, 0), values, inverse)).astype(BF16)
    shares.finish()


def encoder_back(lens, which, g1, g2, x, mid, e, r, so_far, weights, state):
    return pl.pallas_call(
        encoder_back_kernel,
        in_specs=[SMEM, SMEM, *(VMEM for _ in range(7)), ANY, *(ANY for _ in ENC_STATE)],
        out_specs=(VMEM, VMEM, ANY),
        out_shape=(ROWS, TOTALS, sds((2, SHARE, D, D), BF16)),
        scratch_shapes=[
            *WEIGHT_SCRATCH,
            pltpu.VMEM((PAD, CAP), BF16),
            pltpu.VMEM((CAP, PAD), BF16),
            pltpu.VMEM((PAD, D), BF16),
            scratch(ROWS),
            scratch(ROWS),
            pltpu.VMEM((3, CAP, D), BF16),
            pltpu.VMEM((CAP, D), F32),
            pltpu.VMEM((3 * BLOCKS, D, D), BF16),
            COPIES,
            *map(scratch, ENC_STATE),
        ],
        compiler_params=params(58),
        name="encoder_back",
    )(lens, which, g1, g2, x, mid, e, r, so_far, weights, *state)


def table_rows(indices, table):
    places = lax.broadcasted_iota(jnp.int32, (indices.shape[0], table.shape[0]), 1)
    chosen = jnp.where(places == indices[...], 1.0, 0.0).astype(BF16)
    values = table[...]
    top = values.astype(BF16)
    values = values - top.astype(F32)
    middle = values.astype(BF16)
    bottom = (values - middle.astype(F32)).astype(BF16)
    return (dot(chosen, top) + dot(chosen, middle)) + dot(chosen, bottom)


def regressor_before_kernel(lens, which, queries, vis, mask, table, e, given, normed, packed, sources, held, flat, regroup, ungroup, semaphores):
    copies = Copies(semaphores)
    weights = Weights(copies, given, [held])
    weights.start(0, 1, 2)
    group_matrices(lens, which[0], regroup, ungroup)
    sources[1] = table_rows(vis, table)
    residual = queries[...].astype(F32)
    source = residual + table_rows(mask, table)
    sources[0] = source
    centred, _ = normalize(source)
    normed[0] = (centred * row(e, 0) + row(e, 1)).astype(BF16)
    normed[1] = (centred * row(e, 2) + row(e, 3)).astype(BF16)
    centred, _ = normalize(residual)
    normed[2] = (centred * row(e, 4) + row(e, 5)).astype(BF16)
    weights.wait(0, 1, 2)
    flat[0] = ((dot(normed[0], held[:, columns(0)]) + row(e, 6)).astype(BF16) * 0.125).astype(BF16)
    flat[1] = dot(normed[1], held[:, columns(1)]).astype(BF16)
    flat[2] = (dot(normed[2], held[:, columns(2)]) + row(e, 7)).astype(BF16)
    for m in range(3):
        packed[m] = dot(regroup[...], flat[m]).astype(BF16)


def regressor_before(lens, which, queries, vis, mask, table, e, weights):
    return pl.pallas_call(
        regressor_before_kernel,
        in_specs=[SMEM, SMEM, *(VMEM for _ in range(5)), ANY],
        out_specs=(VMEM, VMEM, VMEM),
        out_shape=REG_BEFORE,
        scratch_shapes=[
            pltpu.VMEM((D, FF), BF16),
            pltpu.VMEM((3, CAP, D), BF16),
            pltpu.VMEM((PAD, CAP), BF16),
            pltpu.VMEM((CAP, PAD), BF16),
            COPIES,
        ],
        compiler_params=params(48),
        name="regressor_before",
    )(lens, which, queries, vis, mask, table, e, weights)


def regressor_kernel(
    lens, which, latents, queries, cot, e, r, c, so_far, given, packed_before, sources_before,
    regressed, d_latents, d_queries, totals, *refs,
):
    kept, refs = refs[: len(REG_STATE)], refs[len(REG_STATE) :]
    (
        *held, regroup, ungroup, packed, probs, mixed_slots, d_slots, sources, branch, slope, f_branch, mid, residual,
        flat, semaphores, normed, d_flat, mixed, d_branch, f_normed, _, active, d_f_branch,
    ) = refs
    pack = which[0]
    copies = Copies(semaphores)
    weights = Weights(copies, given, held)
    in_sources = copies.start(sources_before, sources)
    weights.start(1, 2)
    in_packed = [copies.start(packed_before.at[i], packed.at[m]) for i, m in enumerate((0, 3, 4))]
    weights.start(3, *UPS, *DOWNS, 0)
    qkvo = weights.held[0]
    group_matrices(lens, pack, regroup, ungroup)
    incoming = latents[...].astype(F32)
    centred, _ = normalize(incoming)
    normed[1] = (centred * row(e, 4) + row(e, 5)).astype(BF16)
    in_sources.wait()
    k_source = incoming + sources[1]
    sources[1] = k_source
    centred, _ = normalize(k_source)
    normed[0] = (centred * row(e, 2) + row(e, 3)).astype(BF16)
    copies.leave(normed, kept[0])
    weights.wait(1)
    flat[0] = dot(normed[0], qkvo[:, columns(1)]).astype(BF16)
    weights.wait(2)
    flat[1] = (dot(normed[1], qkvo[:, columns(2)]) + row(e, 7)).astype(BF16)
    for m in range(2):
        packed[1 + m] = dot(regroup[...], flat[m]).astype(BF16)
    for copy in in_packed:
        copy.wait()
    attend(lens, pack, packed, probs, mixed_slots, 2, nothing)
    mixed[...] = dot(ungroup[...], mixed_slots[...]).astype(BF16)
    copies.leave(mixed, kept[2])
    weights.wait(3)
    summed = dot_nt(mixed[...], qkvo[:, columns(3)]) + row(e, 8)
    branch[...] = summed.astype(BF16)
    mid[...] = (queries[...].astype(F32) + row(e, 9) * summed).astype(BF16)

    half_made = copies.halves((active, kept[6]))

    def forward_made(name):
        if not isinstance(name, str):
            half_made(name)
        elif name == "normed":
            copies.leave(f_normed, kept[4])

    feed_forward(weights, mid, r, c, regressed, (f_normed, active, slope, f_branch), forward_made)

    totals[...] = so_far[...]
    waited = Weights(copies, given, held)
    waited.wait = nothing_more

    def back_made(name):
        if name == "branch":
            copies.leave(d_f_branch, kept[7])
        else:
            copies.leave(slope.at[:, columns(name)], kept[5].at[:, columns(name)])

    feed_forward_back(
        waited, nothing, cot[...].astype(F32), mid, r, (slope, f_branch, d_f_branch), totals, residual, back_made
    )

    def attention_made(name):
        if name == "branch":
            copies.leave(d_branch, kept[3])
        else:
            copies.leave(d_flat.at[name], kept[1].at[name])

    attention_back(
        2, waited, e, (residual, branch, d_branch, regroup, ungroup, packed, probs, mixed_slots, d_slots, d_flat),
        totals, nothing, attention_made, nothing,
    )
    weights.wait(0)
    add_row(totals, 6, colsum(d_flat[0].astype(F32)))
    add_row(totals, 7, colsum(d_flat[2].astype(F32)) + colsum(d_flat[4].astype(F32)))
    values, inverse = normalize(sources[0])
    grad = dot_nt(d_flat[0], qkvo[:, columns(0)])
    add_row(totals, 0, colsum(grad * values))
    add_row(totals, 1, colsum(grad))
    scaled = grad * row(e, 0)
    grad = dot_nt(d_flat[3], qkvo[:, columns(1)])
    k_gain = colsum(grad * values)
    k_offset = colsum(grad)
    scaled += grad * row(e, 2)
    total = residual[...] + scaled_norm_back(scaled, values, inverse)
    values, inverse = normalize(queries[...].astype(F32))
    grad = dot_nt(d_flat[4], qkvo[:, columns(2)])
    v_gain = colsum(grad * values)
    v_offset = colsum(grad)
    total += norm_back(grad, row(e, 4), values, inverse)
    d_queries[...] = total.astype(BF16)
    values, inverse = normalize(sources[1])
    grad = dot_nt(d_flat[1], qkvo[:, columns(1)])
    add_row(totals, 2, k_gain + colsum(grad * values))
    add_row(totals, 3, k_offset + colsum(grad))
    total = norm_back(grad, row(e, 2), values, inverse)
    values, inverse = normalize(latents[...].astype(F32))
    grad = dot_nt(d_flat[2], qkvo[:, columns(2)])
    add_row(totals, 4, v_gain + colsum(grad * values))
    add_row(totals, 5, v_offset + colsum(grad))
    total += norm_back(grad, row(e, 4), values, inverse)
    d_latents[...] = total.astype(BF16)
    copies.finish()


def nothing_more(*which):
    del which


def regressor(lens, which, latents, queries, cot, e, r, c, so_far, weights, before):
    made = pl.pallas_call(
        regressor_kernel,
        in_specs=[SMEM, SMEM, *(VMEM for _ in range(7)), ANY, ANY, ANY],
        out_specs=(VMEM, VMEM, VMEM, VMEM, *(ANY for _ in REG_STATE)),
        out_shape=(ROWS, ROWS, ROWS, TOTALS, *REG_STATE),
        scratch_shapes=[
            *WEIGHT_SCRATCH,
            pltpu.VMEM((PAD, CAP), BF16),
            pltpu.VMEM((CAP, PAD), BF16),
            pltpu.VMEM((5, PAD, D), BF16),
            pltpu.VMEM((IMGS, PAIRS, 4 * SLOT, SLOT), BF16),
            pltpu.VMEM((PAD, D), BF16),
            pltpu.VMEM((PAD, D), BF16),
            pltpu.VMEM((2, CAP, D), F32),
            scratch(ROWS),
            scratch(WIDE),
            scratch(ROWS),
            scratch(ROWS),
            pltpu.VMEM((CAP, D), F32),
            pltpu.VMEM((2, CAP, D), BF16),
            COPIES,
            *(scratch(s) if i != 5 else pltpu.VMEM((8, LANES), BF16) for i, s in enumerate(REG_STATE)),
        ],
        compiler_params=params(60),
        name="regressor",
    )(lens, which, latents, queries, cot, e, r, c, so_far, weights, before[1], before[2])
    return (*made[:4], tuple(made[4:]))


SHARE = BLOCKS + BLOCKS // 2


def weight_grads_kernel(*refs):
    sources, share, held, blocks, semaphores = refs[:9], refs[9], refs[10:19], refs[19], refs[20]
    copies = Copies(semaphores)
    order = (5, 6, 7, 8, 0, 1, 2, 3, 4)
    started = {i: copies.start(sources[i], held[i]) for i in order}
    before, normed, d_flat, mixed, d_branch, f_normed, d_hidden, active, d_f_branch = held
    shares = Shares(copies, blocks, share)
    for i in order[:4]:
        started[i].wait()
    work = shares.feed_forward(f_normed, d_hidden, active, d_f_branch)

    def ffn_blocks(i, carry):
        work(i)()
        return carry

    lax.fori_loop(0, BLOCKS, ffn_blocks, 0)
    for i in order[4:]:
        started[i].wait()
    shares.put(0, 0, dot_tn(before[0], d_flat[0]))

    def pair_block(i, carry):
        shares.put(0, i, dot_tn(normed[i - 1], d_flat[i]) + dot_tn(before[i], d_flat[i + 2]))
        return carry

    lax.fori_loop(1, 3, pair_block, 0)
    shares.put(0, 3, dot_tn(d_branch[...], mixed[...]))
    shares.finish()


def weight_grads(before, state):
    return pl.pallas_call(
        weight_grads_kernel,
        in_specs=[ANY] * 9,
        out_specs=ANY,
        out_shape=sds((2, SHARE, D, D), BF16),
        scratch_shapes=[
            scratch(REG_BEFORE[0]),
            *map(scratch, REG_STATE),
            pltpu.VMEM((3 * BLOCKS, D, D), BF16),
            COPIES,
        ],
        compiler_params=params(),
        name="weight_grads",
    )(before[0], *state)


MESH = pl.DeviceIdType.MESH


def gather_weights_kernel(matrix, down, weights, send, receive, local):
    dp, section = lax.axis_index("dp"), lax.axis_index("section")
    odd = lax.rem(section, 2)
    partner = (dp, section + 1 - 2 * odd)
    barrier = pltpu.get_barrier_semaphore()
    pl.semaphore_signal(barrier, inc=1, device_id=partner, device_id_type=MESH)
    pl.semaphore_wait(barrier, 1)
    places = [(matrix.at[0, :, pl.ds(i * D, D)], odd * BLOCKS + i) for i in range(BLOCKS)]
    places += [(down.at[pl.ds(i * D, D), :], 2 * BLOCKS + odd * (BLOCKS // 2) + i) for i in range(BLOCKS // 2)]
    copies = []
    for i, (source, place) in enumerate(places):
        away = pltpu.make_async_remote_copy(
            source, weights.at[place], send.at[i], receive.at[i], device_id=partner, device_id_type=MESH
        )
        away.start()
        here = pltpu.make_async_copy(source, weights.at[place], local.at[i])
        here.start()
        copies += [away, here]
    for copy in copies:
        copy.wait()


def gather_weights(matrix, down):
    vmem = pl.BlockSpec(memory_space=pltpu.VMEM)
    return pl.pallas_call(
        gather_weights_kernel,
        in_specs=[vmem, vmem],
        out_specs=ANY,
        out_shape=sds((3 * BLOCKS, D, D), matrix.dtype),
        scratch_shapes=[pltpu.SemaphoreType.DMA((SHARE,)) for _ in range(3)],
        compiler_params=params(collective_id=1, has_side_effects=True),
        name="gather_weights",
    )(matrix, down)


RING = 8
SEGMENT = D // RING
PART = SEGMENT // 2
CHAIN = SHARE // 2


def ring_place(d):
    odd = lax.rem(d, 2)
    return (1 - odd) * lax.div(d, 2) + odd * (RING - 1 - lax.div(d, 2))


def ring_device(place):
    place = lax.rem(place + RING, RING)
    late = lax.div(place, RING // 2)
    return (1 - late) * 2 * place + late * (2 * (RING - 1 - place) + 1)


def reduce_kernel(
    grads1, grads2, swapping1, swapping2, vectors, out, swapped1, swapped2, out_vectors,
    mine, partner_part, landing, final, v_sum, v_in,
    out_sem, pair_send, pair_receive, own_sem, ring_send, ring_receive, last_send, last_receive,
    v_send, v_receive, swap_send, swap_receive,
):
    d, section = lax.axis_index("dp"), lax.axis_index("section")
    odd = lax.rem(section, 2)
    place = ring_place(d)
    across = (d, section + 2 - 4 * lax.div(section, 2))
    pair = (d, section + 1 - 2 * odd)
    ways = ((ring_device(place + 1), section), (ring_device(place - 1), section))
    packs = (grads1, grads2)

    def flipped(bit):
        return d + bit - 2 * bit * lax.rem(lax.div(d, bit), 2)

    levels = (pair, (flipped(1), section), (flipped(2), section), (flipped(4), section), across)
    barrier = pltpu.get_barrier_semaphore()
    for other in (*ways, *levels):
        pl.semaphore_signal(barrier, inc=1, device_id=other, device_id_type=MESH)

    def rows_of(step, way):
        segment = lax.rem(place + (step if way else -step) + 2 * RING, RING)
        return pl.ds(pl.multiple_of(segment * SEGMENT + way * PART, 8), PART)

    def own_copy(step, way, k):
        rows = rows_of(step, way)
        return pltpu.make_async_copy(
            packs[k].at[odd, :, rows, :], mine.at[k, :, rows, :], own_sem.at[step, way, k]
        )

    pl.semaphore_wait(barrier, len(ways) + len(levels))

    def remote(source, target, send, receive, device):
        return pltpu.make_async_remote_copy(source, target, send, receive, device_id=device, device_id_type=MESH)

    def pair_copy(step, way, k):
        rows = rows_of(step, way)
        return remote(
            packs[k].at[1 - odd, :, rows, :], partner_part.at[k, :, rows, :],
            pair_send.at[step, way, k], pair_receive.at[step, way, k], pair,
        )

    def start_inputs(step):
        for way in range(2):
            for k in range(2):
                pair_copy(step, way, k).start()
                own_copy(step, way, k).start()

    start_inputs(0)
    start_inputs(1)
    swaps = [
        remote(source, target, swap_send.at[k], swap_receive.at[k], across)
        for k, (source, target) in enumerate(((swapping1, swapped1), (swapping2, swapped2)))
    ]
    for swap in swaps:
        swap.start()

    def vector_copy(level):
        return remote(v_sum.at[level], v_in.at[level], v_send.at[level], v_receive.at[level], levels[level])

    def vector_next(level):
        vector_copy(level).wait()
        if level + 1 < len(levels):
            v_sum[level + 1] = v_sum[level] + v_in[level]
            vector_copy(level + 1).start()

    v_sum[0] = vectors[...]
    vector_copy(0).start()

    def blocks(chain):
        return pl.ds(chain * CHAIN, CHAIN)

    def ring_copy(step, way, chain):
        rows = rows_of(step, way)
        return remote(
            mine.at[0, blocks(chain), rows, :], landing.at[blocks(chain), rows, :],
            ring_send.at[step, way, chain], ring_receive.at[step, way, chain], ways[way],
        )

    def incoming(step, way, chain):
        rows = rows_of(step + 1, way)
        return remote(
            mine.at[0, blocks(chain), rows, :], landing.at[blocks(chain), rows, :],
            ring_send.at[step, way, chain], ring_receive.at[step, way, chain], ways[way],
        )

    def own_total(chain, rows):
        part = (blocks(chain), rows, slice(None))
        both = [ref[(k, *part)].astype(F32) for ref in (mine, partner_part) for k in range(2)]
        return (both[0] + both[1]) + (both[2] + both[3])

    def total_of(chain, rows):
        return (own_total(chain, rows) + landing[blocks(chain), rows, :].astype(F32)).astype(BF16)

    def pair_here(step, way):
        for k in range(2):
            own_copy(step, way, k).wait()
            pair_copy(step, way, k).wait_recv()

    for way in range(2):
        pair_here(0, way)
        rows = rows_of(0, way)
        for chain in range(2):
            mine[0, blocks(chain), rows, :] = own_total(chain, rows).astype(BF16)
            ring_copy(0, way, chain).start()
    start_inputs(2)
    vector_next(0)

    def reduce_step(step, carry):
        for chain in range(2):
            for way in range(2):
                if chain == 0:
                    pair_here(step, way)
                incoming(step - 1, way, chain).wait_recv()
                rows = rows_of(step, way)
                mine[0, blocks(chain), rows, :] = total_of(chain, rows)
                ring_copy(step, way, chain).start()

        @pl.when(step + 2 < RING)
        def _():
            start_inputs(step + 2)

        return carry

    lax.fori_loop(1, RING - 1, reduce_step, 0)
    vector_next(1)

    def last_copy(step, way, chain, arriving=0):
        rows = rows_of(step + RING - 1 + arriving, way)
        return remote(
            final.at[blocks(chain), rows, :], final.at[blocks(chain), rows, :],
            last_send.at[step, way, chain], last_receive.at[step, way, chain], ways[way],
        )

    def out_copy(step, way, chain):
        part = (blocks(chain), rows_of(step + RING - 1, way), slice(None))
        return pltpu.make_async_copy(final.at[part], out.at[part], out_sem.at[step, way, chain])

    for chain in range(2):
        for way in range(2):
            if chain == 0:
                pair_here(RING - 1, way)
            incoming(RING - 2, way, chain).wait_recv()
            rows = rows_of(RING - 1, way)
            final[blocks(chain), rows, :] = total_of(chain, rows)
            last_copy(0, way, chain).start()
            out_copy(0, way, chain).start()
    vector_next(2)

    def gather_step(step, carry):
        for chain in range(2):
            for way in range(2):
                last_copy(step - 1, way, chain, 1).wait_recv()
                last_copy(step, way, chain).start()
                out_copy(step, way, chain).start()
        return carry

    lax.fori_loop(1, 3, gather_step, 0)
    vector_next(3)
    lax.fori_loop(3, 5, gather_step, 0)
    vector_next(4)
    out_vectors[0] = v_sum[len(levels) - 1]
    out_vectors[1] = v_in[len(levels) - 1]
    lax.fori_loop(5, RING - 1, gather_step, 0)

    def all_sent(step, carry):
        for way in range(2):
            for chain in range(2):
                ring_copy(step, way, chain).wait_send()
        return carry

    def pair_sent(step, carry):
        for way in range(2):
            for k in range(2):
                pair_copy(step, way, k).wait_send()
        return carry

    lax.fori_loop(0, RING - 1, all_sent, 0)
    lax.fori_loop(0, RING, pair_sent, 0)
    for swap in swaps:
        swap.wait()
    for chain in range(2):
        for way in range(2):
            last_copy(RING - 2, way, chain, 1).wait_recv()
            out_copy(RING - 1, way, chain).start()

    def last_sent(step, carry):
        for way in range(2):
            for chain in range(2):
                last_copy(step, way, chain).wait_send()
        return carry

    def written(step, carry):
        for way in range(2):
            for chain in range(2):
                out_copy(step, way, chain).wait()
        return carry

    lax.fori_loop(0, RING - 1, last_sent, 0)
    lax.fori_loop(0, RING, written, 0)


def reduce_grads(grads, swapping, vectors):
    share = (SHARE, D, D)
    dma = pltpu.SemaphoreType.DMA
    return pl.pallas_call(
        reduce_kernel,
        in_specs=[ANY, ANY, ANY, ANY, VMEM],
        out_specs=(ANY, ANY, ANY, VMEM),
        out_shape=(sds(share, BF16), ROWS, ROWS, sds((2, VECTORS, D), F32)),
        scratch_shapes=[
            pltpu.VMEM((2, *share), BF16),
            pltpu.VMEM((2, *share), BF16),
            pltpu.VMEM(share, BF16),
            pltpu.VMEM(share, BF16),
            pltpu.VMEM((5, VECTORS, D), F32),
            pltpu.VMEM((5, VECTORS, D), F32),
            dma((RING, 2, 2)),
            dma((RING, 2, 2)),
            dma((RING, 2, 2)),
            dma((RING, 2, 2)),
            dma((RING - 1, 2, 2)),
            dma((RING - 1, 2, 2)),
            dma((RING - 1, 2, 2)),
            dma((RING - 1, 2, 2)),
            dma((5,)),
            dma((5,)),
            dma((2,)),
            dma((2,)),
        ],
        compiler_params=params(56, collective_id=2, has_side_effects=True),
        name="reduce_grads",
    )(*grads, *swapping, vectors)


def spread_kernel(layer, total, vectors, *refs):
    of_encoder, of_regressor, refs = refs[:4], refs[4:8], refs[8:]
    matrix, down, *picked, enc_out, reg_out, mlp_out, hidden_out = refs[:10]
    low, wide_rows, rows, sums, enc, reg, mlp, hidden, low_sem, wide_sem, rows_sem, picked_sem, sums_sem = refs[10:]
    in_sums = pltpu.make_async_copy(vectors, sums, sums_sem.at[0])
    in_sums.start()
    low_copies = [pltpu.make_async_copy(total.at[i], low.at[i], low_sem.at[i]) for i in range(SHARE)]
    for copy in low_copies:
        copy.start()
    for which, sources in enumerate((of_encoder, of_regressor)):

        @pl.when(layer[0] == which)
        def _(sources=sources):
            for k, source in enumerate(sources):
                pltpu.make_async_copy(source, rows.at[k], rows_sem.at[k]).start()

    copies = []
    in_sums.wait()
    for which in range(2):

        @pl.when(layer[0] == which)
        def _(which=which):
            enc[...] = sums[which, :6]
            reg[...] = sums[1 - which, :FFN_AT]
            for block, of in enumerate((which, 1 - which)):
                mlp[block] = sums[of, FFN_AT:HIDDEN_AT]
                for i in ALL_BLOCKS:
                    hidden[block : block + 1, columns(i)] = sums[of, HIDDEN_AT + i : HIDDEN_AT + i + 1]

    for k, (source, target) in enumerate(((enc, enc_out), (reg, reg_out), (mlp, mlp_out), (hidden, hidden_out))):
        copies.append(pltpu.make_async_copy(source, target, sums_sem.at[1 + k]))
        copies[k].start()

    for i in range(SHARE):
        low_copies[i].wait()
        wide_rows[i] = low[i].astype(F32)
        target = matrix.at[0, :, columns(i)] if i < BLOCKS else down.at[columns(i - BLOCKS), :]
        copies.append(pltpu.make_async_copy(wide_rows.at[i], target, wide_sem.at[i]))
        copies[-1].start()
    for k, target in enumerate(picked):
        pltpu.make_async_copy(of_encoder[k], rows.at[k], rows_sem.at[k]).wait()
        copies.append(pltpu.make_async_copy(rows.at[k], target, picked_sem.at[k]))
        copies[-1].start()
    for copy in copies:
        copy.wait()


def spread(layer, total, vectors, of_encoder, of_regressor):
    dma = pltpu.SemaphoreType.DMA
    return pl.pallas_call(
        spread_kernel,
        in_specs=[SMEM, *(ANY for _ in range(10))],
        out_specs=tuple(ANY for _ in range(10)),
        out_shape=(
            sds((1, D, FF), F32),
            sds((FF // 2, D), F32),
            *(ROWS for _ in range(4)),
            sds((6, D), F32),
            sds((FFN_AT, D), F32),
            sds((2, 4, D), F32),
            sds((2, FF), F32),
        ),
        scratch_shapes=[
            pltpu.VMEM((SHARE, D, D), BF16),
            pltpu.VMEM((SHARE, D, D), F32),
            pltpu.VMEM((4, CAP, D), BF16),
            pltpu.VMEM((2, VECTORS, D), F32),
            pltpu.VMEM((6, D), F32),
            pltpu.VMEM((FFN_AT, D), F32),
            pltpu.VMEM((2, 4, D), F32),
            pltpu.VMEM((2, FF), F32),
            dma((SHARE,)),
            dma((SHARE,)),
            dma((4,)),
            dma((4,)),
            dma((5,)),
        ],
        compiler_params=params(60),
        name="spread",
    )(layer, total, vectors, *of_encoder, *of_regressor)


def plain_reduce_grads(grads, swapping, vectors):
    odd = lax.rem(lax.axis_index("section"), 2)
    pair = [(0, 1), (1, 0), (2, 3), (3, 2)]
    grads = grads[0] + grads[1]
    theirs = lax.dynamic_index_in_dim(grads, 1 - odd, 0, keepdims=False)
    mine = lax.dynamic_index_in_dim(grads, odd, 0, keepdims=False)
    total = lax.psum(mine + lax.ppermute(theirs, "section", pair), "dp")
    vectors = lax.psum(vectors + lax.ppermute(vectors, "section", pair), "dp")
    return total, *map(swap_layers, swapping), jnp.stack([vectors, swap_layers(vectors)])


def swap_layers(block):
    return lax.ppermute(block, "section", [(0, 2), (1, 3), (2, 0), (3, 1)])


def to_regressor(block):
    return lax.ppermute(block, "section", [(0, 2), (1, 3)])


def to_encoder(block):
    return lax.ppermute(block, "section", [(2, 0), (3, 1)])


def body(
    vis_embed, latent_cot, reg_queries, out_cot, section_matrix, down_weight, enc_vectors, reg_vectors,
    mlp_vectors, hidden_bias, pos_table, image_lengths, vis_index, mask_index,
):
    section = lax.axis_index("section")
    odd = lax.rem(section, 2)
    is_reg = section >= 2
    layer = jnp.where(is_reg, 1, 0)
    weights = gather_weights(section_matrix, down_weight)
    r = lax.dynamic_index_in_dim(mlp_vectors, layer, 0, keepdims=False)
    c = lax.dynamic_slice_in_dim(hidden_bias, layer, 1, 0)
    packs = [(odd + 2 * i).reshape(1).astype(jnp.int32) for i in range(2)]
    vis = [lax.dynamic_slice_in_dim(vis_index, (odd + 2 * i) * CAP, CAP)[:, None] for i in range(2)]
    mask = [lax.dynamic_slice_in_dim(mask_index, (odd + 2 * i) * CAP, CAP)[:, None] for i in range(2)]

    rows_out, cot_out = lax.optimization_barrier(
        (jnp.where(is_reg, vis_embed, reg_queries), jnp.where(is_reg, latent_cot, out_cot))
    )
    incoming = swap_layers(rows_out)
    x = [vis_embed, incoming]
    queries = [incoming, reg_queries]

    def on_encoder(work, otherwise):
        return lax.cond(is_reg, otherwise, work)

    def on_regressor(work, otherwise):
        return lax.cond(is_reg, work, otherwise)

    def enc_forward(i):
        return encoder_forward(image_lengths, packs[i], x[i], enc_vectors, r, c, weights)

    def no_enc_forward():
        made = unset((ROWS, ROWS, *ENC_STATE))
        return made[0], made[1], tuple(made[2:])

    def enc_back(i, d_latents, kept, so_far):
        return encoder_back(
            image_lengths, packs[i], lat_cot[i], d_latents, x[i], kept[0], enc_vectors, r, so_far, weights, kept[2]
        )

    def reg_before():
        return tuple(
            tuple(regressor_before(image_lengths, packs[i], queries[i], vis[i], mask[i], pos_table, reg_vectors, weights))
            for i in range(2)
        )

    def no_reg_before():
        made = unset((*REG_BEFORE, *REG_BEFORE))
        return tuple(made[: len(REG_BEFORE)]), tuple(made[len(REG_BEFORE) :])

    def reg_work(i, latents, so_far):
        return lambda: regressor(
            image_lengths, packs[i], latents, queries[i], cot[i], reg_vectors, r, c, so_far, weights, before[i]
        )

    def no_reg_work():
        made = unset((ROWS, ROWS, ROWS, TOTALS, *REG_STATE))
        return (*made[:4], tuple(made[4:]))

    none = jnp.zeros((VECTORS, D), F32)
    enc1 = on_encoder(lambda: enc_forward(0), no_enc_forward)
    latents1 = to_regressor(enc1[1])
    before = on_regressor(reg_before, no_reg_before)
    swapped_cot = swap_layers(cot_out)
    lat_cot = [latent_cot, swapped_cot]
    cot = [swapped_cot, out_cot]
    enc2 = on_encoder(lambda: enc_forward(1), no_enc_forward)
    latents2 = to_regressor(enc2[1])
    reg1 = on_regressor(reg_work(0, latents1, none), no_reg_work)
    d_latents1 = to_encoder(reg1[1])
    reg2 = on_regressor(reg_work(1, latents2, reg1[3]), no_reg_work)
    d_latents2 = to_encoder(reg2[1])
    shares1, enc_totals, vis_grad1 = lax.cond(
        is_reg,
        lambda: (weight_grads(before[0], reg1[4]), *unset((TOTALS, ROWS))),
        lambda: enc_back(0, d_latents1, enc1, none)[::-1],
    )
    shares2, vectors, swapping = lax.cond(
        is_reg,
        lambda: (weight_grads(before[1], reg2[4]), reg2[3], reg1[0]),
        lambda: enc_back(1, d_latents2, enc2, enc_totals)[::-1],
    )
    reduce = reduce_grads if lax.axis_size("dp") == RING else plain_reduce_grads
    total, swapped1, swapped2, vectors = reduce((shares1, shares2), (swapping, reg1[2]), vectors)
    matrix_grad, down_grad, *others = spread(
        layer.reshape(1).astype(jnp.int32),
        total,
        vectors,
        (enc1[1], swapped1, vis_grad1, swapped2),
        (latents2, reg2[0], swapped1, reg2[2]),
    )
    return (*others[:4], matrix_grad, down_grad, *others[4:])


def solution(mesh):
    rows = P(("dp", "section"), None)
    in_specs = (
        rows, rows, rows, rows, P("section", None, None), P("section", None),
        P(), P(), P(), P(), P(), P("dp", None), P("dp"), P("dp"),
    )
    out_specs = (rows, rows, rows, rows, P("section", None, None), P("section", None), P(), P(), P(), P())
    return jax.shard_map(body, mesh=mesh, in_specs=in_specs, out_specs=out_specs, check_vma=False)
```

```python
import functools

import jax
import jax.numpy as jnp
from jax import lax
from jax.experimental import pallas as pl
from jax.experimental.pallas import tpu as pltpu
from jax.sharding import PartitionSpec as P

F32 = jnp.float32
BF16 = jnp.bfloat16
CAP = 384
IMGS = 4
SLOT = 128
PAD = IMGS * SLOT
D = 768
FF = 3072
LANES = 128
PAIRS = D // LANES
BLOCKS = FF // D
VECTORS = 24
EPS = 1e-06
MIB = 1 << 20
ANY = pl.BlockSpec(memory_space=pl.ANY)
SMEM = pl.BlockSpec(memory_space=pltpu.SMEM)


def params(limit=48, **more):
    return pltpu.CompilerParams(vmem_limit_bytes=limit * MIB, **more)


def sds(shape, dtype):
    return jax.ShapeDtypeStruct(shape, dtype)


def dot(a, b):
    return jnp.dot(a, b, preferred_element_type=F32)


def dot_nt(a, b):
    return lax.dot_general(a, b, (((1,), (1,)), ((), ())), preferred_element_type=F32)


def dot_tn(a, b):
    return lax.dot_general(a, b, (((0,), (0,)), ((), ())), preferred_element_type=F32)


def row(ref, i):
    return ref[i : i + 1, :]


def colsum(values):
    return jnp.sum(values, axis=0, keepdims=True)


def normalize(values):
    centred = values - jnp.mean(values, axis=-1, keepdims=True)
    spread = jnp.mean(centred * centred, axis=-1, keepdims=True)
    inverse = lax.rsqrt(spread + EPS)
    return centred * inverse, inverse


def norm_back(gradient, gain, normed, inverse):
    return scaled_norm_back(gradient * gain, normed, inverse)


def scaled_norm_back(scaled, normed, inverse):
    level = jnp.mean(scaled, axis=-1, keepdims=True)
    slope = jnp.mean(scaled * normed, axis=-1, keepdims=True)
    return inverse * (scaled - level - normed * slope)


def gelu_parts(t):
    e = jnp.exp(-0.5 * t * t)
    k = 1.0 / (1.0 + (0.3275911 * 0.7071067811865476) * jnp.abs(t))
    poly = k * (
        0.127414796
        + k * (-0.142248368 + k * (0.7107068705 + k * (-0.7265760135 + k * 0.5307027145)))
    )
    tail = poly * e
    phi = jnp.where(t >= 0.0, 1.0 - tail, tail)
    return t * phi, phi + t * (e * 0.3989422804014327)


def group_matrices(lens, pack, regroup, ungroup):
    def image(j, start):
        size = lens[pack, j]
        slots = pl.ds(pl.multiple_of(j * SLOT, SLOT), SLOT)
        place = lax.broadcasted_iota(jnp.int32, (SLOT, CAP), 0)
        rows = lax.broadcasted_iota(jnp.int32, (SLOT, CAP), 1)
        hit = (place + start == rows) & (place < size)
        regroup[slots, :] = jnp.where(hit, 1.0, 0.0).astype(BF16)
        place = lax.broadcasted_iota(jnp.int32, (CAP, SLOT), 1)
        rows = lax.broadcasted_iota(jnp.int32, (CAP, SLOT), 0)
        hit = (place + start == rows) & (place < size)
        ungroup[:, slots] = jnp.where(hit, 1.0, 0.0).astype(BF16)
        return start + size

    lax.fori_loop(0, IMGS, image, jnp.int32(0))


def lane_halves():
    lane = lax.broadcasted_iota(jnp.int32, (1, LANES), 1)
    first = jnp.where(lane < LANES // 2, 1.0, 0.0)
    return first.astype(BF16), (1.0 - first).astype(BF16)


def both_heads(block, halves):
    return jnp.concatenate([block * halves[0], block * halves[1]], axis=0)


def merge_heads(stacked):
    keys = stacked.shape[0] // 2
    lane = lax.broadcasted_iota(jnp.int32, (keys, LANES), 1)
    return jnp.where(lane < LANES // 2, stacked[:keys], stacked[keys:])


def softmax(scores):
    raised = jnp.exp(scores - jnp.max(scores, axis=0, keepdims=True))
    return (raised * (1.0 / jnp.sum(raised, axis=0, keepdims=True))).astype(BF16)


def keys_of(packed, first, parts, rows, cols, halves):
    return both_heads(
        jnp.concatenate([packed[first + 2 * m, rows, cols] for m in range(parts)], axis=0), halves
    )


def attend(lens, pack, packed, probs, mixed_slots, parts, done):
    halves = lane_halves()
    keys = SLOT * parts
    place = lax.bitwise_and(lax.broadcasted_iota(jnp.int32, (keys, SLOT), 0), SLOT - 1)
    for j in range(IMGS):
        rows = slice(j * SLOT, (j + 1) * SLOT)
        valid = place < lens[pack, j]
        for g in range(PAIRS):
            cols = slice(g * LANES, (g + 1) * LANES)
            scores = dot_nt(keys_of(packed, 1, parts, rows, cols, halves), packed[0, rows, cols])
            low = jnp.concatenate(
                [softmax(jnp.where(valid, part, -1e30)) for part in (scores[:keys], scores[keys:])], axis=0
            )
            probs[j, g] = low
            mixed_slots[rows, cols] = dot_tn(low, keys_of(packed, 2, parts, rows, cols, halves)).astype(BF16)
        done(j)


def attend_back(packed, probs, mixed_slots, d_mixed_slots, parts, ready, beside):
    halves = lane_halves()
    keys = SLOT * parts
    less = both_heads(jnp.full((keys, LANES), -1.0, BF16), halves)

    def image(j, carry):
        ready(j)
        rows = pl.ds(pl.multiple_of(j * SLOT, SLOT), SLOT)
        after = beside(j)
        for g in range(PAIRS):
            cols = slice(g * LANES, (g + 1) * LANES)
            d_out = d_mixed_slots[rows, cols]
            centre = (d_out.astype(F32) * mixed_slots[rows, cols].astype(F32)).astype(BF16)
            low = probs[j, g]
            d_prob = dot_nt(
                jnp.concatenate([keys_of(packed, 2, parts, rows, cols, halves), less], axis=1),
                jnp.concatenate([d_out, centre], axis=1),
            )
            d_scores = (low.astype(F32) * d_prob).astype(BF16)
            q = packed[0, rows, cols]
            zero = jnp.zeros_like(q)
            sides = jnp.concatenate(
                [jnp.concatenate([q, zero], axis=1), jnp.concatenate([zero, d_out], axis=1)], axis=0
            )
            d_kv = dot(jnp.concatenate([d_scores, low], axis=1), sides)
            d_q = dot_tn(d_scores, keys_of(packed, 1, parts, rows, cols, halves)) * 0.125
            packed[0, rows, cols] = d_q.astype(BF16)
            for side in range(2):
                merged = merge_heads(d_kv[:, side * LANES : (side + 1) * LANES]).astype(BF16)
                for m in range(parts):
                    packed[1 + side + 2 * m, rows, cols] = merged[m * SLOT : (m + 1) * SLOT]
        if after is not None:
            after()
        return carry

    lax.fori_loop(0, IMGS, image, 0)


ROWS = sds((CAP, D), BF16)
WIDE = sds((CAP, FF), BF16)
TOTALS = sds((VECTORS, D), F32)
FFN_AT = 10
HIDDEN_AT = FFN_AT + 4
ENC_STATE = (
    ROWS,
    sds((3, PAD, D), BF16),
    sds((IMGS, PAIRS, 2 * SLOT, SLOT), BF16),
    sds((PAD, D), BF16),
    ROWS,
    ROWS,
    ROWS,
    WIDE,
    WIDE,
    ROWS,
)
REG_BEFORE = (
    sds((3, CAP, D), BF16),
    sds((3, PAD, D), BF16),
    sds((2, CAP, D), F32),
)
REG_STATE = (
    sds((2, CAP, D), BF16),
    sds((5, CAP, D), BF16),
    ROWS,
    ROWS,
    ROWS,
    WIDE,
    WIDE,
    ROWS,
)


def full(shape):
    return pl.BlockSpec(shape, lambda i: (0,) * len(shape))


VMEM = pl.BlockSpec(memory_space=pltpu.VMEM)


def scratch(shape):
    return pltpu.VMEM(shape.shape, shape.dtype)


def unset(shapes):
    def kernel(*refs):
        del refs

    return pl.pallas_call(
        kernel, out_shape=shapes, out_specs=tuple(ANY for _ in shapes), name="unset"
    )()


class Copies:
    def __init__(self, semaphores):
        self.semaphores, self.used, self.open = semaphores, 0, []

    def take(self, count=1):
        self.used += count
        return self.used - count

    def start(self, source, target):
        copy = pltpu.make_async_copy(source, target, self.semaphores.at[self.take()])
        copy.start()
        return copy

    def leave(self, source, target):
        self.open.append(self.start(source, target))

    def halves(self, *pairs):
        first = self.take(2 * len(pairs))

        def copies(i):
            rows = half_rows(i)
            return [
                pltpu.make_async_copy(source.at[rows, :], target.at[rows, :], self.semaphores.at[first + 2 * k + i])
                for k, (source, target) in enumerate(pairs)
            ]

        def start(i):
            for copy in copies(i):
                copy.start()

        self.open += copies(0) + copies(1)
        return start

    def finish(self):
        for copy in self.open:
            copy.wait()


COPIES = pltpu.SemaphoreType.DMA((80,))


def columns(i):
    return slice(i * D, (i + 1) * D)


class Weights:
    def __init__(self, copies, weights, held):
        self.copies, self.weights, self.held, self.started = copies, weights, held, {}

    def target(self, i):
        kind, block = divmod(i, BLOCKS)
        held = self.held[kind]
        return held.at[columns(block), :] if kind == 2 else held.at[:, columns(block)]

    def start(self, *order):
        for i in order:
            self.started[i] = self.copies.start(self.weights.at[i], self.target(i))

    def wait(self, *which):
        for i in which:
            self.started[i].wait()


WEIGHT_SCRATCH = [pltpu.VMEM((D, FF), BF16), pltpu.VMEM((D, FF), BF16), pltpu.VMEM((FF, D), BF16)]
ALL_BLOCKS = range(BLOCKS)
UPS = [BLOCKS + i for i in ALL_BLOCKS]
DOWNS = [2 * BLOCKS + i for i in ALL_BLOCKS]


def wide(i):
    return pl.ds(pl.multiple_of(i * D, D), D)


HALF = CAP // 2


def half_rows(i):
    return pl.ds(pl.multiple_of(i * HALF, HALF), HALF)


def feed_forward(weights, mid, r, c, out, state, made):
    normed, active, slope, branch = state
    centred, _ = normalize(mid[...].astype(F32))
    normed[...] = (centred * row(r, 0) + row(r, 1)).astype(BF16)
    made("normed")
    _, up, down = weights.held
    weights.wait(*UPS, *DOWNS)

    def part(i, carry):
        rows = half_rows(i)
        value, steep = gelu_parts(dot(normed[rows, :], up[...]) + c[...])
        active[rows, :] = value.astype(BF16)
        slope[rows, :] = steep.astype(BF16)
        made(i)
        summed = dot(active[rows, :], down[...]) + row(r, 2)
        branch[rows, :] = summed.astype(BF16)
        out[rows, :] = (mid[rows, :].astype(F32) + row(r, 3) * summed).astype(BF16)
        return carry

    lax.fori_loop(0, 2, part, 0)
    made("branch")


def feed_forward_back(weights, ready, g, mid, r, refs, totals, residual, made):
    slope, branch, d_branch = refs
    _, up, down = weights.held
    d_branch[...] = (g * row(r, 3)).astype(BF16)
    made("branch")
    add_row(totals, FFN_AT + 2, colsum(d_branch[...].astype(F32)))
    ready("branch")
    add_row(totals, FFN_AT + 3, colsum(g * branch[...].astype(F32)))
    for i in ALL_BLOCKS:
        weights.wait(2 * BLOCKS + i)
        ready(i)
        d_active = dot_nt(d_branch[...], down[columns(i), :])
        d_hidden = (d_active * slope[:, columns(i)].astype(F32)).astype(BF16)
        slope[:, columns(i)] = d_hidden
        made(i)
        add_row(totals, HIDDEN_AT + i, colsum(d_hidden.astype(F32)))
    weights.wait(*UPS)
    d_normed = dot_nt(slope[...], up[...])
    normed, inverse = normalize(mid[...].astype(F32))
    add_row(totals, FFN_AT, colsum(d_normed * normed))
    add_row(totals, FFN_AT + 1, colsum(d_normed))
    residual[...] = (g + norm_back(d_normed, row(r, 0), normed, inverse)).astype(BF16).astype(F32)


def attention_back(parts, weights, e, refs, totals, ready, made, beside):
    residual, branch, d_branch, regroup, ungroup, packed, probs, mixed_slots, d_slots, d_flat = refs
    last = 1 + 4 * parts
    g = residual[...]
    ready("branch")
    d_branch[...] = (g * row(e, last)).astype(BF16)
    made("branch")
    add_row(totals, last, colsum(g * branch[...].astype(F32)))
    add_row(totals, last - 1, colsum(d_branch[...].astype(F32)))
    weights.wait(3)
    d_mixed = dot(d_branch[...], weights.held[0][:, columns(3)]).astype(BF16)
    d_slots[...] = dot(regroup[...], d_mixed).astype(BF16)
    ready("packed")
    attend_back(packed, probs, mixed_slots, d_slots, parts, ready, beside)
    for m in range(1 + 2 * parts):
        d_flat[m] = dot(ungroup[...], packed[m]).astype(BF16)
        made(m)


def add_row(totals, i, value):
    totals[i : i + 1] += value


def nothing(name):
    del name


class Shares:
    def __init__(self, copies, blocks, share):
        self.semaphores, self.blocks, self.share = copies.semaphores, blocks, share
        self.first = copies.take(3 * BLOCKS)

    def copy(self, kind, i):
        section, block = (lax.div(i, 2), BLOCKS + lax.rem(i, 2)) if kind == 2 else (kind, i)
        place = kind * BLOCKS + i
        return pltpu.make_async_copy(
            self.blocks.at[place], self.share.at[section, block], self.semaphores.at[self.first + place]
        )

    def put(self, kind, i, product):
        self.blocks[kind * BLOCKS + i] = product.astype(BF16)
        self.copy(kind, i).start()

    def feed_forward(self, normed, d_hidden, active, d_branch):
        def step(i):
            self.blocks[BLOCKS + i] = dot_tn(normed[...], d_hidden[:, wide(i)]).astype(BF16)
            self.blocks[2 * BLOCKS + i] = dot_tn(active[:, wide(i)], d_branch[...]).astype(BF16)

            def after():
                for kind in (1, 2):
                    self.copy(kind, i).start()

            return after

        return step

    def finish(self):
        for kind in range(3):
            for i in ALL_BLOCKS:
                self.copy(kind, i).wait()


def encoder_forward_kernel(lens, which, x, e, r, c, given, mid, out, *refs):
    kept, scratch = refs[: len(ENC_STATE)], refs[len(ENC_STATE) :]
    *held, flat, regroup, ungroup, semaphores = scratch[: 3 + 4]
    state = scratch[3 + 4 :]
    normed, packed, probs, mixed_slots, mixed, branch, *ffn = state
    pack = which[0]
    copies = Copies(semaphores)
    weights = Weights(copies, given, held)
    weights.start(*ALL_BLOCKS, *UPS, *DOWNS)
    values = x[...].astype(F32)
    centred, _ = normalize(values)
    normed[...] = (centred * row(e, 0) + row(e, 1)).astype(BF16)
    copies.leave(normed, kept[0])
    group_matrices(lens, pack, regroup, ungroup)
    qkvo = weights.held[0]
    weights.wait(0)
    flat[0] = ((dot(normed[...], qkvo[:, columns(0)]) + row(e, 2)).astype(BF16) * 0.125).astype(BF16)
    weights.wait(1)
    flat[1] = dot(normed[...], qkvo[:, columns(1)]).astype(BF16)
    weights.wait(2)
    flat[2] = (dot(normed[...], qkvo[:, columns(2)]) + row(e, 3)).astype(BF16)
    for m in range(3):
        packed[m] = dot(regroup[...], flat[m]).astype(BF16)
        copies.leave(packed.at[m], kept[1].at[m])
    attend(lens, pack, packed, probs, mixed_slots, 1, lambda j: copies.leave(probs.at[j], kept[2].at[j]))
    copies.leave(mixed_slots, kept[3])
    mixed[...] = dot(ungroup[...], mixed_slots[...]).astype(BF16)
    copies.leave(mixed, kept[4])
    weights.wait(3)
    summed = dot_nt(mixed[...], qkvo[:, columns(3)]) + row(e, 4)
    branch[...] = summed.astype(BF16)
    copies.leave(branch, kept[5])
    mid[...] = (values + row(e, 5) * summed).astype(BF16)

    half_made = copies.halves((ffn[1], kept[7]), (ffn[2], kept[8]))

    def made(name):
        if isinstance(name, str):
            source, target = (ffn[0], kept[6]) if name == "normed" else (ffn[3], kept[9])
            copies.leave(source, target)
        else:
            half_made(name)

    feed_forward(weights, mid, r, c, out, ffn, made)
    copies.finish()


def encoder_forward(lens, which, x, e, r, c, weights):
    made = pl.pallas_call(
        encoder_forward_kernel,
        in_specs=[SMEM, SMEM, VMEM, VMEM, VMEM, VMEM, ANY],
        out_specs=(VMEM, VMEM, *(ANY for _ in ENC_STATE)),
        out_shape=(ROWS, ROWS, *ENC_STATE),
        scratch_shapes=[
            *WEIGHT_SCRATCH,
            pltpu.VMEM((3, CAP, D), BF16),
            pltpu.VMEM((PAD, CAP), BF16),
            pltpu.VMEM((CAP, PAD), BF16),
            COPIES,
            *map(scratch, ENC_STATE),
        ],
        compiler_params=params(58),
        name="encoder_forward",
    )(lens, which, x, e, r, c, weights)
    return made[0], made[1], tuple(made[2:])


def encoder_back_kernel(lens, which, g1, g2, x, mid, e, r, so_far, given, *refs):
    state, refs = refs[: len(ENC_STATE)], refs[len(ENC_STATE) :]
    d_x, totals, share, *held, regroup, ungroup, d_slots, d_branch, d_f_branch, d_flat, residual, blocks, semaphores = (
        refs[: 3 + 3 + 9]
    )
    normed, packed, probs, mixed_slots, mixed, branch, f_normed, active, slope, f_branch = refs[3 + 3 + 9 :]
    copies = Copies(semaphores)
    weights = Weights(copies, given, held)
    coming = {"branch": copies.start(state[9], f_branch)}
    for i in ALL_BLOCKS:
        weights.start(2 * BLOCKS + i)
        coming[i] = copies.start(state[8].at[:, columns(i)], slope.at[:, columns(i)])
    weights.start(*UPS, 3)
    later = {"branch": copies.start(state[5], branch)}
    later["packed"] = copies.start(state[1], packed)
    later["mixed"] = copies.start(state[3], mixed_slots)
    probs_in = [copies.start(state[2].at[j], probs.at[j]) for j in range(IMGS)]
    late = [copies.start(state[i], ref) for i, ref in ((6, f_normed), (7, active), (0, normed), (4, mixed))]
    weights.start(0, 1, 2)
    shares = Shares(copies, blocks, share)
    totals[...] = so_far[...]
    group_matrices(lens, which[0], regroup, ungroup)
    g = g1[...].astype(F32) + g2[...].astype(F32)
    feed_forward_back(
        weights, lambda name: coming[name].wait(), g, mid, r, (slope, f_branch, d_f_branch), totals, residual, nothing
    )
    for copy in late:
        copy.wait()

    def ready(name):
        if name == "branch":
            later["branch"].wait()
        elif name == "packed":
            later["packed"].wait()
            later["mixed"].wait()
            for copy in probs_in:
                copy.wait()

    attention_back(
        1, weights, e, (residual, branch, d_branch, regroup, ungroup, packed, probs, mixed_slots, d_slots, d_flat),
        totals, ready, nothing, shares.feed_forward(f_normed, slope, active, d_f_branch),
    )

    def first_block(i, carry):
        shares.put(0, i, dot_tn(normed[...], d_flat[i]))
        return carry

    lax.fori_loop(0, 3, first_block, 0)
    shares.put(0, 3, dot_tn(d_branch[...], mixed[...]))
    weights.wait(0, 1, 2)
    qkvo = weights.held[0]
    d_normed = dot_nt(d_flat[0], qkvo[:, columns(0)])
    for m in (1, 2):
        d_normed += dot_nt(d_flat[m], qkvo[:, columns(m)])
    values, inverse = normalize(x[...].astype(F32))
    add_row(totals, 0, colsum(d_normed * values))
    add_row(totals, 1, colsum(d_normed))
    add_row(totals, 2, colsum(d_flat[0].astype(F32)))
    add_row(totals, 3, colsum(d_flat[2].astype(F32)))
    d_x[...] = (residual[...] + norm_back(d_normed, row(e, 0), values, inverse)).astype(BF16)
    shares.finish()


def encoder_back(lens, which, g1, g2, x, mid, e, r, so_far, weights, state):
    return pl.pallas_call(
        encoder_back_kernel,
        in_specs=[SMEM, SMEM, *(VMEM for _ in range(7)), ANY, *(ANY for _ in ENC_STATE)],
        out_specs=(VMEM, VMEM, ANY),
        out_shape=(ROWS, TOTALS, sds((2, SHARE, D, D), BF16)),
        scratch_shapes=[
            *WEIGHT_SCRATCH,
            pltpu.VMEM((PAD, CAP), BF16),
            pltpu.VMEM((CAP, PAD), BF16),
            pltpu.VMEM((PAD, D), BF16),
            scratch(ROWS),
            scratch(ROWS),
            pltpu.VMEM((3, CAP, D), BF16),
            pltpu.VMEM((CAP, D), F32),
            pltpu.VMEM((3 * BLOCKS, D, D), BF16),
            COPIES,
            *map(scratch, ENC_STATE),
        ],
        compiler_params=params(58),
        name="encoder_back",
    )(lens, which, g1, g2, x, mid, e, r, so_far, weights, *state)


def table_rows(indices, table):
    places = lax.broadcasted_iota(jnp.int32, (indices.shape[0], table.shape[0]), 1)
    chosen = jnp.where(places == indices[...], 1.0, 0.0).astype(BF16)
    values = table[...]
    top = values.astype(BF16)
    values = values - top.astype(F32)
    middle = values.astype(BF16)
    bottom = (values - middle.astype(F32)).astype(BF16)
    return (dot(chosen, top) + dot(chosen, middle)) + dot(chosen, bottom)


def regressor_before_kernel(lens, which, queries, vis, mask, table, e, given, normed, packed, sources, held, flat, regroup, ungroup, semaphores):
    copies = Copies(semaphores)
    weights = Weights(copies, given, [held])
    weights.start(0, 1, 2)
    group_matrices(lens, which[0], regroup, ungroup)
    sources[1] = table_rows(vis, table)
    residual = queries[...].astype(F32)
    source = residual + table_rows(mask, table)
    sources[0] = source
    centred, _ = normalize(source)
    normed[0] = (centred * row(e, 0) + row(e, 1)).astype(BF16)
    normed[1] = (centred * row(e, 2) + row(e, 3)).astype(BF16)
    centred, _ = normalize(residual)
    normed[2] = (centred * row(e, 4) + row(e, 5)).astype(BF16)
    weights.wait(0, 1, 2)
    flat[0] = ((dot(normed[0], held[:, columns(0)]) + row(e, 6)).astype(BF16) * 0.125).astype(BF16)
    flat[1] = dot(normed[1], held[:, columns(1)]).astype(BF16)
    flat[2] = (dot(normed[2], held[:, columns(2)]) + row(e, 7)).astype(BF16)
    for m in range(3):
        packed[m] = dot(regroup[...], flat[m]).astype(BF16)


def regressor_before(lens, which, queries, vis, mask, table, e, weights):
    return pl.pallas_call(
        regressor_before_kernel,
        in_specs=[SMEM, SMEM, *(VMEM for _ in range(5)), ANY],
        out_specs=(VMEM, VMEM, VMEM),
        out_shape=REG_BEFORE,
        scratch_shapes=[
            pltpu.VMEM((D, FF), BF16),
            pltpu.VMEM((3, CAP, D), BF16),
            pltpu.VMEM((PAD, CAP), BF16),
            pltpu.VMEM((CAP, PAD), BF16),
            COPIES,
        ],
        compiler_params=params(48),
        name="regressor_before",
    )(lens, which, queries, vis, mask, table, e, weights)


def regressor_kernel(
    lens, which, latents, queries, cot, e, r, c, so_far, given, packed_before, sources_before,
    regressed, d_latents, d_queries, totals, *refs,
):
    kept, refs = refs[: len(REG_STATE)], refs[len(REG_STATE) :]
    (
        *held, regroup, ungroup, packed, probs, mixed_slots, d_slots, sources, branch, slope, f_branch, mid, residual,
        flat, semaphores, normed, d_flat, mixed, d_branch, f_normed, _, active, d_f_branch,
    ) = refs
    pack = which[0]
    copies = Copies(semaphores)
    weights = Weights(copies, given, held)
    in_sources = copies.start(sources_before, sources)
    weights.start(1, 2)
    in_packed = [copies.start(packed_before.at[i], packed.at[m]) for i, m in enumerate((0, 3, 4))]
    weights.start(3, *UPS, *DOWNS, 0)
    in_cot = copies.start(cot, d_f_branch)
    qkvo = weights.held[0]
    group_matrices(lens, pack, regroup, ungroup)
    incoming = latents[...].astype(F32)
    centred, _ = normalize(incoming)
    normed[1] = (centred * row(e, 4) + row(e, 5)).astype(BF16)
    in_sources.wait()
    k_source = incoming + sources[1]
    sources[1] = k_source
    centred, _ = normalize(k_source)
    normed[0] = (centred * row(e, 2) + row(e, 3)).astype(BF16)
    copies.leave(normed, kept[0])
    weights.wait(1)
    flat[0] = dot(normed[0], qkvo[:, columns(1)]).astype(BF16)
    weights.wait(2)
    flat[1] = (dot(normed[1], qkvo[:, columns(2)]) + row(e, 7)).astype(BF16)
    for m in range(2):
        packed[1 + m] = dot(regroup[...], flat[m]).astype(BF16)
    for copy in in_packed:
        copy.wait()
    attend(lens, pack, packed, probs, mixed_slots, 2, nothing)
    mixed[...] = dot(ungroup[...], mixed_slots[...]).astype(BF16)
    copies.leave(mixed, kept[2])
    weights.wait(3)
    summed = dot_nt(mixed[...], qkvo[:, columns(3)]) + row(e, 8)
    branch[...] = summed.astype(BF16)
    mid[...] = (queries[...].astype(F32) + row(e, 9) * summed).astype(BF16)

    half_made = copies.halves((active, kept[6]))

    def forward_made(name):
        if not isinstance(name, str):
            half_made(name)
        elif name == "normed":
            copies.leave(f_normed, kept[4])

    feed_forward(weights, mid, r, c, regressed, (f_normed, active, slope, f_branch), forward_made)

    totals[...] = so_far[...]
    waited = Weights(copies, given, held)
    waited.wait = nothing_more

    def back_made(name):
        if name == "branch":
            copies.leave(d_f_branch, kept[7])
        else:
            copies.leave(slope.at[:, columns(name)], kept[5].at[:, columns(name)])

    in_cot.wait()
    feed_forward_back(
        waited, nothing, d_f_branch[...].astype(F32), mid, r, (slope, f_branch, d_f_branch), totals, residual, back_made
    )

    def attention_made(name):
        if name == "branch":
            copies.leave(d_branch, kept[3])
        else:
            copies.leave(d_flat.at[name], kept[1].at[name])

    attention_back(
        2, waited, e, (residual, branch, d_branch, regroup, ungroup, packed, probs, mixed_slots, d_slots, d_flat),
        totals, nothing, attention_made, nothing,
    )
    weights.wait(0)
    add_row(totals, 6, colsum(d_flat[0].astype(F32)))
    add_row(totals, 7, colsum(d_flat[2].astype(F32)) + colsum(d_flat[4].astype(F32)))
    values, inverse = normalize(sources[0])
    grad = dot_nt(d_flat[0], qkvo[:, columns(0)])
    add_row(totals, 0, colsum(grad * values))
    add_row(totals, 1, colsum(grad))
    scaled = grad * row(e, 0)
    grad = dot_nt(d_flat[3], qkvo[:, columns(1)])
    k_gain = colsum(grad * values)
    k_offset = colsum(grad)
    scaled += grad * row(e, 2)
    total = residual[...] + scaled_norm_back(scaled, values, inverse)
    values, inverse = normalize(queries[...].astype(F32))
    grad = dot_nt(d_flat[4], qkvo[:, columns(2)])
    v_gain = colsum(grad * values)
    v_offset = colsum(grad)
    total += norm_back(grad, row(e, 4), values, inverse)
    d_queries[...] = total.astype(BF16)
    values, inverse = normalize(sources[1])
    grad = dot_nt(d_flat[1], qkvo[:, columns(1)])
    add_row(totals, 2, k_gain + colsum(grad * values))
    add_row(totals, 3, k_offset + colsum(grad))
    total = norm_back(grad, row(e, 2), values, inverse)
    values, inverse = normalize(latents[...].astype(F32))
    grad = dot_nt(d_flat[2], qkvo[:, columns(2)])
    add_row(totals, 4, v_gain + colsum(grad * values))
    add_row(totals, 5, v_offset + colsum(grad))
    total += norm_back(grad, row(e, 4), values, inverse)
    d_latents[...] = total.astype(BF16)
    copies.finish()


def nothing_more(*which):
    del which


def regressor(lens, which, latents, queries, cot, e, r, c, so_far, weights, before):
    made = pl.pallas_call(
        regressor_kernel,
        in_specs=[SMEM, SMEM, VMEM, VMEM, ANY, *(VMEM for _ in range(4)), ANY, ANY, ANY],
        out_specs=(VMEM, VMEM, VMEM, VMEM, *(ANY for _ in REG_STATE)),
        out_shape=(ROWS, ROWS, ROWS, TOTALS, *REG_STATE),
        scratch_shapes=[
            *WEIGHT_SCRATCH,
            pltpu.VMEM((PAD, CAP), BF16),
            pltpu.VMEM((CAP, PAD), BF16),
            pltpu.VMEM((5, PAD, D), BF16),
            pltpu.VMEM((IMGS, PAIRS, 4 * SLOT, SLOT), BF16),
            pltpu.VMEM((PAD, D), BF16),
            pltpu.VMEM((PAD, D), BF16),
            pltpu.VMEM((2, CAP, D), F32),
            scratch(ROWS),
            scratch(WIDE),
            scratch(ROWS),
            scratch(ROWS),
            pltpu.VMEM((CAP, D), F32),
            pltpu.VMEM((2, CAP, D), BF16),
            COPIES,
            *(scratch(s) if i != 5 else pltpu.VMEM((8, LANES), BF16) for i, s in enumerate(REG_STATE)),
        ],
        compiler_params=params(60),
        name="regressor",
    )(lens, which, latents, queries, cot, e, r, c, so_far, weights, before[1], before[2])
    return (*made[:4], tuple(made[4:]))


SHARE = BLOCKS + BLOCKS // 2


def weight_grads_kernel(*refs):
    sources, share, held, blocks, semaphores = refs[:9], refs[9], refs[10:19], refs[19], refs[20]
    copies = Copies(semaphores)
    order = (5, 6, 7, 8, 0, 1, 2, 3, 4)
    started = {i: copies.start(sources[i], held[i]) for i in order}
    before, normed, d_flat, mixed, d_branch, f_normed, d_hidden, active, d_f_branch = held
    shares = Shares(copies, blocks, share)
    for i in order[:4]:
        started[i].wait()
    work = shares.feed_forward(f_normed, d_hidden, active, d_f_branch)

    def ffn_blocks(i, carry):
        work(i)()
        return carry

    lax.fori_loop(0, BLOCKS, ffn_blocks, 0)
    for i in order[4:]:
        started[i].wait()
    shares.put(0, 0, dot_tn(before[0], d_flat[0]))

    def pair_block(i, carry):
        shares.put(0, i, dot_tn(normed[i - 1], d_flat[i]) + dot_tn(before[i], d_flat[i + 2]))
        return carry

    lax.fori_loop(1, 3, pair_block, 0)
    shares.put(0, 3, dot_tn(d_branch[...], mixed[...]))
    shares.finish()


def weight_grads(before, state):
    return pl.pallas_call(
        weight_grads_kernel,
        in_specs=[ANY] * 9,
        out_specs=ANY,
        out_shape=sds((2, SHARE, D, D), BF16),
        scratch_shapes=[
            scratch(REG_BEFORE[0]),
            *map(scratch, REG_STATE),
            pltpu.VMEM((3 * BLOCKS, D, D), BF16),
            COPIES,
        ],
        compiler_params=params(),
        name="weight_grads",
    )(before[0], *state)


MESH = pl.DeviceIdType.MESH


def gather_weights_kernel(matrix, down, weights, send, receive, local):
    dp, section = lax.axis_index("dp"), lax.axis_index("section")
    odd = lax.rem(section, 2)
    partner = (dp, section + 1 - 2 * odd)
    barrier = pltpu.get_barrier_semaphore()
    pl.semaphore_signal(barrier, inc=1, device_id=partner, device_id_type=MESH)
    pl.semaphore_wait(barrier, 1)
    places = [(matrix.at[0, :, pl.ds(i * D, D)], odd * BLOCKS + i) for i in range(BLOCKS)]
    places += [(down.at[pl.ds(i * D, D), :], 2 * BLOCKS + odd * (BLOCKS // 2) + i) for i in range(BLOCKS // 2)]
    copies = []
    for i, (source, place) in enumerate(places):
        away = pltpu.make_async_remote_copy(
            source, weights.at[place], send.at[i], receive.at[i], device_id=partner, device_id_type=MESH
        )
        away.start()
        here = pltpu.make_async_copy(source, weights.at[place], local.at[i])
        here.start()
        copies += [away, here]
    for copy in copies:
        copy.wait()


def gather_weights(matrix, down):
    vmem = pl.BlockSpec(memory_space=pltpu.VMEM)
    return pl.pallas_call(
        gather_weights_kernel,
        in_specs=[vmem, vmem],
        out_specs=ANY,
        out_shape=sds((3 * BLOCKS, D, D), matrix.dtype),
        scratch_shapes=[pltpu.SemaphoreType.DMA((SHARE,)) for _ in range(3)],
        compiler_params=params(collective_id=1, has_side_effects=True),
        name="gather_weights",
    )(matrix, down)


RING = 8
SEGMENT = D // RING
PART = SEGMENT // 2
CHAIN = SHARE // 2


def ring_place(d):
    odd = lax.rem(d, 2)
    return (1 - odd) * lax.div(d, 2) + odd * (RING - 1 - lax.div(d, 2))


def ring_device(place):
    place = lax.rem(place + RING, RING)
    late = lax.div(place, RING // 2)
    return (1 - late) * 2 * place + late * (2 * (RING - 1 - place) + 1)


def reduce_kernel(
    grads1, grads2, swapping1, swapping2, vectors, out, swapped1, swapped2, out_vectors,
    mine, partner_part, landing, final, v_sum, v_in,
    out_sem, pair_send, pair_receive, own_sem, ring_send, ring_receive, last_send, last_receive,
    v_send, v_receive, swap_send, swap_receive,
):
    d, section = lax.axis_index("dp"), lax.axis_index("section")
    odd = lax.rem(section, 2)
    place = ring_place(d)
    across = (d, section + 2 - 4 * lax.div(section, 2))
    pair = (d, section + 1 - 2 * odd)
    ways = ((ring_device(place + 1), section), (ring_device(place - 1), section))
    packs = (grads1, grads2)

    def flipped(bit):
        return d + bit - 2 * bit * lax.rem(lax.div(d, bit), 2)

    levels = (pair, (flipped(1), section), (flipped(2), section), (flipped(4), section), across)
    barrier = pltpu.get_barrier_semaphore()
    for other in (*ways, *levels):
        pl.semaphore_signal(barrier, inc=1, device_id=other, device_id_type=MESH)

    def rows_of(step, way):
        segment = lax.rem(place + (step if way else -step) + 2 * RING, RING)
        return pl.ds(pl.multiple_of(segment * SEGMENT + way * PART, 8), PART)

    def own_copy(step, way, k):
        rows = rows_of(step, way)
        return pltpu.make_async_copy(
            packs[k].at[odd, :, rows, :], mine.at[k, :, rows, :], own_sem.at[step, way, k]
        )

    pl.semaphore_wait(barrier, len(ways) + len(levels))

    def remote(source, target, send, receive, device):
        return pltpu.make_async_remote_copy(source, target, send, receive, device_id=device, device_id_type=MESH)

    def pair_copy(step, way, k):
        rows = rows_of(step, way)
        return remote(
            packs[k].at[1 - odd, :, rows, :], partner_part.at[k, :, rows, :],
            pair_send.at[step, way, k], pair_receive.at[step, way, k], pair,
        )

    def start_inputs(step):
        for way in range(2):
            for k in range(2):
                pair_copy(step, way, k).start()
                own_copy(step, way, k).start()

    start_inputs(0)
    start_inputs(1)
    swaps = [
        remote(source, target, swap_send.at[k], swap_receive.at[k], across)
        for k, (source, target) in enumerate(((swapping1, swapped1), (swapping2, swapped2)))
    ]
    for swap in swaps:
        swap.start()

    def vector_copy(level):
        return remote(v_sum.at[level], v_in.at[level], v_send.at[level], v_receive.at[level], levels[level])

    def vector_next(level):
        vector_copy(level).wait()
        if level + 1 < len(levels):
            v_sum[level + 1] = v_sum[level] + v_in[level]
            vector_copy(level + 1).start()

    v_sum[0] = vectors[...]
    vector_copy(0).start()

    def blocks(chain):
        return pl.ds(chain * CHAIN, CHAIN)

    def ring_copy(step, way, chain):
        rows = rows_of(step, way)
        return remote(
            mine.at[0, blocks(chain), rows, :], landing.at[blocks(chain), rows, :],
            ring_send.at[step, way, chain], ring_receive.at[step, way, chain], ways[way],
        )

    def incoming(step, way, chain):
        rows = rows_of(step + 1, way)
        return remote(
            mine.at[0, blocks(chain), rows, :], landing.at[blocks(chain), rows, :],
            ring_send.at[step, way, chain], ring_receive.at[step, way, chain], ways[way],
        )

    def own_total(chain, rows):
        part = (blocks(chain), rows, slice(None))
        both = [ref[(k, *part)].astype(F32) for ref in (mine, partner_part) for k in range(2)]
        return (both[0] + both[1]) + (both[2] + both[3])

    def total_of(chain, rows):
        return (own_total(chain, rows) + landing[blocks(chain), rows, :].astype(F32)).astype(BF16)

    def pair_here(step, way):
        for k in range(2):
            own_copy(step, way, k).wait()
            pair_copy(step, way, k).wait_recv()

    for way in range(2):
        pair_here(0, way)
        rows = rows_of(0, way)
        for chain in range(2):
            mine[0, blocks(chain), rows, :] = own_total(chain, rows).astype(BF16)
            ring_copy(0, way, chain).start()
    start_inputs(2)
    vector_next(0)

    def reduce_step(step, carry):
        for chain in range(2):
            for way in range(2):
                if chain == 0:
                    pair_here(step, way)
                incoming(step - 1, way, chain).wait_recv()
                rows = rows_of(step, way)
                mine[0, blocks(chain), rows, :] = total_of(chain, rows)
                ring_copy(step, way, chain).start()

        @pl.when(step + 2 < RING)
        def _():
            start_inputs(step + 2)

        return carry

    lax.fori_loop(1, RING - 1, reduce_step, 0)
    vector_next(1)

    def last_copy(step, way, chain, arriving=0):
        rows = rows_of(step + RING - 1 + arriving, way)
        return remote(
            final.at[blocks(chain), rows, :], final.at[blocks(chain), rows, :],
            last_send.at[step, way, chain], last_receive.at[step, way, chain], ways[way],
        )

    def out_copy(step, way, chain):
        part = (blocks(chain), rows_of(step + RING - 1, way), slice(None))
        return pltpu.make_async_copy(final.at[part], out.at[part], out_sem.at[step, way, chain])

    for chain in range(2):
        for way in range(2):
            if chain == 0:
                pair_here(RING - 1, way)
            incoming(RING - 2, way, chain).wait_recv()
            rows = rows_of(RING - 1, way)
            final[blocks(chain), rows, :] = total_of(chain, rows)
            last_copy(0, way, chain).start()
            out_copy(0, way, chain).start()
    vector_next(2)

    def gather_step(step, carry):
        for chain in range(2):
            for way in range(2):
                last_copy(step - 1, way, chain, 1).wait_recv()
                last_copy(step, way, chain).start()
                out_copy(step, way, chain).start()
        return carry

    lax.fori_loop(1, 3, gather_step, 0)
    vector_next(3)
    lax.fori_loop(3, 5, gather_step, 0)
    vector_next(4)
    out_vectors[0] = v_sum[len(levels) - 1]
    out_vectors[1] = v_in[len(levels) - 1]
    lax.fori_loop(5, RING - 1, gather_step, 0)

    def all_sent(step, carry):
        for way in range(2):
            for chain in range(2):
                ring_copy(step, way, chain).wait_send()
        return carry

    def pair_sent(step, carry):
        for way in range(2):
            for k in range(2):
                pair_copy(step, way, k).wait_send()
        return carry

    lax.fori_loop(0, RING - 1, all_sent, 0)
    lax.fori_loop(0, RING, pair_sent, 0)
    for swap in swaps:
        swap.wait()
    for chain in range(2):
        for way in range(2):
            last_copy(RING - 2, way, chain, 1).wait_recv()
            out_copy(RING - 1, way, chain).start()

    def last_sent(step, carry):
        for way in range(2):
            for chain in range(2):
                last_copy(step, way, chain).wait_send()
        return carry

    def written(step, carry):
        for way in range(2):
            for chain in range(2):
                out_copy(step, way, chain).wait()
        return carry

    lax.fori_loop(0, RING - 1, last_sent, 0)
    lax.fori_loop(0, RING, written, 0)


def reduce_grads(grads, swapping, vectors):
    share = (SHARE, D, D)
    dma = pltpu.SemaphoreType.DMA
    return pl.pallas_call(
        reduce_kernel,
        in_specs=[ANY, ANY, ANY, ANY, VMEM],
        out_specs=(ANY, ANY, ANY, VMEM),
        out_shape=(sds(share, BF16), ROWS, ROWS, sds((2, VECTORS, D), F32)),
        scratch_shapes=[
            pltpu.VMEM((2, *share), BF16),
            pltpu.VMEM((2, *share), BF16),
            pltpu.VMEM(share, BF16),
            pltpu.VMEM(share, BF16),
            pltpu.VMEM((5, VECTORS, D), F32),
            pltpu.VMEM((5, VECTORS, D), F32),
            dma((RING, 2, 2)),
            dma((RING, 2, 2)),
            dma((RING, 2, 2)),
            dma((RING, 2, 2)),
            dma((RING - 1, 2, 2)),
            dma((RING - 1, 2, 2)),
            dma((RING - 1, 2, 2)),
            dma((RING - 1, 2, 2)),
            dma((5,)),
            dma((5,)),
            dma((2,)),
            dma((2,)),
        ],
        compiler_params=params(56, collective_id=2, has_side_effects=True),
        name="reduce_grads",
    )(*grads, *swapping, vectors)


def spread_kernel(layer, total, vectors, *refs):
    of_encoder, of_regressor, refs = refs[:4], refs[4:8], refs[8:]
    matrix, down, *picked, enc_out, reg_out, mlp_out, hidden_out = refs[:10]
    low, wide_rows, rows, sums, enc, reg, mlp, hidden, low_sem, wide_sem, rows_sem, picked_sem, sums_sem = refs[10:]
    in_sums = pltpu.make_async_copy(vectors, sums, sums_sem.at[0])
    in_sums.start()
    low_copies = [pltpu.make_async_copy(total.at[i], low.at[i], low_sem.at[i]) for i in range(SHARE)]
    for copy in low_copies:
        copy.start()
    for which, sources in enumerate((of_encoder, of_regressor)):

        @pl.when(layer[0] == which)
        def _(sources=sources):
            for k, source in enumerate(sources):
                pltpu.make_async_copy(source, rows.at[k], rows_sem.at[k]).start()

    copies = []
    in_sums.wait()
    for which in range(2):

        @pl.when(layer[0] == which)
        def _(which=which):
            enc[...] = sums[which, :6]
            reg[...] = sums[1 - which, :FFN_AT]
            for block, of in enumerate((which, 1 - which)):
                mlp[block] = sums[of, FFN_AT:HIDDEN_AT]
                for i in ALL_BLOCKS:
                    hidden[block : block + 1, columns(i)] = sums[of, HIDDEN_AT + i : HIDDEN_AT + i + 1]

    for k, (source, target) in enumerate(((enc, enc_out), (reg, reg_out), (mlp, mlp_out), (hidden, hidden_out))):
        copies.append(pltpu.make_async_copy(source, target, sums_sem.at[1 + k]))
        copies[k].start()

    for i in range(SHARE):
        low_copies[i].wait()
        wide_rows[i] = low[i].astype(F32)
        target = matrix.at[0, :, columns(i)] if i < BLOCKS else down.at[columns(i - BLOCKS), :]
        copies.append(pltpu.make_async_copy(wide_rows.at[i], target, wide_sem.at[i]))
        copies[-1].start()
    for k, target in enumerate(picked):
        pltpu.make_async_copy(of_encoder[k], rows.at[k], rows_sem.at[k]).wait()
        copies.append(pltpu.make_async_copy(rows.at[k], target, picked_sem.at[k]))
        copies[-1].start()
    for copy in copies:
        copy.wait()


def spread(layer, total, vectors, of_encoder, of_regressor):
    dma = pltpu.SemaphoreType.DMA
    return pl.pallas_call(
        spread_kernel,
        in_specs=[SMEM, *(ANY for _ in range(10))],
        out_specs=tuple(ANY for _ in range(10)),
        out_shape=(
            sds((1, D, FF), F32),
            sds((FF // 2, D), F32),
            *(ROWS for _ in range(4)),
            sds((6, D), F32),
            sds((FFN_AT, D), F32),
            sds((2, 4, D), F32),
            sds((2, FF), F32),
        ),
        scratch_shapes=[
            pltpu.VMEM((SHARE, D, D), BF16),
            pltpu.VMEM((SHARE, D, D), F32),
            pltpu.VMEM((4, CAP, D), BF16),
            pltpu.VMEM((2, VECTORS, D), F32),
            pltpu.VMEM((6, D), F32),
            pltpu.VMEM((FFN_AT, D), F32),
            pltpu.VMEM((2, 4, D), F32),
            pltpu.VMEM((2, FF), F32),
            dma((SHARE,)),
            dma((SHARE,)),
            dma((4,)),
            dma((4,)),
            dma((5,)),
        ],
        compiler_params=params(60),
        name="spread",
    )(layer, total, vectors, *of_encoder, *of_regressor)


def plain_reduce_grads(grads, swapping, vectors):
    odd = lax.rem(lax.axis_index("section"), 2)
    pair = [(0, 1), (1, 0), (2, 3), (3, 2)]
    grads = grads[0] + grads[1]
    theirs = lax.dynamic_index_in_dim(grads, 1 - odd, 0, keepdims=False)
    mine = lax.dynamic_index_in_dim(grads, odd, 0, keepdims=False)
    total = lax.psum(mine + lax.ppermute(theirs, "section", pair), "dp")
    vectors = lax.psum(vectors + lax.ppermute(vectors, "section", pair), "dp")
    return total, *map(swap_layers, swapping), jnp.stack([vectors, swap_layers(vectors)])


def swap_layers(block):
    return lax.ppermute(block, "section", [(0, 2), (1, 3), (2, 0), (3, 1)])


def to_regressor(block):
    return lax.ppermute(block, "section", [(0, 2), (1, 3)])


def to_encoder(block):
    return lax.ppermute(block, "section", [(2, 0), (3, 1)])


def body(
    vis_embed, latent_cot, reg_queries, out_cot, section_matrix, down_weight, enc_vectors, reg_vectors,
    mlp_vectors, hidden_bias, pos_table, image_lengths, vis_index, mask_index,
):
    section = lax.axis_index("section")
    odd = lax.rem(section, 2)
    is_reg = section >= 2
    layer = jnp.where(is_reg, 1, 0)
    weights = gather_weights(section_matrix, down_weight)
    r = lax.dynamic_index_in_dim(mlp_vectors, layer, 0, keepdims=False)
    c = lax.dynamic_slice_in_dim(hidden_bias, layer, 1, 0)
    packs = [(odd + 2 * i).reshape(1).astype(jnp.int32) for i in range(2)]
    vis = [lax.dynamic_slice_in_dim(vis_index, (odd + 2 * i) * CAP, CAP)[:, None] for i in range(2)]
    mask = [lax.dynamic_slice_in_dim(mask_index, (odd + 2 * i) * CAP, CAP)[:, None] for i in range(2)]

    rows_out, cot_out = lax.optimization_barrier(
        (jnp.where(is_reg, vis_embed, reg_queries), jnp.where(is_reg, latent_cot, out_cot))
    )
    incoming = swap_layers(rows_out)
    x = [vis_embed, incoming]
    queries = [incoming, reg_queries]

    def on_encoder(work, otherwise):
        return lax.cond(is_reg, otherwise, work)

    def on_regressor(work, otherwise):
        return lax.cond(is_reg, work, otherwise)

    def enc_forward(i):
        return encoder_forward(image_lengths, packs[i], x[i], enc_vectors, r, c, weights)

    def no_enc_forward():
        made = unset((ROWS, ROWS, *ENC_STATE))
        return made[0], made[1], tuple(made[2:])

    def enc_back(i, d_latents, kept, so_far):
        return encoder_back(
            image_lengths, packs[i], lat_cot[i], d_latents, x[i], kept[0], enc_vectors, r, so_far, weights, kept[2]
        )

    def reg_before():
        return tuple(
            tuple(regressor_before(image_lengths, packs[i], queries[i], vis[i], mask[i], pos_table, reg_vectors, weights))
            for i in range(2)
        )

    def no_reg_before():
        made = unset((*REG_BEFORE, *REG_BEFORE))
        return tuple(made[: len(REG_BEFORE)]), tuple(made[len(REG_BEFORE) :])

    def reg_work(i, latents, so_far):
        return lambda: regressor(
            image_lengths, packs[i], latents, queries[i], cot[i], reg_vectors, r, c, so_far, weights, before[i]
        )

    def no_reg_work():
        made = unset((ROWS, ROWS, ROWS, TOTALS, *REG_STATE))
        return (*made[:4], tuple(made[4:]))

    none = jnp.zeros((VECTORS, D), F32)
    enc1 = on_encoder(lambda: enc_forward(0), no_enc_forward)
    latents1 = to_regressor(enc1[1])
    before = on_regressor(reg_before, no_reg_before)
    swapped_cot = swap_layers(cot_out)
    lat_cot = [latent_cot, swapped_cot]
    cot = [swapped_cot, out_cot]
    enc2 = on_encoder(lambda: enc_forward(1), no_enc_forward)
    latents2 = to_regressor(enc2[1])
    reg1 = on_regressor(reg_work(0, latents1, none), no_reg_work)
    d_latents1 = to_encoder(reg1[1])
    reg2 = on_regressor(reg_work(1, latents2, reg1[3]), no_reg_work)
    d_latents2 = to_encoder(reg2[1])
    shares1, enc_totals, vis_grad1 = lax.cond(
        is_reg,
        lambda: (weight_grads(before[0], reg1[4]), *unset((TOTALS, ROWS))),
        lambda: enc_back(0, d_latents1, enc1, none)[::-1],
    )
    shares2, vectors, swapping = lax.cond(
        is_reg,
        lambda: (weight_grads(before[1], reg2[4]), reg2[3], reg1[0]),
        lambda: enc_back(1, d_latents2, enc2, enc_totals)[::-1],
    )
    reduce = reduce_grads if lax.axis_size("dp") == RING else plain_reduce_grads
    total, swapped1, swapped2, vectors = reduce((shares1, shares2), (swapping, reg1[2]), vectors)
    matrix_grad, down_grad, *others = spread(
        layer.reshape(1).astype(jnp.int32),
        total,
        vectors,
        (enc1[1], swapped1, vis_grad1, swapped2),
        (latents2, reg2[0], swapped1, reg2[2]),
    )
    return (*others[:4], matrix_grad, down_grad, *others[4:])


def solution(mesh):
    rows = P(("dp", "section"), None)
    in_specs = (
        rows, rows, rows, rows, P("section", None, None), P("section", None),
        P(), P(), P(), P(), P(), P("dp", None), P("dp"), P("dp"),
    )
    out_specs = (rows, rows, rows, rows, P("section", None, None), P("section", None), P(), P(), P(), P())
    return jax.shard_map(body, mesh=mesh, in_specs=in_specs, out_specs=out_specs, check_vma=False)
```
